32 devices in a mesh: dp: 8 (over z, y), ctx: 4 (over x, core).
Axes of the slice: x: 2, y: 2, z: 4, core: 2. Of those that a mesh axis runs over, the one named last changes fastest.
Arguments:
- tokens: bfloat16 [2, 8, 1024, 1024], P(None, 'dp', 'ctx'), may hold values from -6 to 6
- cotangent: bfloat16 [2, 8, 1024, 1024], P(None, 'dp', 'ctx'), may hold values from -6 to 6
- starts: int32 [2, 8, 1024], P(None, 'dp', 'ctx'), may hold values from 0 to 1, as said below
- norm_gain: bfloat16 [2, 1024], P(None, ('dp', 'ctx')), may hold values from 0.5 to 1.5
- qkv_weight: bfloat16 [3, 1024, 1024], P(None, ('dp', 'ctx')), may hold values from -0.1875 to 0.1875
- conv_weight: bfloat16 [12, 1024], P(None, ('dp', 'ctx')), may hold values from -3 to 3
- beta_weight: bfloat16 [1024, 8], P(('dp', 'ctx')), may hold values from -0.1875 to 0.1875
- head_gain: bfloat16 [128], P(('dp', 'ctx')), may hold values from 0.5 to 1.5
- out_weight: bfloat16 [1024, 1024], P(('dp', 'ctx')), may hold values from -0.1875 to 0.1875
- gate_up_weight: bfloat16 [2, 1024, 2816], P(None, ('dp', 'ctx')), may hold values from -0.1875 to 0.1875
- down_weight: bfloat16 [1024, 2816], P(('dp', 'ctx')), may hold values from -0.109375 to 0.109375
Outputs:
- layer_out: bfloat16 [2, 8, 1024, 1024], P(None, 'dp', 'ctx')
- input_grad: bfloat16 [2, 8, 1024, 1024], P(None, 'dp', 'ctx')
- norm_gain_grad: float32 [2, 1024], P(None, ('dp', 'ctx'))
- qkv_grad: float32 [3, 1024, 1024], P(None, ('dp', 'ctx'))
- conv_grad: float32 [12, 1024], P(None, ('dp', 'ctx'))
- beta_grad: float32 [1024, 8], P(('dp', 'ctx'))
- head_gain_grad: float32 [128], P(('dp', 'ctx'))
- out_grad: float32 [1024, 1024], P(('dp', 'ctx'))
- gate_up_grad: float32 [2, 1024, 2816], P(None, ('dp', 'ctx'))
- down_grad: float32 [1024, 2816], P(('dp', 'ctx'))
The draws below stay inside these ranges and needn't reach their ends.
Inputs may be any that keep to these rules, and one draw needn't show every extreme that they name: `starts`: position 0 of every sequence is 1. For each sequence row s, in one micro-batch chosen by the seed no other position is 1, so that one document fills that whole sequence.
All inputs are finite; a program needn't handle non-finite values.
Results may differ from the reference program's by a relative error of at most 0.02.
Values may be sent and summed in bfloat16 or wider, within the bound.
A program may use at most 256 MiB of HBM per device.

```python
import math
import jax
import jax.numpy as jnp
from jax import lax

D = 1024
H = 8
HD = 128
FF = 2816
CONV = 4
CH = 64
LEN = 1024
MB = 2
SEQS = 8


def draw_starts(key, part):
    rate_key, mark_key, pick_key = jax.random.split(key, 3)
    exponent = jax.random.randint(rate_key, (MB, SEQS, 1), 3, 10)
    spacing = jnp.left_shift(jnp.ones((MB, SEQS, 1), jnp.int32), exponent.astype(jnp.int32))
    drawn = jax.random.randint(mark_key, (MB, SEQS, LEN), 0, 1 << 20)
    marked = (drawn % spacing == 0).astype(jnp.int32)
    opening = (jnp.arange(LEN).astype(jnp.int32) == 0).astype(jnp.int32)[None, None, :]
    chosen = jax.random.randint(pick_key, (1, SEQS, 1), 0, MB)
    single = jnp.arange(MB).astype(jnp.int32)[:, None, None] == chosen
    return jnp.where(single, opening, jnp.maximum(marked, opening)).astype(jnp.int32)


def steps_of(own_key, dims, cuts, least, high):
    gain, own = 1.0, jax.random.fold_in(own_key, 6)
    for axis_at, shards_of in cuts:
        steps = jnp.exp(jax.random.uniform(jax.random.fold_in(own, axis_at), (shards_of,), jnp.float32, least / len(cuts), high / len(cuts)))
        gain = gain * jnp.repeat(steps, dims[axis_at] // shards_of).reshape([-1 if axis == axis_at else 1 for axis in range(len(dims))])
    return gain


def scatter_about(key, dims, deviation, bound, shards=(), kind=jnp.bfloat16):
    level = steps_of(key, dims, shards, -0.22, 0.18) if shards else 1.0
    array = jax.random.normal(key, dims, jnp.float32) * deviation * level
    return jnp.minimum(jnp.maximum(array, -bound), bound).astype(kind)


def setup_inputs(seed: int = 0) -> dict:
    arg_keys = jax.random.split(jax.random.key(seed), 12)
    tokens = scatter_about(arg_keys[0], (MB, SEQS, LEN, D), 1.0, 6.0, ((1, 8), (2, 4)))
    cotangent = scatter_about(arg_keys[1], (MB, SEQS, LEN, D), 1.0, 6.0, ((1, 8), (2, 4)))
    starts = draw_starts(jax.random.fold_in(arg_keys[11], 71), 0)
    norm_gain = jnp.clip(1.0 + 0.1 * jax.random.normal(arg_keys[3], (2, D), jnp.float32), 0.5, 1.5).astype(jnp.bfloat16)
    qkv_weight = scatter_about(arg_keys[4], (3, D, D), D ** -0.5, 0.1875, ((1, 32),))
    conv_weight = scatter_about(arg_keys[5], (3 * CONV, D), CONV ** -0.5, 3.0, ((1, 32),))
    beta_weight = scatter_about(arg_keys[6], (D, H), D ** -0.5, 0.1875, ((0, 32),))
    head_gain = jnp.clip(1.0 + 0.1 * jax.random.normal(arg_keys[7], (HD,), jnp.float32), 0.5, 1.5).astype(jnp.bfloat16)
    out_weight = scatter_about(arg_keys[8], (D, D), D ** -0.5, 0.1875, ((0, 32),))
    gate_up_weight = scatter_about(arg_keys[9], (2, D, FF), D ** -0.5, 0.1875, ((1, 32),))
    down_weight = scatter_about(arg_keys[10], (D, FF), FF ** -0.5, 0.109375, ((0, 32),))
    return dict(tokens=tokens, cotangent=cotangent, starts=starts, norm_gain=norm_gain, qkv_weight=qkv_weight, conv_weight=conv_weight, beta_weight=beta_weight, head_gain=head_gain, out_weight=out_weight, gate_up_weight=gate_up_weight, down_weight=down_weight)


highest = lax.Precision.HIGHEST

@jax.custom_vjp
def low(v):
    return lax.optimization_barrier(v.astype(jnp.bfloat16)).astype(jnp.float32)

@jax.custom_vjp
def low_back(v):
    return v

def low_keep(v):
    return (low(v), None)

def low_pass(kept, grad):
    return (grad,)

def back_keep(v):
    return (v, None)

def back_low(kept, grad):
    return (low(grad),)
low.defvjp(low_keep, low_pass)
low_back.defvjp(back_keep, back_low)

def rms_norm(values, gain_vec, epsilon):
    return values * lax.rsqrt(lax.optimization_barrier(jnp.mean(values * values, axis=-1, keepdims=True)) + epsilon) * gain_vec

def unit_rows(values):
    return values * lax.rsqrt(lax.optimization_barrier(jnp.sum(values * values, axis=-1, keepdims=True)) + 1e-06)

def conv_mix(projected, conv_taps, segment):
    length = projected.shape[1]
    mixed = projected * conv_taps[CONV - 1]
    for offset in range(1, CONV):
        moved = jnp.pad(projected, ((0, 0), (offset, 0), (0, 0)))[:, :length]
        moved_seg = jnp.pad(segment, ((0, 0), (offset, 0)), constant_values=-1)[:, :length]
        keep_mask = (moved_seg == segment).astype(jnp.float32)[..., None]
        mixed = mixed + conv_taps[CONV - 1 - offset] * moved * keep_mask
    return mixed

def delta_span(carry, block_in):
    state_now, last_seg = carry
    queries, key_rows, value_rows, strength, segment = block_in
    carried = (segment == last_seg[:, None]).astype(jnp.float32)
    same_doc = (segment[:, :, None] == segment[:, None, :]).astype(jnp.float32)[:, None]
    strict = jnp.tril(jnp.ones((CH, CH), jnp.float32), -1)
    upto = jnp.tril(jnp.ones((CH, CH), jnp.float32))
    keyed = jnp.einsum('ghid,ghjd->ghij', key_rows, key_rows, precision=highest)
    lower_part = strength[..., None] * keyed * same_doc * strict
    known = jnp.einsum('ghid,ghde->ghie', key_rows, state_now, precision=highest)
    right_side = strength[..., None] * (value_rows - carried[:, None, :, None] * known)
    solved = jax.scipy.linalg.solve_triangular(jnp.eye(CH, dtype=jnp.float32) + lower_part, right_side, lower=True, unit_diagonal=True)
    scores = jnp.einsum('ghid,ghjd->ghij', queries, key_rows, precision=highest) * same_doc * upto
    output = carried[:, None, :, None] * jnp.einsum('ghid,ghde->ghie', queries, state_now, precision=highest)
    output = output + jnp.einsum('ghij,ghje->ghie', scores, solved, precision=highest)
    ending = (segment == segment[:, -1:]).astype(jnp.float32)
    state_next = carried[:, -1][:, None, None, None] * state_now + jnp.einsum('ghid,ghie->ghde', key_rows, ending[:, None, :, None] * solved, precision=highest)
    return ((state_next, segment[:, -1]), output)

def block_forward(tokens, segment, params):
    norm_gain, qkv_weight, conv_weight, beta_weight, head_gain, out_weight, gate_up_weight, down_weight = params
    group_size, length = (tokens.shape[0], tokens.shape[1])
    spans = length // CH
    normed = low(rms_norm(tokens, norm_gain[0], 1e-05))
    projected = low(low_back(jnp.einsum('gtd,jde->gtje', normed, qkv_weight, precision=highest)))
    projected = projected.reshape(group_size, length, 3 * D)
    conv_taps = conv_weight.reshape(3, CONV, D).transpose(1, 0, 2).reshape(CONV, 3 * D)
    mixed = jax.nn.silu(conv_mix(projected, conv_taps, segment)).reshape(group_size, length, 3, H, HD)
    queries = low(unit_rows(mixed[:, :, 0]))
    key_rows = low(unit_rows(mixed[:, :, 1]))
    value_rows = low(mixed[:, :, 2])
    strength = jax.nn.sigmoid(low_back(jnp.einsum('gtd,dh->gth', normed, beta_weight, precision=highest)))

    def blocked(values):
        return jnp.moveaxis(values.reshape(group_size, spans, CH, H, values.shape[-1]), (1, 3), (0, 2))
    start_carry = (jnp.zeros((group_size, H, HD, HD), jnp.float32), jnp.full((group_size,), -1, jnp.int32))
    seg_blocks = jnp.moveaxis(segment.reshape(group_size, spans, CH), 1, 0)
    unused, outputs = lax.scan(jax.checkpoint(delta_span), start_carry, (blocked(queries), blocked(key_rows), blocked(value_rows), blocked(strength[..., None])[..., 0], seg_blocks))
    head_out = jnp.moveaxis(outputs, (0, 2), (1, 3)).reshape(group_size, length, H, HD)
    headed = low(rms_norm(head_out, head_gain, 1e-05)).reshape(group_size, length, D)
    attended = low_back(jnp.einsum('gtd,de->gte', headed, out_weight, precision=highest))
    residual = tokens + attended
    normed2 = low(rms_norm(residual, norm_gain[1], 1e-05))
    gate_up = low_back(jnp.einsum('gtd,jdf->gtjf', normed2, gate_up_weight, precision=highest))
    hidden = low(jax.nn.silu(gate_up[:, :, 0]) * gate_up[:, :, 1])
    ffn_out = low_back(jnp.einsum('gtf,df->gtd', hidden, down_weight, precision=highest))
    return residual + ffn_out

def reference(tokens, cotangent, starts, norm_gain, qkv_weight, conv_weight, beta_weight, head_gain, out_weight, gate_up_weight, down_weight):
    params = tuple((weight.astype(jnp.float32) for weight in (norm_gain, qkv_weight, conv_weight, beta_weight, head_gain, out_weight, gate_up_weight, down_weight)))
    seq_count = MB * SEQS
    group_size = math.gcd(seq_count, max(1, 4096 // LEN))
    token_groups = tokens.astype(jnp.float32).reshape(seq_count // group_size, group_size, LEN, D)
    grad_groups = cotangent.astype(jnp.float32).reshape(seq_count // group_size, group_size, LEN, D)
    start_groups = starts.reshape(seq_count // group_size, group_size, LEN)

    def group_step(totals, block_in):
        token_block, grad_block, start_block = block_in
        segment = jnp.cumsum(start_block, axis=1).astype(jnp.int32)
        result, pull_back = jax.vjp(lambda token_in, param_in: block_forward(token_in, segment, param_in), token_block, params)
        grad_tokens, grad_params = pull_back(grad_block)
        totals = tuple((total_now + grad_now for total_now, grad_now in zip(totals, grad_params)))
        return (totals, (result.astype(jnp.bfloat16), grad_tokens.astype(jnp.bfloat16)))
    zero_totals = tuple((jnp.zeros_like(weight) for weight in params))
    grads, (results, input_grads) = lax.scan(group_step, zero_totals, (token_groups, grad_groups, start_groups))
    return (results.reshape(MB, SEQS, LEN, D), input_grads.reshape(MB, SEQS, LEN, D), grads[0], grads[1], grads[2], grads[3], grads[4], grads[5], grads[6], grads[7])
```

```python
import functools

import jax
import jax.numpy as jnp
from jax import lax
from jax.experimental import pallas as pl
from jax.experimental.pallas import tpu as pltpu
from jax.sharding import PartitionSpec as P

MESH = pl.DeviceIdType.MESH
ANY = pl.ANY
VM = pltpu.VMEM
MIB = 1 << 20
f32 = jnp.float32
bf16 = jnp.bfloat16


def route(block, order):
    dz, fx, fy = block
    rank = {dim: place for place, dim in enumerate(order)}
    last = max([-1] + [rank[d] for d, on in (("z", dz), ("x", fx), ("y", fy)) if on])
    hops = []
    for dim in order:
        if dim == "z":
            if dz == 0 and rank["z"] > last:
                hops += ["up", "dn"]
            elif dz != 0 and last == rank["z"]:
                hops.append("up" if dz < 0 else "dn")
        elif rank[dim] > last:
            hops.append(dim)
    came = None
    if last >= 0:
        came = order[last]
        if came == "z":
            came = "up" if dz < 0 else "dn"
    return hops, came


def blocks_of(levels):
    named = [
        (dz, fx, fy)
        for dz in range(1 - levels, levels)
        for fx in (0, 1)
        for fy in (0, 1)
    ]
    return sorted(named, key=lambda b: (abs(b[0]) + b[1] + b[2], abs(b[0]), b))


class Place:
    def __init__(self, levels):
        i = lax.axis_index("dp")
        c = lax.axis_index("ctx")
        self.levels = levels
        self.i, self.c = i, c
        self.z, self.y = i // 2, i % 2
        self.x, self.t = c // 2, c % 2

    def device(self, hop):
        i, c = self.i, self.c
        if hop == "x":
            return {"dp": i, "ctx": (1 - self.x) * 2 + self.t}
        if hop == "y":
            return {"dp": self.z * 2 + 1 - self.y, "ctx": c}
        if hop == "up":
            return {"dp": i + 2, "ctx": c}
        if hop == "dn":
            return {"dp": i - 2, "ctx": c}
        return {"dp": i, "ctx": self.x * 2 + 1 - self.t}

    def valid(self, block, hop=None):
        dz = block[0]
        terms = []
        if dz > 0:
            terms.append(self.z + dz < self.levels)
        if dz < 0:
            terms.append(self.z + dz >= 0)
        if hop == "up" and dz <= 0:
            terms.append(self.z + 1 < self.levels)
        if hop == "dn" and dz >= 0:
            terms.append(self.z >= 1)
        if not terms:
            return None
        return functools.reduce(jnp.logical_and, terms)

    def level(self, block):
        return self.z + block[0]

    def shard(self, block, half):
        z = self.z + block[0]
        y = 1 - self.y if block[2] else self.y
        x = 1 - self.x if block[1] else self.x
        return ((z * 2 + y) * 2 + x) * 2 + half

    def meet(self, hops):
        barrier = pltpu.get_barrier_semaphore()
        count = 0
        for hop in hops:
            def greet(hop=hop):
                pl.semaphore_signal(
                    barrier, inc=1, device_id=self.device(hop), device_id_type=MESH
                )
            if hop in ("up", "dn"):
                here = (self.z + 1 < self.levels) if hop == "up" else (self.z >= 1)
                pl.when(here)(greet)
                count = count + here.astype(jnp.int32)
            else:
                greet()
                count = count + 1
        pl.semaphore_wait(barrier, count)


def when(condition, action):
    if condition is None:
        action()
    else:
        pl.when(condition)(action)


def send_slots(order):
    table = {}
    for fx in (0, 1):
        for fy in (0, 1):
            for dz in (-1, 0, 1):
                for hop in route((dz, fx, fy), order)[0]:
                    table.setdefault((hop, fx, fy), len(table))
    return table


class Gather:
    def __init__(self, place, src, ref, half, order, send_sem, recv_sem):
        self.place, self.src, self.ref, self.half = place, src, ref, half
        self.order = order
        self.slots = send_slots(order)
        self.send_sem, self.recv_sem = send_sem, recv_sem

    @staticmethod
    def sems(levels, order):
        return len(send_slots(order)) * levels, 4 * levels

    def copy(self, block, hop):
        place = self.place
        dz, fx, fy = block
        where = place.shard(block, self.half)
        level = place.level(block)
        there = (fx ^ (hop == "x"), fy ^ (hop == "y"))
        return pltpu.make_async_remote_copy(
            src_ref=self.ref.at[where],
            dst_ref=self.ref.at[where],
            send_sem=self.send_sem.at[self.slots[hop, fx, fy] * place.levels + level],
            recv_sem=self.recv_sem.at[(there[0] * 2 + there[1]) * place.levels + level],
            device_id=place.device(hop),
            device_id_type=MESH,
        )

    def arrival(self, block):
        place = self.place
        dz, fx, fy = block
        where = place.shard(block, self.half)
        came = route(block, self.order)[1]
        back = {"up": "dn", "dn": "up"}.get(came, came)
        return pltpu.make_async_remote_copy(
            src_ref=self.ref.at[where],
            dst_ref=self.ref.at[where],
            send_sem=self.send_sem.at[0],
            recv_sem=self.recv_sem.at[(fx * 2 + fy) * place.levels + place.level(block)],
            device_id=place.device(back),
            device_id_type=MESH,
        )

    def wait(self, block):
        when(self.place.valid(block), lambda: self.arrival(block).wait_recv())

    def pass_on(self, block):
        for hop in route(block, self.order)[0]:
            when(self.place.valid(block, hop), lambda hop=hop: self.copy(block, hop).start())

    def drain(self, blocks):
        for block in blocks:
            for hop in route(block, self.order)[0]:
                when(
                    self.place.valid(block, hop),
                    lambda hop=hop: self.copy(block, hop).wait_send(),
                )


class Scatter:
    def __init__(self, place, ref, room, final, half, order, send_sem, recv_sem):
        self.place, self.ref, self.room, self.final = place, ref, room, final
        self.half, self.order = half, order
        self.slots = send_slots(order)
        self.send_sem, self.recv_sem = send_sem, recv_sem

    @staticmethod
    def slots_of(levels, order):
        return len(send_slots(order)) * levels, 4 * levels

    def slot(self, block, hop):
        return self.slots[hop, block[1], block[2]] * self.place.levels + self.place.level(block)

    def copy(self, block, src):
        place = self.place
        dz, fx, fy = block
        came = route(block, self.order)[1]
        back = {"up": "dn", "dn": "up"}.get(came, came)
        key = (came, fx ^ (came == "x"), fy ^ (came == "y"))
        slot = self.slots[key] * place.levels + place.level(block)
        return pltpu.make_async_remote_copy(
            src_ref=src,
            dst_ref=self.room.at[slot],
            send_sem=self.send_sem.at[(fx * 2 + fy) * place.levels + place.level(block)],
            recv_sem=self.recv_sem.at[slot],
            device_id=place.device(back),
            device_id_type=MESH,
        )

    def arrive(self, block, hop):
        slot = self.slot(block, hop)
        pltpu.make_async_remote_copy(
            src_ref=self.room.at[slot],
            dst_ref=self.room.at[slot],
            send_sem=self.send_sem.at[0],
            recv_sem=self.recv_sem.at[slot],
            device_id=self.place.device(hop),
            device_id_type=MESH,
        ).wait_recv()

    def total(self, block, hops, put):
        where = self.place.shard(block, self.half)
        slots = [self.slot(block, hop) for hop in hops]
        rows = self.ref.shape[1]
        step = min(16, rows)

        def one(k, carry):
            at = pl.ds(pl.multiple_of(k * step, step), step)
            value = self.ref[where, at, :].astype(f32)
            for slot in slots:
                value = value + self.room[slot, at, :].astype(f32)
            put(at, value)
            return carry

        lax.fori_loop(0, rows // step, one, 0)

    def branch(self, maybe, using, go):
        if not maybe:
            go(using)
            return
        hop, place = maybe[0], self.place
        here = place.z + 1 < place.levels if hop == "up" else place.z >= 1
        pl.when(here)(lambda: self.branch(maybe[1:], using + [hop], go))
        pl.when(jnp.logical_not(here))(lambda: self.branch(maybe[1:], using, go))

    def forward(self, block):
        place = self.place
        hops = route(block, self.order)[0]
        sure = [h for h in hops if h in ("x", "y")]
        maybe = [h for h in hops if h not in ("x", "y")]

        def go(using):
            for hop in using:
                self.arrive(block, hop)
            if not using:
                self.copy(block, self.ref.at[place.shard(block, self.half)]).start()
                return
            slot = self.slot(block, using[0])

            def put(at, value):
                self.room[slot, at, :] = value.astype(bf16)

            self.total(block, using, put)
            self.copy(block, self.room.at[slot]).start()

        def both():
            self.branch(maybe, sure, go)

        when(place.valid(block), both)

    def finish(self):
        own = (0, 0, 0)
        place = self.place
        hops = route(own, self.order)[0]
        sure = [h for h in hops if h in ("x", "y")]
        for hop in sure:
            self.arrive(own, hop)

        def put(at, value):
            self.final[self.half, at, :] = value

        self.total(own, sure, put)
        for hop in hops:
            if hop in sure:
                continue

            def add(hop=hop):
                self.arrive(own, hop)
                slot = self.slot(own, hop)
                self.final[self.half] = self.final[self.half] + self.room[slot].astype(f32)

            when(place.valid(own, hop), add)

    def drain(self, blocks):
        for block in blocks:
            if block == (0, 0, 0):
                continue
            when(
                self.place.valid(block),
                lambda block=block: self.copy(
                    block, self.ref.at[self.place.shard(block, self.half)]
                ).wait_send(),
            )


HD = 128
CONV = 4
SPAN = 128


def mm(a, b):
    return jnp.dot(a, b, preferred_element_type=f32)


def mm_nt(a, b):
    return lax.dot_general(a, b, (((1,), (1,)), ((), ())), preferred_element_type=f32)


def mm_tn(a, b):
    return lax.dot_general(a, b, (((0,), (0,)), ((), ())), preferred_element_type=f32)


def lanes(h):
    return pl.ds(pl.multiple_of(h * HD, HD), HD)


def set_masks(segc, keep):
    rows = lax.broadcasted_iota(jnp.int32, segc.shape, 0)
    seg = segc[...]
    for o in range(1, CONV):
        same = (pltpu.roll(seg, o, 0) == seg) & (rows >= o)
        keep[o - 1] = same.astype(f32)


def shifted(value, keep, o):
    return value if o == 0 else pltpu.roll(value, o, 0) * keep[o - 1]


def conv_of(proj, taps, keep, j, h, heads):
    at = lanes(j * heads + h)
    value = proj[:, at].astype(f32)
    total = taps[pl.ds(j * CONV + CONV - 1, 1), lanes(h)] * value
    for o in range(1, CONV):
        total = total + taps[pl.ds(j * CONV + CONV - 1 - o, 1), lanes(h)] * shifted(value, keep, o)
    return total


def span_masks(segc, segr, n):
    at = slice(n * SPAN, (n + 1) * SPAN)
    col = segc[at, :]
    same = col == jnp.broadcast_to(segr[0:1, at], (SPAN, SPAN))
    if n:
        carried = (col == segc[n * SPAN - 1 : n * SPAN, :]).astype(f32)
    else:
        carried = jnp.zeros((SPAN, HD), f32)
    ending = (col == col[SPAN - 1 : SPAN, :]).astype(f32)
    return carried, same, ending


def iotas():
    i = lax.broadcasted_iota(jnp.int32, (SPAN, SPAN), 0)
    j = lax.broadcasted_iota(jnp.int32, (SPAN, SPAN), 1)
    return i, j


def unit_inverses(lowers):
    i, j = iotas()
    apart = i ^ j
    invs = [jnp.where(apart == 1, -low, 0.0) for low in lowers]
    size, bits = 2, 1
    while size < SPAN:
        pairs = lax.shift_right_logical(apart, bits) == 1
        part = [jnp.where(pairs, low, 0.0) for low in lowers]
        small = [inv.astype(bf16) for inv in invs]
        left = [p + mm(s, p.astype(bf16)) for p, s in zip(part, small)]
        both = [w + mm(w.astype(bf16), s) for w, s in zip(left, small)]
        invs = [inv - b for inv, b in zip(invs, both)]
        size, bits = size * 2, bits + 1
    return invs


def forward_kernel(heads, proj, logit, taps, segc, segr, gain,
                   headed, out, qs, ks, vs, fs, ws, ns, ps, ss,
                   keep, us, cqs):
    spans = segc.shape[0] // SPAN
    set_masks(segc, keep)
    i, j = iotas()

    def prepare(h, carry):
        mixed = []
        for which in range(3):
            value = conv_of(proj, taps, keep, which, h, heads)
            mixed.append(value * jax.nn.sigmoid(value))
        for which, dest in ((0, qs), (1, ks)):
            w = mixed[which]
            unit = w * lax.rsqrt(jnp.sum(w * w, axis=-1, keepdims=True) + 1e-6)
            dest[:, lanes(h)] = unit.astype(bf16)
        vs[:, lanes(h)] = mixed[2].astype(bf16)
        lowers, rights = [], []
        for n in range(spans):
            at = slice(n * SPAN, (n + 1) * SPAN)
            k = ks[at, lanes(h)]
            q = qs[at, lanes(h)]
            v = vs[at, lanes(h)]
            beta = jax.nn.sigmoid(logit[at, lanes(h)])
            carried, same, ending = span_masks(segc, segr, n)
            lowers.append(jnp.where(same & (i > j), beta * mm_nt(k, k), 0.0))
            ps[h * spans + n] = jnp.where(same & (i >= j), mm_nt(q, k), 0.0).astype(bf16)
            cqs[at, lanes(h)] = (carried * q.astype(f32)).astype(bf16)
            rights.append(
                jnp.concatenate(
                    [beta * v.astype(f32), (beta * carried) * k.astype(f32)], axis=1
                )
            )
        for n, inv in enumerate(unit_inverses(lowers)):
            at = slice(n * SPAN, (n + 1) * SPAN)
            small = inv.astype(bf16)
            ns[h * spans + n] = small
            both = rights[n] + mm(small, rights[n].astype(bf16))
            us[at, lanes(h)] = both[:, :HD]
            ws[at, lanes(h)] = both[:, HD:].astype(bf16)
        return carry

    lax.fori_loop(0, heads, prepare, 0)
    states = [jnp.zeros((HD, HD), f32) for _ in range(heads)]
    for n in range(spans):
        at = slice(n * SPAN, (n + 1) * SPAN)
        carried, same, ending = span_masks(segc, segr, n)
        for h in range(heads):
            head = slice(h * HD, (h + 1) * HD)
            state = states[h].astype(bf16)
            ss[h * spans + n] = state
            seen = mm(jnp.concatenate([ws[at, head], cqs[at, head]], axis=0), state)
            fresh = us[at, head] - seen[:SPAN]
            small = fresh.astype(bf16)
            fs[at, head] = small
            out[at, head] = seen[SPAN:] + mm(ps[h * spans + n], small)
            states[h] = carried[SPAN - 1 : SPAN, :] * states[h] + mm_tn(
                ks[at, head], (ending * fresh).astype(bf16)
            )
    for h in range(heads):
        head = slice(h * HD, (h + 1) * HD)
        o = out[:, head]
        scale = lax.rsqrt(jnp.mean(o * o, axis=-1, keepdims=True) + 1e-5)
        headed[:, head] = (o * scale * gain[0:1, :]).astype(bf16)


def delta_forward(proj, logit, taps, segc, segr, gain):
    rows, width = logit.shape
    heads = width // HD
    spans = rows // SPAN
    wide = jax.ShapeDtypeStruct((rows, width), bf16)
    square = jax.ShapeDtypeStruct((heads * spans, SPAN, SPAN), bf16)
    return pl.pallas_call(
        functools.partial(forward_kernel, heads),
        out_shape=[wide, jax.ShapeDtypeStruct((rows, width), f32)] + [wide] * 5 + [square] * 3,
        in_specs=[pl.BlockSpec(memory_space=VM)] * 6,
        out_specs=[pl.BlockSpec(memory_space=VM)] * 10,
        scratch_shapes=[
            VM((CONV - 1, rows, HD), f32),
            VM((rows, width), f32),
            VM((rows, width), bf16),
        ],
        compiler_params=pltpu.CompilerParams(vmem_limit_bytes=56 * MIB),
    )(proj, logit, taps, segc, segr, gain)


def backward_kernel(heads, dheaded, out, proj, logit, taps, segc, segr, gain,
                    qs, ks, vs, fs, ws, ns, ps, ss,
                    dproj, dtaps, dgain,
                    keep, douts, xs, hs, gs, ys, dqs, dks, dvs):
    spans = segc.shape[0] // SPAN
    set_masks(segc, keep)
    i, j = iotas()
    first = lax.broadcasted_iota(jnp.int32, (SPAN, HD), 1) == 0

    def norm_back(h, dgain_sum):
        o = out[:, lanes(h)]
        dy = dheaded[:, lanes(h)].astype(f32)
        r = lax.rsqrt(jnp.mean(o * o, axis=-1, keepdims=True) + 1e-5)
        scaled = dy * gain[0:1, :]
        dout = r * scaled - o * (r * r * r * jnp.mean(scaled * o, axis=-1, keepdims=True))
        douts[:, lanes(h)] = dout
        dgain_sum = dgain_sum + jnp.sum(dy * o * r, axis=0, keepdims=True)
        for n in range(spans):
            at = slice(n * SPAN, (n + 1) * SPAN)
            carried, same, ending = span_masks(segc, segr, n)
            small = dout[at].astype(bf16)
            x = mm_tn(ps[h * spans + n], small)
            xs[at, lanes(h)] = x
            cdout = (carried * dout[at]).astype(bf16)
            hs[h * spans + n] = mm_tn(qs[at, lanes(h)], cdout) - mm_tn(
                ws[at, lanes(h)], x.astype(bf16)
            )
        return dgain_sum

    dgain_sum = lax.fori_loop(0, heads, norm_back, jnp.zeros((1, HD), f32))
    dgain[...] = jnp.broadcast_to(dgain_sum, dgain.shape)

    grads = [jnp.zeros((HD, HD), f32) for _ in range(heads)]
    for n in reversed(range(spans)):
        at = slice(n * SPAN, (n + 1) * SPAN)
        carried, same, ending = span_masks(segc, segr, n)
        for h in range(heads):
            head = slice(h * HD, (h + 1) * HD)
            g = grads[h].astype(bf16)
            gs[h * spans + n] = g
            y = ending * mm(ks[at, head], g)
            ys[at, head] = y.astype(bf16)
            if n:
                grads[h] = (
                    carried[SPAN - 1 : SPAN, :] * grads[h]
                    - mm_tn(ws[at, head], y.astype(bf16))
                    + hs[h * spans + n]
                )

    def pull(h, carry):
        head = lanes(h)
        for n in range(spans):
            at = slice(n * SPAN, (n + 1) * SPAN)
            carried, same, ending = span_masks(segc, segr, n)
            which = h * spans + n
            q, k, v, f = qs[at, head], ks[at, head], vs[at, head], fs[at, head]
            state, g, p, inv = ss[which], gs[which], ps[which], ns[which]
            beta = jax.nn.sigmoid(logit[at, head])
            dout = douts[at, head]
            small = dout.astype(bf16)
            df = xs[at, head] + ys[at, head].astype(f32)
            z = df + mm_tn(inv, df.astype(bf16))
            zb = z.astype(bf16)
            dp = jnp.where(same & (i >= j), mm_nt(small, f), 0.0).astype(bf16)
            dl = jnp.where(same & (i > j), -mm_nt(zb, f), 0.0)
            known = v.astype(f32) - carried * mm(k, state)
            dbeta = jnp.sum(z * known + dl * mm_nt(k, k), axis=-1, keepdims=True)
            b = beta[:, 0:1]
            dlogit = dbeta * b * (1.0 - b)
            dproj[at, pl.ds(pl.multiple_of((3 * heads + h) * HD, HD), HD)] = jnp.where(
                first, jnp.broadcast_to(dlogit, (SPAN, HD)), 0.0
            ).astype(bf16)
            e = (beta * dl).astype(bf16)
            dqs[at, :] = carried * mm_nt(small, state) + mm(dp, k)
            dvs[at, :] = beta * z
            dks[at, :] = (
                mm(e, k)
                + mm_tn(e, k)
                + mm_tn(dp, q)
                - (carried * beta) * mm_nt(zb, state)
                + ending * mm_nt(f, g)
            )
        for which, dref in ((0, dqs), (1, dks), (2, dvs)):
            c = conv_of(proj, taps, keep, which, h, heads)
            s = jax.nn.sigmoid(c)
            d = dref[...]
            if which < 2:
                w = c * s
                r = lax.rsqrt(jnp.sum(w * w, axis=-1, keepdims=True) + 1e-6)
                d = r * d - w * (r * r * r * jnp.sum(w * d, axis=-1, keepdims=True))
            dc = d * (s * (1.0 + c * (1.0 - s)))
            at = lanes(which * heads + h)
            value = proj[:, at].astype(f32)
            total = None
            rows = segc.shape[0]
            for o in range(CONV):
                row = which * CONV + CONV - 1 - o
                tap = taps[pl.ds(row, 1), lanes(h)]
                dtaps[pl.ds(row, 1), lanes(h)] = jnp.sum(
                    dc * shifted(value, keep, o), axis=0, keepdims=True
                )
                if o == 0:
                    total = tap * dc
                else:
                    total = total + tap * pltpu.roll(dc * keep[o - 1], rows - o, 0)
            dproj[:, at] = total.astype(bf16)
        return carry

    lax.fori_loop(0, heads, pull, 0)


def delta_backward(dheaded, out, proj, logit, taps, segc, segr, gain, saved):
    rows, width = logit.shape
    heads = width // HD
    spans = rows // SPAN
    return pl.pallas_call(
        functools.partial(backward_kernel, heads),
        out_shape=[
            jax.ShapeDtypeStruct((rows, 4 * width), bf16),
            jax.ShapeDtypeStruct(taps.shape, f32),
            jax.ShapeDtypeStruct((8, HD), f32),
        ],
        in_specs=[pl.BlockSpec(memory_space=VM)] * 16,
        out_specs=[pl.BlockSpec(memory_space=VM)] * 3,
        scratch_shapes=[
            VM((CONV - 1, rows, HD), f32),
            VM((rows, width), f32),
            VM((rows, width), f32),
            VM((heads * spans, HD, HD), f32),
            VM((heads * spans, HD, HD), bf16),
            VM((rows, width), bf16),
            VM((rows, HD), f32),
            VM((rows, HD), f32),
            VM((rows, HD), f32),
        ],
        compiler_params=pltpu.CompilerParams(vmem_limit_bytes=56 * MIB),
    )(dheaded, out, proj, logit, taps, segc, segr, gain, *saved)


STREAMS = (
    (0, 0, "zxy"),
    (0, 1, "zyx"),
    (1, 0, "zxy"),
    (1, 1, "zyx"),
    (2, 0, "xyz"),
    (2, 1, "yxz"),
)
NEIGHBOURS = ("x", "y", "up", "dn", "core")


def gather_kernel(levels, cut, *refs):
    w_in, p_in = refs[:3], refs[3:6]
    w_out, p_out, wo = refs[6:9], refs[9:12], refs[12]
    loc_sem, mate_sem, mate_rsem = refs[13:16]
    sems = refs[16:]
    pc = Place(levels)
    pc.meet(NEIGHBOURS)
    streams = [
        Gather(pc, None, w_out[a], half, order, sems[2 * k], sems[2 * k + 1])
        for k, (a, half, order) in enumerate(STREAMS)
    ]
    own = pc.shard((0, 0, 0), pc.t)
    mate = pc.device("core")
    started = []

    def send(src, dst, k, hop="core"):
        copy = pltpu.make_async_remote_copy(
            src_ref=src,
            dst_ref=dst,
            send_sem=mate_sem.at[k],
            recv_sem=mate_rsem.at[k],
            device_id=pc.device(hop),
            device_id_type=MESH,
        )
        copy.start()
        return copy

    def local(src, dst, k):
        copy = pltpu.make_async_copy(src, dst, loc_sem.at[k])
        copy.start()
        return copy

    for a in range(3):
        started.append(local(w_in[a].at[pc.t], w_out[a].at[own], a))
        started.append(send(w_in[a].at[1 - pc.t], w_out[a].at[own], a))
    for copy in started:
        copy.wait()
    order = blocks_of(levels)
    start = (0, 0, 0)
    for stream in streams:
        stream.pass_on(start)
    pieces, crossing = [], []
    for a in range(3):
        pieces.append(local(p_in[a].at[pc.x], p_out[a].at[pc.c], 3 + a))
        pieces.append(send(p_in[a].at[pc.x], p_out[a].at[pc.c], 3 + a))
        crossing.append(send(p_in[a].at[1 - pc.x], p_out[a].at[pc.c], 6 + a, "x"))
    for block in order:
        for stream in streams:
            if block != start and route(block, stream.order)[0]:
                stream.wait(block)
                stream.pass_on(block)
    far = (1 - pc.x) * 2 + pc.t
    for a in range(3):
        crossing[a].wait()
        pieces.append(send(p_out[a].at[far], p_out[a].at[far], 9 + a))
    for block in order:
        for stream in streams:
            if block != start and not route(block, stream.order)[0]:
                stream.wait(block)
    shards = w_out[0].shape[0] // 2
    half = wo.shape[-1] // 2
    mine = pl.ds(pl.multiple_of(pc.t * half, half), half)
    rows = lambda t: pl.ds(pl.multiple_of(t * shards, shards), shards)
    pieces.append(
        local(w_out[0].at[rows(pc.t), :, pl.ds(cut, half)], wo.at[:, :, mine], 6)
    )
    pieces.append(
        send(w_out[0].at[rows(1 - pc.t), :, pl.ds(cut, half)], wo.at[:, :, mine], 12)
    )
    for stream in streams:
        stream.drain(order)
    for copy in pieces:
        copy.wait()


def gather(weights, pieces, cut, levels):
    shards = levels * 8
    ctx = 4
    sems = []
    for a, half, order in STREAMS:
        sent, got = Gather.sems(levels, order)
        sems += [pltpu.SemaphoreType.DMA((sent,)), pltpu.SemaphoreType.DMA((got,))]
    rows = weights[0].shape[1]
    outs = [jax.ShapeDtypeStruct((shards,) + w.shape[1:], bf16) for w in weights]
    outs += [jax.ShapeDtypeStruct((ctx,) + p.shape[1:], bf16) for p in pieces]
    outs += [jax.ShapeDtypeStruct((shards // 2, rows, shards * rows), bf16)]
    return pl.pallas_call(
        functools.partial(gather_kernel, levels, cut),
        out_shape=outs,
        in_specs=[pl.BlockSpec(memory_space=ANY)] * 6,
        out_specs=[pl.BlockSpec(memory_space=ANY)] * 7,
        scratch_shapes=[pltpu.SemaphoreType.DMA((7,))]
        + [pltpu.SemaphoreType.DMA((13,))] * 2
        + sems,
        compiler_params=pltpu.CompilerParams(collective_id=1, has_side_effects=True),
    )(*weights, *pieces)


def swap_kernel(src, dst, send_sem, recv_sem):
    c = lax.axis_index("ctx")
    mate = {"dp": lax.axis_index("dp"), "ctx": c + 1 - 2 * (c % 2)}
    barrier = pltpu.get_barrier_semaphore()
    pl.semaphore_signal(barrier, inc=1, device_id=mate, device_id_type=MESH)
    pl.semaphore_wait(barrier, 1)
    copy = pltpu.make_async_remote_copy(
        src_ref=src,
        dst_ref=dst,
        send_sem=send_sem,
        recv_sem=recv_sem,
        device_id=mate,
        device_id_type=MESH,
    )
    copy.start()
    copy.wait()


def swap(value, number):
    return pl.pallas_call(
        swap_kernel,
        out_shape=jax.ShapeDtypeStruct(value.shape, value.dtype),
        in_specs=[pl.BlockSpec(memory_space=ANY)],
        out_specs=pl.BlockSpec(memory_space=ANY),
        scratch_shapes=[pltpu.SemaphoreType.DMA, pltpu.SemaphoreType.DMA],
        compiler_params=pltpu.CompilerParams(collective_id=number, has_side_effects=True),
    )(value)


RETURNS = STREAMS[4:] + STREAMS[2:4] + STREAMS[:2]


def scatter_kernel(levels, *refs):
    g_in, p_in = refs[:3], refs[3:5]
    out, p_out = refs[5:8], refs[8:10]
    finals = refs[10:13]
    mate_sem, mate_rsem = refs[13:15]
    rest = refs[15:]
    pc = Place(levels)
    pc.meet(NEIGHBOURS)
    crossing = []
    for a in range(2):
        copy = pltpu.make_async_remote_copy(
            src_ref=p_in[a],
            dst_ref=p_out[a],
            send_sem=mate_sem.at[3 + a],
            recv_sem=mate_rsem.at[3 + a],
            device_id=pc.device("x"),
            device_id_type=MESH,
        )
        copy.start()
        crossing.append(copy)
    streams = [
        Scatter(pc, g_in[a], rest[3 * k], finals[a], half, order, rest[3 * k + 1], rest[3 * k + 2])
        for k, (a, half, order) in enumerate(RETURNS)
    ]
    order = blocks_of(levels)[::-1]
    for block in order:
        for stream in streams:
            if block != (0, 0, 0):
                stream.forward(block)
    for stream in streams:
        stream.finish()
    for a in range(3):
        copy = pltpu.make_async_remote_copy(
            src_ref=finals[a].at[1 - pc.t],
            dst_ref=out[a].at[pc.t],
            send_sem=mate_sem.at[a],
            recv_sem=mate_rsem.at[a],
            device_id=pc.device("core"),
            device_id_type=MESH,
        )
        copy.start()
        crossing.append(copy)
        out[a][pc.t] = finals[a][pc.t]
    for stream in streams:
        stream.drain(order)
    for copy in crossing:
        copy.wait()


def scatter(grads, pieces, levels):
    rows = grads[0].shape[1]
    room = []
    for a, half, order in RETURNS:
        slots, sent = Scatter.slots_of(levels, order)
        room += [
            VM((slots, rows, grads[a].shape[2]), bf16),
            pltpu.SemaphoreType.DMA((sent,)),
            pltpu.SemaphoreType.DMA((slots,)),
        ]
    out = [jax.ShapeDtypeStruct((2, rows, g.shape[2]), f32) for g in grads]
    out += [jax.ShapeDtypeStruct(p.shape, p.dtype) for p in pieces]
    return pl.pallas_call(
        functools.partial(scatter_kernel, levels),
        out_shape=out,
        in_specs=[pl.BlockSpec(memory_space=VM)] * 3 + [pl.BlockSpec(memory_space=ANY)] * 2,
        out_specs=[pl.BlockSpec(memory_space=VM)] * 3 + [pl.BlockSpec(memory_space=ANY)] * 2,
        scratch_shapes=[VM((2, rows, g.shape[2]), f32) for g in grads]
        + [pltpu.SemaphoreType.DMA((5,))] * 2
        + room,
        compiler_params=pltpu.CompilerParams(
            collective_id=2, has_side_effects=True, vmem_limit_bytes=60 * MIB
        ),
    )(*grads, *pieces)


def norm_parts(values, epsilon):
    inv = lax.rsqrt(jnp.mean(values * values, axis=-1, keepdims=True) + epsilon)
    return inv


def norm_back(values, gain, grad, epsilon):
    inv = norm_parts(values, epsilon)
    scaled = gain * grad
    back = inv * scaled - values * (
        inv * inv * inv * jnp.mean(scaled * values, axis=-1, keepdims=True)
    )
    return back, grad * values * inv


def body(tokens, cotangent, starts, norm_gain, qkv_weight, conv_weight, beta_weight,
         head_gain, out_weight, gate_up_weight, down_weight):
    levels = lax.axis_size("dp") // 2
    ctx = lax.axis_size("ctx")
    device = lax.axis_index("dp") * ctx + lax.axis_index("ctx")
    t = lax.axis_index("ctx") % 2
    m = lax.axis_index("ctx") // 2
    batches, _, piece, width = tokens.shape
    rows = ctx * piece
    share = qkv_weight.shape[1]
    hidden = gate_up_weight.shape[2]
    half, fhalf = width // 2, hidden // 2
    heads_all = beta_weight.shape[1]
    heads = heads_all // 2
    per = head_gain.shape[0]
    small = 2 + 3 * CONV + heads_all + 1

    gain_rows = jnp.zeros((share, 1), bf16).at[:per, 0].set(head_gain)
    extra = jnp.concatenate(
        [norm_gain.T, conv_weight.T, beta_weight, gain_rows, jnp.zeros((share, HD - small), bf16)],
        axis=1,
    )
    split = lambda w: jnp.moveaxis(w.reshape(w.shape[0], share, 2, -1), (2, 1), (0, 1))
    first = jnp.concatenate(
        [
            split(qkv_weight).reshape(2, share, 3 * half),
            split(out_weight[None]).reshape(2, share, half),
            jnp.stack([extra, extra]),
        ],
        axis=2,
    )
    second = split(gate_up_weight).reshape(2, share, 2 * fhalf)
    third = split(down_weight[None]).reshape(2, share, fhalf)
    flags = jnp.broadcast_to(
        starts.reshape(batches, piece, 1).astype(bf16), (batches, piece, HD)
    )
    first, w_gu, w_down, x, dy, marks, w_out = gather(
        (first, second, third),
        (tokens[:, 0], cotangent[:, 0], flags),
        3 * half,
        levels,
    )
    first = first.reshape(width, -1)
    w_gu = w_gu.reshape(width, 2 * fhalf)
    w_down = w_down.reshape(width, fhalf)
    w_out = w_out.reshape(half, width)
    x = x.reshape(rows, width)
    dy = dy.reshape(rows, width)
    marks = marks.reshape(rows, HD)

    extra = first[:, 4 * half : 4 * half + HD]
    small_rows = extra.T.astype(f32)
    g0, g1 = small_rows[0:1], small_rows[1:2]
    taps = lax.dynamic_slice_in_dim(small_rows[2 : 2 + 3 * CONV], t * half, half, axis=1)
    taps = jnp.concatenate([taps, jnp.zeros((16 - 3 * CONV, half), f32)], axis=0)
    w_beta = lax.dynamic_slice_in_dim(extra[:, 2 + 3 * CONV :], t * heads, heads, axis=1)
    w_beta = jnp.repeat(w_beta, HD, axis=1)
    hgain = small_rows[small - 1].reshape(-1, share)[:, :per].reshape(1, HD)
    hgain = jnp.broadcast_to(hgain, (8, HD))
    w_mix = jnp.concatenate([first[:, : 3 * half], w_beta], axis=1)

    upto = jnp.tril(jnp.ones((rows, rows), bf16))
    segc = jnp.dot(upto, marks, preferred_element_type=f32)
    segr = segc[:, :8].T

    xf = x.astype(f32)
    normed = (xf * norm_parts(xf, 1e-5) * g0).astype(bf16)
    proj = jnp.dot(normed, w_mix[:, : 3 * half], preferred_element_type=f32).astype(bf16)
    logit = jnp.dot(normed, w_beta, preferred_element_type=f32)
    headed, out, *saved = delta_forward(proj, logit, taps, segc, segr, hgain)

    mine = jnp.dot(headed, w_out, preferred_element_type=f32).astype(bf16)
    residual = xf + mine.astype(f32) + swap(mine, 3).astype(f32)
    inv1 = norm_parts(residual, 1e-5)
    normed2 = (residual * inv1 * g1).astype(bf16)
    gate = jnp.dot(normed2, w_gu[:, :fhalf], preferred_element_type=f32)
    up = jnp.dot(normed2, w_gu[:, fhalf:], preferred_element_type=f32)
    sg = jax.nn.sigmoid(gate)
    act = (gate * sg * up).astype(bf16)

    def by_parity(value):
        parts = value.reshape(ctx // 2, 2, piece, width)
        return lax.dynamic_index_in_dim(parts, t, 1, False), lax.dynamic_index_in_dim(
            parts, 1 - t, 1, False
        )

    ffn, ffn_other = by_parity(
        lax.dot_general(act, w_down, (((1,), (1,)), ((), ())), preferred_element_type=f32).astype(bf16)
    )
    res_own = by_parity(residual)[0]
    result = (res_own + ffn.astype(f32) + swap(ffn_other, 4).astype(f32)).astype(bf16)

    dact = jnp.dot(dy, w_down, preferred_element_type=f32)
    g_down = lax.dot_general(dy, act, (((0,), (0,)), ((), ())), preferred_element_type=f32).astype(bf16)
    dgate = (dact * up * sg * (1.0 + gate * (1.0 - sg))).astype(bf16)
    dup = (dact * gate * sg).astype(bf16)
    dgu = jnp.concatenate([dgate, dup], axis=1)
    g_gu = lax.dot_general(normed2, dgu, (((0,), (0,)), ((), ())), preferred_element_type=f32).astype(bf16)
    mine = lax.dot_general(dgu, w_gu, (((1,), (1,)), ((), ())), preferred_element_type=f32).astype(bf16)
    dnormed2 = mine.astype(f32) + swap(mine, 5).astype(f32)
    dres, gain1 = norm_back(residual, g1, dnormed2, 1e-5)
    dres = dres + dy.astype(f32)
    datt = dres.astype(bf16)
    gain1 = jnp.sum(by_parity(gain1)[0], axis=(0, 1))
    g_out = lax.dot_general(headed, datt, (((0,), (0,)), ((), ())), preferred_element_type=f32).astype(bf16)
    dheaded = lax.dot_general(datt, w_out, (((1,), (1,)), ((), ())), preferred_element_type=f32)
    dproj, dtaps, dgain = delta_backward(dheaded, out, proj, logit, taps, segc, segr, hgain, saved)

    g_mix = lax.dot_general(normed, dproj, (((0,), (0,)), ((), ())), preferred_element_type=f32)
    mine = lax.dot_general(dproj, w_mix, (((1,), (1,)), ((), ())), preferred_element_type=f32).astype(bf16)
    mine, other = by_parity(mine)
    dnormed = mine.astype(f32) + swap(other, 6).astype(f32)
    x_own = by_parity(xf)[0]
    dx, gain0 = norm_back(x_own, g0[None], dnormed, 1e-5)
    dx = (dx + by_parity(dres)[0]).astype(bf16)
    gain0 = jnp.sum(gain0, axis=(0, 1))

    g_beta = g_mix[:, 3 * half :].reshape(width, heads, HD)[:, :, 0]
    zeros = jnp.zeros((width, heads), f32)
    g_beta = jnp.where(t == 0, jnp.concatenate([g_beta, zeros], 1), jnp.concatenate([zeros, g_beta], 1))
    g_taps = dtaps[: 3 * CONV].T
    zeros = jnp.zeros((half, 3 * CONV), f32)
    g_taps = jnp.where(t == 0, jnp.concatenate([g_taps, zeros], 0), jnp.concatenate([zeros, g_taps], 0))
    g_head = jnp.zeros((width // share, share), f32).at[:, :per].set(dgain[0].reshape(-1, per))
    g_small = jnp.concatenate(
        [
            gain0[:, None],
            gain1[:, None],
            g_taps,
            g_beta,
            g_head.reshape(width, 1),
            jnp.zeros((width, HD - small), f32),
        ],
        axis=1,
    ).astype(bf16)
    sides = g_out.reshape(half, 2, half)
    kept = lax.dynamic_index_in_dim(sides, t, 1, False)
    other = swap(lax.dynamic_index_in_dim(sides, 1 - t, 1, False), 7)
    g_out = jnp.where(t == 0, jnp.concatenate([kept, other], 0), jnp.concatenate([other, kept], 0))
    g_first = jnp.concatenate([g_mix[:, : 3 * half].astype(bf16), g_out, g_small], axis=1)
    shaped = lambda g: g.reshape(width // share, share, -1)
    pick = lambda parts, k: lax.dynamic_index_in_dim(parts, k, 0, False)
    o_first, o_gu, o_down, got_y, got_x = scatter(
        (shaped(g_first), shaped(g_gu), shaped(g_down)),
        (pick(result, 1 - m), pick(dx, 1 - m)),
        levels,
    )
    ordered = lambda own, got: jnp.stack(
        [jnp.where(m == 0, own, got), jnp.where(m == 0, got, own)]
    )[:, None]
    layer_out = ordered(pick(result, m), got_y)
    input_grad = ordered(pick(dx, m), got_x)
    join = lambda o, n: jnp.moveaxis(o.reshape(2, share, n, -1), (2, 1), (0, 1)).reshape(n, share, -1)
    o_small = jnp.sum(o_first[:, :, 4 * half :], axis=0)
    return (
        layer_out,
        input_grad,
        o_small[:, 0:2].T,
        join(o_first[:, :, : 3 * half], 3),
        o_small[:, 2 : 2 + 3 * CONV].T,
        o_small[:, 2 + 3 * CONV : 2 + 3 * CONV + heads_all],
        o_small[:per, small - 1],
        join(o_first[:, :, 3 * half : 4 * half], 1)[0],
        join(o_gu, 2),
        join(o_down, 1)[0],
    )


def solution(mesh):
    both = ("dp", "ctx")
    acts = P(None, "dp", "ctx", None)
    return jax.shard_map(
        body,
        mesh=mesh,
        in_specs=(
            acts,
            acts,
            P(None, "dp", "ctx"),
            P(None, both),
            P(None, both, None),
            P(None, both),
            P(both, None),
            P(both),
            P(both, None),
            P(None, both, None),
            P(both, None),
        ),
        out_specs=(
            acts,
            acts,
            P(None, both),
            P(None, both, None),
            P(None, both),
            P(both, None),
            P(both),
            P(both, None),
            P(None, both, None),
            P(both, None),
        ),
        check_vma=False,
    )
```

```python
import functools

import jax
import jax.numpy as jnp
from jax import lax
from jax.experimental import pallas as pl
from jax.experimental.pallas import tpu as pltpu
from jax.sharding import PartitionSpec as P

MESH = pl.DeviceIdType.MESH
ANY = pl.ANY
VM = pltpu.VMEM
MIB = 1 << 20
f32 = jnp.float32
bf16 = jnp.bfloat16


def route(block, order):
    dz, fx, fy = block
    rank = {dim: place for place, dim in enumerate(order)}
    last = max([-1] + [rank[d] for d, on in (("z", dz), ("x", fx), ("y", fy)) if on])
    hops = []
    for dim in order:
        if dim == "z":
            if dz == 0 and rank["z"] > last:
                hops += ["up", "dn"]
            elif dz != 0 and last == rank["z"]:
                hops.append("up" if dz < 0 else "dn")
        elif rank[dim] > last:
            hops.append(dim)
    came = None
    if last >= 0:
        came = order[last]
        if came == "z":
            came = "up" if dz < 0 else "dn"
    return hops, came


def blocks_of(levels):
    named = [
        (dz, fx, fy)
        for dz in range(1 - levels, levels)
        for fx in (0, 1)
        for fy in (0, 1)
    ]
    return sorted(named, key=lambda b: (abs(b[0]) + b[1] + b[2], abs(b[0]), b))


class Place:
    def __init__(self, levels):
        i = lax.axis_index("dp")
        c = lax.axis_index("ctx")
        self.levels = levels
        self.i, self.c = i, c
        self.z, self.y = i // 2, i % 2
        self.x, self.t = c // 2, c % 2

    def device(self, hop):
        i, c = self.i, self.c
        if hop == "x":
            return {"dp": i, "ctx": (1 - self.x) * 2 + self.t}
        if hop == "y":
            return {"dp": self.z * 2 + 1 - self.y, "ctx": c}
        if hop == "up":
            return {"dp": i + 2, "ctx": c}
        if hop == "dn":
            return {"dp": i - 2, "ctx": c}
        return {"dp": i, "ctx": self.x * 2 + 1 - self.t}

    def valid(self, block, hop=None):
        dz = block[0]
        terms = []
        if dz > 0:
            terms.append(self.z + dz < self.levels)
        if dz < 0:
            terms.append(self.z + dz >= 0)
        if hop == "up" and dz <= 0:
            terms.append(self.z + 1 < self.levels)
        if hop == "dn" and dz >= 0:
            terms.append(self.z >= 1)
        if not terms:
            return None
        return functools.reduce(jnp.logical_and, terms)

    def level(self, block):
        return self.z + block[0]

    def shard(self, block, half):
        z = self.z + block[0]
        y = 1 - self.y if block[2] else self.y
        x = 1 - self.x if block[1] else self.x
        return ((z * 2 + y) * 2 + x) * 2 + half

    def meet(self, hops):
        barrier = pltpu.get_barrier_semaphore()
        count = 0
        for hop in hops:
            def greet(hop=hop):
                pl.semaphore_signal(
                    barrier, inc=1, device_id=self.device(hop), device_id_type=MESH
                )
            if hop in ("up", "dn"):
                here = (self.z + 1 < self.levels) if hop == "up" else (self.z >= 1)
                pl.when(here)(greet)
                count = count + here.astype(jnp.int32)
            else:
                greet()
                count = count + 1
        pl.semaphore_wait(barrier, count)


def when(condition, action):
    if condition is None:
        action()
    else:
        pl.when(condition)(action)


def send_slots(order):
    table = {}
    for fx in (0, 1):
        for fy in (0, 1):
            for dz in (-1, 0, 1):
                for hop in route((dz, fx, fy), order)[0]:
                    table.setdefault((hop, fx, fy), len(table))
    return table


class Gather:
    def __init__(self, place, src, ref, half, order, send_sem, recv_sem):
        self.place, self.src, self.ref, self.half = place, src, ref, half
        self.order = order
        self.slots = send_slots(order)
        self.send_sem, self.recv_sem = send_sem, recv_sem

    @staticmethod
    def sems(levels, order):
        return len(send_slots(order)) * levels, 4 * levels

    def copy(self, block, hop):
        place = self.place
        dz, fx, fy = block
        where = place.shard(block, self.half)
        level = place.level(block)
        there = (fx ^ (hop == "x"), fy ^ (hop == "y"))
        return pltpu.make_async_remote_copy(
            src_ref=self.ref.at[where],
            dst_ref=self.ref.at[where],
            send_sem=self.send_sem.at[self.slots[hop, fx, fy] * place.levels + level],
            recv_sem=self.recv_sem.at[(there[0] * 2 + there[1]) * place.levels + level],
            device_id=place.device(hop),
            device_id_type=MESH,
        )

    def arrival(self, block):
        place = self.place
        dz, fx, fy = block
        where = place.shard(block, self.half)
        came = route(block, self.order)[1]
        back = {"up": "dn", "dn": "up"}.get(came, came)
        return pltpu.make_async_remote_copy(
            src_ref=self.ref.at[where],
            dst_ref=self.ref.at[where],
            send_sem=self.send_sem.at[0],
            recv_sem=self.recv_sem.at[(fx * 2 + fy) * place.levels + place.level(block)],
            device_id=place.device(back),
            device_id_type=MESH,
        )

    def wait(self, block):
        when(self.place.valid(block), lambda: self.arrival(block).wait_recv())

    def pass_on(self, block, only=("x", "y", "up", "dn")):
        for hop in route(block, self.order)[0]:
            if hop not in only:
                continue
            when(self.place.valid(block, hop), lambda hop=hop: self.copy(block, hop).start())

    def drain(self, blocks):
        for block in blocks:
            for hop in route(block, self.order)[0]:
                when(
                    self.place.valid(block, hop),
                    lambda hop=hop: self.copy(block, hop).wait_send(),
                )


class Scatter:
    def __init__(self, place, ref, room, final, half, order, send_sem, recv_sem):
        self.place, self.ref, self.room, self.final = place, ref, room, final
        self.half, self.order = half, order
        self.slots = send_slots(order)
        self.send_sem, self.recv_sem = send_sem, recv_sem

    @staticmethod
    def slots_of(levels, order):
        return len(send_slots(order)) * levels, 4 * levels

    def slot(self, block, hop):
        return self.slots[hop, block[1], block[2]] * self.place.levels + self.place.level(block)

    def copy(self, block, src):
        place = self.place
        dz, fx, fy = block
        came = route(block, self.order)[1]
        back = {"up": "dn", "dn": "up"}.get(came, came)
        key = (came, fx ^ (came == "x"), fy ^ (came == "y"))
        slot = self.slots[key] * place.levels + place.level(block)
        return pltpu.make_async_remote_copy(
            src_ref=src,
            dst_ref=self.room.at[slot],
            send_sem=self.send_sem.at[(fx * 2 + fy) * place.levels + place.level(block)],
            recv_sem=self.recv_sem.at[slot],
            device_id=place.device(back),
            device_id_type=MESH,
        )

    def arrive(self, block, hop):
        slot = self.slot(block, hop)
        pltpu.make_async_remote_copy(
            src_ref=self.room.at[slot],
            dst_ref=self.room.at[slot],
            send_sem=self.send_sem.at[0],
            recv_sem=self.recv_sem.at[slot],
            device_id=self.place.device(hop),
            device_id_type=MESH,
        ).wait_recv()

    def total(self, block, hops, put):
        where = self.place.shard(block, self.half)
        slots = [self.slot(block, hop) for hop in hops]
        rows = self.ref.shape[1]
        step = min(16, rows)

        def one(k, carry):
            at = pl.ds(pl.multiple_of(k * step, step), step)
            value = self.ref[where, at, :].astype(f32)
            for slot in slots:
                value = value + self.room[slot, at, :].astype(f32)
            put(at, value)
            return carry

        lax.fori_loop(0, rows // step, one, 0)

    def branch(self, maybe, using, go):
        if not maybe:
            go(using)
            return
        hop, place = maybe[0], self.place
        here = place.z + 1 < place.levels if hop == "up" else place.z >= 1
        pl.when(here)(lambda: self.branch(maybe[1:], using + [hop], go))
        pl.when(jnp.logical_not(here))(lambda: self.branch(maybe[1:], using, go))

    def forward(self, block):
        place = self.place
        hops = route(block, self.order)[0]
        sure = [h for h in hops if h in ("x", "y")]
        maybe = [h for h in hops if h not in ("x", "y")]

        def go(using):
            for hop in using:
                self.arrive(block, hop)
            if not using:
                self.copy(block, self.ref.at[place.shard(block, self.half)]).start()
                return
            slot = self.slot(block, using[0])

            def put(at, value):
                self.room[slot, at, :] = value.astype(bf16)

            self.total(block, using, put)
            self.copy(block, self.room.at[slot]).start()

        def both():
            self.branch(maybe, sure, go)

        when(place.valid(block), both)

    def finish(self):
        own = (0, 0, 0)
        place = self.place
        hops = route(own, self.order)[0]
        sure = [h for h in hops if h in ("x", "y")]
        for hop in sure:
            self.arrive(own, hop)

        def put(at, value):
            self.final[self.half, at, :] = value

        self.total(own, sure, put)
        for hop in hops:
            if hop in sure:
                continue

            def add(hop=hop):
                self.arrive(own, hop)
                slot = self.slot(own, hop)
                self.final[self.half] = self.final[self.half] + self.room[slot].astype(f32)

            when(place.valid(own, hop), add)

    def drain(self, blocks):
        for block in blocks:
            if block == (0, 0, 0):
                continue
            when(
                self.place.valid(block),
                lambda block=block: self.copy(
                    block, self.ref.at[self.place.shard(block, self.half)]
                ).wait_send(),
            )


HD = 128
CONV = 4
SPAN = 128


def mm(a, b):
    return jnp.dot(a, b, preferred_element_type=f32)


def mm_nt(a, b):
    return lax.dot_general(a, b, (((1,), (1,)), ((), ())), preferred_element_type=f32)


def mm_tn(a, b):
    return lax.dot_general(a, b, (((0,), (0,)), ((), ())), preferred_element_type=f32)


def lanes(h):
    return pl.ds(pl.multiple_of(h * HD, HD), HD)


def set_masks(segc, keep):
    rows = lax.broadcasted_iota(jnp.int32, segc.shape, 0)
    seg = segc[...]
    for o in range(1, CONV):
        same = (pltpu.roll(seg, o, 0) == seg) & (rows >= o)
        keep[o - 1] = same.astype(f32)


def shifted(value, keep, o):
    return value if o == 0 else pltpu.roll(value, o, 0) * keep[o - 1]


def conv_of(proj, taps, keep, j, h, heads):
    at = lanes(j * heads + h)
    value = proj[:, at].astype(f32)
    total = taps[pl.ds(j * CONV + CONV - 1, 1), lanes(h)] * value
    for o in range(1, CONV):
        total = total + taps[pl.ds(j * CONV + CONV - 1 - o, 1), lanes(h)] * shifted(value, keep, o)
    return total


def span_masks(segc, segr, n):
    at = slice(n * SPAN, (n + 1) * SPAN)
    col = segc[at, :]
    same = col == jnp.broadcast_to(segr[0:1, at], (SPAN, SPAN))
    if n:
        carried = (col == segc[n * SPAN - 1 : n * SPAN, :]).astype(f32)
    else:
        carried = jnp.zeros((SPAN, HD), f32)
    ending = (col == col[SPAN - 1 : SPAN, :]).astype(f32)
    return carried, same, ending


def iotas():
    i = lax.broadcasted_iota(jnp.int32, (SPAN, SPAN), 0)
    j = lax.broadcasted_iota(jnp.int32, (SPAN, SPAN), 1)
    return i, j


def unit_inverses(lowers):
    i, j = iotas()
    apart = i ^ j
    invs = [jnp.where(apart == 1, -low, 0.0) for low in lowers]
    size, bits = 2, 1
    while size < SPAN:
        pairs = lax.shift_right_logical(apart, bits) == 1
        part = [jnp.where(pairs, low, 0.0) for low in lowers]
        small = [inv.astype(bf16) for inv in invs]
        left = [p + mm(s, p.astype(bf16)) for p, s in zip(part, small)]
        both = [w + mm(w.astype(bf16), s) for w, s in zip(left, small)]
        invs = [inv - b for inv, b in zip(invs, both)]
        size, bits = size * 2, bits + 1
    return invs


def backward_kernel(heads, dheaded, out, proj, logit, taps, segc, segr, gain,
                    qs, ks, vs, fs, ws, ns, ps, ss,
                    dproj, dtaps, dgain,
                    keep, douts, xs, hs, gs, ys, dqs, dks, dvs):
    spans = segc.shape[0] // SPAN
    set_masks(segc, keep)
    i, j = iotas()
    first = lax.broadcasted_iota(jnp.int32, (SPAN, HD), 1) == 0

    def norm_back(h, dgain_sum):
        o = out[:, lanes(h)]
        dy = dheaded[:, lanes(h)].astype(f32)
        r = lax.rsqrt(jnp.mean(o * o, axis=-1, keepdims=True) + 1e-5)
        scaled = dy * gain[0:1, :]
        dout = r * scaled - o * (r * r * r * jnp.mean(scaled * o, axis=-1, keepdims=True))
        douts[:, lanes(h)] = dout
        dgain_sum = dgain_sum + jnp.sum(dy * o * r, axis=0, keepdims=True)
        for n in range(spans):
            at = slice(n * SPAN, (n + 1) * SPAN)
            carried, same, ending = span_masks(segc, segr, n)
            small = dout[at].astype(bf16)
            x = mm_tn(ps[h * spans + n], small)
            xs[at, lanes(h)] = x
            cdout = (carried * dout[at]).astype(bf16)
            hs[h * spans + n] = mm_tn(qs[at, lanes(h)], cdout) - mm_tn(
                ws[at, lanes(h)], x.astype(bf16)
            )
        return dgain_sum

    dgain_sum = lax.fori_loop(0, heads, norm_back, jnp.zeros((1, HD), f32))
    dgain[...] = jnp.broadcast_to(dgain_sum, dgain.shape)

    grads = [jnp.zeros((HD, HD), f32) for _ in range(heads)]
    for n in reversed(range(spans)):
        at = slice(n * SPAN, (n + 1) * SPAN)
        carried, same, ending = span_masks(segc, segr, n)
        for h in range(heads):
            head = slice(h * HD, (h + 1) * HD)
            g = grads[h].astype(bf16)
            gs[h * spans + n] = g
            y = ending * mm(ks[at, head], g)
            ys[at, head] = y.astype(bf16)
            if n:
                grads[h] = (
                    carried[SPAN - 1 : SPAN, :] * grads[h]
                    - mm_tn(ws[at, head], y.astype(bf16))
                    + hs[h * spans + n]
                )

    def pull(h, carry):
        head = lanes(h)
        for n in range(spans):
            at = slice(n * SPAN, (n + 1) * SPAN)
            carried, same, ending = span_masks(segc, segr, n)
            which = h * spans + n
            q, k, v, f = qs[at, head], ks[at, head], vs[at, head], fs[at, head]
            state, g, p, inv = ss[which], gs[which], ps[which], ns[which]
            beta = jax.nn.sigmoid(logit[at, head])
            dout = douts[at, head]
            small = dout.astype(bf16)
            df = xs[at, head] + ys[at, head].astype(f32)
            z = df + mm_tn(inv, df.astype(bf16))
            zb = z.astype(bf16)
            dp = jnp.where(same & (i >= j), mm_nt(small, f), 0.0).astype(bf16)
            dl = jnp.where(same & (i > j), -mm_nt(zb, f), 0.0)
            known = v.astype(f32) - carried * mm(k, state)
            dbeta = jnp.sum(z * known + dl * mm_nt(k, k), axis=-1, keepdims=True)
            b = beta[:, 0:1]
            dlogit = dbeta * b * (1.0 - b)
            dproj[at, pl.ds(pl.multiple_of((3 * heads + h) * HD, HD), HD)] = jnp.where(
                first, jnp.broadcast_to(dlogit, (SPAN, HD)), 0.0
            ).astype(bf16)
            e = (beta * dl).astype(bf16)
            dqs[at, :] = carried * mm_nt(small, state) + mm(dp, k)
            dvs[at, :] = beta * z
            dks[at, :] = (
                mm(e, k)
                + mm_tn(e, k)
                + mm_tn(dp, q)
                - (carried * beta) * mm_nt(zb, state)
                + ending * mm_nt(f, g)
            )
        for which, dref in ((0, dqs), (1, dks), (2, dvs)):
            c = conv_of(proj, taps, keep, which, h, heads)
            s = jax.nn.sigmoid(c)
            d = dref[...]
            if which < 2:
                w = c * s
                r = lax.rsqrt(jnp.sum(w * w, axis=-1, keepdims=True) + 1e-6)
                d = r * d - w * (r * r * r * jnp.sum(w * d, axis=-1, keepdims=True))
            dc = d * (s * (1.0 + c * (1.0 - s)))
            at = lanes(which * heads + h)
            value = proj[:, at].astype(f32)
            total = None
            rows = segc.shape[0]
            for o in range(CONV):
                row = which * CONV + CONV - 1 - o
                tap = taps[pl.ds(row, 1), lanes(h)]
                dtaps[pl.ds(row, 1), lanes(h)] = jnp.sum(
                    dc * shifted(value, keep, o), axis=0, keepdims=True
                )
                if o == 0:
                    total = tap * dc
                else:
                    total = total + tap * pltpu.roll(dc * keep[o - 1], rows - o, 0)
            dproj[:, at] = total.astype(bf16)
        return carry

    lax.fori_loop(0, heads, pull, 0)


def delta_backward(dheaded, out, proj, logit, taps, segc, segr, gain, saved):
    rows, width = logit.shape
    heads = width // HD
    spans = rows // SPAN
    return pl.pallas_call(
        functools.partial(backward_kernel, heads),
        out_shape=[
            jax.ShapeDtypeStruct((rows, 4 * width), bf16),
            jax.ShapeDtypeStruct(taps.shape, f32),
            jax.ShapeDtypeStruct((8, HD), f32),
        ],
        in_specs=[pl.BlockSpec(memory_space=VM)] * 16,
        out_specs=[pl.BlockSpec(memory_space=VM)] * 3,
        scratch_shapes=[
            VM((CONV - 1, rows, HD), f32),
            VM((rows, width), f32),
            VM((rows, width), f32),
            VM((heads * spans, HD, HD), f32),
            VM((heads * spans, HD, HD), bf16),
            VM((rows, width), bf16),
            VM((rows, HD), f32),
            VM((rows, HD), f32),
            VM((rows, HD), f32),
        ],
        compiler_params=pltpu.CompilerParams(vmem_limit_bytes=56 * MIB),
    )(dheaded, out, proj, logit, taps, segc, segr, gain, *saved)


class Names:
    def __init__(self, names, refs):
        self.__dict__.update(zip(names, refs, strict=True))


class Sems:
    def __init__(self, ref):
        self.ref, self.used = ref, 0

    def take(self):
        self.used += 1
        return self.ref.at[self.used - 1]


def call(kernel, ins, outs, scratch, number, limit, *static):
    names = list(ins) + list(outs) + list(scratch)

    def run(*refs):
        kernel(Names(names, refs), *static)

    results = pl.pallas_call(
        run,
        out_shape=list(outs.values()),
        in_specs=[pl.BlockSpec(memory_space=ANY)] * len(ins),
        out_specs=[pl.BlockSpec(memory_space=ANY)] * len(outs),
        scratch_shapes=list(scratch.values()),
        compiler_params=pltpu.CompilerParams(
            collective_id=number, has_side_effects=True, vmem_limit_bytes=limit * MIB
        ),
    )(*ins.values())
    return dict(zip(outs, results, strict=True))


class Local:
    def __init__(self, sems):
        self.sems, self.open = sems, []

    def start(self, src, dst):
        copy = pltpu.make_async_copy(src, dst, self.sems.take())
        copy.start()
        self.open.append(copy)
        return copy

    def holds(self, copy):
        return any(copy is other for other in self.open)

    def wait(self, copy):
        copy.wait()
        self.open = [other for other in self.open if other is not copy]

    def done(self):
        for copy in self.open:
            copy.wait()
        self.open = []


class Remote:
    def __init__(self, place, sent, got):
        self.place, self.sent, self.got, self.open = place, sent, got, []

    def start(self, src, dst, hop):
        copy = pltpu.make_async_remote_copy(
            src_ref=src,
            dst_ref=dst,
            send_sem=self.sent.take(),
            recv_sem=self.got.take(),
            device_id=self.place.device(hop),
            device_id_type=MESH,
        )
        copy.start()
        self.open.append(copy)
        return copy

    def drain(self):
        for copy in self.open:
            copy.wait_send()
        self.open = []


class Later:
    def __init__(self):
        self.steps = []

    def add(self, step):
        self.steps.append(step)

    def tick(self, count):
        now, self.steps = self.steps[:count], self.steps[count:]
        for step in now:
            step()

    def finish(self):
        self.tick(len(self.steps))


def flat(ref, cols):
    value = ref[:, :, cols]
    shape = (value.shape[0] * value.shape[1], value.shape[2])
    if value.shape[1] % 16:
        return value.astype(f32).reshape(shape).astype(bf16)
    return value.reshape(shape)


STREAMS = (
    (0, 0, "zxy"),
    (0, 1, "zyx"),
    (1, 0, "zxy"),
    (1, 1, "zyx"),
    (2, 0, "xyz"),
    (2, 1, "yxz"),
)
NEIGHBOURS = ("x", "y", "up", "dn", "core")
OWN = (0, 0, 0)


def forward_kernel(r, levels, cfg):
    heads, spans, per, share = cfg["heads"], cfg["spans"], cfg["per"], cfg["share"]
    width, half, fhalf, heads_all = cfg["width"], cfg["half"], cfg["fhalf"], cfg["heads_all"]
    piece, rows = cfg["piece"], cfg["rows"]
    pc = Place(levels)
    loc = Local(Sems(r.loc_sem))
    rem = Remote(pc, Sems(r.send_sem), Sems(r.recv_sem))
    pc.meet(NEIGHBOURS)
    own = pc.shard(OWN, pc.t)
    targets = (r.w1, r.w_gu, r.w_down)
    streams = [
        Gather(pc, None, targets[a], hf, order, r.__dict__["gs%d" % k], r.__dict__["gr%d" % k])
        for k, (a, hf, order) in enumerate(STREAMS)
    ]
    s0, s1, s2 = streams[0:2], streams[2:4], streams[4:6]

    def both(src_at, dst):
        return [loc.start(src_at(pc.t), dst), rem.start(src_at(1 - pc.t), dst, "core")]

    def cut(n, t):
        return pl.ds(pl.multiple_of(t * n, n), n)

    opening = []
    for j in range(3):
        opening += both(
            lambda t, j=j: r.qkv.at[j, :, cut(half, t)],
            r.w1.at[own, :, j * half : (j + 1) * half],
        )
    opening += both(lambda t: r.out_w.at[:, cut(half, t)], r.w1.at[own, :, 3 * half : 4 * half])
    opening += both(lambda t: r.ext, r.w1.at[own, :, 4 * half : 4 * half + HD])
    pieces = both(lambda t: r.tok.at[pc.x], r.x.at[pc.c])
    pieces += both(lambda t: r.flags.at[pc.x], r.marks.at[pc.c])

    def arrived(copies):
        for copy in copies:
            if loc.holds(copy):
                loc.wait(copy)
            else:
                copy.wait_recv()

    arrived(opening)
    for s in s0:
        s.pass_on(OWN)
    cross = [
        rem.start(r.tok.at[1 - pc.x], r.x.at[pc.c], "x"),
        rem.start(r.flags.at[1 - pc.x], r.marks.at[pc.c], "x"),
    ]
    second = []
    for j in range(2):
        second += both(
            lambda t, j=j: r.gu.at[j, :, cut(fhalf, t)],
            r.w_gu.at[own, :, j * fhalf : (j + 1) * fhalf],
        )
    second += both(lambda t: r.dn.at[:, cut(fhalf, t)], r.w_down.at[own])
    second += both(lambda t: r.cot.at[pc.x], r.dy.at[pc.c])

    ordered = blocks_of(levels)

    def moves(block, s):
        return block != OWN and route(block, s.order)[0]

    arrived(second[:6])
    for s in s1:
        s.pass_on(OWN, ("up", "dn"))
    far = (1 - pc.x) * 2 + pc.t
    for block in ordered:
        depth = abs(block[0]) + block[1] + block[2]
        for s in s0:
            if moves(block, s) and depth == 1:
                s.wait(block)
                s.pass_on(block)
    for s in s1:
        for block in ((-1, 0, 0), (1, 0, 0)):
            s.wait(block)
            s.pass_on(block, ("up", "dn"))
    for copy in cross:
        copy.wait_recv()
    arrived(pieces)
    pieces = [
        rem.start(r.x.at[far], r.x.at[far], "core"),
        rem.start(r.marks.at[far], r.marks.at[far], "core"),
    ]
    for block in ordered:
        depth = abs(block[0]) + block[1] + block[2]
        for s in s0:
            if moves(block, s) and depth > 1:
                s.wait(block)
                s.pass_on(block)
    for s in s2:
        s.pass_on(OWN)
    for s in s1:
        s.pass_on(OWN, ("x", "y"))
    arrived(pieces)

    i, j = iotas()
    upto = (i >= j).astype(bf16)
    base = jnp.zeros((1, HD), f32)
    for n in range(spans):
        q, at = divmod(n * SPAN, piece)
        marks = r.marks[q, at : at + SPAN, :]
        seg = mm(upto, marks) + base
        r.segc[n * SPAN : (n + 1) * SPAN, :] = seg
        r.segr[:, n * SPAN : (n + 1) * SPAN] = jnp.transpose(seg)[0:8, :]
        base = seg[SPAN - 1 : SPAN, :]
    set_masks(r.segc, r.keep)
    loc.start(r.segc, r.segc_out)
    loc.start(r.segr, r.segr_out)

    for block in ordered:
        for s in s0:
            if block != OWN and not route(block, s.order)[0]:
                s.wait(block)
    shards = levels * 8 // 2
    mine = cut(half, pc.t)
    rows_of = lambda t: pl.ds(pl.multiple_of(t * shards, shards), shards)
    side = pl.ds(3 * half, half)
    swap_out = [
        loc.start(r.w1.at[rows_of(pc.t), :, side], r.wo.at[:, :, mine]),
        rem.start(r.w1.at[rows_of(1 - pc.t), :, side], r.wo.at[:, :, mine], "core"),
    ]

    later = Later()
    for block in ordered:
        if abs(block[0]) > 1 and not block[1] and not block[2]:
            for s in s1:
                later.add(
                    lambda s=s, block=block: (s.wait(block), s.pass_on(block, ("up", "dn")))
                )
    cot_cross = []
    for block in ordered:
        for s in s1:
            if block != OWN and not block[1] and not block[2]:
                later.add(lambda s=s, block=block: s.pass_on(block, ("x", "y")))
            elif moves(block, s):
                later.add(lambda s=s, block=block: (s.wait(block), s.pass_on(block)))
        for s in s2:
            if moves(block, s):
                later.add(lambda s=s, block=block: (s.wait(block), s.pass_on(block)))
        if block == ordered[len(ordered) // 2]:
            later.add(
                lambda: cot_cross.append(rem.start(r.cot.at[1 - pc.x], r.dy.at[pc.c], "x"))
            )

    extra = flat(r.w1, slice(4 * half, 4 * half + HD))
    for n in range(width // SPAN):
        at = slice(n * SPAN, (n + 1) * SPAN)
        r.small[:, at] = jnp.transpose(extra[at, :].astype(f32))[0:32, :]
    r.gains[...] = r.small[0:8, :]
    r.taps[...] = jnp.zeros(r.taps.shape, f32)
    r.taps[0 : 3 * CONV, :] = r.small[2 : 2 + 3 * CONV, cut(half, pc.t)]
    place_r = lax.broadcasted_iota(jnp.int32, (width, HD), 0)
    place_c = lax.broadcasted_iota(jnp.int32, (width, HD), 1)
    chosen = (place_r == share * (place_c // per) + place_c % per).astype(bf16)
    at = 2 + 3 * CONV + heads_all
    r.hgain[...] = jnp.broadcast_to(
        mm(r.small[at - at % 8 : at - at % 8 + 8, :].astype(bf16), chosen)[at % 8 : at % 8 + 1, :],
        (8, HD),
    )
    pick_r = lax.broadcasted_iota(jnp.int32, (HD, half), 0)
    pick_c = lax.broadcasted_iota(jnp.int32, (HD, half), 1)
    chosen = (pick_r == 2 + 3 * CONV + heads * pc.t + pick_c // HD).astype(bf16)
    r.wmix[:, 3 * half :] = mm(extra, chosen).astype(bf16)
    for k in range(3):
        r.wmix[:, k * half : (k + 1) * half] = flat(r.w1, slice(k * half, (k + 1) * half))
    loc.start(r.wmix, r.wmix_out)
    loc.start(r.taps, r.taps_out)
    loc.start(r.gains, r.gains_out)
    loc.start(r.hgain, r.hgain_out)

    g0 = r.gains[0:1, :]
    for n in range(rows // piece):
        x = r.x[n].astype(f32)
        inv = lax.rsqrt(jnp.mean(x * x, axis=-1, keepdims=True) + 1e-5)
        r.normed[n * piece : (n + 1) * piece, :] = (x * inv * g0).astype(bf16)
    loc.start(r.normed, r.normed_out)
    loc.start(r.x, r.x_out)

    def project(k, carry):
        at = pl.ds(pl.multiple_of(k * piece, piece), piece)
        left = r.normed[at, :]
        r.proj[at, :] = mm(left, r.wmix[:, : 3 * half]).astype(bf16)
        r.logit[at, :] = mm(left, r.wmix[:, 3 * half :])
        return carry

    lax.fori_loop(0, rows // piece, project, 0)
    loc.start(r.proj, r.proj_out)
    loc.start(r.logit, r.logit_out)
    later.tick(cfg["ticks"][0])

    batches = []
    for h in range(heads):
        now, later.steps = later.steps[: cfg["ticks"][1]], later.steps[cfg["ticks"][1] :]
        batches.append(now)

    def prepare(h, carry):
        for k, now in enumerate(batches):
            if now:
                pl.when(h == k)(lambda now=now: [step() for step in now] and None)
        delta_prepare(r, h, heads, spans)
        return carry

    lax.fori_loop(0, heads, prepare, 0)
    for src, dst in ((r.qs, r.qs_out), (r.ks, r.ks_out), (r.vs, r.vs_out), (r.ws, r.ws_out),
                     (r.ns, r.ns_out), (r.ps, r.ps_out)):
        loc.start(src, dst)
    delta_chain(r, heads, spans, lambda: later.tick(cfg["ticks"][2]))
    for h in range(heads):
        head = slice(h * HD, (h + 1) * HD)
        o = r.out[:, head]
        scale = lax.rsqrt(jnp.mean(o * o, axis=-1, keepdims=True) + 1e-5)
        r.headed[:, head] = (o * scale * r.hgain[0:1, :]).astype(bf16)
    for src, dst in ((r.fs, r.fs_out), (r.ss, r.ss_out), (r.out, r.out_out),
                     (r.headed, r.headed_out)):
        loc.start(src, dst)
    arrived(swap_out)
    loc.start(r.wo, r.wo_out)
    wo = flat(r.wo, slice(None))
    sent = []
    for n in range(rows // piece):
        r.mine[n] = mm(r.headed[n * piece : (n + 1) * piece, :], wo).astype(bf16)
        sent.append(rem.start(r.mine.at[n], r.theirs.at[n], "core"))
    later.tick(cfg["ticks"][3])
    g1 = r.gains[1:2, :]
    for n in range(rows // piece):
        sent[n].wait_recv()
        at = slice(n * piece, (n + 1) * piece)
        res = r.x[n].astype(f32) + r.mine[n].astype(f32) + r.theirs[n].astype(f32)
        r.res[at, :] = res
        inv = lax.rsqrt(jnp.mean(res * res, axis=-1, keepdims=True) + 1e-5)
        r.normed2[at, :] = (res * inv * g1).astype(bf16)
    loc.start(r.res, r.res_out)
    loc.start(r.normed2, r.normed2_out)
    later.finish()
    cot_cross[0].wait_recv()
    arrived(second[6:])
    last = rem.start(r.dy.at[far], r.dy.at[far], "core")
    for block in ordered:
        for s in s1 + s2:
            if block != OWN and not route(block, s.order)[0]:
                s.wait(block)
    last.wait_recv()
    for s in streams:
        s.drain(ordered)
    rem.drain()
    loc.done()


def delta_prepare(r, h, heads, spans):
    i, j = iotas()
    mixed = []
    for which in range(3):
        value = conv_of(r.proj, r.taps, r.keep, which, h, heads)
        mixed.append(value * jax.nn.sigmoid(value))
    for which, dest in ((0, r.qs), (1, r.ks)):
        w = mixed[which]
        unit = w * lax.rsqrt(jnp.sum(w * w, axis=-1, keepdims=True) + 1e-6)
        dest[:, lanes(h)] = unit.astype(bf16)
    r.vs[:, lanes(h)] = mixed[2].astype(bf16)
    lowers, rights = [], []
    for n in range(spans):
        at = slice(n * SPAN, (n + 1) * SPAN)
        k = r.ks[at, lanes(h)]
        q = r.qs[at, lanes(h)]
        v = r.vs[at, lanes(h)]
        beta = jax.nn.sigmoid(r.logit[at, lanes(h)])
        carried, same, ending = span_masks(r.segc, r.segr, n)
        lowers.append(jnp.where(same & (i > j), beta * mm_nt(k, k), 0.0))
        r.ps[h * spans + n] = jnp.where(same & (i >= j), mm_nt(q, k), 0.0).astype(bf16)
        r.cqs[at, lanes(h)] = (carried * q.astype(f32)).astype(bf16)
        rights.append(
            jnp.concatenate([beta * v.astype(f32), (beta * carried) * k.astype(f32)], axis=1)
        )
    for n, inv in enumerate(unit_inverses(lowers)):
        at = slice(n * SPAN, (n + 1) * SPAN)
        small = inv.astype(bf16)
        r.ns[h * spans + n] = small
        both = rights[n] + mm(small, rights[n].astype(bf16))
        r.us[at, lanes(h)] = both[:, :HD]
        r.ws[at, lanes(h)] = both[:, HD:].astype(bf16)


def delta_chain(r, heads, spans, between):
    states = [jnp.zeros((HD, HD), f32) for _ in range(heads)]
    for n in range(spans):
        at = slice(n * SPAN, (n + 1) * SPAN)
        carried, same, ending = span_masks(r.segc, r.segr, n)
        for h in range(heads):
            head = slice(h * HD, (h + 1) * HD)
            state = states[h].astype(bf16)
            r.ss[h * spans + n] = state
            seen = mm(jnp.concatenate([r.ws[at, head], r.cqs[at, head]], axis=0), state)
            fresh = r.us[at, head] - seen[:SPAN]
            small = fresh.astype(bf16)
            r.fs[at, head] = small
            r.out[at, head] = seen[SPAN:] + mm(r.ps[h * spans + n], small)
            states[h] = carried[SPAN - 1 : SPAN, :] * states[h] + mm_tn(
                r.ks[at, head], (ending * fresh).astype(bf16)
            )
        between()


def forward(qkv, out_w, gu, dn, ext, tok, cot, flags, levels, per, heads_all):
    share = qkv.shape[1]
    width = qkv.shape[2]
    half, fhalf = width // 2, dn.shape[1] // 2
    piece = tok.shape[1]
    rows = 4 * piece
    heads = half // HD
    spans = rows // SPAN
    shards = levels * 8
    sds = jax.ShapeDtypeStruct
    wide, square = sds((rows, half), bf16), sds((heads * spans, SPAN, SPAN), bf16)
    seg = dict(
        segc=sds((rows, HD), f32),
        segr=sds((8, rows), f32),
        wmix=sds((width, 4 * half), bf16),
        taps=sds((16, half), f32),
        gains=sds((8, width), f32),
        hgain=sds((8, HD), f32),
        normed=sds((rows, width), bf16),
        x=sds((4, piece, width), bf16),
        proj=sds((rows, 3 * half), bf16),
        logit=sds((rows, half), f32),
        qs=wide, ks=wide, vs=wide, fs=wide, ws=wide, headed=wide,
        ns=square, ps=square, ss=square,
        out=sds((rows, half), f32),
        wo=sds((shards // 2, share, width), bf16),
        res=sds((rows, width), f32),
        normed2=sds((rows, width), bf16),
    )
    ins = dict(qkv=qkv, out_w=out_w, gu=gu, dn=dn, ext=ext, tok=tok, cot=cot, flags=flags)
    outs = {
        "w_gu": sds((shards, share, 2 * fhalf), bf16),
        "w_down": sds((shards, share, fhalf), bf16),
        "dy": sds((4, piece, width), bf16),
    }
    outs.update({k + "_out": v for k, v in seg.items()})
    scratch = {k: VM(v.shape, v.dtype) for k, v in seg.items()}
    scratch.update(
        w1=VM((shards, share, 4 * half + HD), bf16),
        marks=VM((4, piece, HD), bf16),
        keep=VM((CONV - 1, rows, HD), f32),
        small=VM((32, width), f32),
        us=VM((rows, half), f32),
        cqs=VM((rows, half), bf16),
        mine=VM((4, piece, width), bf16),
        theirs=VM((4, piece, width), bf16),
        loc_sem=pltpu.SemaphoreType.DMA((48,)),
        send_sem=pltpu.SemaphoreType.DMA((32,)),
        recv_sem=pltpu.SemaphoreType.DMA((32,)),
    )
    for k, (a, hf, order) in enumerate(STREAMS):
        sent, got = Gather.sems(levels, order)
        scratch["gs%d" % k] = pltpu.SemaphoreType.DMA((sent,))
        scratch["gr%d" % k] = pltpu.SemaphoreType.DMA((got,))
    cfg = dict(
        heads=heads, spans=spans, per=per, share=share, width=width, half=half, fhalf=fhalf,
        heads_all=heads_all, piece=piece, rows=rows, ticks=(6, 5, 1, 4),
    )
    return call(forward_kernel, ins, outs, scratch, 1, 58, levels, cfg)


def swap_kernel(src, dst, send_sem, recv_sem):
    c = lax.axis_index("ctx")
    mate = {"dp": lax.axis_index("dp"), "ctx": c + 1 - 2 * (c % 2)}
    barrier = pltpu.get_barrier_semaphore()
    pl.semaphore_signal(barrier, inc=1, device_id=mate, device_id_type=MESH)
    pl.semaphore_wait(barrier, 1)
    copy = pltpu.make_async_remote_copy(
        src_ref=src,
        dst_ref=dst,
        send_sem=send_sem,
        recv_sem=recv_sem,
        device_id=mate,
        device_id_type=MESH,
    )
    copy.start()
    copy.wait()


def swap(value, number):
    return pl.pallas_call(
        swap_kernel,
        out_shape=jax.ShapeDtypeStruct(value.shape, value.dtype),
        in_specs=[pl.BlockSpec(memory_space=ANY)],
        out_specs=pl.BlockSpec(memory_space=ANY),
        scratch_shapes=[pltpu.SemaphoreType.DMA, pltpu.SemaphoreType.DMA],
        compiler_params=pltpu.CompilerParams(collective_id=number, has_side_effects=True),
    )(value)


RETURNS = STREAMS[4:] + STREAMS[2:4] + STREAMS[:2]


def scatter_kernel(levels, *refs):
    g_in, p_in = refs[:3], refs[3:5]
    out, p_out = refs[5:8], refs[8:10]
    finals = refs[10:13]
    mate_sem, mate_rsem = refs[13:15]
    rest = refs[15:]
    pc = Place(levels)
    pc.meet(NEIGHBOURS)
    crossing = []
    for a in range(2):
        copy = pltpu.make_async_remote_copy(
            src_ref=p_in[a],
            dst_ref=p_out[a],
            send_sem=mate_sem.at[3 + a],
            recv_sem=mate_rsem.at[3 + a],
            device_id=pc.device("x"),
            device_id_type=MESH,
        )
        copy.start()
        crossing.append(copy)
    streams = [
        Scatter(pc, g_in[a], rest[3 * k], finals[a], half, order, rest[3 * k + 1], rest[3 * k + 2])
        for k, (a, half, order) in enumerate(RETURNS)
    ]
    order = blocks_of(levels)[::-1]
    for block in order:
        for stream in streams:
            if block != (0, 0, 0):
                stream.forward(block)
    for stream in streams:
        stream.finish()
    for a in range(3):
        copy = pltpu.make_async_remote_copy(
            src_ref=finals[a].at[1 - pc.t],
            dst_ref=out[a].at[pc.t],
            send_sem=mate_sem.at[a],
            recv_sem=mate_rsem.at[a],
            device_id=pc.device("core"),
            device_id_type=MESH,
        )
        copy.start()
        crossing.append(copy)
        out[a][pc.t] = finals[a][pc.t]
    for stream in streams:
        stream.drain(order)
    for copy in crossing:
        copy.wait()


def scatter(grads, pieces, levels):
    rows = grads[0].shape[1]
    room = []
    for a, half, order in RETURNS:
        slots, sent = Scatter.slots_of(levels, order)
        room += [
            VM((slots, rows, grads[a].shape[2]), bf16),
            pltpu.SemaphoreType.DMA((sent,)),
            pltpu.SemaphoreType.DMA((slots,)),
        ]
    out = [jax.ShapeDtypeStruct((2, rows, g.shape[2]), f32) for g in grads]
    out += [jax.ShapeDtypeStruct(p.shape, p.dtype) for p in pieces]
    return pl.pallas_call(
        functools.partial(scatter_kernel, levels),
        out_shape=out,
        in_specs=[pl.BlockSpec(memory_space=VM)] * 3 + [pl.BlockSpec(memory_space=ANY)] * 2,
        out_specs=[pl.BlockSpec(memory_space=VM)] * 3 + [pl.BlockSpec(memory_space=ANY)] * 2,
        scratch_shapes=[VM((2, rows, g.shape[2]), f32) for g in grads]
        + [pltpu.SemaphoreType.DMA((5,))] * 2
        + room,
        compiler_params=pltpu.CompilerParams(
            collective_id=2, has_side_effects=True, vmem_limit_bytes=60 * MIB
        ),
    )(*grads, *pieces)


def norm_parts(values, epsilon):
    inv = lax.rsqrt(jnp.mean(values * values, axis=-1, keepdims=True) + epsilon)
    return inv


def norm_back(values, gain, grad, epsilon):
    inv = norm_parts(values, epsilon)
    scaled = gain * grad
    back = inv * scaled - values * (
        inv * inv * inv * jnp.mean(scaled * values, axis=-1, keepdims=True)
    )
    return back, grad * values * inv


def body(tokens, cotangent, starts, norm_gain, qkv_weight, conv_weight, beta_weight,
         head_gain, out_weight, gate_up_weight, down_weight):
    levels = lax.axis_size("dp") // 2
    ctx = lax.axis_size("ctx")
    device = lax.axis_index("dp") * ctx + lax.axis_index("ctx")
    t = lax.axis_index("ctx") % 2
    m = lax.axis_index("ctx") // 2
    batches, _, piece, width = tokens.shape
    rows = ctx * piece
    share = qkv_weight.shape[1]
    hidden = gate_up_weight.shape[2]
    half, fhalf = width // 2, hidden // 2
    heads_all = beta_weight.shape[1]
    heads = heads_all // 2
    per = head_gain.shape[0]
    small = 2 + 3 * CONV + heads_all + 1

    gain_rows = jnp.zeros((share, 1), bf16).at[:per, 0].set(head_gain)
    ext = jnp.concatenate(
        [norm_gain.T, conv_weight.T, beta_weight, gain_rows, jnp.zeros((share, HD - small), bf16)],
        axis=1,
    )
    flags = jnp.broadcast_to(
        starts.reshape(batches, piece, 1).astype(bf16), (batches, piece, HD)
    )
    f = forward(
        qkv_weight, out_weight, gate_up_weight, down_weight, ext,
        tokens[:, 0], cotangent[:, 0], flags, levels, per, heads_all,
    )
    w_gu = f["w_gu"].reshape(width, 2 * fhalf)
    w_down = f["w_down"].reshape(width, fhalf)
    w_out = f["wo_out"].reshape(half, width)
    w_mix = f["wmix_out"]
    dy = f["dy"].reshape(rows, width)
    xf = f["x_out"].reshape(rows, width).astype(f32)
    gains, taps, hgain = f["gains_out"], f["taps_out"], f["hgain_out"]
    g0, g1 = gains[0:1], gains[1:2]
    segc, segr = f["segc_out"], f["segr_out"]
    normed, proj, logit = f["normed_out"], f["proj_out"], f["logit_out"]
    headed, out = f["headed_out"], f["out_out"]
    saved = [f[k + "_out"] for k in ("qs", "ks", "vs", "fs", "ws", "ns", "ps", "ss")]
    residual, normed2 = f["res_out"], f["normed2_out"]
    gate = jnp.dot(normed2, w_gu[:, :fhalf], preferred_element_type=f32)
    up = jnp.dot(normed2, w_gu[:, fhalf:], preferred_element_type=f32)
    sg = jax.nn.sigmoid(gate)
    act = (gate * sg * up).astype(bf16)

    def by_parity(value):
        parts = value.reshape(ctx // 2, 2, piece, width)
        return lax.dynamic_index_in_dim(parts, t, 1, False), lax.dynamic_index_in_dim(
            parts, 1 - t, 1, False
        )

    ffn, ffn_other = by_parity(
        lax.dot_general(act, w_down, (((1,), (1,)), ((), ())), preferred_element_type=f32).astype(bf16)
    )
    res_own = by_parity(residual)[0]
    result = (res_own + ffn.astype(f32) + swap(ffn_other, 4).astype(f32)).astype(bf16)

    dact = jnp.dot(dy, w_down, preferred_element_type=f32)
    g_down = lax.dot_general(dy, act, (((0,), (0,)), ((), ())), preferred_element_type=f32).astype(bf16)
    dgate = (dact * up * sg * (1.0 + gate * (1.0 - sg))).astype(bf16)
    dup = (dact * gate * sg).astype(bf16)
    dgu = jnp.concatenate([dgate, dup], axis=1)
    g_gu = lax.dot_general(normed2, dgu, (((0,), (0,)), ((), ())), preferred_element_type=f32).astype(bf16)
    mine = lax.dot_general(dgu, w_gu, (((1,), (1,)), ((), ())), preferred_element_type=f32).astype(bf16)
    dnormed2 = mine.astype(f32) + swap(mine, 5).astype(f32)
    dres, gain1 = norm_back(residual, g1, dnormed2, 1e-5)
    dres = dres + dy.astype(f32)
    datt = dres.astype(bf16)
    gain1 = jnp.sum(by_parity(gain1)[0], axis=(0, 1))
    g_out = lax.dot_general(headed, datt, (((0,), (0,)), ((), ())), preferred_element_type=f32).astype(bf16)
    dheaded = lax.dot_general(datt, w_out, (((1,), (1,)), ((), ())), preferred_element_type=f32)
    dproj, dtaps, dgain = delta_backward(dheaded, out, proj, logit, taps, segc, segr, hgain, saved)

    g_mix = lax.dot_general(normed, dproj, (((0,), (0,)), ((), ())), preferred_element_type=f32)
    mine = lax.dot_general(dproj, w_mix, (((1,), (1,)), ((), ())), preferred_element_type=f32).astype(bf16)
    mine, other = by_parity(mine)
    dnormed = mine.astype(f32) + swap(other, 6).astype(f32)
    x_own = by_parity(xf)[0]
    dx, gain0 = norm_back(x_own, g0[None], dnormed, 1e-5)
    dx = (dx + by_parity(dres)[0]).astype(bf16)
    gain0 = jnp.sum(gain0, axis=(0, 1))

    g_beta = g_mix[:, 3 * half :].reshape(width, heads, HD)[:, :, 0]
    zeros = jnp.zeros((width, heads), f32)
    g_beta = jnp.where(t == 0, jnp.concatenate([g_beta, zeros], 1), jnp.concatenate([zeros, g_beta], 1))
    g_taps = dtaps[: 3 * CONV].T
    zeros = jnp.zeros((half, 3 * CONV), f32)
    g_taps = jnp.where(t == 0, jnp.concatenate([g_taps, zeros], 0), jnp.concatenate([zeros, g_taps], 0))
    g_head = jnp.zeros((width // share, share), f32).at[:, :per].set(dgain[0].reshape(-1, per))
    g_small = jnp.concatenate(
        [
            gain0[:, None],
            gain1[:, None],
            g_taps,
            g_beta,
            g_head.reshape(width, 1),
            jnp.zeros((width, HD - small), f32),
        ],
        axis=1,
    ).astype(bf16)
    sides = g_out.reshape(half, 2, half)
    kept = lax.dynamic_index_in_dim(sides, t, 1, False)
    other = swap(lax.dynamic_index_in_dim(sides, 1 - t, 1, False), 7)
    g_out = jnp.where(t == 0, jnp.concatenate([kept, other], 0), jnp.concatenate([other, kept], 0))
    g_first = jnp.concatenate([g_mix[:, : 3 * half].astype(bf16), g_out, g_small], axis=1)
    shaped = lambda g: g.reshape(width // share, share, -1)
    pick = lambda parts, k: lax.dynamic_index_in_dim(parts, k, 0, False)
    o_first, o_gu, o_down, got_y, got_x = scatter(
        (shaped(g_first), shaped(g_gu), shaped(g_down)),
        (pick(result, 1 - m), pick(dx, 1 - m)),
        levels,
    )
    ordered = lambda own, got: jnp.stack(
        [jnp.where(m == 0, own, got), jnp.where(m == 0, got, own)]
    )[:, None]
    layer_out = ordered(pick(result, m), got_y)
    input_grad = ordered(pick(dx, m), got_x)
    join = lambda o, n: jnp.moveaxis(o.reshape(2, share, n, -1), (2, 1), (0, 1)).reshape(n, share, -1)
    o_small = jnp.sum(o_first[:, :, 4 * half :], axis=0)
    return (
        layer_out,
        input_grad,
        o_small[:, 0:2].T,
        join(o_first[:, :, : 3 * half], 3),
        o_small[:, 2 : 2 + 3 * CONV].T,
        o_small[:, 2 + 3 * CONV : 2 + 3 * CONV + heads_all],
        o_small[:per, small - 1],
        join(o_first[:, :, 3 * half : 4 * half], 1)[0],
        join(o_gu, 2),
        join(o_down, 1)[0],
    )


def solution(mesh):
    both = ("dp", "ctx")
    acts = P(None, "dp", "ctx", None)
    return jax.shard_map(
        body,
        mesh=mesh,
        in_specs=(
            acts,
            acts,
            P(None, "dp", "ctx"),
            P(None, both),
            P(None, both, None),
            P(None, both),
            P(both, None),
            P(both),
            P(both, None),
            P(None, both, None),
            P(both, None),
        ),
        out_specs=(
            acts,
            acts,
            P(None, both),
            P(None, both, None),
            P(None, both),
            P(both, None),
            P(both),
            P(both, None),
            P(None, both, None),
            P(both, None),
        ),
        check_vma=False,
    )
```

```python
import functools

import jax
import jax.numpy as jnp
from jax import lax
from jax.experimental import pallas as pl
from jax.experimental.pallas import tpu as pltpu
from jax.sharding import PartitionSpec as P

MESH = pl.DeviceIdType.MESH
ANY = pl.ANY
VM = pltpu.VMEM
MIB = 1 << 20
f32 = jnp.float32
bf16 = jnp.bfloat16


def route(block, order):
    dz, fx, fy = block
    rank = {dim: place for place, dim in enumerate(order)}
    last = max([-1] + [rank[d] for d, on in (("z", dz), ("x", fx), ("y", fy)) if on])
    hops = []
    for dim in order:
        if dim == "z":
            if dz == 0 and rank["z"] > last:
                hops += ["up", "dn"]
            elif dz != 0 and last == rank["z"]:
                hops.append("up" if dz < 0 else "dn")
        elif rank[dim] > last:
            hops.append(dim)
    came = None
    if last >= 0:
        came = order[last]
        if came == "z":
            came = "up" if dz < 0 else "dn"
    return hops, came


def blocks_of(levels):
    named = [
        (dz, fx, fy)
        for dz in range(1 - levels, levels)
        for fx in (0, 1)
        for fy in (0, 1)
    ]
    return sorted(named, key=lambda b: (abs(b[0]) + b[1] + b[2], abs(b[0]), b))


class Place:
    def __init__(self, levels):
        i = lax.axis_index("dp")
        c = lax.axis_index("ctx")
        self.levels = levels
        self.i, self.c = i, c
        self.z, self.y = i // 2, i % 2
        self.x, self.t = c // 2, c % 2

    def device(self, hop):
        i, c = self.i, self.c
        if hop == "x":
            return {"dp": i, "ctx": (1 - self.x) * 2 + self.t}
        if hop == "y":
            return {"dp": self.z * 2 + 1 - self.y, "ctx": c}
        if hop == "up":
            return {"dp": i + 2, "ctx": c}
        if hop == "dn":
            return {"dp": i - 2, "ctx": c}
        return {"dp": i, "ctx": self.x * 2 + 1 - self.t}

    def valid(self, block, hop=None):
        dz = block[0]
        terms = []
        if dz > 0:
            terms.append(self.z + dz < self.levels)
        if dz < 0:
            terms.append(self.z + dz >= 0)
        if hop == "up" and dz <= 0:
            terms.append(self.z + 1 < self.levels)
        if hop == "dn" and dz >= 0:
            terms.append(self.z >= 1)
        if not terms:
            return None
        return functools.reduce(jnp.logical_and, terms)

    def level(self, block):
        return self.z + block[0]

    def shard(self, block, half):
        z = self.z + block[0]
        y = 1 - self.y if block[2] else self.y
        x = 1 - self.x if block[1] else self.x
        return ((z * 2 + y) * 2 + x) * 2 + half

    def meet(self, hops):
        barrier = pltpu.get_barrier_semaphore()
        count = 0
        for hop in hops:
            def greet(hop=hop):
                pl.semaphore_signal(
                    barrier, inc=1, device_id=self.device(hop), device_id_type=MESH
                )
            if hop in ("up", "dn"):
                here = (self.z + 1 < self.levels) if hop == "up" else (self.z >= 1)
                pl.when(here)(greet)
                count = count + here.astype(jnp.int32)
            else:
                greet()
                count = count + 1
        pl.semaphore_wait(barrier, count)


def when(condition, action):
    if condition is None:
        action()
    else:
        pl.when(condition)(action)


def send_slots(order):
    table = {}
    for fx in (0, 1):
        for fy in (0, 1):
            for dz in (-1, 0, 1):
                for hop in route((dz, fx, fy), order)[0]:
                    table.setdefault((hop, fx, fy), len(table))
    return table


class Gather:
    def __init__(self, place, src, ref, half, order, send_sem, recv_sem):
        self.place, self.src, self.ref, self.half = place, src, ref, half
        self.order = order
        self.slots = send_slots(order)
        self.send_sem, self.recv_sem = send_sem, recv_sem

    @staticmethod
    def sems(levels, order):
        return len(send_slots(order)) * levels, 4 * levels

    def copy(self, block, hop):
        place = self.place
        dz, fx, fy = block
        where = place.shard(block, self.half)
        level = place.level(block)
        there = (fx ^ (hop == "x"), fy ^ (hop == "y"))
        return pltpu.make_async_remote_copy(
            src_ref=self.ref.at[where],
            dst_ref=self.ref.at[where],
            send_sem=self.send_sem.at[self.slots[hop, fx, fy] * place.levels + level],
            recv_sem=self.recv_sem.at[(there[0] * 2 + there[1]) * place.levels + level],
            device_id=place.device(hop),
            device_id_type=MESH,
        )

    def arrival(self, block):
        place = self.place
        dz, fx, fy = block
        where = place.shard(block, self.half)
        came = route(block, self.order)[1]
        back = {"up": "dn", "dn": "up"}.get(came, came)
        return pltpu.make_async_remote_copy(
            src_ref=self.ref.at[where],
            dst_ref=self.ref.at[where],
            send_sem=self.send_sem.at[0],
            recv_sem=self.recv_sem.at[(fx * 2 + fy) * place.levels + place.level(block)],
            device_id=place.device(back),
            device_id_type=MESH,
        )

    def wait(self, block):
        when(self.place.valid(block), lambda: self.arrival(block).wait_recv())

    def pass_on(self, block, only=("x", "y", "up", "dn")):
        for hop in route(block, self.order)[0]:
            if hop not in only:
                continue
            when(self.place.valid(block, hop), lambda hop=hop: self.copy(block, hop).start())

    def drain(self, blocks):
        for block in blocks:
            for hop in route(block, self.order)[0]:
                when(
                    self.place.valid(block, hop),
                    lambda hop=hop: self.copy(block, hop).wait_send(),
                )


def room_table(order, levels):
    table, used = {}, 0
    for fx in (0, 1):
        for fy in (0, 1):
            here = route((0, fx, fy), order)[0]
            away = route((1, fx, fy), order)[0] + route((-1, fx, fy), order)[0]
            for hop in ("x", "y"):
                if hop in here or hop in away:
                    table[hop, fx, fy] = (used, hop in away)
                    used += levels if hop in away else 1
            if "up" in here + away or "dn" in here + away:
                table["z", fx, fy] = (used, True)
                used += levels + 1
    return table, used


class Scatter:
    def __init__(self, place, ref, room, final, half, order, send_sem, recv_sem):
        self.place, self.ref, self.room, self.final = place, ref, room, final
        self.half, self.order = half, order
        self.table = room_table(order, place.levels)[0]
        self.send_sem, self.recv_sem = send_sem, recv_sem

    @staticmethod
    def slots_of(levels, order):
        return room_table(order, levels)[1], 4 * levels

    def slot_at(self, hop, dz, fx, fy, level):
        base, many = self.table["z" if hop in ("up", "dn") else hop, fx, fy]
        if hop == "dn" and dz == 0:
            return base + self.place.levels
        return base + level if many else base

    def slot(self, block, hop):
        return self.slot_at(hop, *block, self.place.level(block))

    def copy(self, block, src):
        place = self.place
        dz, fx, fy = block
        came = route(block, self.order)[1]
        back = {"up": "dn", "dn": "up"}.get(came, came)
        there = (
            dz + (came == "up") - (came == "dn"),
            fx ^ (came == "x"),
            fy ^ (came == "y"),
        )
        slot = self.slot_at(came, *there, place.level(block))
        return pltpu.make_async_remote_copy(
            src_ref=src,
            dst_ref=self.room.at[slot],
            send_sem=self.send_sem.at[(fx * 2 + fy) * place.levels + place.level(block)],
            recv_sem=self.recv_sem.at[slot],
            device_id=place.device(back),
            device_id_type=MESH,
        )

    def arrive(self, block, hop):
        slot = self.slot(block, hop)
        pltpu.make_async_remote_copy(
            src_ref=self.room.at[slot],
            dst_ref=self.room.at[slot],
            send_sem=self.send_sem.at[0],
            recv_sem=self.recv_sem.at[slot],
            device_id=self.place.device(hop),
            device_id_type=MESH,
        ).wait_recv()

    def total(self, block, hops, put):
        where = self.place.shard(block, self.half)
        slots = [self.slot(block, hop) for hop in hops]
        rows = self.ref.shape[1]
        step = min(16, rows)

        def one(k, carry):
            at = pl.ds(pl.multiple_of(k * step, step), step)
            value = self.ref[where, at, :].astype(f32)
            for slot in slots:
                value = value + self.room[slot, at, :].astype(f32)
            put(at, value)
            return carry

        lax.fori_loop(0, rows // step, one, 0)

    def branch(self, maybe, using, go):
        if not maybe:
            go(using)
            return
        hop, place = maybe[0], self.place
        here = place.z + 1 < place.levels if hop == "up" else place.z >= 1
        pl.when(here)(lambda: self.branch(maybe[1:], using + [hop], go))
        pl.when(jnp.logical_not(here))(lambda: self.branch(maybe[1:], using, go))

    def forward(self, block):
        place = self.place
        hops = route(block, self.order)[0]
        sure = [h for h in hops if h in ("x", "y")]
        maybe = [h for h in hops if h not in ("x", "y")]

        def go(using):
            for hop in using:
                self.arrive(block, hop)
            if not using:
                self.copy(block, self.ref.at[place.shard(block, self.half)]).start()
                return
            slot = self.slot(block, using[0])

            def put(at, value):
                self.room[slot, at, :] = value.astype(bf16)

            self.total(block, using, put)
            self.copy(block, self.room.at[slot]).start()

        def both():
            self.branch(maybe, sure, go)

        when(place.valid(block), both)

    def finish(self):
        own = (0, 0, 0)
        place = self.place
        hops = route(own, self.order)[0]
        sure = [h for h in hops if h in ("x", "y")]
        for hop in sure:
            self.arrive(own, hop)

        def put(at, value):
            self.final[self.half, at, :] = value

        self.total(own, sure, put)
        for hop in hops:
            if hop in sure:
                continue

            def add(hop=hop):
                self.arrive(own, hop)
                slot = self.slot(own, hop)
                self.final[self.half] = self.final[self.half] + self.room[slot].astype(f32)

            when(place.valid(own, hop), add)

    def drain(self, blocks):
        for block in blocks:
            if block == (0, 0, 0):
                continue
            when(
                self.place.valid(block),
                lambda block=block: self.copy(
                    block, self.ref.at[self.place.shard(block, self.half)]
                ).wait_send(),
            )


HD = 128
CONV = 4
SPAN = 128


def mm(a, b):
    return jnp.dot(a, b, preferred_element_type=f32)


def mm_nt(a, b):
    return lax.dot_general(a, b, (((1,), (1,)), ((), ())), preferred_element_type=f32)


def mm_tn(a, b):
    return lax.dot_general(a, b, (((0,), (0,)), ((), ())), preferred_element_type=f32)


def lanes(h):
    return pl.ds(pl.multiple_of(h * HD, HD), HD)


def set_masks(segc, keep):
    rows = lax.broadcasted_iota(jnp.int32, segc.shape, 0)
    seg = segc[...]
    for o in range(1, CONV):
        same = (pltpu.roll(seg, o, 0) == seg) & (rows >= o)
        keep[o - 1] = same.astype(f32)


def shifted(value, keep, o):
    return value if o == 0 else pltpu.roll(value, o, 0) * keep[o - 1]


def conv_of(proj, taps, keep, j, h, heads):
    at = lanes(j * heads + h)
    value = proj[:, at].astype(f32)
    total = taps[pl.ds(j * CONV + CONV - 1, 1), lanes(h)] * value
    for o in range(1, CONV):
        total = total + taps[pl.ds(j * CONV + CONV - 1 - o, 1), lanes(h)] * shifted(value, keep, o)
    return total


def span_masks(segc, segr, n):
    at = slice(n * SPAN, (n + 1) * SPAN)
    col = segc[at, :]
    same = col == jnp.broadcast_to(segr[0:1, at], (SPAN, SPAN))
    if n:
        carried = (col == segc[n * SPAN - 1 : n * SPAN, :]).astype(f32)
    else:
        carried = jnp.zeros((SPAN, HD), f32)
    ending = (col == col[SPAN - 1 : SPAN, :]).astype(f32)
    return carried, same, ending


def iotas():
    i = lax.broadcasted_iota(jnp.int32, (SPAN, SPAN), 0)
    j = lax.broadcasted_iota(jnp.int32, (SPAN, SPAN), 1)
    return i, j


def unit_inverses(lowers):
    i, j = iotas()
    apart = i ^ j
    invs = [jnp.where(apart == 1, -low, 0.0) for low in lowers]
    size, bits = 2, 1
    while size < SPAN:
        pairs = lax.shift_right_logical(apart, bits) == 1
        part = [jnp.where(pairs, low, 0.0) for low in lowers]
        small = [inv.astype(bf16) for inv in invs]
        left = [p + mm(s, p.astype(bf16)) for p, s in zip(part, small)]
        both = [w + mm(w.astype(bf16), s) for w, s in zip(left, small)]
        invs = [inv - b for inv, b in zip(invs, both)]
        size, bits = size * 2, bits + 1
    return invs


class Names:
    def __init__(self, names, refs):
        self.__dict__.update(zip(names, refs, strict=True))


class Sems:
    def __init__(self, ref):
        self.ref, self.used = ref, 0

    def take(self):
        self.used += 1
        return self.ref.at[self.used - 1]


def call(kernel, ins, outs, scratch, number, limit, *static):
    names = list(ins) + list(outs) + list(scratch)

    def run(*refs):
        kernel(Names(names, refs), *static)

    results = pl.pallas_call(
        run,
        out_shape=list(outs.values()),
        in_specs=[pl.BlockSpec(memory_space=ANY)] * len(ins),
        out_specs=[pl.BlockSpec(memory_space=ANY)] * len(outs),
        scratch_shapes=list(scratch.values()),
        compiler_params=pltpu.CompilerParams(
            collective_id=number, has_side_effects=True, vmem_limit_bytes=limit * MIB
        ),
    )(*ins.values())
    return dict(zip(outs, results, strict=True))


class Local:
    def __init__(self, sems):
        self.sems, self.open = sems, []

    def start(self, src, dst):
        copy = pltpu.make_async_copy(src, dst, self.sems.take())
        copy.start()
        self.open.append(copy)
        return copy

    def holds(self, copy):
        return any(copy is other for other in self.open)

    def wait(self, copy):
        copy.wait()
        self.open = [other for other in self.open if other is not copy]

    def done(self):
        for copy in self.open:
            copy.wait()
        self.open = []


class Remote:
    def __init__(self, place, sent, got):
        self.place, self.sent, self.got, self.open = place, sent, got, []

    def start(self, src, dst, hop):
        copy = pltpu.make_async_remote_copy(
            src_ref=src,
            dst_ref=dst,
            send_sem=self.sent.take(),
            recv_sem=self.got.take(),
            device_id=self.place.device(hop),
            device_id_type=MESH,
        )
        copy.start()
        self.open.append(copy)
        return copy

    def drain(self):
        for copy in self.open:
            copy.wait_send()
        self.open = []


class Later:
    def __init__(self):
        self.steps = []

    def add(self, step):
        self.steps.append(step)

    def tick(self, count):
        now, self.steps = self.steps[:count], self.steps[count:]
        for step in now:
            step()

    def finish(self):
        self.tick(len(self.steps))


def flat(ref, cols):
    value = ref[:, :, cols]
    shape = (value.shape[0] * value.shape[1], value.shape[2])
    if value.shape[1] % 16:
        return value.astype(f32).reshape(shape).astype(bf16)
    return value.reshape(shape)


STREAMS = (
    (0, 0, "zxy"),
    (0, 1, "zyx"),
    (1, 0, "zxy"),
    (1, 1, "zyx"),
    (2, 0, "xyz"),
    (2, 1, "yxz"),
)
NEIGHBOURS = ("x", "y", "up", "dn", "core")
OWN = (0, 0, 0)


def forward_kernel(r, levels, cfg):
    heads, spans, per, share = cfg["heads"], cfg["spans"], cfg["per"], cfg["share"]
    width, half, fhalf, heads_all = cfg["width"], cfg["half"], cfg["fhalf"], cfg["heads_all"]
    piece, rows = cfg["piece"], cfg["rows"]
    pc = Place(levels)
    loc = Local(Sems(r.loc_sem))
    rem = Remote(pc, Sems(r.send_sem), Sems(r.recv_sem))
    pc.meet(NEIGHBOURS)
    own = pc.shard(OWN, pc.t)
    targets = (r.w1, r.w_gu, r.w_down)
    streams = [
        Gather(pc, None, targets[a], hf, order, r.__dict__["gs%d" % k], r.__dict__["gr%d" % k])
        for k, (a, hf, order) in enumerate(STREAMS)
    ]
    s0, s1, s2 = streams[0:2], streams[2:4], streams[4:6]

    def both(src_at, dst):
        return [loc.start(src_at(pc.t), dst), rem.start(src_at(1 - pc.t), dst, "core")]

    def cut(n, t):
        return pl.ds(pl.multiple_of(t * n, n), n)

    opening = []
    for j in range(3):
        opening += both(
            lambda t, j=j: r.qkv.at[j, :, cut(half, t)],
            r.w1.at[own, :, j * half : (j + 1) * half],
        )
    opening += both(lambda t: r.out_w.at[:, cut(half, t)], r.w1.at[own, :, 3 * half : 4 * half])
    opening += both(lambda t: r.ext, r.w1.at[own, :, 4 * half : 4 * half + HD])
    pieces = both(lambda t: r.tok.at[pc.x], r.x.at[pc.c])
    pieces += both(lambda t: r.flags.at[pc.x], r.marks.at[pc.c])

    def arrived(copies):
        for copy in copies:
            if loc.holds(copy):
                loc.wait(copy)
            else:
                copy.wait_recv()

    arrived(opening)
    for s in s0:
        s.pass_on(OWN)
    cross = [
        rem.start(r.tok.at[1 - pc.x], r.x.at[pc.c], "x"),
        rem.start(r.flags.at[1 - pc.x], r.marks.at[pc.c], "x"),
    ]
    second = []
    for j in range(2):
        second += both(
            lambda t, j=j: r.gu.at[j, :, cut(fhalf, t)],
            r.w_gu.at[own, :, j * fhalf : (j + 1) * fhalf],
        )
    second += both(lambda t: r.dn.at[:, cut(fhalf, t)], r.w_down.at[own])
    second += both(lambda t: r.cot.at[pc.x], r.dy.at[pc.c])

    ordered = blocks_of(levels)

    def moves(block, s):
        return block != OWN and route(block, s.order)[0]

    arrived(second[:6])
    for s in s1:
        s.pass_on(OWN, ("up", "dn"))
    far = (1 - pc.x) * 2 + pc.t
    for block in ordered:
        depth = abs(block[0]) + block[1] + block[2]
        for s in s0:
            if moves(block, s) and depth == 1:
                s.wait(block)
                s.pass_on(block)
    for s in s1:
        for block in ((-1, 0, 0), (1, 0, 0)):
            s.wait(block)
            s.pass_on(block, ("up", "dn"))
    for copy in cross:
        copy.wait_recv()
    arrived(pieces)
    pieces = [
        rem.start(r.x.at[far], r.x.at[far], "core"),
        rem.start(r.marks.at[far], r.marks.at[far], "core"),
    ]
    for block in ordered:
        depth = abs(block[0]) + block[1] + block[2]
        for s in s0:
            if moves(block, s) and depth > 1:
                s.wait(block)
                s.pass_on(block)
    for s in s2:
        s.pass_on(OWN)
    for s in s1:
        s.pass_on(OWN, ("x", "y"))
    arrived(pieces)

    i, j = iotas()
    upto = (i >= j).astype(bf16)
    base = jnp.zeros((1, HD), f32)
    for n in range(spans):
        q, at = divmod(n * SPAN, piece)
        marks = r.marks[q, at : at + SPAN, :]
        seg = mm(upto, marks) + base
        r.segc[n * SPAN : (n + 1) * SPAN, :] = seg
        r.segr[:, n * SPAN : (n + 1) * SPAN] = jnp.transpose(seg)[0:8, :]
        base = seg[SPAN - 1 : SPAN, :]
    set_masks(r.segc, r.keep)
    loc.start(r.segc, r.segc_out)
    loc.start(r.segr, r.segr_out)

    for block in ordered:
        for s in s0:
            if block != OWN and not route(block, s.order)[0]:
                s.wait(block)
    shards = levels * 8 // 2
    mine = cut(half, pc.t)
    rows_of = lambda t: pl.ds(pl.multiple_of(t * shards, shards), shards)
    side = pl.ds(3 * half, half)
    swap_out = [
        loc.start(r.w1.at[rows_of(pc.t), :, side], r.wo.at[:, :, mine]),
        rem.start(r.w1.at[rows_of(1 - pc.t), :, side], r.wo.at[:, :, mine], "core"),
    ]

    later = Later()
    for block in ordered:
        if abs(block[0]) > 1 and not block[1] and not block[2]:
            for s in s1:
                later.add(
                    lambda s=s, block=block: (s.wait(block), s.pass_on(block, ("up", "dn")))
                )
    cot_cross = []
    for block in ordered:
        for s in s1:
            if block != OWN and not block[1] and not block[2]:
                later.add(lambda s=s, block=block: s.pass_on(block, ("x", "y")))
            elif moves(block, s):
                later.add(lambda s=s, block=block: (s.wait(block), s.pass_on(block)))
        for s in s2:
            if moves(block, s):
                later.add(lambda s=s, block=block: (s.wait(block), s.pass_on(block)))
        if block == ordered[len(ordered) // 2]:
            later.add(
                lambda: cot_cross.append(rem.start(r.cot.at[1 - pc.x], r.dy.at[pc.c], "x"))
            )

    extra = flat(r.w1, slice(4 * half, 4 * half + HD))
    for n in range(width // SPAN):
        at = slice(n * SPAN, (n + 1) * SPAN)
        r.small[:, at] = jnp.transpose(extra[at, :].astype(f32))[0:32, :]
    r.gains[...] = r.small[0:8, :]
    r.taps[...] = jnp.zeros(r.taps.shape, f32)
    r.taps[0 : 3 * CONV, :] = r.small[2 : 2 + 3 * CONV, cut(half, pc.t)]
    place_r = lax.broadcasted_iota(jnp.int32, (width, HD), 0)
    place_c = lax.broadcasted_iota(jnp.int32, (width, HD), 1)
    chosen = (place_r == share * (place_c // per) + place_c % per).astype(bf16)
    at = 2 + 3 * CONV + heads_all
    r.hgain[...] = jnp.broadcast_to(
        mm(r.small[at - at % 8 : at - at % 8 + 8, :].astype(bf16), chosen)[at % 8 : at % 8 + 1, :],
        (8, HD),
    )
    pick_r = lax.broadcasted_iota(jnp.int32, (HD, half), 0)
    pick_c = lax.broadcasted_iota(jnp.int32, (HD, half), 1)
    chosen = (pick_r == 2 + 3 * CONV + heads * pc.t + pick_c // HD).astype(bf16)
    r.wmix[:, 3 * half :] = mm(extra, chosen).astype(bf16)
    for k in range(3):
        r.wmix[:, k * half : (k + 1) * half] = flat(r.w1, slice(k * half, (k + 1) * half))
    loc.start(r.wmix, r.wmix_out)
    loc.start(r.taps, r.taps_out)
    loc.start(r.gains, r.gains_out)
    loc.start(r.hgain, r.hgain_out)

    g0 = r.gains[0:1, :]
    for n in range(rows // piece):
        x = r.x[n].astype(f32)
        inv = lax.rsqrt(jnp.mean(x * x, axis=-1, keepdims=True) + 1e-5)
        r.normed[n * piece : (n + 1) * piece, :] = (x * inv * g0).astype(bf16)
    loc.start(r.normed, r.normed_out)
    loc.start(r.x, r.x_out)

    def project(k, carry):
        at = pl.ds(pl.multiple_of(k * piece, piece), piece)
        left = r.normed[at, :]
        r.proj[at, :] = mm(left, r.wmix[:, : 3 * half]).astype(bf16)
        r.logit[at, :] = mm(left, r.wmix[:, 3 * half :])
        return carry

    lax.fori_loop(0, rows // piece, project, 0)
    loc.start(r.proj, r.proj_out)
    loc.start(r.logit, r.logit_out)
    later.tick(cfg["ticks"][0])

    batches = []
    for h in range(heads):
        now, later.steps = later.steps[: cfg["ticks"][1]], later.steps[cfg["ticks"][1] :]
        batches.append(now)

    def prepare(h, carry):
        for k, now in enumerate(batches):
            if now:
                pl.when(h == k)(lambda now=now: [step() for step in now] and None)
        delta_prepare(r, h, heads, spans)
        return carry

    lax.fori_loop(0, heads, prepare, 0)
    for src, dst in ((r.qs, r.qs_out), (r.ks, r.ks_out), (r.vs, r.vs_out), (r.ws, r.ws_out),
                     (r.ns, r.ns_out), (r.ps, r.ps_out)):
        loc.start(src, dst)
    delta_chain(r, heads, spans, lambda: later.tick(cfg["ticks"][2]))
    for h in range(heads):
        head = slice(h * HD, (h + 1) * HD)
        o = r.out[:, head]
        scale = lax.rsqrt(jnp.mean(o * o, axis=-1, keepdims=True) + 1e-5)
        r.headed[:, head] = (o * scale * r.hgain[0:1, :]).astype(bf16)
    for src, dst in ((r.fs, r.fs_out), (r.ss, r.ss_out), (r.out, r.out_out),
                     (r.headed, r.headed_out)):
        loc.start(src, dst)
    arrived(swap_out)
    loc.start(r.wo, r.wo_out)
    wo = flat(r.wo, slice(None))
    sent = []
    for n in range(rows // piece):
        r.mine[n] = mm(r.headed[n * piece : (n + 1) * piece, :], wo).astype(bf16)
        sent.append(rem.start(r.mine.at[n], r.theirs.at[n], "core"))
    later.tick(cfg["ticks"][3])
    g1 = r.gains[1:2, :]
    for n in range(rows // piece):
        sent[n].wait_recv()
        at = slice(n * piece, (n + 1) * piece)
        res = r.x[n].astype(f32) + r.mine[n].astype(f32) + r.theirs[n].astype(f32)
        r.res[at, :] = res
        inv = lax.rsqrt(jnp.mean(res * res, axis=-1, keepdims=True) + 1e-5)
        r.normed2[at, :] = (res * inv * g1).astype(bf16)
    loc.start(r.res, r.res_out)
    loc.start(r.normed2, r.normed2_out)
    later.finish()
    cot_cross[0].wait_recv()
    arrived(second[6:])
    last = rem.start(r.dy.at[far], r.dy.at[far], "core")
    for block in ordered:
        for s in s1 + s2:
            if block != OWN and not route(block, s.order)[0]:
                s.wait(block)
    last.wait_recv()
    for s in streams:
        s.drain(ordered)
    rem.drain()
    loc.done()


def delta_prepare(r, h, heads, spans):
    i, j = iotas()
    mixed = []
    for which in range(3):
        value = conv_of(r.proj, r.taps, r.keep, which, h, heads)
        mixed.append(value * jax.nn.sigmoid(value))
    for which, dest in ((0, r.qs), (1, r.ks)):
        w = mixed[which]
        unit = w * lax.rsqrt(jnp.sum(w * w, axis=-1, keepdims=True) + 1e-6)
        dest[:, lanes(h)] = unit.astype(bf16)
    r.vs[:, lanes(h)] = mixed[2].astype(bf16)
    lowers, rights = [], []
    for n in range(spans):
        at = slice(n * SPAN, (n + 1) * SPAN)
        k = r.ks[at, lanes(h)]
        q = r.qs[at, lanes(h)]
        v = r.vs[at, lanes(h)]
        beta = jax.nn.sigmoid(r.logit[at, lanes(h)])
        carried, same, ending = span_masks(r.segc, r.segr, n)
        lowers.append(jnp.where(same & (i > j), beta * mm_nt(k, k), 0.0))
        r.ps[h * spans + n] = jnp.where(same & (i >= j), mm_nt(q, k), 0.0).astype(bf16)
        r.cqs[at, lanes(h)] = (carried * q.astype(f32)).astype(bf16)
        rights.append(
            jnp.concatenate([beta * v.astype(f32), (beta * carried) * k.astype(f32)], axis=1)
        )
    for n, inv in enumerate(unit_inverses(lowers)):
        at = slice(n * SPAN, (n + 1) * SPAN)
        small = inv.astype(bf16)
        r.ns[h * spans + n] = small
        both = rights[n] + mm(small, rights[n].astype(bf16))
        r.us[at, lanes(h)] = both[:, :HD]
        r.ws[at, lanes(h)] = both[:, HD:].astype(bf16)


def delta_chain(r, heads, spans, between):
    states = [jnp.zeros((HD, HD), f32) for _ in range(heads)]
    for n in range(spans):
        at = slice(n * SPAN, (n + 1) * SPAN)
        carried, same, ending = span_masks(r.segc, r.segr, n)
        for h in range(heads):
            head = slice(h * HD, (h + 1) * HD)
            state = states[h].astype(bf16)
            r.ss[h * spans + n] = state
            seen = mm(jnp.concatenate([r.ws[at, head], r.cqs[at, head]], axis=0), state)
            fresh = r.us[at, head] - seen[:SPAN]
            small = fresh.astype(bf16)
            r.fs[at, head] = small
            r.out[at, head] = seen[SPAN:] + mm(r.ps[h * spans + n], small)
            states[h] = carried[SPAN - 1 : SPAN, :] * states[h] + mm_tn(
                r.ks[at, head], (ending * fresh).astype(bf16)
            )
        between()


def forward(qkv, out_w, gu, dn, ext, tok, cot, flags, levels, per, heads_all):
    share = qkv.shape[1]
    width = qkv.shape[2]
    half, fhalf = width // 2, dn.shape[1] // 2
    piece = tok.shape[1]
    rows = 4 * piece
    heads = half // HD
    spans = rows // SPAN
    shards = levels * 8
    sds = jax.ShapeDtypeStruct
    wide, square = sds((rows, half), bf16), sds((heads * spans, SPAN, SPAN), bf16)
    seg = dict(
        segc=sds((rows, HD), f32),
        segr=sds((8, rows), f32),
        wmix=sds((width, 4 * half), bf16),
        taps=sds((16, half), f32),
        gains=sds((8, width), f32),
        hgain=sds((8, HD), f32),
        normed=sds((rows, width), bf16),
        x=sds((4, piece, width), bf16),
        proj=sds((rows, 3 * half), bf16),
        logit=sds((rows, half), f32),
        qs=wide, ks=wide, vs=wide, fs=wide, ws=wide, headed=wide,
        ns=square, ps=square, ss=square,
        out=sds((rows, half), f32),
        wo=sds((shards // 2, share, width), bf16),
        res=sds((rows, width), f32),
        normed2=sds((rows, width), bf16),
    )
    ins = dict(qkv=qkv, out_w=out_w, gu=gu, dn=dn, ext=ext, tok=tok, cot=cot, flags=flags)
    outs = {
        "w_gu": sds((shards, share, 2 * fhalf), bf16),
        "w_down": sds((shards, share, fhalf), bf16),
        "dy": sds((4, piece, width), bf16),
    }
    outs.update({k + "_out": v for k, v in seg.items()})
    scratch = {k: VM(v.shape, v.dtype) for k, v in seg.items()}
    scratch.update(
        w1=VM((shards, share, 4 * half + HD), bf16),
        marks=VM((4, piece, HD), bf16),
        keep=VM((CONV - 1, rows, HD), f32),
        small=VM((32, width), f32),
        us=VM((rows, half), f32),
        cqs=VM((rows, half), bf16),
        mine=VM((4, piece, width), bf16),
        theirs=VM((4, piece, width), bf16),
        loc_sem=pltpu.SemaphoreType.DMA((48,)),
        send_sem=pltpu.SemaphoreType.DMA((32,)),
        recv_sem=pltpu.SemaphoreType.DMA((32,)),
    )
    for k, (a, hf, order) in enumerate(STREAMS):
        sent, got = Gather.sems(levels, order)
        scratch["gs%d" % k] = pltpu.SemaphoreType.DMA((sent,))
        scratch["gr%d" % k] = pltpu.SemaphoreType.DMA((got,))
    cfg = dict(
        heads=heads, spans=spans, per=per, share=share, width=width, half=half, fhalf=fhalf,
        heads_all=heads_all, piece=piece, rows=rows, ticks=(6, 5, 1, 4),
    )
    return call(forward_kernel, ins, outs, scratch, 1, 58, levels, cfg)


def unflat(value, share):
    return value.reshape(value.shape[0] // share, share, value.shape[1]).astype(bf16)


def backward_kernel(r, levels, cfg):
    heads, spans, per, share = cfg["heads"], cfg["spans"], cfg["per"], cfg["share"]
    width, half, heads_all = cfg["width"], cfg["half"], cfg["heads_all"]
    piece, rows = cfg["piece"], cfg["rows"]
    pc = Place(levels)
    loc = Local(Sems(r.loc_sem))
    rem = Remote(pc, Sems(r.send_sem), Sems(r.recv_sem))
    pc.meet(NEIGHBOURS)
    pieces = rows // piece
    first_in = [
        [rem.start(r.mine_in.at[n], r.theirs.at[n], "core"), loc.start(r.mine_in.at[n], r.mine.at[n]),
         loc.start(r.res_in.at[n], r.res.at[n])]
        + [loc.start(r.dy_in.at[n, :, pl.ds(c * half, half)],
                     r.datt.at[c, pl.ds(n * piece, piece), :]) for c in range(2)]
        for n in range(pieces)
    ]
    small_in = [loc.start(a, b) for a, b in (
        (r.gains_in, r.gains), (r.hgain_in, r.hgain), (r.taps_in, r.taps), (r.segc_in, r.segc),
        (r.segr_in, r.segr), (r.headed_in, r.headed), (r.wo_in, r.wo))]
    grads = (None, r.g_gu, r.g_down)
    finals = (None, r.f_gu, r.f_down)
    load = [loc.start(r.g_down_in, r.g_down), loc.start(r.g_gu_in, r.g_gu)]
    delta_in = [loc.start(a, b) for a, b in (
        (r.out_in, r.out), (r.logit_in, r.logit), (r.proj_in, r.dproj.at[:, pl.ds(0, 3 * half)]),
        (r.qs_in, r.sv.at[0]), (r.ks_in, r.sv.at[1]), (r.vs_in, r.sv.at[2]),
        (r.fs_in, r.sv.at[3]), (r.ws_in, r.sv.at[4]),
        (r.ns_in, r.sq.at[0]), (r.ps_in, r.sq.at[1]), (r.ss_in, r.sq.at[2]))]
    streams = [
        Scatter(pc, grads[a], r.__dict__["room%d" % k], finals[a], hf, order,
                r.__dict__["ss%d" % k], r.__dict__["sr%d" % k])
        for k, (a, hf, order) in enumerate(RETURNS)
    ]
    def arrived(copies):
        for copy in copies:
            if loc.holds(copy):
                loc.wait(copy)
            else:
                copy.wait_recv()

    ordered = blocks_of(levels)[::-1]
    arrived(load)
    for s in streams:
        for block in ordered:
            if not route(block, s.order)[0]:
                s.forward(block)
    crossing = rem.start(r.lo_in, r.lo_out, "x")
    later = Later()
    for block in ordered:
        for s in streams:
            if block != OWN and route(block, s.order)[0]:
                later.add(lambda s=s, block=block: s.forward(block))

    arrived(small_in)
    g1 = r.gains[1:2, :]
    gain1 = jnp.zeros((1, width), f32)
    for n in range(pieces):
        arrived(first_in[n])
        v = r.res[n]
        grad = r.mine[n].astype(f32) + r.theirs[n].astype(f32)
        inv = lax.rsqrt(jnp.mean(v * v, axis=-1, keepdims=True) + 1e-5)
        scaled = grad * g1
        back = inv * scaled - v * (inv * inv * inv * jnp.mean(scaled * v, axis=-1, keepdims=True))
        at = slice(n * piece, (n + 1) * piece)
        dres = back + jnp.concatenate([r.datt[0, at, :], r.datt[1, at, :]], axis=1).astype(f32)
        ours = (pc.t == n % 2).astype(f32)
        gain1 = gain1 + ours * jnp.sum(grad * v * inv, axis=0, keepdims=True)

        def keep_own(n=n, dres=dres):
            r.res[n // 2] = dres

        pl.when(pc.t == n % 2)(keep_own)
        low = dres.astype(bf16)
        r.datt[0, at, :] = low[:, :half]
        r.datt[1, at, :] = low[:, half:]
    r.cols[...] = jnp.zeros(r.cols.shape, f32)
    r.cols[1:2, :] = gain1
    later.tick(cfg["ticks"][0])
    wo = flat(r.wo, slice(None))
    for c in range(2):
        at = slice(c * heads * HD // share, (c + 1) * heads * HD // share)
        r.gm[0, at] = unflat(mm_tn(r.headed[...], r.datt[c]), share)

    def cut(n, t):
        return pl.ds(pl.multiple_of(t * n, n), n)

    shards = levels * 8 // 2
    rows_of = lambda t: pl.ds(pl.multiple_of(t * shards, shards), shards)
    side = pl.ds(3 * half, half)
    gout = [
        loc.start(r.gm.at[0, rows_of(pc.t)], r.g_first.at[rows_of(pc.t), :, side]),
        rem.start(r.gm.at[0, rows_of(1 - pc.t)], r.g_first.at[rows_of(pc.t), :, side], "core"),
    ]
    for n in range(pieces):
        at = slice(n * piece, (n + 1) * piece)
        r.dheaded[at, :] = (
            mm_nt(r.datt[0, at, :], wo[:, :half]) + mm_nt(r.datt[1, at, :], wo[:, half:])
        ).astype(bf16)
    later.tick(cfg["ticks"][1])

    arrived(delta_in)
    set_masks(r.segc, r.keep)
    qs, ks, vs, fs, ws = (r.sv.at[k] for k in range(5))
    ns, ps, ss = (r.sq.at[k] for k in range(3))
    douts, xs = r.datt.at[0], r.datt.at[1]
    ys, hs, gs = r.headed, r.out, r.dheaded
    i, j = iotas()
    first = lax.broadcasted_iota(jnp.int32, (SPAN, HD), 1) == 0

    def in_loop(h, count):
        now = []
        for k in range(heads):
            now.append(later.steps[:count])
            later.steps = later.steps[count:]
        for k, steps in enumerate(now):
            if steps:
                pl.when(h == k)(lambda steps=steps: [step() for step in steps] and None)

    def norm_back(h, dgain_sum):
        o = r.out[:, lanes(h)]
        dyh = r.dheaded[:, lanes(h)].astype(f32)
        inv = lax.rsqrt(jnp.mean(o * o, axis=-1, keepdims=True) + 1e-5)
        scaled = dyh * r.hgain[0:1, :]
        dout = inv * scaled - o * (inv * inv * inv * jnp.mean(scaled * o, axis=-1, keepdims=True))
        dgain_sum = dgain_sum + jnp.sum(dyh * o * inv, axis=0, keepdims=True)
        for n in range(spans):
            at = slice(n * SPAN, (n + 1) * SPAN)
            carried, same, ending = span_masks(r.segc, r.segr, n)
            small = dout[at].astype(bf16)
            douts[at, lanes(h)] = small
            x = mm_tn(ps[h * spans + n], small).astype(bf16)
            xs[at, lanes(h)] = x
            cdout = (carried * dout[at]).astype(bf16)
            hs[at, lanes(h)] = mm_tn(qs[at, lanes(h)], cdout) - mm_tn(ws[at, lanes(h)], x)
        in_loop(h, cfg["ticks"][2])
        return dgain_sum

    dgain = lax.fori_loop(0, heads, norm_back, jnp.zeros((1, HD), f32))
    grads_s = [jnp.zeros((HD, HD), f32) for _ in range(heads)]
    for n in reversed(range(spans)):
        at = slice(n * SPAN, (n + 1) * SPAN)
        carried, same, ending = span_masks(r.segc, r.segr, n)
        for h in range(heads):
            head = slice(h * HD, (h + 1) * HD)
            g = grads_s[h].astype(bf16)
            gs[at, head] = g
            y = (ending * mm(ks[at, head], g)).astype(bf16)
            ys[at, head] = y
            if n:
                grads_s[h] = (
                    carried[SPAN - 1 : SPAN, :] * grads_s[h]
                    - mm_tn(ws[at, head], y)
                    + hs[at, head]
                )
        later.tick(cfg["ticks"][3])

    per_piece = piece // SPAN

    def spot(which, n):
        return (
            pieces // 2 + which // 2,
            slice((n % per_piece) * SPAN, (n % per_piece + 1) * SPAN),
            slice(
                ((which % 2) * pieces + n // per_piece) * HD,
                ((which % 2) * pieces + n // per_piece + 1) * HD,
            ),
        )

    def put(which, n, value):
        r.res[spot(which, n)] = value

    def taken(which):
        return jnp.concatenate([r.res[spot(which, n)] for n in range(spans)], axis=0)

    def pull(h, carry):
        head = lanes(h)
        for n in range(spans):
            at = slice(n * SPAN, (n + 1) * SPAN)
            carried, same, ending = span_masks(r.segc, r.segr, n)
            which = h * spans + n
            q, k, v, f = qs[at, head], ks[at, head], vs[at, head], fs[at, head]
            state, g, p, inv = ss[which], gs[at, head], ps[which], ns[which]
            beta = jax.nn.sigmoid(r.logit[at, head])
            small = douts[at, head]
            df = xs[at, head].astype(f32) + ys[at, head].astype(f32)
            z = df + mm_tn(inv, df.astype(bf16))
            zb = z.astype(bf16)
            dp = jnp.where(same & (i >= j), mm_nt(small, f), 0.0).astype(bf16)
            dl = jnp.where(same & (i > j), -mm_nt(zb, f), 0.0)
            known = v.astype(f32) - carried * mm(k, state)
            dbeta = jnp.sum(z * known + dl * mm_nt(k, k), axis=-1, keepdims=True)
            b = beta[:, 0:1]
            dlogit = dbeta * b * (1.0 - b)
            r.dproj[at, pl.ds(pl.multiple_of((3 * heads + h) * HD, HD), HD)] = jnp.where(
                first, jnp.broadcast_to(dlogit, (SPAN, HD)), 0.0
            ).astype(bf16)
            e = (beta * dl).astype(bf16)
            put(0, n, carried * mm_nt(small, state) + mm(dp, k))
            put(2, n, beta * z)
            put(1, n, (
                mm(e, k)
                + mm_tn(e, k)
                + mm_tn(dp, q)
                - (carried * beta) * mm_nt(zb, state)
                + ending * mm_nt(f, g)
            ))
        for which in range(3):
            c = conv_of(r.dproj, r.taps, r.keep, which, h, heads)
            s = jax.nn.sigmoid(c)
            d = taken(which)
            if which < 2:
                w = c * s
                n = lax.rsqrt(jnp.sum(w * w, axis=-1, keepdims=True) + 1e-6)
                d = n * d - w * (n * n * n * jnp.sum(w * d, axis=-1, keepdims=True))
            dc = d * (s * (1.0 + c * (1.0 - s)))
            at = lanes(which * heads + h)
            value = r.dproj[:, at].astype(f32)
            total = None
            for o in range(CONV):
                row = which * CONV + CONV - 1 - o
                tap = r.taps[pl.ds(row, 1), lanes(h)]
                r.dtaps[pl.ds(row, 1), lanes(h)] = jnp.sum(
                    dc * shifted(value, r.keep, o), axis=0, keepdims=True
                )
                if o == 0:
                    total = tap * dc
                else:
                    total = total + tap * pltpu.roll(dc * r.keep[o - 1], rows - o, 0)
            r.dproj[:, at] = total.astype(bf16)
        in_loop(h, cfg["ticks"][4])
        return carry

    lax.fori_loop(0, heads, pull, 0)

    weights_in = [
        loc.start(r.wmix_in.at[:, pl.ds(k * half, half)], r.sv.at[k]) for k in range(4)
    ]
    normed_in = [
        loc.start(r.normed_in.at[:, pl.ds(0, half)], r.sv.at[4]),
        loc.start(r.normed_in.at[:, pl.ds(half, half)], r.headed),
    ]
    x_in = [
        loc.start(r.x_in.at[2 * k + pc.t], r.theirs.at[2 + k]) for k in range(pieces // 2)
    ]
    arrived(weights_in)

    def partial(which, at):
        n = which
        where = pl.ds(pl.multiple_of(n * piece, piece), piece)
        total = mm_nt(r.dproj[where, :half], r.sv[0])
        for k in range(1, 4):
            total = total + mm_nt(r.dproj[where, k * half : (k + 1) * half], r.sv[k])
        r.mine[at] = total.astype(bf16)

    sent = []
    for k in range(pieces // 2):
        partial(2 * k + 1 - pc.t, 2 + k)
        sent.append(rem.start(r.mine.at[2 + k], r.theirs3.at[k], "core"))
    for k in range(pieces // 2):
        partial(2 * k + pc.t, k)
    later.tick(cfg["ticks"][5])
    arrived(normed_in)
    arrived(gout[:1])
    gout[1].wait_send()
    rem.open = [copy for copy in rem.open if copy is not gout[1]]
    hw = half // share
    for k in range(3):
        for c, left in enumerate((r.sv.at[4], r.headed)):
            at = slice(c * hw, (c + 1) * hw)
            r.gm[k, at] = unflat(mm_tn(left[...], r.dproj[:, k * half : (k + 1) * half]), share)
        loc.start(r.gm.at[k], r.g_first.at[:, :, pl.ds(k * half, half)])
        later.tick(cfg["ticks"][6])

    arrived(x_in)
    g0 = r.gains[0:1, :]
    gain0 = jnp.zeros((1, width), f32)
    for k in range(pieces // 2):
        sent[k].wait_recv()
        v = r.theirs[2 + k].astype(f32)
        grad = r.mine[k].astype(f32) + r.theirs3[k].astype(f32)
        inv = lax.rsqrt(jnp.mean(v * v, axis=-1, keepdims=True) + 1e-5)
        scaled = grad * g0
        back = inv * scaled - v * (inv * inv * inv * jnp.mean(scaled * v, axis=-1, keepdims=True))
        gain0 = gain0 + jnp.sum(grad * v * inv, axis=0, keepdims=True)
        r.theirs[k] = (back + r.res[k]).astype(bf16)
        loc.start(r.theirs.at[k], r.dx.at[k])
    r.cols[0:1, :] = gain0
    r.cols[2 : 2 + 3 * CONV, cut(half, pc.t)] = r.dtaps[0 : 3 * CONV, :]
    place_r = lax.broadcasted_iota(jnp.int32, (HD, width), 0)
    place_c = lax.broadcasted_iota(jnp.int32, (HD, width), 1)
    spread = ((place_c // share * per + place_c % share == place_r) & (place_c % share < per)).astype(bf16)
    at = 2 + 3 * CONV + heads_all
    r.cols[at : at + 1, :] = mm(jnp.broadcast_to(dgain, (8, HD)).astype(bf16), spread)[0:1, :]
    pick_r = lax.broadcasted_iota(jnp.int32, (half, HD), 0)
    pick_c = lax.broadcasted_iota(jnp.int32, (half, HD), 1)
    chosen = (
        (pick_c == 2 + 3 * CONV + heads * pc.t + pick_r // HD) & (pick_r % HD == 0)
    ).astype(bf16)
    for c, left in enumerate((r.sv.at[4], r.headed)):
        beta = mm(mm_tn(left[...], r.dproj[:, 3 * half :]).astype(bf16), chosen)
        for n in range(half // SPAN):
            at = c * half + n * SPAN
            rows_in = jnp.concatenate(
                [r.cols[:, at : at + SPAN], jnp.zeros((HD - 32, SPAN), f32)], axis=0
            )
            block = jnp.transpose(rows_in) + beta[n * SPAN : (n + 1) * SPAN]
            r.ge[at // share : (at + SPAN) // share] = unflat(block, share)
    loc.start(r.ge, r.g_first.at[:, :, pl.ds(4 * half, HD)])
    gout[1].wait_recv()
    later.finish()
    for s in streams:
        s.finish()
    last = []
    for src, dst in ((r.f_down, r.o_down), (r.f_gu, r.o_gu)):
        loc.start(src.at[pc.t], dst.at[pc.t])
        last.append(rem.start(src.at[1 - pc.t], dst.at[pc.t], "core"))
    for copy in last:
        copy.wait_recv()
    crossing.wait_recv()
    for s in streams:
        s.drain(ordered)
    rem.drain()
    loc.done()


RETURNS = ((2, 0, "xyz"), (2, 1, "yxz"), (1, 0, "zxy"), (1, 1, "zyx"))


def backward(f, mine, g_gu, g_down, lo, levels, per, heads_all):
    width = f["normed_out"].shape[1]
    rows = f["normed_out"].shape[0]
    half = f["logit_out"].shape[1]
    piece = rows // 4
    share = f["wo_out"].shape[1]
    heads = half // HD
    spans = rows // SPAN
    shards = levels * 8
    sds = jax.ShapeDtypeStruct
    ins = dict(
        mine_in=mine.reshape(4, piece, width),
        res_in=f["res_out"].reshape(4, piece, width),
        dy_in=f["dy"],
        x_in=f["x_out"],
        gains_in=f["gains_out"], hgain_in=f["hgain_out"], taps_in=f["taps_out"],
        segc_in=f["segc_out"], segr_in=f["segr_out"], headed_in=f["headed_out"],
        wo_in=f["wo_out"], out_in=f["out_out"], logit_in=f["logit_out"], proj_in=f["proj_out"],
        normed_in=f["normed_out"], wmix_in=f["wmix_out"],
        g_gu_in=g_gu, g_down_in=g_down, lo_in=lo,
    )
    ins.update({k + "_in": f[k + "_out"] for k in ("qs", "ks", "vs", "fs", "ws", "ns", "ps", "ss")})
    outs = dict(
        g_first=sds((shards, share, 4 * half + HD), bf16),
        dx=sds((2, piece, width), bf16),
        o_gu=sds((2, share, g_gu.shape[2]), f32),
        o_down=sds((2, share, g_down.shape[2]), f32),
        lo_out=sds(lo.shape, bf16),
    )
    scratch = dict(
        mine=VM((4, piece, width), bf16),
        theirs=VM((4, piece, width), bf16),
        theirs3=VM((2, piece, width), bf16),
        res=VM((4, piece, width), f32),
        gains=VM((8, width), f32),
        hgain=VM((8, HD), f32),
        taps=VM((16, half), f32),
        dtaps=VM((16, half), f32),
        segc=VM((rows, HD), f32),
        segr=VM((8, rows), f32),
        headed=VM((rows, half), bf16),
        wo=VM((shards // 2, share, width), bf16),
        datt=VM((2, rows, half), bf16),
        cols=VM((32, width), f32),
        gm=VM((3, shards, share, half), bf16),
        ge=VM((shards, share, HD), bf16),
        dheaded=VM((rows, half), bf16),
        sv=VM((5, rows, half), bf16),
        sq=VM((3, heads * spans, SPAN, SPAN), bf16),
        out=VM((rows, half), f32),
        logit=VM((rows, half), f32),
        dproj=VM((rows, 4 * half), bf16),
        keep=VM((CONV - 1, rows, HD), f32),
        g_gu=VM(g_gu.shape, bf16),
        g_down=VM(g_down.shape, bf16),
        f_gu=VM((2,) + g_gu.shape[1:], f32),
        f_down=VM((2,) + g_down.shape[1:], f32),
        loc_sem=pltpu.SemaphoreType.DMA((64,)),
        send_sem=pltpu.SemaphoreType.DMA((16,)),
        recv_sem=pltpu.SemaphoreType.DMA((16,)),
    )
    sizes = {1: g_gu.shape[1:], 2: g_down.shape[1:]}
    for k, (a, hf, order) in enumerate(RETURNS):
        slots, sent = Scatter.slots_of(levels, order)
        scratch["room%d" % k] = VM((slots,) + sizes[a], bf16)
        scratch["ss%d" % k] = pltpu.SemaphoreType.DMA((sent,))
        scratch["sr%d" % k] = pltpu.SemaphoreType.DMA((slots,))
    cfg = dict(
        heads=heads, spans=spans, per=per, share=share, width=width, half=half,
        heads_all=heads_all, piece=piece, rows=rows, ticks=(4, 4, 5, 2, 6, 4, 3),
    )
    return call(backward_kernel, ins, outs, scratch, 2, 63, levels, cfg)


LAST = ((0, 0, "zxy"), (0, 1, "zyx"))


def last_kernel(r, levels, cfg):
    pc = Place(levels)
    loc = Local(Sems(r.loc_sem))
    rem = Remote(pc, Sems(r.send_sem), Sems(r.recv_sem))
    load = loc.start(r.g_in, r.g)
    pc.meet(NEIGHBOURS)
    streams = [
        Scatter(pc, r.g, r.__dict__["room%d" % k], r.final, hf, order,
                r.__dict__["ss%d" % k], r.__dict__["sr%d" % k])
        for k, (a, hf, order) in enumerate(LAST)
    ]
    ordered = blocks_of(levels)[::-1]
    loc.wait(load)
    for s in streams:
        for block in ordered:
            if not route(block, s.order)[0]:
                s.forward(block)
    crossing = rem.start(r.dx_in, r.dx_out, "x")
    for block in ordered:
        for s in streams:
            if block != OWN and route(block, s.order)[0]:
                s.forward(block)
    for s in streams:
        s.finish()
    loc.start(r.final.at[pc.t], r.o_first.at[pc.t])
    copy = rem.start(r.final.at[1 - pc.t], r.o_first.at[pc.t], "core")
    copy.wait_recv()
    crossing.wait_recv()
    for s in streams:
        s.drain(ordered)
    rem.drain()
    loc.done()


def last_scatter(g, dx, levels):
    sds = jax.ShapeDtypeStruct
    scratch = dict(
        g=VM(g.shape, bf16),
        final=VM((2,) + g.shape[1:], f32),
        loc_sem=pltpu.SemaphoreType.DMA((8,)),
        send_sem=pltpu.SemaphoreType.DMA((8,)),
        recv_sem=pltpu.SemaphoreType.DMA((8,)),
    )
    for k, (a, hf, order) in enumerate(LAST):
        slots, sent = Scatter.slots_of(levels, order)
        scratch["room%d" % k] = VM((slots,) + g.shape[1:], bf16)
        scratch["ss%d" % k] = pltpu.SemaphoreType.DMA((sent,))
        scratch["sr%d" % k] = pltpu.SemaphoreType.DMA((slots,))
    return call(
        last_kernel,
        dict(g_in=g, dx_in=dx),
        dict(o_first=sds((2,) + g.shape[1:], f32), dx_out=sds(dx.shape, bf16)),
        scratch, 3, 40, levels, {},
    )


def swap_kernel(src, dst, send_sem, recv_sem):
    c = lax.axis_index("ctx")
    mate = {"dp": lax.axis_index("dp"), "ctx": c + 1 - 2 * (c % 2)}
    barrier = pltpu.get_barrier_semaphore()
    pl.semaphore_signal(barrier, inc=1, device_id=mate, device_id_type=MESH)
    pl.semaphore_wait(barrier, 1)
    copy = pltpu.make_async_remote_copy(
        src_ref=src,
        dst_ref=dst,
        send_sem=send_sem,
        recv_sem=recv_sem,
        device_id=mate,
        device_id_type=MESH,
    )
    copy.start()
    copy.wait()


def swap(value, number):
    return pl.pallas_call(
        swap_kernel,
        out_shape=jax.ShapeDtypeStruct(value.shape, value.dtype),
        in_specs=[pl.BlockSpec(memory_space=ANY)],
        out_specs=pl.BlockSpec(memory_space=ANY),
        scratch_shapes=[pltpu.SemaphoreType.DMA, pltpu.SemaphoreType.DMA],
        compiler_params=pltpu.CompilerParams(collective_id=number, has_side_effects=True),
    )(value)


def norm_parts(values, epsilon):
    inv = lax.rsqrt(jnp.mean(values * values, axis=-1, keepdims=True) + epsilon)
    return inv


def norm_back(values, gain, grad, epsilon):
    inv = norm_parts(values, epsilon)
    scaled = gain * grad
    back = inv * scaled - values * (
        inv * inv * inv * jnp.mean(scaled * values, axis=-1, keepdims=True)
    )
    return back, grad * values * inv


def body(tokens, cotangent, starts, norm_gain, qkv_weight, conv_weight, beta_weight,
         head_gain, out_weight, gate_up_weight, down_weight):
    levels = lax.axis_size("dp") // 2
    ctx = lax.axis_size("ctx")
    device = lax.axis_index("dp") * ctx + lax.axis_index("ctx")
    t = lax.axis_index("ctx") % 2
    m = lax.axis_index("ctx") // 2
    batches, _, piece, width = tokens.shape
    rows = ctx * piece
    share = qkv_weight.shape[1]
    hidden = gate_up_weight.shape[2]
    half, fhalf = width // 2, hidden // 2
    heads_all = beta_weight.shape[1]
    heads = heads_all // 2
    per = head_gain.shape[0]
    small = 2 + 3 * CONV + heads_all + 1

    gain_rows = jnp.zeros((share, 1), bf16).at[:per, 0].set(head_gain)
    ext = jnp.concatenate(
        [norm_gain.T, conv_weight.T, beta_weight, gain_rows, jnp.zeros((share, HD - small), bf16)],
        axis=1,
    )
    flags = jnp.broadcast_to(
        starts.reshape(batches, piece, 1).astype(bf16), (batches, piece, HD)
    )
    f = forward(
        qkv_weight, out_weight, gate_up_weight, down_weight, ext,
        tokens[:, 0], cotangent[:, 0], flags, levels, per, heads_all,
    )
    w_gu = f["w_gu"].reshape(width, 2 * fhalf)
    w_down = f["w_down"].reshape(width, fhalf)
    w_out = f["wo_out"].reshape(half, width)
    w_mix = f["wmix_out"]
    dy = f["dy"].reshape(rows, width)
    residual, normed2 = f["res_out"], f["normed2_out"]
    gate = jnp.dot(normed2, w_gu[:, :fhalf], preferred_element_type=f32)
    up = jnp.dot(normed2, w_gu[:, fhalf:], preferred_element_type=f32)
    sg = jax.nn.sigmoid(gate)
    act = (gate * sg * up).astype(bf16)

    def by_parity(value):
        parts = value.reshape(ctx // 2, 2, piece, width)
        return lax.dynamic_index_in_dim(parts, t, 1, False), lax.dynamic_index_in_dim(
            parts, 1 - t, 1, False
        )

    ffn, ffn_other = by_parity(
        lax.dot_general(act, w_down, (((1,), (1,)), ((), ())), preferred_element_type=f32).astype(bf16)
    )
    res_own = by_parity(residual)[0]
    result = (res_own + ffn.astype(f32) + swap(ffn_other, 4).astype(f32)).astype(bf16)

    dact = jnp.dot(dy, w_down, preferred_element_type=f32)
    g_down = lax.dot_general(dy, act, (((0,), (0,)), ((), ())), preferred_element_type=f32).astype(bf16)
    dgate = (dact * up * sg * (1.0 + gate * (1.0 - sg))).astype(bf16)
    dup = (dact * gate * sg).astype(bf16)
    dgu = jnp.concatenate([dgate, dup], axis=1)
    g_gu = lax.dot_general(normed2, dgu, (((0,), (0,)), ((), ())), preferred_element_type=f32).astype(bf16)
    mine = lax.dot_general(dgu, w_gu, (((1,), (1,)), ((), ())), preferred_element_type=f32).astype(bf16)
    shaped = lambda g: g.reshape(width // share, share, -1)
    pick = lambda parts, k: lax.dynamic_index_in_dim(parts, k, 0, False)
    b = backward(
        f, mine, shaped(g_gu), shaped(g_down), pick(result, 1 - m), levels, per, heads_all
    )
    dx, o_gu, o_down, got_y = b["dx"], b["o_gu"], b["o_down"], b["lo_out"]
    e = last_scatter(b["g_first"], pick(dx, 1 - m), levels)
    o_first, got_x = e["o_first"], e["dx_out"]
    ordered = lambda own, got: jnp.stack(
        [jnp.where(m == 0, own, got), jnp.where(m == 0, got, own)]
    )[:, None]
    layer_out = ordered(pick(result, m), got_y)
    input_grad = ordered(pick(dx, m), got_x)
    join = lambda o, n: jnp.moveaxis(o.reshape(2, share, n, -1), (2, 1), (0, 1)).reshape(n, share, -1)
    o_small = jnp.sum(o_first[:, :, 4 * half :], axis=0)
    return (
        layer_out,
        input_grad,
        o_small[:, 0:2].T,
        join(o_first[:, :, : 3 * half], 3),
        o_small[:, 2 : 2 + 3 * CONV].T,
        o_small[:, 2 + 3 * CONV : 2 + 3 * CONV + heads_all],
        o_small[:per, small - 1],
        join(o_first[:, :, 3 * half : 4 * half], 1)[0],
        join(o_gu, 2),
        join(o_down, 1)[0],
    )


def solution(mesh):
    both = ("dp", "ctx")
    acts = P(None, "dp", "ctx", None)
    return jax.shard_map(
        body,
        mesh=mesh,
        in_specs=(
            acts,
            acts,
            P(None, "dp", "ctx"),
            P(None, both),
            P(None, both, None),
            P(None, both),
            P(both, None),
            P(both),
            P(both, None),
            P(None, both, None),
            P(both, None),
        ),
        out_specs=(
            acts,
            acts,
            P(None, both),
            P(None, both, None),
            P(None, both),
            P(both, None),
            P(both),
            P(both, None),
            P(None, both, None),
            P(both, None),
        ),
        check_vma=False,
    )
```

```python
import functools

import jax
import jax.numpy as jnp
from jax import lax
from jax.experimental import pallas as pl
from jax.experimental.pallas import tpu as pltpu
from jax.sharding import PartitionSpec as P

MESH = pl.DeviceIdType.MESH
ANY = pl.ANY
VM = pltpu.VMEM
MIB = 1 << 20
f32 = jnp.float32
bf16 = jnp.bfloat16


def route(block, order):
    dz, fx, fy = block
    rank = {dim: place for place, dim in enumerate(order)}
    last = max([-1] + [rank[d] for d, on in (("z", dz), ("x", fx), ("y", fy)) if on])
    hops = []
    for dim in order:
        if dim == "z":
            if dz == 0 and rank["z"] > last:
                hops += ["up", "dn"]
            elif dz != 0 and last == rank["z"]:
                hops.append("up" if dz < 0 else "dn")
        elif rank[dim] > last:
            hops.append(dim)
    came = None
    if last >= 0:
        came = order[last]
        if came == "z":
            came = "up" if dz < 0 else "dn"
    return hops, came


def blocks_of(levels):
    named = [
        (dz, fx, fy)
        for dz in range(1 - levels, levels)
        for fx in (0, 1)
        for fy in (0, 1)
    ]
    return sorted(named, key=lambda b: (abs(b[0]) + b[1] + b[2], abs(b[0]), b))


class Place:
    def __init__(self, levels):
        i = lax.axis_index("dp")
        c = lax.axis_index("ctx")
        self.levels = levels
        self.i, self.c = i, c
        self.z, self.y = i // 2, i % 2
        self.x, self.t = c // 2, c % 2

    def device(self, hop):
        i, c = self.i, self.c
        if hop == "x":
            return {"dp": i, "ctx": (1 - self.x) * 2 + self.t}
        if hop == "y":
            return {"dp": self.z * 2 + 1 - self.y, "ctx": c}
        if hop == "up":
            return {"dp": i + 2, "ctx": c}
        if hop == "dn":
            return {"dp": i - 2, "ctx": c}
        return {"dp": i, "ctx": self.x * 2 + 1 - self.t}

    def valid(self, block, hop=None):
        dz = block[0]
        terms = []
        if dz > 0:
            terms.append(self.z + dz < self.levels)
        if dz < 0:
            terms.append(self.z + dz >= 0)
        if hop == "up" and dz <= 0:
            terms.append(self.z + 1 < self.levels)
        if hop == "dn" and dz >= 0:
            terms.append(self.z >= 1)
        if not terms:
            return None
        return functools.reduce(jnp.logical_and, terms)

    def level(self, block):
        return self.z + block[0]

    def shard(self, block, half):
        z = self.z + block[0]
        y = 1 - self.y if block[2] else self.y
        x = 1 - self.x if block[1] else self.x
        return ((z * 2 + y) * 2 + x) * 2 + half

    def meet(self, hops):
        barrier = pltpu.get_barrier_semaphore()
        count = 0
        for hop in hops:
            def greet(hop=hop):
                pl.semaphore_signal(
                    barrier, inc=1, device_id=self.device(hop), device_id_type=MESH
                )
            if hop in ("up", "dn"):
                here = (self.z + 1 < self.levels) if hop == "up" else (self.z >= 1)
                pl.when(here)(greet)
                count = count + here.astype(jnp.int32)
            else:
                greet()
                count = count + 1
        pl.semaphore_wait(barrier, count)


def when(condition, action):
    if condition is None:
        action()
    else:
        pl.when(condition)(action)


def send_slots(order):
    table = {}
    for fx in (0, 1):
        for fy in (0, 1):
            for dz in (-1, 0, 1):
                for hop in route((dz, fx, fy), order)[0]:
                    table.setdefault((hop, fx, fy), len(table))
    return table


class Gather:
    def __init__(self, place, ref, half, cols, order, send_sem, recv_sem):
        self.place, self.ref, self.half = place, ref, half
        self.cols = slice(*cols)
        self.order = order
        self.slots = send_slots(order)
        self.send_sem, self.recv_sem = send_sem, recv_sem

    @staticmethod
    def sems(levels, order):
        return len(send_slots(order)) * levels, 4 * levels

    def copy(self, block, hop):
        place = self.place
        dz, fx, fy = block
        where = place.shard(block, self.half)
        level = place.level(block)
        there = (fx ^ (hop == "x"), fy ^ (hop == "y"))
        return pltpu.make_async_remote_copy(
            src_ref=self.ref.at[where, :, self.cols],
            dst_ref=self.ref.at[where, :, self.cols],
            send_sem=self.send_sem.at[self.slots[hop, fx, fy] * place.levels + level],
            recv_sem=self.recv_sem.at[(there[0] * 2 + there[1]) * place.levels + level],
            device_id=place.device(hop),
            device_id_type=MESH,
        )

    def arrival(self, block):
        place = self.place
        dz, fx, fy = block
        where = place.shard(block, self.half)
        came = route(block, self.order)[1]
        back = {"up": "dn", "dn": "up"}.get(came, came)
        return pltpu.make_async_remote_copy(
            src_ref=self.ref.at[where, :, self.cols],
            dst_ref=self.ref.at[where, :, self.cols],
            send_sem=self.send_sem.at[0],
            recv_sem=self.recv_sem.at[(fx * 2 + fy) * place.levels + place.level(block)],
            device_id=place.device(back),
            device_id_type=MESH,
        )

    def wait(self, block):
        when(self.place.valid(block), lambda: self.arrival(block).wait_recv())

    def pass_on(self, block, only=("x", "y", "up", "dn")):
        for hop in route(block, self.order)[0]:
            if hop not in only:
                continue
            when(self.place.valid(block, hop), lambda hop=hop: self.copy(block, hop).start())

    def drain(self, blocks):
        for block in blocks:
            for hop in route(block, self.order)[0]:
                when(
                    self.place.valid(block, hop),
                    lambda hop=hop: self.copy(block, hop).wait_send(),
                )


def room_table(order, levels):
    table, used = {}, 0
    for fx in (0, 1):
        for fy in (0, 1):
            here = route((0, fx, fy), order)[0]
            away = route((1, fx, fy), order)[0] + route((-1, fx, fy), order)[0]
            for hop in ("x", "y"):
                if hop in here or hop in away:
                    table[hop, fx, fy] = (used, hop in away)
                    used += levels if hop in away else 1
            if "up" in here + away or "dn" in here + away:
                table["z", fx, fy] = (used, True)
                used += levels + 1
    return table, used


class Scatter:
    def __init__(self, place, ref, room, final, half, cols, order, send_sem, recv_sem):
        self.place, self.ref, self.room, self.final = place, ref, room, final
        self.half, self.order = half, order
        self.cols = slice(*cols)
        self.table = room_table(order, place.levels)[0]
        self.send_sem, self.recv_sem = send_sem, recv_sem

    @staticmethod
    def slots_of(levels, order):
        return room_table(order, levels)[1], 4 * levels

    def slot_at(self, hop, dz, fx, fy, level):
        base, many = self.table["z" if hop in ("up", "dn") else hop, fx, fy]
        if hop == "dn" and dz == 0:
            return base + self.place.levels
        return base + level if many else base

    def slot(self, block, hop):
        return self.slot_at(hop, *block, self.place.level(block))

    def copy(self, block, src):
        place = self.place
        dz, fx, fy = block
        came = route(block, self.order)[1]
        back = {"up": "dn", "dn": "up"}.get(came, came)
        there = (
            dz + (came == "up") - (came == "dn"),
            fx ^ (came == "x"),
            fy ^ (came == "y"),
        )
        slot = self.slot_at(came, *there, place.level(block))
        return pltpu.make_async_remote_copy(
            src_ref=src,
            dst_ref=self.room.at[slot],
            send_sem=self.send_sem.at[(fx * 2 + fy) * place.levels + place.level(block)],
            recv_sem=self.recv_sem.at[slot],
            device_id=place.device(back),
            device_id_type=MESH,
        )

    def arrive(self, block, hop):
        slot = self.slot(block, hop)
        pltpu.make_async_remote_copy(
            src_ref=self.room.at[slot],
            dst_ref=self.room.at[slot],
            send_sem=self.send_sem.at[0],
            recv_sem=self.recv_sem.at[slot],
            device_id=self.place.device(hop),
            device_id_type=MESH,
        ).wait_recv()

    def total(self, block, hops, put):
        where = self.place.shard(block, self.half)
        slots = [self.slot(block, hop) for hop in hops]
        rows = self.ref.shape[1]
        step = min(16, rows)

        def one(k, carry):
            at = pl.ds(pl.multiple_of(k * step, step), step)
            value = self.ref[where, at, self.cols].astype(f32)
            for slot in slots:
                value = value + self.room[slot, at, :].astype(f32)
            put(at, value)
            return carry

        lax.fori_loop(0, rows // step, one, 0)

    def branch(self, maybe, using, go):
        if not maybe:
            go(using)
            return
        hop, place = maybe[0], self.place
        here = place.z + 1 < place.levels if hop == "up" else place.z >= 1
        pl.when(here)(lambda: self.branch(maybe[1:], using + [hop], go))
        pl.when(jnp.logical_not(here))(lambda: self.branch(maybe[1:], using, go))

    def forward(self, block):
        place = self.place
        hops = route(block, self.order)[0]
        sure = [h for h in hops if h in ("x", "y")]
        maybe = [h for h in hops if h not in ("x", "y")]

        def go(using):
            for hop in using:
                self.arrive(block, hop)
            if not using:
                self.copy(block, self.ref.at[place.shard(block, self.half), :, self.cols]).start()
                return
            slot = self.slot(block, using[0])

            def put(at, value):
                self.room[slot, at, :] = value.astype(bf16)

            self.total(block, using, put)
            self.copy(block, self.room.at[slot]).start()

        def both():
            self.branch(maybe, sure, go)

        when(place.valid(block), both)

    def finish(self):
        own = (0, 0, 0)
        place = self.place
        hops = route(own, self.order)[0]
        sure = [h for h in hops if h in ("x", "y")]
        for hop in sure:
            self.arrive(own, hop)

        def put(at, value):
            self.final[self.half, at, self.cols] = value

        self.total(own, sure, put)
        for hop in hops:
            if hop in sure:
                continue

            def add(hop=hop):
                self.arrive(own, hop)
                slot = self.slot(own, hop)
                self.final[self.half, :, self.cols] = self.final[
                    self.half, :, self.cols
                ] + self.room[slot].astype(f32)

            when(place.valid(own, hop), add)

    def drain(self, blocks):
        for block in blocks:
            if block == (0, 0, 0):
                continue
            when(
                self.place.valid(block),
                lambda block=block: self.copy(
                    block, self.ref.at[self.place.shard(block, self.half), :, self.cols]
                ).wait_send(),
            )


OWN = (0, 0, 0)

RATE = 0.038
HOP = 1.6


class Step:
    def __init__(self, run, valid, needs, sends, cost, group, rank):
        self.run, self.valid, self.needs, self.sends = run, valid, needs, sends
        self.cost, self.group, self.rank = cost, group, rank


def exists(block, z, levels):
    return 0 <= z + block[0] < levels


def can_hop(z, hop, levels):
    return {"up": z + 1 < levels, "dn": z >= 1}.get(hop, True)


def moved(block, hop):
    dz, fx, fy = block
    return (dz - (hop == "up") + (hop == "dn"), fx ^ (hop == "x"), fy ^ (hop == "y"))


def level_of(z, hop):
    return z + (hop == "up") - (hop == "dn")


def height(block, order, levels):
    if abs(block[0]) >= levels:
        return -1
    return max([0] + [1 + height(moved(block, h), order, levels) for h in route(block, order)[0]])


def crossing_step(run, size, group, key):
    return Step(
        run, lambda z: True, lambda z: [("own", group)], lambda z: [("x", size, (key, z))],
        0.2, group, 0,
    )


def gather_steps(streams, group_of, size_of, levels, begin=None):
    steps = []
    for k, s in enumerate(streams):
        for block in blocks_of(levels):
            hops = route(block, s.order)[0]
            if not hops:
                continue

            def needs(z, k=k, block=block):
                return [("own", group_of[k])] if block == OWN else [(k, z, block)]

            def sends(z, k=k, block=block, hops=hops):
                return [
                    (h, size_of[k], (k, level_of(z, h), moved(block, h)))
                    for h in hops
                    if can_hop(z, h, levels)
                ]

            def run(s=s, k=k, block=block):
                if block != OWN:
                    s.wait(block)
                else:
                    begin(group_of[k])
                s.pass_on(block)

            steps.append(
                Step(
                    run,
                    lambda z, block=block: exists(block, z, levels),
                    needs,
                    sends,
                    0.15,
                    group_of[k],
                    -height(block, s.order, levels),
                )
            )
    return steps


def scatter_steps(streams, group_of, size_of, levels):
    steps = []
    for k, s in enumerate(streams):
        for block in blocks_of(levels)[::-1]:
            if block == OWN:
                continue
            hops, came = route(block, s.order)
            back = {"up": "dn", "dn": "up"}.get(came, came)

            def needs(z, k=k, block=block, hops=hops):
                got = [(k, z, block, h) for h in hops if can_hop(z, h, levels)]
                return got or [("own", group_of[k])]

            def sends(z, k=k, block=block, came=came, back=back):
                there = moved(block, back)
                return [(back, size_of[k], (k, level_of(z, back), there, came))]

            steps.append(
                Step(
                    lambda s=s, block=block: s.forward(block),
                    lambda z, block=block: exists(block, z, levels),
                    needs,
                    sends,
                    0.15 + (1.5 * size_of[k] if hops else 0.0),
                    group_of[k],
                    -abs(block[0]) - block[1] - block[2],
                )
            )
    return steps


def plan(steps, program, levels, own, gates):
    now = [0.0] * levels
    free = [dict(x=0.0, y=0.0, up=0.0, dn=0.0) for _ in range(levels)]
    there = {("own", g): at for g, at in own.items()}
    left = list(steps)
    out = []

    def ready(step):
        times = []
        for z in range(levels):
            if not step.valid(z):
                continue
            for key in step.needs(z):
                if key not in there:
                    return None
                times.append((there[key], now[z]))
        return times

    def do(step):
        for z in range(levels):
            if not step.valid(z):
                continue
            now[z] = max([now[z]] + [there[key] for key in step.needs(z)]) + step.cost
        for z in range(levels):
            if not step.valid(z):
                continue
            for hop, size, key in step.sends(z):
                begin = max(now[z], free[z][hop])
                free[z][hop] = begin + size / RATE
                there[key] = free[z][hop] + HOP
        left.remove(step)

    def quick(step):
        times = ready(step)
        return times is not None and all(at <= when + 0.3 for at, when in times)

    def drain_ready(batch, held):
        while True:
            able = [s for s in left if s.group not in held and quick(s)]
            if not able:
                return
            step = min(able, key=lambda s: (s.group, s.rank))
            do(step)
            batch.append(step)

    def wait_for(step):
        return max([max(at - when, 0.0) for at, when in ready(step)] + [0.0])

    def until(batch, done):
        while left and not done():
            able = [s for s in left if ready(s) is not None]
            if not able:
                return
            first = min(s.group for s in able)

            def idle(s):
                return all(
                    free[z][hop] <= now[z] + 1.0
                    for z in range(levels)
                    if s.valid(z)
                    for hop, _, _ in s.sends(z)
                )

            pool = [s for s in able if s.group == first or idle(s)]
            step = min(pool, key=lambda s: (round(wait_for(s), 1), s.group, s.rank))
            do(step)
            batch.append(step)

    for place, duration in enumerate(program):
        batch = []
        keys = gates.get(place)
        if keys:
            until(
                batch,
                lambda: all(k in there for z in range(levels) for k in keys(z))
                and not any(s.group == 0 for s in left),
            )
            for z in range(levels):
                now[z] = max([now[z]] + [there[k] for k in keys(z)])
        drain_ready(batch, ())
        out.append(batch)
        for z in range(levels):
            now[z] += duration
    batch = []
    until(batch, lambda: False)
    out.append(batch)
    return out, max(now), max([at for at in there.values()] + [0.0])


class Planned:
    def __init__(self, batches):
        self.batches = list(batches)

    def take(self):
        return self.batches.pop(0)

    def tick(self):
        for step in self.take():
            step.run()

    def looped(self, count, each=1):
        now = [self.take() for _ in range(count * each)]

        def at(index, which=0):
            for k, steps in enumerate(now[which::each]):
                if steps:
                    pl.when(index == k)(lambda steps=steps: [s.run() for s in steps] and None)

        return at

    def finish(self):
        while self.batches:
            self.tick()


HD = 128
CONV = 4
SPAN = 128


def mm(a, b):
    return jnp.dot(a, b, preferred_element_type=f32)


def mm_nt(a, b):
    return lax.dot_general(a, b, (((1,), (1,)), ((), ())), preferred_element_type=f32)


def mm_tn(a, b):
    return lax.dot_general(a, b, (((0,), (0,)), ((), ())), preferred_element_type=f32)


def lanes(h):
    return pl.ds(pl.multiple_of(h * HD, HD), HD)


def set_masks(segc, keep):
    rows = lax.broadcasted_iota(jnp.int32, segc.shape, 0)
    seg = segc[...]
    for o in range(1, CONV):
        same = (pltpu.roll(seg, o, 0) == seg) & (rows >= o)
        keep[o - 1] = same.astype(f32)


def shifted(value, keep, o):
    return value if o == 0 else pltpu.roll(value, o, 0) * keep[o - 1]


def conv_of(proj, taps, keep, j, h, heads):
    at = lanes(j * heads + h)
    value = proj[:, at].astype(f32)
    total = taps[pl.ds(j * CONV + CONV - 1, 1), lanes(h)] * value
    for o in range(1, CONV):
        total = total + taps[pl.ds(j * CONV + CONV - 1 - o, 1), lanes(h)] * shifted(value, keep, o)
    return total


def span_masks(segc, segr, n):
    at = slice(n * SPAN, (n + 1) * SPAN)
    col = segc[at, :]
    same = col == jnp.broadcast_to(segr[0:1, at], (SPAN, SPAN))
    if n:
        carried = (col == segc[n * SPAN - 1 : n * SPAN, :]).astype(f32)
    else:
        carried = jnp.zeros((SPAN, HD), f32)
    ending = (col == col[SPAN - 1 : SPAN, :]).astype(f32)
    return carried, same, ending


def iotas():
    i = lax.broadcasted_iota(jnp.int32, (SPAN, SPAN), 0)
    j = lax.broadcasted_iota(jnp.int32, (SPAN, SPAN), 1)
    return i, j


def unit_inverses(lowers):
    i, j = iotas()
    apart = i ^ j
    invs = [jnp.where(apart == 1, -low, 0.0) for low in lowers]
    size, bits = 2, 1
    while size < SPAN:
        pairs = lax.shift_right_logical(apart, bits) == 1
        part = [jnp.where(pairs, low, 0.0) for low in lowers]
        small = [inv.astype(bf16) for inv in invs]
        left = [p + mm(s, p.astype(bf16)) for p, s in zip(part, small)]
        both = [w + mm(w.astype(bf16), s) for w, s in zip(left, small)]
        invs = [inv - b for inv, b in zip(invs, both)]
        size, bits = size * 2, bits + 1
    return invs


class Names:
    def __init__(self, names, refs):
        self.__dict__.update(zip(names, refs, strict=True))


class Sems:
    def __init__(self, ref):
        self.ref, self.used = ref, 0

    def take(self):
        self.used += 1
        return self.ref.at[self.used - 1]


def call(kernel, ins, outs, scratch, number, limit, *static):
    names = list(ins) + list(outs) + list(scratch)

    def run(*refs):
        kernel(Names(names, refs), *static)

    results = pl.pallas_call(
        run,
        out_shape=list(outs.values()),
        in_specs=[pl.BlockSpec(memory_space=ANY)] * len(ins),
        out_specs=[pl.BlockSpec(memory_space=ANY)] * len(outs),
        scratch_shapes=list(scratch.values()),
        compiler_params=pltpu.CompilerParams(
            collective_id=number, has_side_effects=True, vmem_limit_bytes=limit * MIB
        ),
    )(*ins.values())
    return dict(zip(outs, results, strict=True))


class Local:
    def __init__(self, sems):
        self.sems, self.open = sems, []

    def start(self, src, dst):
        copy = pltpu.make_async_copy(src, dst, self.sems.take())
        copy.start()
        self.open.append(copy)
        return copy

    def holds(self, copy):
        return any(copy is other for other in self.open)

    def wait(self, copy):
        copy.wait()
        self.open = [other for other in self.open if other is not copy]

    def done(self):
        for copy in self.open:
            copy.wait()
        self.open = []


class Remote:
    def __init__(self, place, sent, got):
        self.place, self.sent, self.got, self.open = place, sent, got, []

    def start(self, src, dst, hop):
        copy = pltpu.make_async_remote_copy(
            src_ref=src,
            dst_ref=dst,
            send_sem=self.sent.take(),
            recv_sem=self.got.take(),
            device_id=self.place.device(hop),
            device_id_type=MESH,
        )
        copy.start()
        self.open.append(copy)
        return copy

    def drain(self):
        for copy in self.open:
            copy.wait_send()
        self.open = []


def flat(ref, cols):
    value = ref[:, :, cols]
    shape = (value.shape[0] * value.shape[1], value.shape[2])
    if value.shape[1] % 16:
        return value.astype(f32).reshape(shape).astype(bf16)
    return value.reshape(shape)


STREAMS = (
    (0, 0, None, "zxy"),
    (0, 1, None, "zxy"),
    (1, 0, None, "zxy"),
    (1, 1, None, "zyx"),
    (2, 0, None, "xyz"),
    (2, 1, None, "yxz"),
)


def span_of(cols, ref):
    if cols is None:
        return 0, ref.shape[2]
    first, last = cols
    return first * HD, ref.shape[2] if last is None else last * HD


NEIGHBOURS = ("x", "y", "up", "dn", "core")


def forward_kernel(r, levels, cfg):
    heads, spans, per, share = cfg["heads"], cfg["spans"], cfg["per"], cfg["share"]
    width, half, fhalf, heads_all = cfg["width"], cfg["half"], cfg["fhalf"], cfg["heads_all"]
    piece, rows = cfg["piece"], cfg["rows"]
    pc = Place(levels)
    loc = Local(Sems(r.loc_sem))
    rem = Remote(pc, Sems(r.send_sem), Sems(r.recv_sem))
    pc.meet(NEIGHBOURS)
    own = pc.shard(OWN, pc.t)
    targets = (r.w1, r.w_gu, r.w_down)
    streams = [
        Gather(pc, targets[a], hf, span_of(cols, targets[a]), order,
               r.__dict__["gs%d" % k], r.__dict__["gr%d" % k])
        for k, (a, hf, cols, order) in enumerate(STREAMS)
    ]
    def both(src_at, dst):
        return [loc.start(src_at(pc.t), dst), rem.start(src_at(1 - pc.t), dst, "core")]

    def cut(n, t):
        return pl.ds(pl.multiple_of(t * n, n), n)

    opening = []
    for j in range(3):
        opening += both(
            lambda t, j=j: r.qkv.at[j, :, cut(half, t)],
            r.w1.at[own, :, j * half : (j + 1) * half],
        )
    opening += both(lambda t: r.out_w.at[:, cut(half, t)], r.w1.at[own, :, 3 * half : 4 * half])
    opening += both(lambda t: r.ext, r.w1.at[own, :, 4 * half : 4 * half + HD])
    pieces = both(lambda t: r.tok.at[pc.x], r.x.at[pc.c])
    pieces += both(lambda t: r.flags.at[pc.x], r.marks.at[pc.c])

    def arrived(copies):
        for copy in copies:
            if loc.holds(copy):
                loc.wait(copy)
            else:
                copy.wait_recv()

    arrived(opening)
    second = []
    for j in range(2):
        second += both(
            lambda t, j=j: r.gu.at[j, :, cut(fhalf, t)],
            r.w_gu.at[own, :, j * fhalf : (j + 1) * fhalf],
        )
    second += both(lambda t: r.dn.at[:, cut(fhalf, t)], r.w_down.at[own])
    second += both(lambda t: r.cot.at[pc.x], r.dy.at[pc.c])
    hold = {1: second[:4], 2: second[4:6]}
    far = (1 - pc.x) * 2 + pc.t
    crossed = {}

    def cross(name, src, dst):
        crossed[name] = rem.start(src.at[1 - pc.x], dst.at[pc.c], "x")

    groups = [a for a, *_ in STREAMS]
    firsts = [k for k, a in enumerate(groups) if a == 0]
    mb = lambda n, m: 2e-6 * n * m
    steps = gather_steps(
        streams, groups, [mb(share, s.cols.stop - s.cols.start) for s in streams], levels,
        lambda a: arrived(hold.pop(a, [])),
    )
    steps.append(crossing_step(lambda: (cross("x", r.tok, r.x), cross("m", r.flags, r.marks)),
                               mb(piece, width + HD), 0, "tok"))
    steps.append(crossing_step(lambda: cross("dy", r.cot, r.dy), mb(piece, width), 3, "cot"))
    ordered = blocks_of(levels)

    def gate(z):
        return [("tok", z)] + [
            (k, z, block)
            for k in firsts
            for block in ordered
            if block != OWN and exists(block, z, levels)
        ]

    later = Planned(
        plan(steps, cfg["program"], levels, {0: 4.0, 1: 6.0, 2: 7.0, 3: 7.0}, {0: gate})[0]
    )
    later.tick()
    crossed["x"].wait_recv()
    crossed["m"].wait_recv()
    arrived(pieces)
    pieces = [
        rem.start(r.x.at[far], r.x.at[far], "core"),
        rem.start(r.marks.at[far], r.marks.at[far], "core"),
    ]
    for block in ordered:
        for k in firsts:
            s = streams[k]
            if block != OWN and not route(block, s.order)[0]:
                s.wait(block)
    arrived(pieces)

    i, j = iotas()
    upto = (i >= j).astype(bf16)
    base = jnp.zeros((1, HD), f32)
    for n in range(spans):
        q, at = divmod(n * SPAN, piece)
        marks = r.marks[q, at : at + SPAN, :]
        seg = mm(upto, marks) + base
        r.segc[n * SPAN : (n + 1) * SPAN, :] = seg
        r.segr[:, n * SPAN : (n + 1) * SPAN] = jnp.transpose(seg)[0:8, :]
        base = seg[SPAN - 1 : SPAN, :]
    set_masks(r.segc, r.keep)
    loc.start(r.segc, r.segc_out)
    loc.start(r.segr, r.segr_out)

    shards = levels * 8 // 2
    mine = cut(half, pc.t)
    rows_of = lambda t: pl.ds(pl.multiple_of(t * shards, shards), shards)
    side = pl.ds(3 * half, half)
    swap_out = [
        loc.start(r.w1.at[rows_of(pc.t), :, side], r.wo.at[:, :, mine]),
        rem.start(r.w1.at[rows_of(1 - pc.t), :, side], r.wo.at[:, :, mine], "core"),
    ]

    extra = flat(r.w1, slice(4 * half, 4 * half + HD))
    for n in range(width // SPAN):
        at = slice(n * SPAN, (n + 1) * SPAN)
        r.small[:, at] = jnp.transpose(extra[at, :].astype(f32))[0:32, :]
    r.gains[...] = r.small[0:8, :]
    r.taps[...] = jnp.zeros(r.taps.shape, f32)
    r.taps[0 : 3 * CONV, :] = r.small[2 : 2 + 3 * CONV, cut(half, pc.t)]
    place_r = lax.broadcasted_iota(jnp.int32, (width, HD), 0)
    place_c = lax.broadcasted_iota(jnp.int32, (width, HD), 1)
    chosen = (place_r == share * (place_c // per) + place_c % per).astype(bf16)
    at = 2 + 3 * CONV + heads_all
    r.hgain[...] = jnp.broadcast_to(
        mm(r.small[at - at % 8 : at - at % 8 + 8, :].astype(bf16), chosen)[at % 8 : at % 8 + 1, :],
        (8, HD),
    )
    pick_r = lax.broadcasted_iota(jnp.int32, (HD, half), 0)
    pick_c = lax.broadcasted_iota(jnp.int32, (HD, half), 1)
    chosen = (pick_r == 2 + 3 * CONV + heads * pc.t + pick_c // HD).astype(bf16)
    r.wmix[:, 3 * half :] = mm(extra, chosen).astype(bf16)
    for k in range(3):
        r.wmix[:, k * half : (k + 1) * half] = flat(r.w1, slice(k * half, (k + 1) * half))
    loc.start(r.wmix, r.wmix_out)
    loc.start(r.taps, r.taps_out)
    loc.start(r.gains, r.gains_out)
    loc.start(r.hgain, r.hgain_out)

    g0 = r.gains[0:1, :]
    for n in range(rows // piece):
        x = r.x[n].astype(f32)
        inv = lax.rsqrt(jnp.mean(x * x, axis=-1, keepdims=True) + 1e-5)
        r.normed[n * piece : (n + 1) * piece, :] = (x * inv * g0).astype(bf16)
    loc.start(r.normed, r.normed_out)
    loc.start(r.x, r.x_out)

    steps_at = later.looped(rows // piece)

    def project(k, carry):
        steps_at(k)
        at = pl.ds(pl.multiple_of(k * piece, piece), piece)
        left = r.normed[at, :]
        r.proj[at, :] = mm(left, r.wmix[:, : 3 * half]).astype(bf16)
        r.logit[at, :] = mm(left, r.wmix[:, 3 * half :])
        return carry

    lax.fori_loop(0, rows // piece, project, 0)
    loc.start(r.proj, r.proj_out)
    loc.start(r.logit, r.logit_out)

    prepare_at = later.looped(heads)

    def prepare(h, carry):
        prepare_at(h)
        delta_prepare(r, h, heads, spans)
        return carry

    lax.fori_loop(0, heads, prepare, 0)
    for src, dst in ((r.qs, r.qs_out), (r.ks, r.ks_out), (r.vs, r.vs_out), (r.ws, r.ws_out),
                     (r.ns, r.ns_out), (r.ps, r.ps_out)):
        loc.start(src, dst)
    delta_chain(r, heads, spans, later.tick)
    for h in range(heads):
        head = slice(h * HD, (h + 1) * HD)
        o = r.out[:, head]
        scale = lax.rsqrt(jnp.mean(o * o, axis=-1, keepdims=True) + 1e-5)
        r.headed[:, head] = (o * scale * r.hgain[0:1, :]).astype(bf16)
    for src, dst in ((r.fs, r.fs_out), (r.ss, r.ss_out), (r.out, r.out_out),
                     (r.headed, r.headed_out)):
        loc.start(src, dst)
    later.tick()
    arrived(swap_out)
    loc.start(r.wo, r.wo_out)
    wo = flat(r.wo, slice(None))
    sent = []
    for n in range(rows // piece):
        r.mine[n] = mm(r.headed[n * piece : (n + 1) * piece, :], wo).astype(bf16)
        sent.append(rem.start(r.mine.at[n], r.theirs.at[n], "core"))
    later.tick()
    g1 = r.gains[1:2, :]
    for n in range(rows // piece):
        sent[n].wait_recv()
        at = slice(n * piece, (n + 1) * piece)
        res = r.x[n].astype(f32) + r.mine[n].astype(f32) + r.theirs[n].astype(f32)
        r.res[at, :] = res
        inv = lax.rsqrt(jnp.mean(res * res, axis=-1, keepdims=True) + 1e-5)
        r.normed2[at, :] = (res * inv * g1).astype(bf16)
    loc.start(r.res, r.res_out)
    loc.start(r.normed2, r.normed2_out)
    later.finish()
    crossed["dy"].wait_recv()
    arrived(second[6:])
    last = rem.start(r.dy.at[far], r.dy.at[far], "core")
    for block in ordered:
        for k, s in enumerate(streams):
            if k not in firsts and block != OWN and not route(block, s.order)[0]:
                s.wait(block)
    last.wait_recv()
    for s in streams:
        s.drain(ordered)
    rem.drain()
    loc.done()


def delta_prepare(r, h, heads, spans):
    i, j = iotas()
    mixed = []
    for which in range(3):
        value = conv_of(r.proj, r.taps, r.keep, which, h, heads)
        mixed.append(value * jax.nn.sigmoid(value))
    for which, dest in ((0, r.qs), (1, r.ks)):
        w = mixed[which]
        unit = w * lax.rsqrt(jnp.sum(w * w, axis=-1, keepdims=True) + 1e-6)
        dest[:, lanes(h)] = unit.astype(bf16)
    r.vs[:, lanes(h)] = mixed[2].astype(bf16)
    lowers, rights = [], []
    for n in range(spans):
        at = slice(n * SPAN, (n + 1) * SPAN)
        k = r.ks[at, lanes(h)]
        q = r.qs[at, lanes(h)]
        v = r.vs[at, lanes(h)]
        beta = jax.nn.sigmoid(r.logit[at, lanes(h)])
        carried, same, ending = span_masks(r.segc, r.segr, n)
        lowers.append(jnp.where(same & (i > j), beta * mm_nt(k, k), 0.0))
        r.ps[h * spans + n] = jnp.where(same & (i >= j), mm_nt(q, k), 0.0).astype(bf16)
        r.cqs[at, lanes(h)] = (carried * q.astype(f32)).astype(bf16)
        rights.append(
            jnp.concatenate([beta * v.astype(f32), (beta * carried) * k.astype(f32)], axis=1)
        )
    for n, inv in enumerate(unit_inverses(lowers)):
        at = slice(n * SPAN, (n + 1) * SPAN)
        small = inv.astype(bf16)
        r.ns[h * spans + n] = small
        both = rights[n] + mm(small, rights[n].astype(bf16))
        r.us[at, lanes(h)] = both[:, :HD]
        r.ws[at, lanes(h)] = both[:, HD:].astype(bf16)


def delta_chain(r, heads, spans, between):
    states = [jnp.zeros((HD, HD), f32) for _ in range(heads)]
    for n in range(spans):
        at = slice(n * SPAN, (n + 1) * SPAN)
        between()
        carried, same, ending = span_masks(r.segc, r.segr, n)
        for h in range(heads):
            head = slice(h * HD, (h + 1) * HD)
            state = states[h].astype(bf16)
            r.ss[h * spans + n] = state
            seen = mm(jnp.concatenate([r.ws[at, head], r.cqs[at, head]], axis=0), state)
            fresh = r.us[at, head] - seen[:SPAN]
            small = fresh.astype(bf16)
            r.fs[at, head] = small
            r.out[at, head] = seen[SPAN:] + mm(r.ps[h * spans + n], small)
            states[h] = carried[SPAN - 1 : SPAN, :] * states[h] + mm_tn(
                r.ks[at, head], (ending * fresh).astype(bf16)
            )


def forward(qkv, out_w, gu, dn, ext, tok, cot, flags, levels, per, heads_all):
    share = qkv.shape[1]
    width = qkv.shape[2]
    half, fhalf = width // 2, dn.shape[1] // 2
    piece = tok.shape[1]
    rows = 4 * piece
    heads = half // HD
    spans = rows // SPAN
    shards = levels * 8
    sds = jax.ShapeDtypeStruct
    wide, square = sds((rows, half), bf16), sds((heads * spans, SPAN, SPAN), bf16)
    seg = dict(
        segc=sds((rows, HD), f32),
        segr=sds((8, rows), f32),
        wmix=sds((width, 4 * half), bf16),
        taps=sds((16, half), f32),
        gains=sds((8, width), f32),
        hgain=sds((8, HD), f32),
        normed=sds((rows, width), bf16),
        x=sds((4, piece, width), bf16),
        proj=sds((rows, 3 * half), bf16),
        logit=sds((rows, half), f32),
        qs=wide, ks=wide, vs=wide, fs=wide, ws=wide, headed=wide,
        ns=square, ps=square, ss=square,
        out=sds((rows, half), f32),
        wo=sds((shards // 2, share, width), bf16),
        res=sds((rows, width), f32),
        normed2=sds((rows, width), bf16),
    )
    ins = dict(qkv=qkv, out_w=out_w, gu=gu, dn=dn, ext=ext, tok=tok, cot=cot, flags=flags)
    outs = {
        "w_gu": sds((shards, share, 2 * fhalf), bf16),
        "w_down": sds((shards, share, fhalf), bf16),
        "dy": sds((4, piece, width), bf16),
    }
    outs.update({k + "_out": v for k, v in seg.items()})
    scratch = {k: VM(v.shape, v.dtype) for k, v in seg.items()}
    scratch.update(
        w1=VM((shards, share, 4 * half + HD), bf16),
        marks=VM((4, piece, HD), bf16),
        keep=VM((CONV - 1, rows, HD), f32),
        small=VM((32, width), f32),
        us=VM((rows, half), f32),
        cqs=VM((rows, half), bf16),
        mine=VM((4, piece, width), bf16),
        theirs=VM((4, piece, width), bf16),
        loc_sem=pltpu.SemaphoreType.DMA((48,)),
        send_sem=pltpu.SemaphoreType.DMA((32,)),
        recv_sem=pltpu.SemaphoreType.DMA((32,)),
    )
    for k, (a, hf, cols, order) in enumerate(STREAMS):
        sent, got = Gather.sems(levels, order)
        scratch["gs%d" % k] = pltpu.SemaphoreType.DMA((sent,))
        scratch["gr%d" % k] = pltpu.SemaphoreType.DMA((got,))
    cfg = dict(
        heads=heads, spans=spans, per=per, share=share, width=width, half=half, fhalf=fhalf,
        heads_all=heads_all, piece=piece, rows=rows,
        program=[6.0] + [2.0] * (rows // piece) + [4.0] * heads + [0.6] * spans + [1.0, 4.0],
    )
    return call(forward_kernel, ins, outs, scratch, 1, 58, levels, cfg)


def unflat(value, share):
    return value.reshape(value.shape[0] // share, share, value.shape[1]).astype(bf16)


def backward_kernel(r, levels, cfg):
    heads, spans, per, share = cfg["heads"], cfg["spans"], cfg["per"], cfg["share"]
    width, half, heads_all = cfg["width"], cfg["half"], cfg["heads_all"]
    piece, rows = cfg["piece"], cfg["rows"]
    pc = Place(levels)
    loc = Local(Sems(r.loc_sem))
    rem = Remote(pc, Sems(r.send_sem), Sems(r.recv_sem))
    pc.meet(NEIGHBOURS)
    pieces = rows // piece
    first_in = [
        [rem.start(r.mine_in.at[n], r.theirs.at[n], "core"), loc.start(r.mine_in.at[n], r.mine.at[n]),
         loc.start(r.res_in.at[n], r.res.at[n])]
        + [loc.start(r.dy_in.at[n, :, pl.ds(c * half, half)],
                     r.datt.at[c, pl.ds(n * piece, piece), :]) for c in range(2)]
        for n in range(pieces)
    ]
    small_in = [loc.start(a, b) for a, b in (
        (r.gains_in, r.gains), (r.hgain_in, r.hgain), (r.taps_in, r.taps), (r.segc_in, r.segc),
        (r.segr_in, r.segr), (r.headed_in, r.headed), (r.wo_in, r.wo))]
    grads = (None, r.g_gu, r.g_down)
    finals = (None, r.f_gu, r.f_down)
    load = [loc.start(r.g_down_in, r.g_down), loc.start(r.g_gu_in, r.g_gu)]
    delta_in = [loc.start(a, b) for a, b in (
        (r.out_in, r.out), (r.logit_in, r.logit), (r.proj_in, r.dproj.at[:, pl.ds(0, 3 * half)]),
        (r.qs_in, r.sv.at[0]), (r.ks_in, r.sv.at[1]), (r.vs_in, r.sv.at[2]),
        (r.fs_in, r.sv.at[3]), (r.ws_in, r.sv.at[4]),
        (r.ns_in, r.sq.at[0]), (r.ps_in, r.sq.at[1]), (r.ss_in, r.sq.at[2]))]
    streams = [
        Scatter(pc, grads[a], r.__dict__["room%d" % k], finals[a], hf, span_of(cols, grads[a]),
                order, r.__dict__["ss%d" % k], r.__dict__["sr%d" % k])
        for k, (a, hf, cols, order) in enumerate(RETURNS)
    ]
    def arrived(copies):
        for copy in copies:
            if loc.holds(copy):
                loc.wait(copy)
            else:
                copy.wait_recv()

    ordered = blocks_of(levels)[::-1]
    arrived(load)
    crossing = []
    mb = lambda n, m: 2e-6 * n * m
    steps = scatter_steps(
        streams, [0] * len(streams),
        [mb(share, s.cols.stop - s.cols.start) for s in streams], levels,
    )
    steps.append(crossing_step(lambda: crossing.append(rem.start(r.lo_in, r.lo_out, "x")),
                               mb(piece, width), 1, "lo"))
    later = Planned(plan(steps, cfg["program"], levels, {0: 0.0, 1: 0.0}, {})[0])
    later.tick()

    arrived(small_in)
    g1 = r.gains[1:2, :]
    gain1 = jnp.zeros((1, width), f32)
    for n in range(pieces):
        later.tick()
        arrived(first_in[n])
        v = r.res[n]
        grad = r.mine[n].astype(f32) + r.theirs[n].astype(f32)
        inv = lax.rsqrt(jnp.mean(v * v, axis=-1, keepdims=True) + 1e-5)
        scaled = grad * g1
        back = inv * scaled - v * (inv * inv * inv * jnp.mean(scaled * v, axis=-1, keepdims=True))
        at = slice(n * piece, (n + 1) * piece)
        dres = back + jnp.concatenate([r.datt[0, at, :], r.datt[1, at, :]], axis=1).astype(f32)
        ours = (pc.t == n % 2).astype(f32)
        gain1 = gain1 + ours * jnp.sum(grad * v * inv, axis=0, keepdims=True)

        def keep_own(n=n, dres=dres):
            r.res[n // 2] = dres

        pl.when(pc.t == n % 2)(keep_own)
        low = dres.astype(bf16)
        r.datt[0, at, :] = low[:, :half]
        r.datt[1, at, :] = low[:, half:]
    r.cols[...] = jnp.zeros(r.cols.shape, f32)
    r.cols[1:2, :] = gain1
    later.tick()
    wo = flat(r.wo, slice(None))
    for c in range(2):
        at = slice(c * heads * HD // share, (c + 1) * heads * HD // share)
        r.gm[0, at] = unflat(mm_tn(r.headed[...], r.datt[c]), share)

    def cut(n, t):
        return pl.ds(pl.multiple_of(t * n, n), n)

    shards = levels * 8 // 2
    rows_of = lambda t: pl.ds(pl.multiple_of(t * shards, shards), shards)
    side = pl.ds(3 * half, half)
    gout = [
        loc.start(r.gm.at[0, rows_of(pc.t)], r.g_first.at[rows_of(pc.t), :, side]),
        rem.start(r.gm.at[0, rows_of(1 - pc.t)], r.g_first.at[rows_of(pc.t), :, side], "core"),
    ]
    later.tick()
    for n in range(pieces):
        at = slice(n * piece, (n + 1) * piece)
        r.dheaded[at, :] = (
            mm_nt(r.datt[0, at, :], wo[:, :half]) + mm_nt(r.datt[1, at, :], wo[:, half:])
        ).astype(bf16)

    arrived(delta_in)
    set_masks(r.segc, r.keep)
    qs, ks, vs, fs, ws = (r.sv.at[k] for k in range(5))
    ns, ps, ss = (r.sq.at[k] for k in range(3))
    douts, xs = r.datt.at[0], r.datt.at[1]
    ys, hs, gs = r.headed, r.out, r.dheaded
    i, j = iotas()
    first = lax.broadcasted_iota(jnp.int32, (SPAN, HD), 1) == 0

    norm_at = later.looped(heads)

    def norm_back(h, dgain_sum):
        norm_at(h)
        o = r.out[:, lanes(h)]
        dyh = r.dheaded[:, lanes(h)].astype(f32)
        inv = lax.rsqrt(jnp.mean(o * o, axis=-1, keepdims=True) + 1e-5)
        scaled = dyh * r.hgain[0:1, :]
        dout = inv * scaled - o * (inv * inv * inv * jnp.mean(scaled * o, axis=-1, keepdims=True))
        dgain_sum = dgain_sum + jnp.sum(dyh * o * inv, axis=0, keepdims=True)
        for n in range(spans):
            at = slice(n * SPAN, (n + 1) * SPAN)
            carried, same, ending = span_masks(r.segc, r.segr, n)
            small = dout[at].astype(bf16)
            douts[at, lanes(h)] = small
            x = mm_tn(ps[h * spans + n], small).astype(bf16)
            xs[at, lanes(h)] = x
            cdout = (carried * dout[at]).astype(bf16)
            hs[at, lanes(h)] = mm_tn(qs[at, lanes(h)], cdout) - mm_tn(ws[at, lanes(h)], x)
        return dgain_sum

    dgain = lax.fori_loop(0, heads, norm_back, jnp.zeros((1, HD), f32))
    grads_s = [jnp.zeros((HD, HD), f32) for _ in range(heads)]
    for n in reversed(range(spans)):
        later.tick()
        at = slice(n * SPAN, (n + 1) * SPAN)
        carried, same, ending = span_masks(r.segc, r.segr, n)
        for h in range(heads):
            head = slice(h * HD, (h + 1) * HD)
            g = grads_s[h].astype(bf16)
            gs[at, head] = g
            y = (ending * mm(ks[at, head], g)).astype(bf16)
            ys[at, head] = y
            if n:
                grads_s[h] = (
                    carried[SPAN - 1 : SPAN, :] * grads_s[h]
                    - mm_tn(ws[at, head], y)
                    + hs[at, head]
                )

    per_piece = piece // SPAN

    def spot(which, n):
        return (
            pieces // 2 + which // 2,
            slice((n % per_piece) * SPAN, (n % per_piece + 1) * SPAN),
            slice(
                ((which % 2) * pieces + n // per_piece) * HD,
                ((which % 2) * pieces + n // per_piece + 1) * HD,
            ),
        )

    def put(which, n, value):
        r.res[spot(which, n)] = value

    def taken(which):
        return jnp.concatenate([r.res[spot(which, n)] for n in range(spans)], axis=0)

    pull_at = later.looped(heads, 3)

    def pull(h, carry):
        head = lanes(h)
        pull_at(h, 0)
        for n in range(spans):
            at = slice(n * SPAN, (n + 1) * SPAN)
            carried, same, ending = span_masks(r.segc, r.segr, n)
            which = h * spans + n
            if n == spans // 2:
                pull_at(h, 1)
            q, k, v, f = qs[at, head], ks[at, head], vs[at, head], fs[at, head]
            state, g, p, inv = ss[which], gs[at, head], ps[which], ns[which]
            beta = jax.nn.sigmoid(r.logit[at, head])
            small = douts[at, head]
            df = xs[at, head].astype(f32) + ys[at, head].astype(f32)
            z = df + mm_tn(inv, df.astype(bf16))
            zb = z.astype(bf16)
            dp = jnp.where(same & (i >= j), mm_nt(small, f), 0.0).astype(bf16)
            dl = jnp.where(same & (i > j), -mm_nt(zb, f), 0.0)
            known = v.astype(f32) - carried * mm(k, state)
            dbeta = jnp.sum(z * known + dl * mm_nt(k, k), axis=-1, keepdims=True)
            b = beta[:, 0:1]
            dlogit = dbeta * b * (1.0 - b)
            r.dproj[at, pl.ds(pl.multiple_of((3 * heads + h) * HD, HD), HD)] = jnp.where(
                first, jnp.broadcast_to(dlogit, (SPAN, HD)), 0.0
            ).astype(bf16)
            e = (beta * dl).astype(bf16)
            put(0, n, carried * mm_nt(small, state) + mm(dp, k))
            put(2, n, beta * z)
            put(1, n, (
                mm(e, k)
                + mm_tn(e, k)
                + mm_tn(dp, q)
                - (carried * beta) * mm_nt(zb, state)
                + ending * mm_nt(f, g)
            ))
        pull_at(h, 2)
        for which in range(3):
            c = conv_of(r.dproj, r.taps, r.keep, which, h, heads)
            s = jax.nn.sigmoid(c)
            d = taken(which)
            if which < 2:
                w = c * s
                n = lax.rsqrt(jnp.sum(w * w, axis=-1, keepdims=True) + 1e-6)
                d = n * d - w * (n * n * n * jnp.sum(w * d, axis=-1, keepdims=True))
            dc = d * (s * (1.0 + c * (1.0 - s)))
            at = lanes(which * heads + h)
            value = r.dproj[:, at].astype(f32)
            total = None
            for o in range(CONV):
                row = which * CONV + CONV - 1 - o
                tap = r.taps[pl.ds(row, 1), lanes(h)]
                r.dtaps[pl.ds(row, 1), lanes(h)] = jnp.sum(
                    dc * shifted(value, r.keep, o), axis=0, keepdims=True
                )
                if o == 0:
                    total = tap * dc
                else:
                    total = total + tap * pltpu.roll(dc * r.keep[o - 1], rows - o, 0)
            r.dproj[:, at] = total.astype(bf16)
        return carry

    lax.fori_loop(0, heads, pull, 0)

    weights_in = [
        loc.start(r.wmix_in.at[:, pl.ds(k * half, half)], r.sv.at[k]) for k in range(4)
    ]
    normed_in = [
        loc.start(r.normed_in.at[:, pl.ds(0, half)], r.sv.at[4]),
        loc.start(r.normed_in.at[:, pl.ds(half, half)], r.headed),
    ]
    x_in = [
        loc.start(r.x_in.at[2 * k + pc.t], r.theirs.at[2 + k]) for k in range(pieces // 2)
    ]
    arrived(weights_in)

    def partial(which, at):
        n = which
        where = pl.ds(pl.multiple_of(n * piece, piece), piece)
        total = mm_nt(r.dproj[where, :half], r.sv[0])
        for k in range(1, 4):
            total = total + mm_nt(r.dproj[where, k * half : (k + 1) * half], r.sv[k])
        r.mine[at] = total.astype(bf16)

    sent = []
    later.tick()
    for k in range(pieces // 2):
        partial(2 * k + 1 - pc.t, 2 + k)
        sent.append(rem.start(r.mine.at[2 + k], r.theirs3.at[k], "core"))
    later.tick()
    for k in range(pieces // 2):
        partial(2 * k + pc.t, k)
    arrived(normed_in)
    arrived(gout[:1])
    gout[1].wait_send()
    rem.open = [copy for copy in rem.open if copy is not gout[1]]
    hw = half // share
    for k in range(3):
        later.tick()
        for c, left in enumerate((r.sv.at[4], r.headed)):
            at = slice(c * hw, (c + 1) * hw)
            r.gm[k, at] = unflat(mm_tn(left[...], r.dproj[:, k * half : (k + 1) * half]), share)
        loc.start(r.gm.at[k], r.g_first.at[:, :, pl.ds(k * half, half)])

    later.tick()
    arrived(x_in)
    g0 = r.gains[0:1, :]
    gain0 = jnp.zeros((1, width), f32)
    for k in range(pieces // 2):
        sent[k].wait_recv()
        v = r.theirs[2 + k].astype(f32)
        grad = r.mine[k].astype(f32) + r.theirs3[k].astype(f32)
        inv = lax.rsqrt(jnp.mean(v * v, axis=-1, keepdims=True) + 1e-5)
        scaled = grad * g0
        back = inv * scaled - v * (inv * inv * inv * jnp.mean(scaled * v, axis=-1, keepdims=True))
        gain0 = gain0 + jnp.sum(grad * v * inv, axis=0, keepdims=True)
        r.theirs[k] = (back + r.res[k]).astype(bf16)
        loc.start(r.theirs.at[k], r.dx.at[k])
    r.cols[0:1, :] = gain0
    r.cols[2 : 2 + 3 * CONV, cut(half, pc.t)] = r.dtaps[0 : 3 * CONV, :]
    place_r = lax.broadcasted_iota(jnp.int32, (HD, width), 0)
    place_c = lax.broadcasted_iota(jnp.int32, (HD, width), 1)
    spread = ((place_c // share * per + place_c % share == place_r) & (place_c % share < per)).astype(bf16)
    at = 2 + 3 * CONV + heads_all
    r.cols[at : at + 1, :] = mm(jnp.broadcast_to(dgain, (8, HD)).astype(bf16), spread)[0:1, :]
    pick_r = lax.broadcasted_iota(jnp.int32, (half, HD), 0)
    pick_c = lax.broadcasted_iota(jnp.int32, (half, HD), 1)
    chosen = (
        (pick_c == 2 + 3 * CONV + heads * pc.t + pick_r // HD) & (pick_r % HD == 0)
    ).astype(bf16)
    for c, left in enumerate((r.sv.at[4], r.headed)):
        beta = mm(mm_tn(left[...], r.dproj[:, 3 * half :]).astype(bf16), chosen)
        for n in range(half // SPAN):
            at = c * half + n * SPAN
            rows_in = jnp.concatenate(
                [r.cols[:, at : at + SPAN], jnp.zeros((HD - 32, SPAN), f32)], axis=0
            )
            block = jnp.transpose(rows_in) + beta[n * SPAN : (n + 1) * SPAN]
            r.ge[at // share : (at + SPAN) // share] = unflat(block, share)
    loc.start(r.ge, r.g_first.at[:, :, pl.ds(4 * half, HD)])
    gout[1].wait_recv()
    later.finish()
    for s in streams:
        s.finish()
    last = []
    for src, dst in ((r.f_down, r.o_down), (r.f_gu, r.o_gu)):
        loc.start(src.at[pc.t], dst.at[pc.t])
        last.append(rem.start(src.at[1 - pc.t], dst.at[pc.t], "core"))
    for copy in last:
        copy.wait_recv()
    crossing[0].wait_recv()
    for s in streams:
        s.drain(ordered)
    rem.drain()
    loc.done()


RETURNS = (
    (2, 0, None, "xyz"),
    (2, 1, None, "yxz"),
    (1, 0, None, "zxy"),
    (1, 1, None, "zyx"),
)


def backward(f, mine, g_gu, g_down, lo, levels, per, heads_all):
    width = f["normed_out"].shape[1]
    rows = f["normed_out"].shape[0]
    half = f["logit_out"].shape[1]
    piece = rows // 4
    share = f["wo_out"].shape[1]
    heads = half // HD
    spans = rows // SPAN
    shards = levels * 8
    sds = jax.ShapeDtypeStruct
    ins = dict(
        mine_in=mine.reshape(4, piece, width),
        res_in=f["res_out"].reshape(4, piece, width),
        dy_in=f["dy"],
        x_in=f["x_out"],
        gains_in=f["gains_out"], hgain_in=f["hgain_out"], taps_in=f["taps_out"],
        segc_in=f["segc_out"], segr_in=f["segr_out"], headed_in=f["headed_out"],
        wo_in=f["wo_out"], out_in=f["out_out"], logit_in=f["logit_out"], proj_in=f["proj_out"],
        normed_in=f["normed_out"], wmix_in=f["wmix_out"],
        g_gu_in=g_gu, g_down_in=g_down, lo_in=lo,
    )
    ins.update({k + "_in": f[k + "_out"] for k in ("qs", "ks", "vs", "fs", "ws", "ns", "ps", "ss")})
    outs = dict(
        g_first=sds((shards, share, 4 * half + HD), bf16),
        dx=sds((2, piece, width), bf16),
        o_gu=sds((2, share, g_gu.shape[2]), f32),
        o_down=sds((2, share, g_down.shape[2]), f32),
        lo_out=sds(lo.shape, bf16),
    )
    scratch = dict(
        mine=VM((4, piece, width), bf16),
        theirs=VM((4, piece, width), bf16),
        theirs3=VM((2, piece, width), bf16),
        res=VM((4, piece, width), f32),
        gains=VM((8, width), f32),
        hgain=VM((8, HD), f32),
        taps=VM((16, half), f32),
        dtaps=VM((16, half), f32),
        segc=VM((rows, HD), f32),
        segr=VM((8, rows), f32),
        headed=VM((rows, half), bf16),
        wo=VM((shards // 2, share, width), bf16),
        datt=VM((2, rows, half), bf16),
        cols=VM((32, width), f32),
        gm=VM((3, shards, share, half), bf16),
        ge=VM((shards, share, HD), bf16),
        dheaded=VM((rows, half), bf16),
        sv=VM((5, rows, half), bf16),
        sq=VM((3, heads * spans, SPAN, SPAN), bf16),
        out=VM((rows, half), f32),
        logit=VM((rows, half), f32),
        dproj=VM((rows, 4 * half), bf16),
        keep=VM((CONV - 1, rows, HD), f32),
        g_gu=VM(g_gu.shape, bf16),
        g_down=VM(g_down.shape, bf16),
        f_gu=VM((2,) + g_gu.shape[1:], f32),
        f_down=VM((2,) + g_down.shape[1:], f32),
        loc_sem=pltpu.SemaphoreType.DMA((64,)),
        send_sem=pltpu.SemaphoreType.DMA((16,)),
        recv_sem=pltpu.SemaphoreType.DMA((16,)),
    )
    sizes = {1: g_gu, 2: g_down}
    for k, (a, hf, cols, order) in enumerate(RETURNS):
        slots, sent = Scatter.slots_of(levels, order)
        first, last = span_of(cols, sizes[a])
        scratch["room%d" % k] = VM((slots, share, last - first), bf16)
        scratch["ss%d" % k] = pltpu.SemaphoreType.DMA((sent,))
        scratch["sr%d" % k] = pltpu.SemaphoreType.DMA((slots,))
    cfg = dict(
        heads=heads, spans=spans, per=per, share=share, width=width, half=half,
        heads_all=heads_all, piece=piece, rows=rows,
        program=[4.0] + [1.5] * 4 + [3.0, 4.0] + [2.5] * heads + [0.7] * spans
        + [2.0] * (3 * heads) + [2.5] * 2 + [2.0] * 3 + [3.0],
    )
    return call(backward_kernel, ins, outs, scratch, 2, 63, levels, cfg)


LAST = (
    (0, 0, (0, 11), "xyz"),
    (0, 0, (11, None), "zyx"),
    (0, 1, None, "zxy"),
)


def last_kernel(r, levels, cfg):
    pc = Place(levels)
    loc = Local(Sems(r.loc_sem))
    rem = Remote(pc, Sems(r.send_sem), Sems(r.recv_sem))
    load = loc.start(r.g_in, r.g)
    pc.meet(NEIGHBOURS)
    streams = [
        Scatter(pc, r.g, r.__dict__["room%d" % k], r.final, hf, span_of(cols, r.g), order,
                r.__dict__["ss%d" % k], r.__dict__["sr%d" % k])
        for k, (a, hf, cols, order) in enumerate(LAST)
    ]
    ordered = blocks_of(levels)[::-1]
    loc.wait(load)
    crossing = []
    mb = lambda n, m: 2e-6 * n * m
    steps = scatter_steps(
        streams, [0] * len(streams),
        [mb(r.g.shape[1], s.cols.stop - s.cols.start) for s in streams], levels,
    )
    steps.append(crossing_step(lambda: crossing.append(rem.start(r.dx_in, r.dx_out, "x")),
                               mb(*r.dx_in.shape), 1, "dx"))
    Planned(plan(steps, [], levels, {0: 0.0, 1: 0.0}, {})[0]).finish()
    for s in streams:
        s.finish()
    loc.start(r.final.at[pc.t], r.o_first.at[pc.t])
    copy = rem.start(r.final.at[1 - pc.t], r.o_first.at[pc.t], "core")
    copy.wait_recv()
    crossing[0].wait_recv()
    for s in streams:
        s.drain(ordered)
    rem.drain()
    loc.done()


def last_scatter(g, dx, levels):
    sds = jax.ShapeDtypeStruct
    scratch = dict(
        g=VM(g.shape, bf16),
        final=VM((2,) + g.shape[1:], f32),
        loc_sem=pltpu.SemaphoreType.DMA((8,)),
        send_sem=pltpu.SemaphoreType.DMA((8,)),
        recv_sem=pltpu.SemaphoreType.DMA((8,)),
    )
    for k, (a, hf, cols, order) in enumerate(LAST):
        slots, sent = Scatter.slots_of(levels, order)
        first, last = span_of(cols, g)
        scratch["room%d" % k] = VM((slots, g.shape[1], last - first), bf16)
        scratch["ss%d" % k] = pltpu.SemaphoreType.DMA((sent,))
        scratch["sr%d" % k] = pltpu.SemaphoreType.DMA((slots,))
    return call(
        last_kernel,
        dict(g_in=g, dx_in=dx),
        dict(o_first=sds((2,) + g.shape[1:], f32), dx_out=sds(dx.shape, bf16)),
        scratch, 3, 40, levels, {},
    )


def swap_kernel(src, dst, send_sem, recv_sem):
    c = lax.axis_index("ctx")
    mate = {"dp": lax.axis_index("dp"), "ctx": c + 1 - 2 * (c % 2)}
    barrier = pltpu.get_barrier_semaphore()
    pl.semaphore_signal(barrier, inc=1, device_id=mate, device_id_type=MESH)
    pl.semaphore_wait(barrier, 1)
    copy = pltpu.make_async_remote_copy(
        src_ref=src,
        dst_ref=dst,
        send_sem=send_sem,
        recv_sem=recv_sem,
        device_id=mate,
        device_id_type=MESH,
    )
    copy.start()
    copy.wait()


def swap(value, number):
    return pl.pallas_call(
        swap_kernel,
        out_shape=jax.ShapeDtypeStruct(value.shape, value.dtype),
        in_specs=[pl.BlockSpec(memory_space=ANY)],
        out_specs=pl.BlockSpec(memory_space=ANY),
        scratch_shapes=[pltpu.SemaphoreType.DMA, pltpu.SemaphoreType.DMA],
        compiler_params=pltpu.CompilerParams(collective_id=number, has_side_effects=True),
    )(value)


def norm_parts(values, epsilon):
    inv = lax.rsqrt(jnp.mean(values * values, axis=-1, keepdims=True) + epsilon)
    return inv


def norm_back(values, gain, grad, epsilon):
    inv = norm_parts(values, epsilon)
    scaled = gain * grad
    back = inv * scaled - values * (
        inv * inv * inv * jnp.mean(scaled * values, axis=-1, keepdims=True)
    )
    return back, grad * values * inv


def body(tokens, cotangent, starts, norm_gain, qkv_weight, conv_weight, beta_weight,
         head_gain, out_weight, gate_up_weight, down_weight):
    levels = lax.axis_size("dp") // 2
    ctx = lax.axis_size("ctx")
    device = lax.axis_index("dp") * ctx + lax.axis_index("ctx")
    t = lax.axis_index("ctx") % 2
    m = lax.axis_index("ctx") // 2
    batches, _, piece, width = tokens.shape
    rows = ctx * piece
    share = qkv_weight.shape[1]
    hidden = gate_up_weight.shape[2]
    half, fhalf = width // 2, hidden // 2
    heads_all = beta_weight.shape[1]
    heads = heads_all // 2
    per = head_gain.shape[0]
    small = 2 + 3 * CONV + heads_all + 1

    gain_rows = jnp.zeros((share, 1), bf16).at[:per, 0].set(head_gain)
    ext = jnp.concatenate(
        [norm_gain.T, conv_weight.T, beta_weight, gain_rows, jnp.zeros((share, HD - small), bf16)],
        axis=1,
    )
    flags = jnp.broadcast_to(
        starts.reshape(batches, piece, 1).astype(bf16), (batches, piece, HD)
    )
    f = forward(
        qkv_weight, out_weight, gate_up_weight, down_weight, ext,
        tokens[:, 0], cotangent[:, 0], flags, levels, per, heads_all,
    )
    w_gu = f["w_gu"].reshape(width, 2 * fhalf)
    w_down = f["w_down"].reshape(width, fhalf)
    w_out = f["wo_out"].reshape(half, width)
    w_mix = f["wmix_out"]
    dy = f["dy"].reshape(rows, width)
    residual, normed2 = f["res_out"], f["normed2_out"]
    gate = jnp.dot(normed2, w_gu[:, :fhalf], preferred_element_type=f32)
    up = jnp.dot(normed2, w_gu[:, fhalf:], preferred_element_type=f32)
    sg = jax.nn.sigmoid(gate)
    act = (gate * sg * up).astype(bf16)

    def by_parity(value):
        parts = value.reshape(ctx // 2, 2, piece, width)
        return lax.dynamic_index_in_dim(parts, t, 1, False), lax.dynamic_index_in_dim(
            parts, 1 - t, 1, False
        )

    ffn, ffn_other = by_parity(
        lax.dot_general(act, w_down, (((1,), (1,)), ((), ())), preferred_element_type=f32).astype(bf16)
    )
    res_own = by_parity(residual)[0]
    result = (res_own + ffn.astype(f32) + swap(ffn_other, 4).astype(f32)).astype(bf16)

    dact = jnp.dot(dy, w_down, preferred_element_type=f32)
    g_down = lax.dot_general(dy, act, (((0,), (0,)), ((), ())), preferred_element_type=f32).astype(bf16)
    dgate = (dact * up * sg * (1.0 + gate * (1.0 - sg))).astype(bf16)
    dup = (dact * gate * sg).astype(bf16)
    dgu = jnp.concatenate([dgate, dup], axis=1)
    g_gu = lax.dot_general(normed2, dgu, (((0,), (0,)), ((), ())), preferred_element_type=f32).astype(bf16)
    mine = lax.dot_general(dgu, w_gu, (((1,), (1,)), ((), ())), preferred_element_type=f32).astype(bf16)
    shaped = lambda g: g.reshape(width // share, share, -1)
    pick = lambda parts, k: lax.dynamic_index_in_dim(parts, k, 0, False)
    b = backward(
        f, mine, shaped(g_gu), shaped(g_down), pick(result, 1 - m), levels, per, heads_all
    )
    dx, o_gu, o_down, got_y = b["dx"], b["o_gu"], b["o_down"], b["lo_out"]
    e = last_scatter(b["g_first"], pick(dx, 1 - m), levels)
    o_first, got_x = e["o_first"], e["dx_out"]
    ordered = lambda own, got: jnp.stack(
        [jnp.where(m == 0, own, got), jnp.where(m == 0, got, own)]
    )[:, None]
    layer_out = ordered(pick(result, m), got_y)
    input_grad = ordered(pick(dx, m), got_x)
    join = lambda o, n: jnp.moveaxis(o.reshape(2, share, n, -1), (2, 1), (0, 1)).reshape(n, share, -1)
    o_small = jnp.sum(o_first[:, :, 4 * half :], axis=0)
    return (
        layer_out,
        input_grad,
        o_small[:, 0:2].T,
        join(o_first[:, :, : 3 * half], 3),
        o_small[:, 2 : 2 + 3 * CONV].T,
        o_small[:, 2 + 3 * CONV : 2 + 3 * CONV + heads_all],
        o_small[:per, small - 1],
        join(o_first[:, :, 3 * half : 4 * half], 1)[0],
        join(o_gu, 2),
        join(o_down, 1)[0],
    )


def solution(mesh):
    both = ("dp", "ctx")
    acts = P(None, "dp", "ctx", None)
    return jax.shard_map(
        body,
        mesh=mesh,
        in_specs=(
            acts,
            acts,
            P(None, "dp", "ctx"),
            P(None, both),
            P(None, both, None),
            P(None, both),
            P(both, None),
            P(both),
            P(both, None),
            P(None, both, None),
            P(both, None),
        ),
        out_specs=(
            acts,
            acts,
            P(None, both),
            P(None, both, None),
            P(None, both),
            P(both, None),
            P(both),
            P(both, None),
            P(None, both, None),
            P(both, None),
        ),
        check_vma=False,
    )
```

```python
import functools

import jax
import jax.numpy as jnp
from jax import lax
from jax.experimental import pallas as pl
from jax.experimental.pallas import tpu as pltpu
from jax.sharding import PartitionSpec as P

MESH = pl.DeviceIdType.MESH
ANY = pl.ANY
VM = pltpu.VMEM
MIB = 1 << 20
f32 = jnp.float32
bf16 = jnp.bfloat16


def route(block, order):
    dz, fx, fy = block
    rank = {dim: place for place, dim in enumerate(order)}
    last = max([-1] + [rank[d] for d, on in (("z", dz), ("x", fx), ("y", fy)) if on])
    hops = []
    for dim in order:
        if dim == "z":
            if dz == 0 and rank["z"] > last:
                hops += ["up", "dn"]
            elif dz != 0 and last == rank["z"]:
                hops.append("up" if dz < 0 else "dn")
        elif rank[dim] > last:
            hops.append(dim)
    came = None
    if last >= 0:
        came = order[last]
        if came == "z":
            came = "up" if dz < 0 else "dn"
    return hops, came


def blocks_of(levels):
    named = [
        (dz, fx, fy)
        for dz in range(1 - levels, levels)
        for fx in (0, 1)
        for fy in (0, 1)
    ]
    return sorted(named, key=lambda b: (abs(b[0]) + b[1] + b[2], abs(b[0]), b))


class Place:
    def __init__(self, levels):
        i = lax.axis_index("dp")
        c = lax.axis_index("ctx")
        self.levels = levels
        self.i, self.c = i, c
        self.z, self.y = i // 2, i % 2
        self.x, self.t = c // 2, c % 2

    def device(self, hop):
        i, c = self.i, self.c
        if hop == "x":
            return {"dp": i, "ctx": (1 - self.x) * 2 + self.t}
        if hop == "y":
            return {"dp": self.z * 2 + 1 - self.y, "ctx": c}
        if hop == "up":
            return {"dp": i + 2, "ctx": c}
        if hop == "dn":
            return {"dp": i - 2, "ctx": c}
        return {"dp": i, "ctx": self.x * 2 + 1 - self.t}

    def valid(self, block, hop=None):
        dz = block[0]
        terms = []
        if dz > 0:
            terms.append(self.z + dz < self.levels)
        if dz < 0:
            terms.append(self.z + dz >= 0)
        if hop == "up" and dz <= 0:
            terms.append(self.z + 1 < self.levels)
        if hop == "dn" and dz >= 0:
            terms.append(self.z >= 1)
        if not terms:
            return None
        return functools.reduce(jnp.logical_and, terms)

    def level(self, block):
        return self.z + block[0]

    def shard(self, block, half):
        z = self.z + block[0]
        y = 1 - self.y if block[2] else self.y
        x = 1 - self.x if block[1] else self.x
        chip = (z * 2 + y) * 2 + x
        if half is None:
            return pl.ds(chip * 2, 2)
        return chip * 2 + half

    def meet(self, hops):
        barrier = pltpu.get_barrier_semaphore()
        count = 0
        for hop in hops:
            def greet(hop=hop):
                pl.semaphore_signal(
                    barrier, inc=1, device_id=self.device(hop), device_id_type=MESH
                )
            if hop in ("up", "dn"):
                here = (self.z + 1 < self.levels) if hop == "up" else (self.z >= 1)
                pl.when(here)(greet)
                count = count + here.astype(jnp.int32)
            else:
                greet()
                count = count + 1
        pl.semaphore_wait(barrier, count)


def when(condition, action):
    if condition is None:
        action()
    else:
        pl.when(condition)(action)


def send_slots(order):
    table = {}
    for fx in (0, 1):
        for fy in (0, 1):
            for dz in (-1, 0, 1):
                for hop in route((dz, fx, fy), order)[0]:
                    table.setdefault((hop, fx, fy), len(table))
    return table


class Gather:
    def __init__(self, place, ref, half, cols, order, send_sem, recv_sem):
        self.place, self.ref, self.half = place, ref, half
        self.cols = slice(*cols)
        self.order = order
        self.slots = send_slots(order)
        self.send_sem, self.recv_sem = send_sem, recv_sem

    @staticmethod
    def sems(levels, order):
        return len(send_slots(order)) * levels, 4 * levels

    def copy(self, block, hop):
        place = self.place
        dz, fx, fy = block
        where = place.shard(block, self.half)
        level = place.level(block)
        there = (fx ^ (hop == "x"), fy ^ (hop == "y"))
        return pltpu.make_async_remote_copy(
            src_ref=self.ref.at[where, :, self.cols],
            dst_ref=self.ref.at[where, :, self.cols],
            send_sem=self.send_sem.at[self.slots[hop, fx, fy] * place.levels + level],
            recv_sem=self.recv_sem.at[(there[0] * 2 + there[1]) * place.levels + level],
            device_id=place.device(hop),
            device_id_type=MESH,
        )

    def arrival(self, block):
        place = self.place
        dz, fx, fy = block
        where = place.shard(block, self.half)
        came = route(block, self.order)[1]
        back = {"up": "dn", "dn": "up"}.get(came, came)
        return pltpu.make_async_remote_copy(
            src_ref=self.ref.at[where, :, self.cols],
            dst_ref=self.ref.at[where, :, self.cols],
            send_sem=self.send_sem.at[0],
            recv_sem=self.recv_sem.at[(fx * 2 + fy) * place.levels + place.level(block)],
            device_id=place.device(back),
            device_id_type=MESH,
        )

    def wait(self, block):
        when(self.place.valid(block), lambda: self.arrival(block).wait_recv())

    def pass_on(self, block, only=("x", "y", "up", "dn")):
        for hop in route(block, self.order)[0]:
            if hop not in only:
                continue
            when(self.place.valid(block, hop), lambda hop=hop: self.copy(block, hop).start())

    def drain(self, blocks):
        for block in blocks:
            for hop in route(block, self.order)[0]:
                when(
                    self.place.valid(block, hop),
                    lambda hop=hop: self.copy(block, hop).wait_send(),
                )


def room_table(order, levels):
    table, used = {}, 0
    for fx in (0, 1):
        for fy in (0, 1):
            here = route((0, fx, fy), order)[0]
            away = route((1, fx, fy), order)[0] + route((-1, fx, fy), order)[0]
            for hop in ("x", "y"):
                if hop in here or hop in away:
                    table[hop, fx, fy] = (used, hop in away)
                    used += levels if hop in away else 1
            if "up" in here + away or "dn" in here + away:
                table["z", fx, fy] = (used, True)
                used += levels + 1
    return table, used


class Scatter:
    def __init__(self, place, ref, room, final, half, cols, order, send_sem, recv_sem):
        self.place, self.ref, self.room, self.final = place, ref, room, final
        self.half, self.order = half, order
        self.cols = slice(*cols)
        self.table = room_table(order, place.levels)[0]
        self.send_sem, self.recv_sem = send_sem, recv_sem

    @staticmethod
    def slots_of(levels, order):
        return room_table(order, levels)[1], 4 * levels

    def slot_at(self, hop, dz, fx, fy, level):
        base, many = self.table["z" if hop in ("up", "dn") else hop, fx, fy]
        if hop == "dn" and dz == 0:
            return base + self.place.levels
        return base + level if many else base

    def slot(self, block, hop):
        return self.slot_at(hop, *block, self.place.level(block))

    def copy(self, block, src):
        place = self.place
        dz, fx, fy = block
        came = route(block, self.order)[1]
        back = {"up": "dn", "dn": "up"}.get(came, came)
        there = (
            dz + (came == "up") - (came == "dn"),
            fx ^ (came == "x"),
            fy ^ (came == "y"),
        )
        slot = self.slot_at(came, *there, place.level(block))
        return pltpu.make_async_remote_copy(
            src_ref=src,
            dst_ref=self.room.at[slot],
            send_sem=self.send_sem.at[(fx * 2 + fy) * place.levels + place.level(block)],
            recv_sem=self.recv_sem.at[slot],
            device_id=place.device(back),
            device_id_type=MESH,
        )

    def arrive(self, block, hop):
        slot = self.slot(block, hop)
        pltpu.make_async_remote_copy(
            src_ref=self.room.at[slot],
            dst_ref=self.room.at[slot],
            send_sem=self.send_sem.at[0],
            recv_sem=self.recv_sem.at[slot],
            device_id=self.place.device(hop),
            device_id_type=MESH,
        ).wait_recv()

    def in_room(self, slot, at):
        return (slot, at) if self.half is not None else (slot, slice(None), at)

    def in_final(self, at):
        return (slice(None) if self.half is None else self.half, at, self.cols)

    def total(self, block, hops, put):
        where = self.place.shard(block, self.half)
        slots = [self.slot(block, hop) for hop in hops]
        rows = self.ref.shape[1]
        step = min(16, rows)

        def one(k, carry):
            at = pl.ds(pl.multiple_of(k * step, step), step)
            value = self.ref[where, at, self.cols].astype(f32)
            for slot in slots:
                value = value + self.room[self.in_room(slot, at)].astype(f32)
            put(at, value)
            return carry

        lax.fori_loop(0, rows // step, one, 0)

    def branch(self, maybe, using, go):
        if not maybe:
            go(using)
            return
        hop, place = maybe[0], self.place
        here = place.z + 1 < place.levels if hop == "up" else place.z >= 1
        pl.when(here)(lambda: self.branch(maybe[1:], using + [hop], go))
        pl.when(jnp.logical_not(here))(lambda: self.branch(maybe[1:], using, go))

    def forward(self, block):
        place = self.place
        hops = route(block, self.order)[0]
        sure = [h for h in hops if h in ("x", "y")]
        maybe = [h for h in hops if h not in ("x", "y")]

        def go(using):
            for hop in using:
                self.arrive(block, hop)
            if not using:
                self.copy(block, self.ref.at[place.shard(block, self.half), :, self.cols]).start()
                return
            slot = self.slot(block, using[0])

            def put(at, value):
                self.room[self.in_room(slot, at)] = value.astype(bf16)

            self.total(block, using, put)
            self.copy(block, self.room.at[slot]).start()

        def both():
            self.branch(maybe, sure, go)

        when(place.valid(block), both)

    def finish(self):
        own = (0, 0, 0)
        place = self.place
        hops = route(own, self.order)[0]
        sure = [h for h in hops if h in ("x", "y")]
        for hop in sure:
            self.arrive(own, hop)

        def put(at, value):
            self.final[self.in_final(at)] = value

        self.total(own, sure, put)
        for hop in hops:
            if hop in sure:
                continue

            def add(hop=hop):
                self.arrive(own, hop)
                slot = self.slot(own, hop)
                every = self.in_final(slice(None))
                self.final[every] = self.final[every] + self.room[slot].astype(f32)

            when(place.valid(own, hop), add)

    def drain(self, blocks):
        for block in blocks:
            if block == (0, 0, 0):
                continue
            when(
                self.place.valid(block),
                lambda block=block: self.copy(
                    block, self.ref.at[self.place.shard(block, self.half), :, self.cols]
                ).wait_send(),
            )


OWN = (0, 0, 0)

RATE = 0.038
LATE = 2
HOP = 1.6


class Step:
    def __init__(self, run, valid, needs, sends, cost, group, rank):
        self.run, self.valid, self.needs, self.sends = run, valid, needs, sends
        self.cost, self.group, self.rank = cost, group, rank


def exists(block, z, levels):
    return 0 <= z + block[0] < levels


def can_hop(z, hop, levels):
    return {"up": z + 1 < levels, "dn": z >= 1}.get(hop, True)


def moved(block, hop):
    dz, fx, fy = block
    return (dz - (hop == "up") + (hop == "dn"), fx ^ (hop == "x"), fy ^ (hop == "y"))


def level_of(z, hop):
    return z + (hop == "up") - (hop == "dn")


def height(block, order, levels):
    if abs(block[0]) >= levels:
        return -1
    return max([0] + [1 + height(moved(block, h), order, levels) for h in route(block, order)[0]])


def crossing_step(run, size, group, key):
    return Step(
        run, lambda z: True, lambda z: [("own", group)], lambda z: [("x", size, (key, z))],
        0.2, group, 0,
    )


def gather_steps(streams, group_of, size_of, levels, begin=None):
    steps = []
    for k, s in enumerate(streams):
        for block in blocks_of(levels):
            seen = []
            for ways in (("up", "dn"), ("x",), ("y",)):
                hops = [h for h in route(block, s.order)[0] if h in ways]
                if not hops:
                    continue

                def needs(z, k=k, block=block):
                    return [("own", group_of[k])] if block == OWN else [(k, z, block)]

                def sends(z, k=k, block=block, hops=hops):
                    return [
                        (h, size_of[k], (k, level_of(z, h), moved(block, h)))
                        for h in hops
                        if can_hop(z, h, levels)
                    ]

                def run(s=s, k=k, block=block, ways=ways, seen=seen):
                    if not seen:
                        seen.append(True)
                        if block != OWN:
                            s.wait(block)
                        else:
                            begin(group_of[k])
                    s.pass_on(block, ways)

                lane = group_of[k]
                if s.order[0] != "z":
                    lane = LATE if "up" in ways else 0
                steps.append(
                    Step(
                        run,
                        lambda z, block=block: exists(block, z, levels),
                        needs,
                        sends,
                        0.15,
                        lane,
                        -max(1 + height(moved(block, h), s.order, levels) for h in hops),
                    )
                )
    return steps


def scatter_steps(streams, group_of, size_of, levels):
    steps = []
    for k, s in enumerate(streams):
        for block in blocks_of(levels)[::-1]:
            if block == OWN:
                continue
            hops, came = route(block, s.order)
            back = {"up": "dn", "dn": "up"}.get(came, came)

            def needs(z, k=k, block=block, hops=hops):
                got = [(k, z, block, h) for h in hops if can_hop(z, h, levels)]
                return got or [("own", group_of[k])]

            def sends(z, k=k, block=block, came=came, back=back):
                there = moved(block, back)
                return [(back, size_of[k], (k, level_of(z, back), there, came))]

            steps.append(
                Step(
                    lambda s=s, block=block: s.forward(block),
                    lambda z, block=block: exists(block, z, levels),
                    needs,
                    sends,
                    0.15 + (1.5 * size_of[k] if hops else 0.0),
                    group_of[k],
                    -abs(block[0]) - block[1] - block[2],
                )
            )
    return steps


def plan(steps, program, levels, own, gates, slack=0.0, events=None):
    now = [0.0] * levels
    free = [dict(x=0.0, y=0.0, up=0.0, dn=0.0) for _ in range(levels)]
    there = {("own", g): at for g, at in own.items()}
    left = list(steps)
    out = []

    def ready(step):
        times = []
        for z in range(levels):
            if not step.valid(z):
                continue
            for key in step.needs(z):
                if key not in there:
                    return None
                times.append((there[key], now[z]))
        return times

    def do(step):
        for z in range(levels):
            if not step.valid(z):
                continue
            now[z] = max([now[z]] + [there[key] for key in step.needs(z)]) + step.cost
        for z in range(levels):
            if not step.valid(z):
                continue
            for hop, size, key in step.sends(z):
                begin = max(now[z], free[z][hop])
                free[z][hop] = begin + size / RATE
                there[key] = free[z][hop] + HOP
        left.remove(step)

    def quick(step):
        times = ready(step)
        return times is not None and all(at + slack <= when + 0.3 for at, when in times)

    def drain_ready(batch, held):
        while True:
            able = [s for s in left if s.group not in held and quick(s)]
            if not able:
                return
            step = min(able, key=lambda s: (s.group, s.rank))
            do(step)
            batch.append(step)

    def wait_for(step):
        return max([max(at - when, 0.0) for at, when in ready(step)] + [0.0])

    def until(batch, done):
        while left and not done():
            able = [s for s in left if ready(s) is not None]
            if not able:
                return
            first = min(s.group for s in able)

            def idle(s):
                return all(
                    free[z][hop] <= now[z] + 1.0
                    for z in range(levels)
                    if s.valid(z)
                    for hop, _, _ in s.sends(z)
                )

            pool = [s for s in able if s.group == first or idle(s)]
            step = min(pool, key=lambda s: (round(wait_for(s), 1), s.group, s.rank))
            do(step)
            batch.append(step)

    for place, duration in enumerate(program):
        batch = []
        for group in (events or {}).get(place, ()):
            there["own", group] = max(now)
        keys = gates.get(place)
        if keys:
            until(batch, lambda: all(k in there for z in range(levels) for k in keys(z)))
            limit = [max(there[k] for k in keys(z)) for z in range(levels)]
            while True:
                able = [
                    s
                    for s in left
                    if ready(s) is not None
                    and all(
                        max(now[z], *(there[k] for k in s.needs(z))) + s.cost <= limit[z]
                        for z in range(levels)
                        if s.valid(z)
                    )
                ]
                if not able:
                    break
                step = min(able, key=lambda s: (round(wait_for(s), 1), s.group, s.rank))
                do(step)
                batch.append(step)
            for z in range(levels):
                now[z] = max(now[z], limit[z])
        drain_ready(batch, ())
        out.append(batch)
        for z in range(levels):
            now[z] += duration
    batch = []
    for group in (events or {}).get(len(program), ()):
        there["own", group] = max(now)
    until(batch, lambda: False)
    out.append(batch)
    return out, max(now), max([at for at in there.values()] + [0.0])


class Planned:
    def __init__(self, batches):
        self.batches = list(batches)

    def take(self):
        return self.batches.pop(0)

    def tick(self):
        for step in self.take():
            step.run()

    def looped(self, count, each=1):
        now = [self.take() for _ in range(count * each)]

        def at(index, which=0):
            for k, steps in enumerate(now[which::each]):
                if steps:
                    pl.when(index == k)(lambda steps=steps: [s.run() for s in steps] and None)

        return at

    def finish(self):
        while self.batches:
            self.tick()


HD = 128
CONV = 4
SPAN = 128


def mm(a, b):
    return jnp.dot(a, b, preferred_element_type=f32)


def mm_nt(a, b):
    return lax.dot_general(a, b, (((1,), (1,)), ((), ())), preferred_element_type=f32)


def mm_tn(a, b):
    return lax.dot_general(a, b, (((0,), (0,)), ((), ())), preferred_element_type=f32)


def lanes(h):
    return pl.ds(pl.multiple_of(h * HD, HD), HD)


def set_masks(segc, keep):
    rows = lax.broadcasted_iota(jnp.int32, segc.shape, 0)
    seg = segc[...]
    for o in range(1, CONV):
        same = (pltpu.roll(seg, o, 0) == seg) & (rows >= o)
        keep[o - 1] = same.astype(f32)


def shifted(value, keep, o):
    return value if o == 0 else pltpu.roll(value, o, 0) * keep[o - 1]


def conv_of(proj, taps, keep, j, h, heads):
    at = lanes(j * heads + h)
    value = proj[:, at].astype(f32)
    total = taps[pl.ds(j * CONV + CONV - 1, 1), lanes(h)] * value
    for o in range(1, CONV):
        total = total + taps[pl.ds(j * CONV + CONV - 1 - o, 1), lanes(h)] * shifted(value, keep, o)
    return total


def span_masks(segc, segr, n):
    at = slice(n * SPAN, (n + 1) * SPAN)
    col = segc[at, :]
    same = col == jnp.broadcast_to(segr[0:1, at], (SPAN, SPAN))
    if n:
        carried = (col == segc[n * SPAN - 1 : n * SPAN, :]).astype(f32)
    else:
        carried = jnp.zeros((SPAN, HD), f32)
    ending = (col == col[SPAN - 1 : SPAN, :]).astype(f32)
    return carried, same, ending


def iotas():
    i = lax.broadcasted_iota(jnp.int32, (SPAN, SPAN), 0)
    j = lax.broadcasted_iota(jnp.int32, (SPAN, SPAN), 1)
    return i, j


def unit_inverses(lowers):
    i, j = iotas()
    apart = i ^ j
    invs = [jnp.where(apart == 1, -low, 0.0) for low in lowers]
    size, bits = 2, 1
    while size < SPAN:
        pairs = lax.shift_right_logical(apart, bits) == 1
        part = [jnp.where(pairs, low, 0.0) for low in lowers]
        small = [inv.astype(bf16) for inv in invs]
        left = [p + mm(s, p.astype(bf16)) for p, s in zip(part, small)]
        both = [w + mm(w.astype(bf16), s) for w, s in zip(left, small)]
        invs = [inv - b for inv, b in zip(invs, both)]
        size, bits = size * 2, bits + 1
    return invs


SLACK_F = 0.0


class Names:
    def __init__(self, names, refs):
        self.__dict__.update(zip(names, refs, strict=True))


class Sems:
    def __init__(self, ref):
        self.ref, self.used = ref, 0

    def take(self):
        self.used += 1
        return self.ref.at[self.used - 1]


def call(kernel, ins, outs, scratch, number, limit, *static):
    names = list(ins) + list(outs) + list(scratch)

    def run(*refs):
        kernel(Names(names, refs), *static)

    results = pl.pallas_call(
        run,
        out_shape=list(outs.values()),
        in_specs=[pl.BlockSpec(memory_space=ANY)] * len(ins),
        out_specs=[pl.BlockSpec(memory_space=ANY)] * len(outs),
        scratch_shapes=list(scratch.values()),
        compiler_params=pltpu.CompilerParams(
            collective_id=number, has_side_effects=True, vmem_limit_bytes=limit * MIB
        ),
    )(*ins.values())
    return dict(zip(outs, results, strict=True))


class Local:
    def __init__(self, sems):
        self.sems, self.open = sems, []

    def start(self, src, dst):
        copy = pltpu.make_async_copy(src, dst, self.sems.take())
        copy.start()
        self.open.append(copy)
        return copy

    def holds(self, copy):
        return any(copy is other for other in self.open)

    def wait(self, copy):
        copy.wait()
        self.open = [other for other in self.open if other is not copy]

    def done(self):
        for copy in self.open:
            copy.wait()
        self.open = []


class Remote:
    def __init__(self, place, sent, got):
        self.place, self.sent, self.got, self.open = place, sent, got, []

    def start(self, src, dst, hop):
        copy = pltpu.make_async_remote_copy(
            src_ref=src,
            dst_ref=dst,
            send_sem=self.sent.take(),
            recv_sem=self.got.take(),
            device_id=self.place.device(hop),
            device_id_type=MESH,
        )
        copy.start()
        self.open.append(copy)
        return copy

    def drain(self):
        for copy in self.open:
            copy.wait_send()
        self.open = []


def unflat(value, share):
    return value.reshape(value.shape[0] // share, share, value.shape[1]).astype(bf16)


def flat(ref, cols):
    value = ref[:, :, cols]
    shape = (value.shape[0] * value.shape[1], value.shape[2])
    if value.shape[1] % 16:
        return value.astype(f32).reshape(shape).astype(bf16)
    return value.reshape(shape)


STREAMS = (
    (0, 0, (0, 6), "zxy"),
    (0, 0, (6, None), "zyx"),
    (0, 1, (0, 10), "zxy"),
    (0, 1, (10, None), "zyx"),
    (1, 0, None, "zxy"),
    (1, 1, None, "xyz"),
    (2, 0, None, "zyx"),
    (2, 1, None, "zxy"),
)


def span_of(cols, ref):
    if cols is None:
        return 0, ref.shape[2]
    first, last = cols
    return first * HD, ref.shape[2] if last is None else last * HD


NEIGHBOURS = ("x", "y", "up", "dn", "core")


def forward_kernel(r, levels, cfg):
    heads, spans, per, share = cfg["heads"], cfg["spans"], cfg["per"], cfg["share"]
    width, half, fhalf, heads_all = cfg["width"], cfg["half"], cfg["fhalf"], cfg["heads_all"]
    piece, rows = cfg["piece"], cfg["rows"]
    pc = Place(levels)
    loc = Local(Sems(r.loc_sem))
    rem = Remote(pc, Sems(r.send_sem), Sems(r.recv_sem))
    pc.meet(NEIGHBOURS)
    own = pc.shard(OWN, pc.t)
    targets = (r.w1, r.w_gu, r.w_down)
    streams = [
        Gather(pc, targets[a], hf, span_of(cols, targets[a]), order,
               r.__dict__["gs%d" % k], r.__dict__["gr%d" % k])
        for k, (a, hf, cols, order) in enumerate(STREAMS)
    ]
    def both(src_at, dst):
        return [loc.start(src_at(pc.t), dst), rem.start(src_at(1 - pc.t), dst, "core")]

    def cut(n, t):
        return pl.ds(pl.multiple_of(t * n, n), n)

    opening = []
    for j in range(3):
        opening += both(
            lambda t, j=j: r.qkv.at[j, :, cut(half, t)],
            r.w1.at[own, :, j * half : (j + 1) * half],
        )
    opening += both(lambda t: r.out_w.at[:, cut(half, t)], r.w1.at[own, :, 3 * half : 4 * half])
    opening += both(lambda t: r.ext, r.w1.at[own, :, 4 * half : 4 * half + HD])
    pieces = both(lambda t: r.tok.at[pc.x], r.x.at[pc.c])
    pieces += both(lambda t: r.flags.at[pc.x], r.marks.at[pc.c])

    def arrived(copies):
        for copy in copies:
            if loc.holds(copy):
                loc.wait(copy)
            else:
                copy.wait_recv()

    arrived(opening)
    second = []
    for j in range(2):
        second += both(
            lambda t, j=j: r.gu.at[j, :, cut(fhalf, t)],
            r.w_gu.at[own, :, j * fhalf : (j + 1) * fhalf],
        )
    second += both(lambda t: r.dn.at[:, cut(fhalf, t)], r.w_down.at[own])
    second += both(lambda t: r.cot.at[pc.x], r.dy.at[pc.c])
    hold = {1: second[:4], 2: second[4:6]}
    far = (1 - pc.x) * 2 + pc.t
    crossed = {}

    def cross(name, src, dst):
        crossed[name] = rem.start(src.at[1 - pc.x], dst.at[pc.c], "x")

    groups = [a for a, *_ in STREAMS]
    firsts = [k for k, a in enumerate(groups) if a == 0]
    mb = lambda n, m: 2e-6 * n * m
    steps = gather_steps(
        streams, groups, [mb(share, s.cols.stop - s.cols.start) for s in streams], levels,
        lambda a: arrived(hold.pop(a, [])),
    )
    steps.append(crossing_step(lambda: (cross("x", r.tok, r.x), cross("m", r.flags, r.marks)),
                               mb(piece, width + HD), 0, "tok"))
    steps.append(crossing_step(lambda: cross("dy", r.cot, r.dy), mb(piece, width), 3, "cot"))
    ordered = blocks_of(levels)

    def gate(z):
        return [("tok", z)] + [
            (k, z, block)
            for k in firsts
            for block in ordered
            if block != OWN and exists(block, z, levels)
        ]

    def gate1(z):
        return [
            (k, z, block)
            for k, a in enumerate(groups)
            for block in ordered
            if a == 1 and block != OWN and exists(block, z, levels)
        ]

    later = Planned(
        plan(
            steps, cfg["program"], levels, {0: 4.0, 1: 6.0, 2: 7.0, 3: 7.0},
            {0: gate, len(cfg["program"]) - rows // piece: gate1}, SLACK_F,
        )[0]
    )
    later.tick()
    crossed["x"].wait_recv()
    crossed["m"].wait_recv()
    arrived(pieces)
    pieces = [
        rem.start(r.x.at[far], r.x.at[far], "core"),
        rem.start(r.marks.at[far], r.marks.at[far], "core"),
    ]
    for block in ordered:
        for k in firsts:
            s = streams[k]
            if block != OWN and not route(block, s.order)[0]:
                s.wait(block)
    arrived(pieces)

    i, j = iotas()
    upto = (i >= j).astype(bf16)
    base = jnp.zeros((1, HD), f32)
    for n in range(spans):
        q, at = divmod(n * SPAN, piece)
        marks = r.marks[q, at : at + SPAN, :]
        seg = mm(upto, marks) + base
        r.segc[n * SPAN : (n + 1) * SPAN, :] = seg
        r.segr[:, n * SPAN : (n + 1) * SPAN] = jnp.transpose(seg)[0:8, :]
        base = seg[SPAN - 1 : SPAN, :]
    set_masks(r.segc, r.keep)
    loc.start(r.segc, r.segc_out)
    loc.start(r.segr, r.segr_out)

    shards = levels * 8 // 2
    mine = cut(half, pc.t)
    rows_of = lambda t: pl.ds(pl.multiple_of(t * shards, shards), shards)
    side = pl.ds(3 * half, half)
    swap_out = [
        loc.start(r.w1.at[rows_of(pc.t), :, side], r.wo.at[:, :, mine]),
        rem.start(r.w1.at[rows_of(1 - pc.t), :, side], r.wo.at[:, :, mine], "core"),
    ]

    extra = flat(r.w1, slice(4 * half, 4 * half + HD))
    for n in range(width // SPAN):
        at = slice(n * SPAN, (n + 1) * SPAN)
        r.small[:, at] = jnp.transpose(extra[at, :].astype(f32))[0:32, :]
    r.gains[...] = r.small[0:8, :]
    r.taps[...] = jnp.zeros(r.taps.shape, f32)
    r.taps[0 : 3 * CONV, :] = r.small[2 : 2 + 3 * CONV, cut(half, pc.t)]
    place_r = lax.broadcasted_iota(jnp.int32, (width, HD), 0)
    place_c = lax.broadcasted_iota(jnp.int32, (width, HD), 1)
    chosen = (place_r == share * (place_c // per) + place_c % per).astype(bf16)
    at = 2 + 3 * CONV + heads_all
    r.hgain[...] = jnp.broadcast_to(
        mm(r.small[at - at % 8 : at - at % 8 + 8, :].astype(bf16), chosen)[at % 8 : at % 8 + 1, :],
        (8, HD),
    )
    pick_r = lax.broadcasted_iota(jnp.int32, (HD, half), 0)
    pick_c = lax.broadcasted_iota(jnp.int32, (HD, half), 1)
    chosen = (pick_r == 2 + 3 * CONV + heads * pc.t + pick_c // HD).astype(bf16)
    w_beta = mm(extra, chosen)
    r.wbeta[...] = unflat(w_beta, share)
    pick_r = lax.broadcasted_iota(jnp.int32, (HD, HD), 0)
    pick_c = lax.broadcasted_iota(jnp.int32, (HD, HD), 1)
    chosen = ((pick_r == 2 + 3 * CONV + heads * pc.t + pick_c) & (pick_c < heads)).astype(bf16)
    r.wb[...] = unflat(mm(extra, chosen), share)
    loc.start(r.wb, r.wb_out)
    loc.start(r.w1.at[:, :, pl.ds(0, 3 * half)], r.wmix_out)
    loc.start(r.taps, r.taps_out)
    loc.start(r.gains, r.gains_out)
    loc.start(r.hgain, r.hgain_out)

    g0 = r.gains[0:1, :]
    for n in range(rows // piece):
        x = r.x[n].astype(f32)
        inv = lax.rsqrt(jnp.mean(x * x, axis=-1, keepdims=True) + 1e-5)
        r.normed[n * piece : (n + 1) * piece, :] = (x * inv * g0).astype(bf16)
    loc.start(r.normed, r.normed_out)
    loc.start(r.x, r.x_out)

    steps_at = later.looped(rows // piece)

    def project(k, carry):
        steps_at(k)
        at = pl.ds(pl.multiple_of(k * piece, piece), piece)
        left = r.normed[at, :]
        r.proj[at, :] = mm(left, flat(r.w1, slice(0, 3 * half))).astype(bf16)
        r.logit[at, :] = mm(left, flat(r.wbeta, slice(None)))
        r.blog[at, :] = mm(left, flat(r.wb, slice(None)))
        return carry

    lax.fori_loop(0, rows // piece, project, 0)
    loc.start(r.proj, r.proj_out)
    loc.start(r.blog, r.blog_out)

    prepare_at = later.looped(heads)

    def prepare(h, carry):
        prepare_at(h)
        delta_prepare(r, h, heads, spans)
        return carry

    lax.fori_loop(0, heads, prepare, 0)
    for src, dst in ((r.qs, r.qs_out), (r.ks, r.ks_out), (r.vs, r.vs_out), (r.ws, r.ws_out),
                     (r.ns, r.ns_out), (r.ps, r.ps_out)):
        loc.start(src, dst)
    delta_chain(r, heads, spans, later.tick)
    for h in range(heads):
        head = slice(h * HD, (h + 1) * HD)
        o = r.out[:, head]
        scale = lax.rsqrt(jnp.mean(o * o, axis=-1, keepdims=True) + 1e-5)
        r.headed[:, head] = (o * scale * r.hgain[0:1, :]).astype(bf16)
    for src, dst in ((r.fs, r.fs_out), (r.ss, r.ss_out), (r.out, r.out_out),
                     (r.headed, r.headed_out)):
        loc.start(src, dst)
    later.tick()
    arrived(swap_out)
    loc.start(r.wo, r.wo_out)
    wo = flat(r.wo, slice(None))
    sent = []
    for n in range(rows // piece):
        r.mine[n] = mm(r.headed[n * piece : (n + 1) * piece, :], wo).astype(bf16)
        sent.append(rem.start(r.mine.at[n], r.theirs.at[n], "core"))
    later.tick()
    g1 = r.gains[1:2, :]
    for n in range(rows // piece):
        sent[n].wait_recv()
        at = slice(n * piece, (n + 1) * piece)
        res = r.x[n].astype(f32) + r.mine[n].astype(f32) + r.theirs[n].astype(f32)
        r.res[at, :] = res
        inv = lax.rsqrt(jnp.mean(res * res, axis=-1, keepdims=True) + 1e-5)
        r.normed2[at, :] = (res * inv * g1).astype(bf16)
    loc.start(r.res, r.res_out)
    loc.start(r.normed2, r.normed2_out)
    later.tick()
    for block in ordered:
        for n, s in enumerate(streams):
            if groups[n] == 1 and block != OWN and not route(block, s.order)[0]:
                s.wait(block)
    w_gate, w_up = flat(r.w_gu, slice(0, fhalf)), flat(r.w_gu, slice(fhalf, 2 * fhalf))
    loc.start(r.w_gu, r.w_gu_out)
    writes = {}
    few = piece // 2
    for n in range(rows // few):
        if n and n % 2 == 0:
            later.tick()
        at = slice(n * few, (n + 1) * few)
        left = r.normed2[at, :]
        gate, up = mm(left, w_gate), mm(left, w_up)
        sg = jax.nn.sigmoid(gate)
        for copy in writes.get(n % 2, ()):
            loc.wait(copy)
        r.act[n % 2] = (gate * sg * up).astype(bf16)
        r.fgate[n % 2] = (up * sg * (1.0 + gate * (1.0 - sg))).astype(bf16)
        r.fup[n % 2] = (gate * sg).astype(bf16)
        writes[n % 2] = [
            loc.start(src.at[n % 2], dst.at[pl.ds(n * few, few), :])
            for src, dst in ((r.act, r.act_out), (r.fgate, r.fgate_out), (r.fup, r.fup_out))
        ]
    later.finish()
    crossed["dy"].wait_recv()
    arrived(second[6:])
    last = rem.start(r.dy.at[far], r.dy.at[far], "core")
    for block in ordered:
        for k, s in enumerate(streams):
            if groups[k] == 2 and block != OWN and not route(block, s.order)[0]:
                s.wait(block)
    last.wait_recv()
    for s in streams:
        s.drain(ordered)
    rem.drain()
    loc.done()


def delta_prepare(r, h, heads, spans):
    i, j = iotas()
    mixed = []
    for which in range(3):
        value = conv_of(r.proj, r.taps, r.keep, which, h, heads)
        mixed.append(value * jax.nn.sigmoid(value))
    for which, dest in ((0, r.qs), (1, r.ks)):
        w = mixed[which]
        unit = w * lax.rsqrt(jnp.sum(w * w, axis=-1, keepdims=True) + 1e-6)
        dest[:, lanes(h)] = unit.astype(bf16)
    r.vs[:, lanes(h)] = mixed[2].astype(bf16)
    lowers, rights = [], []
    for n in range(spans):
        at = slice(n * SPAN, (n + 1) * SPAN)
        k = r.ks[at, lanes(h)]
        q = r.qs[at, lanes(h)]
        v = r.vs[at, lanes(h)]
        beta = jax.nn.sigmoid(r.logit[at, lanes(h)])
        carried, same, ending = span_masks(r.segc, r.segr, n)
        lowers.append(jnp.where(same & (i > j), beta * mm_nt(k, k), 0.0))
        r.ps[h * spans + n] = jnp.where(same & (i >= j), mm_nt(q, k), 0.0).astype(bf16)
        rights.append(
            jnp.concatenate([beta * v.astype(f32), (beta * carried) * k.astype(f32)], axis=1)
        )
    for n, inv in enumerate(unit_inverses(lowers)):
        at = slice(n * SPAN, (n + 1) * SPAN)
        small = inv.astype(bf16)
        r.ns[h * spans + n] = small
        both = rights[n] + mm(small, rights[n].astype(bf16))
        r.us[at, lanes(h)] = both[:, :HD]
        r.ws[at, lanes(h)] = both[:, HD:].astype(bf16)


def delta_chain(r, heads, spans, between):
    states = [jnp.zeros((HD, HD), f32) for _ in range(heads)]
    for n in range(spans):
        at = slice(n * SPAN, (n + 1) * SPAN)
        between()
        carried, same, ending = span_masks(r.segc, r.segr, n)
        for h in range(heads):
            head = slice(h * HD, (h + 1) * HD)
            state = states[h].astype(bf16)
            r.ss[h * spans + n] = state
            queries = (carried * r.qs[at, head].astype(f32)).astype(bf16)
            seen = mm(jnp.concatenate([r.ws[at, head], queries], axis=0), state)
            fresh = r.us[at, head] - seen[:SPAN]
            small = fresh.astype(bf16)
            r.fs[at, head] = small
            r.out[at, head] = seen[SPAN:] + mm(r.ps[h * spans + n], small)
            states[h] = carried[SPAN - 1 : SPAN, :] * states[h] + mm_tn(
                r.ks[at, head], (ending * fresh).astype(bf16)
            )


def forward(qkv, out_w, gu, dn, ext, tok, cot, flags, levels, per, heads_all):
    share = qkv.shape[1]
    width = qkv.shape[2]
    half, fhalf = width // 2, dn.shape[1] // 2
    piece = tok.shape[1]
    rows = 4 * piece
    heads = half // HD
    spans = rows // SPAN
    shards = levels * 8
    sds = jax.ShapeDtypeStruct
    wide, square = sds((rows, half), bf16), sds((heads * spans, SPAN, SPAN), bf16)
    seg = dict(
        segc=sds((rows, HD), f32),
        segr=sds((8, rows), f32),
        taps=sds((16, half), f32),
        gains=sds((8, width), f32),
        hgain=sds((8, HD), f32),
        normed=sds((rows, width), bf16),
        x=sds((4, piece, width), bf16),
        proj=sds((rows, 3 * half), bf16),
        blog=sds((rows, HD), f32),
        qs=wide, ks=wide, vs=wide, fs=wide, ws=wide, headed=wide,
        ns=square, ps=square, ss=square,
        out=sds((rows, half), f32),
        wo=sds((shards // 2, share, width), bf16),
        res=sds((rows, width), f32),
        normed2=sds((rows, width), bf16),
    )
    ins = dict(qkv=qkv, out_w=out_w, gu=gu, dn=dn, ext=ext, tok=tok, cot=cot, flags=flags)
    outs = {
        "wmix_out": sds((shards, share, 3 * half), bf16),
        "wb_out": sds((shards, share, HD), bf16),
        "w_gu_out": sds((shards, share, 2 * fhalf), bf16),
        "act_out": sds((rows, fhalf), bf16),
        "fgate_out": sds((rows, fhalf), bf16),
        "fup_out": sds((rows, fhalf), bf16),
        "w_down": sds((shards, share, fhalf), bf16),
        "dy": sds((4, piece, width), bf16),
    }
    outs.update({k + "_out": v for k, v in seg.items()})
    scratch = {k: VM(v.shape, v.dtype) for k, v in seg.items()}
    scratch.update(
        w1=VM((shards, share, 4 * half + HD), bf16),
        w_gu=VM((shards, share, 2 * fhalf), bf16),
        act=VM((2, piece // 2, fhalf), bf16),
        fgate=VM((2, piece // 2, fhalf), bf16),
        fup=VM((2, piece // 2, fhalf), bf16),
        wbeta=VM((shards, share, half), bf16),
        wb=VM((shards, share, HD), bf16),
        marks=VM((4, piece, HD), bf16),
        keep=VM((CONV - 1, rows, HD), f32),
        small=VM((32, width), f32),
        us=VM((rows, half), f32),
        logit=VM((rows, half), f32),
        mine=VM((4, piece, width), bf16),
        theirs=VM((4, piece, width), bf16),
        loc_sem=pltpu.SemaphoreType.DMA((80,)),
        send_sem=pltpu.SemaphoreType.DMA((32,)),
        recv_sem=pltpu.SemaphoreType.DMA((32,)),
    )
    for k, (a, hf, cols, order) in enumerate(STREAMS):
        sent, got = Gather.sems(levels, order)
        scratch["gs%d" % k] = pltpu.SemaphoreType.DMA((sent,))
        scratch["gr%d" % k] = pltpu.SemaphoreType.DMA((got,))
    cfg = dict(
        heads=heads, spans=spans, per=per, share=share, width=width, half=half, fhalf=fhalf,
        heads_all=heads_all, piece=piece, rows=rows,
        program=[6.0] + [2.0] * (rows // piece) + [4.0] * heads + [0.6] * spans + [1.0, 4.0]
        + [3.0] * (rows // piece),
    )
    return call(forward_kernel, ins, outs, scratch, 1, 63, levels, cfg)
SLACK_B = 4.0


def backward_kernel(r, levels, cfg):
    heads, spans, per, share = cfg["heads"], cfg["spans"], cfg["per"], cfg["share"]
    width, half, heads_all = cfg["width"], cfg["half"], cfg["heads_all"]
    piece, rows = cfg["piece"], cfg["rows"]
    pc = Place(levels)
    loc = Local(Sems(r.loc_sem))
    rem = Remote(pc, Sems(r.send_sem), Sems(r.recv_sem))
    pc.meet(NEIGHBOURS)
    pieces = rows // piece
    first_in = [
        [rem.start(r.mine_in.at[n], r.theirs.at[n], "core"), loc.start(r.mine_in.at[n], r.mine.at[n]),
         loc.start(r.res_in.at[n], r.res.at[n])]
        + [loc.start(r.dy_in.at[n, :, pl.ds(c * half, half)],
                     r.datt.at[c, pl.ds(n * piece, piece), :]) for c in range(2)]
        for n in range(pieces)
    ]
    small_in = [loc.start(a, b) for a, b in (
        (r.gains_in, r.gains), (r.hgain_in, r.hgain), (r.taps_in, r.taps), (r.segc_in, r.segc),
        (r.segr_in, r.segr), (r.headed_in, r.headed), (r.wo_in, r.wo))]
    load = [loc.start(r.g_gu_in, r.g_gu)]
    delta_in = [loc.start(a, b) for a, b in (
        (r.out_in, r.out), (r.blog_in, r.blog), (r.proj_in, r.dproj), (r.wb_in, r.wb),
        (r.qs_in, r.sv.at[0]), (r.ks_in, r.sv.at[1]), (r.vs_in, r.sv.at[2]),
        (r.fs_in, r.sv.at[3]), (r.ws_in, r.sv.at[4]),
        (r.ns_in, r.sq.at[0]), (r.ps_in, r.sq.at[1]), (r.ss_in, r.sq.at[2]))]
    streams = []
    for k, (name, h, hf, cols, order) in enumerate(RETURNS):
        grad, final = r.__dict__["g_" + name], r.__dict__["f_" + name]
        if h is not None:
            grad, final = grad.at[h], final.at[:, h]
        streams.append(
            Scatter(pc, grad, r.__dict__["room%d" % k], final, hf, span_of(cols, grad),
                    order, r.__dict__["ss%d" % k], r.__dict__["sr%d" % k])
        )

    def arrived(copies):
        for copy in copies:
            if loc.holds(copy):
                loc.wait(copy)
            else:
                copy.wait_recv()

    ordered = blocks_of(levels)[::-1]
    arrived(load)
    crossing = []
    mb = lambda n, m: 2e-6 * n * m
    groups = [
        {"gu": 0, "out": 1, "q": 2 + (h or 0), "small": 2 + heads}[name]
        for name, h, *_ in RETURNS
    ]
    steps = scatter_steps(
        streams, groups,
        [
            mb(share * (1 if s.half is not None else 2), s.cols.stop - s.cols.start)
            for s in streams
        ],
        levels,
    )
    steps.append(
        crossing_step(
            lambda: crossing.append(
                rem.start(r.lo_in.at[1 - pc.x], r.lo_out.at[pc.x], "x")
            ),
            mb(piece, width), 0, "lo",
        )
    )
    loc.start(r.lo_in.at[pc.x], r.lo_out.at[pc.x])
    start = pieces + 3 + heads + 1
    events = {pieces + 3: [1], len(cfg["program"]): [2 + heads]}
    for h in range(heads):
        events[start + h + 1] = [2 + h]
    later = Planned(plan(steps, cfg["program"], levels, {0: 0.0}, {}, SLACK_B, events)[0])
    later.tick()

    arrived(small_in)
    g1 = r.gains[1:2, :]
    gain1 = jnp.zeros((1, width), f32)
    for n in range(pieces):
        later.tick()
        arrived(first_in[n])
        v = r.res[n]
        grad = r.mine[n].astype(f32) + r.theirs[n].astype(f32)
        inv = lax.rsqrt(jnp.mean(v * v, axis=-1, keepdims=True) + 1e-5)
        scaled = grad * g1
        back = inv * scaled - v * (inv * inv * inv * jnp.mean(scaled * v, axis=-1, keepdims=True))
        at = slice(n * piece, (n + 1) * piece)
        dres = back + jnp.concatenate([r.datt[0, at, :], r.datt[1, at, :]], axis=1).astype(f32)
        ours = (pc.t == n % 2).astype(f32)
        gain1 = gain1 + ours * jnp.sum(grad * v * inv, axis=0, keepdims=True)

        def keep_own(n=n, dres=dres):
            r.res[n // 2] = dres

        pl.when(pc.t == n % 2)(keep_own)
        low = dres.astype(bf16)
        r.datt[0, at, :] = low[:, :half]
        r.datt[1, at, :] = low[:, half:]
    r.cols[...] = jnp.zeros(r.cols.shape, f32)
    r.cols[1:2, :] = gain1
    later.tick()
    wo = flat(r.wo, slice(None))
    for n in range(pieces):
        at = slice(n * piece, (n + 1) * piece)
        r.dheaded[at, :] = (
            mm_nt(r.datt[0, at, :], wo[:, :half]) + mm_nt(r.datt[1, at, :], wo[:, half:])
        ).astype(bf16)
    later.tick()
    for c in range(2):
        for n in range(half // piece):
            left = r.headed[:, n * piece : (n + 1) * piece]
            at = slice(n * piece // share, (n + 1) * piece // share)
            r.wo[at, :, c * half : (c + 1) * half] = unflat(mm_tn(left, r.datt[c]), share)

    def cut(n, t):
        return pl.ds(pl.multiple_of(t * n, n), n)

    shards = levels * 8 // 2
    ours = pl.ds(pl.multiple_of(pc.t * shards, shards), shards)
    gout = [
        loc.start(r.wo.at[:, :, cut(half, pc.t)], r.g_out.at[ours]),
        rem.start(r.wo.at[:, :, cut(half, 1 - pc.t)], r.g_out.at[ours], "core"),
    ]
    normed_in = [loc.start(r.normed_in.at[n], r.theirs.at[n]) for n in range(pieces)]

    arrived(delta_in)
    set_masks(r.segc, r.keep)
    arrived(gout)
    qs, ks, vs, fs, ws = (r.sv.at[k] for k in range(5))
    ns, ps, ss = (r.sq.at[k] for k in range(3))
    douts, xs = r.datt.at[0], r.datt.at[1]
    ys, hs, gs = r.headed, r.out, r.dheaded
    i, j = iotas()
    lane = lax.broadcasted_iota(jnp.int32, (SPAN, HD), 1)
    r.dlog[...] = jnp.zeros(r.dlog.shape, f32)

    norm_at = later.looped(heads)

    def norm_back(h, dgain_sum):
        norm_at(h)
        o = r.out[:, lanes(h)]
        dyh = r.dheaded[:, lanes(h)].astype(f32)
        inv = lax.rsqrt(jnp.mean(o * o, axis=-1, keepdims=True) + 1e-5)
        scaled = dyh * r.hgain[0:1, :]
        dout = inv * scaled - o * (inv * inv * inv * jnp.mean(scaled * o, axis=-1, keepdims=True))
        dgain_sum = dgain_sum + jnp.sum(dyh * o * inv, axis=0, keepdims=True)
        for n in range(spans):
            at = slice(n * SPAN, (n + 1) * SPAN)
            carried, same, ending = span_masks(r.segc, r.segr, n)
            small = dout[at].astype(bf16)
            douts[at, lanes(h)] = small
            x = mm_tn(ps[h * spans + n], small).astype(bf16)
            xs[at, lanes(h)] = x
            cdout = (carried * dout[at]).astype(bf16)
            hs[at, lanes(h)] = mm_tn(qs[at, lanes(h)], cdout) - mm_tn(ws[at, lanes(h)], x)
        return dgain_sum

    dgain = lax.fori_loop(0, heads, norm_back, jnp.zeros((1, HD), f32))
    grads_s = [jnp.zeros((HD, HD), f32) for _ in range(heads)]
    later.tick()
    for n in reversed(range(spans)):
        at = slice(n * SPAN, (n + 1) * SPAN)
        carried, same, ending = span_masks(r.segc, r.segr, n)
        for h in range(heads):
            head = slice(h * HD, (h + 1) * HD)
            g = grads_s[h].astype(bf16)
            gs[at, head] = g
            y = (ending * mm(ks[at, head], g)).astype(bf16)
            ys[at, head] = y
            if n:
                grads_s[h] = (
                    carried[SPAN - 1 : SPAN, :] * grads_s[h]
                    - mm_tn(ws[at, head], y)
                    + hs[at, head]
                )

    per_piece = piece // SPAN

    def spot(which, n):
        return (
            pieces // 2 + which // 2,
            slice((n % per_piece) * SPAN, (n % per_piece + 1) * SPAN),
            slice(
                ((which % 2) * pieces + n // per_piece) * HD,
                ((which % 2) * pieces + n // per_piece + 1) * HD,
            ),
        )

    def put(which, n, value):
        r.res[spot(which, n)] = value

    def taken(which):
        return jnp.concatenate([r.res[spot(which, n)] for n in range(spans)], axis=0)

    arrived(normed_in)
    pull_at = later.looped(heads)

    def pull(h, carry):
        head = lanes(h)
        pull_at(h)
        for n in range(spans):
            at = slice(n * SPAN, (n + 1) * SPAN)
            carried, same, ending = span_masks(r.segc, r.segr, n)
            which = h * spans + n
            q, k, v, f = qs[at, head], ks[at, head], vs[at, head], fs[at, head]
            state, g, p, inv = ss[which], gs[at, head], ps[which], ns[which]
            b = jax.nn.sigmoid(
                jnp.sum(jnp.where(lane == h, r.blog[at, :], 0.0), axis=-1, keepdims=True)
            )
            beta = jnp.broadcast_to(b, (SPAN, HD))
            small = douts[at, head]
            df = xs[at, head].astype(f32) + ys[at, head].astype(f32)
            z = df + mm_tn(inv, df.astype(bf16))
            zb = z.astype(bf16)
            dp = jnp.where(same & (i >= j), mm_nt(small, f), 0.0).astype(bf16)
            dl = jnp.where(same & (i > j), -mm_nt(zb, f), 0.0)
            known = v.astype(f32) - carried * mm(k, state)
            dbeta = jnp.sum(z * known + dl * mm_nt(k, k), axis=-1, keepdims=True)
            dlogit = dbeta * b * (1.0 - b)
            r.dlog[at, :] = jnp.where(
                lane == h, jnp.broadcast_to(dlogit, (SPAN, HD)), r.dlog[at, :]
            )
            e = (beta * dl).astype(bf16)
            put(0, n, carried * mm_nt(small, state) + mm(dp, k))
            put(2, n, beta * z)
            put(1, n, (
                mm(e, k)
                + mm_tn(e, k)
                + mm_tn(dp, q)
                - (carried * beta) * mm_nt(zb, state)
                + ending * mm_nt(f, g)
            ))
        for which in range(3):
            c = conv_of(r.dproj, r.taps, r.keep, which, h, heads)
            s = jax.nn.sigmoid(c)
            d = taken(which)
            if which < 2:
                w = c * s
                n = lax.rsqrt(jnp.sum(w * w, axis=-1, keepdims=True) + 1e-6)
                d = n * d - w * (n * n * n * jnp.sum(w * d, axis=-1, keepdims=True))
            dc = d * (s * (1.0 + c * (1.0 - s)))
            at = lanes(which * heads + h)
            value = r.dproj[:, at].astype(f32)
            total = None
            for o in range(CONV):
                row = which * CONV + CONV - 1 - o
                tap = r.taps[pl.ds(row, 1), lanes(h)]
                r.dtaps[pl.ds(row, 1), lanes(h)] = jnp.sum(
                    dc * shifted(value, r.keep, o), axis=0, keepdims=True
                )
                if o == 0:
                    total = tap * dc
                else:
                    total = total + tap * pltpu.roll(dc * r.keep[o - 1], rows - o, 0)
            r.dproj[:, at] = total.astype(bf16)
        grads = jnp.concatenate(
            [r.dproj[:, lanes(which * heads + h)] for which in range(3)], axis=1
        )
        for n in range(width // piece):
            left = r.theirs[:, :, n * piece : (n + 1) * piece].reshape(rows, piece)
            at = slice(n * piece // share, (n + 1) * piece // share)
            r.g_q[h, at] = unflat(mm_tn(left, grads), share)
        return carry

    lax.fori_loop(0, heads, pull, 0)

    weights_in = [
        loc.start(r.wmix_in.at[:, pl.ds(k * half, half)], r.sv.at[k]) for k in range(3)
    ]
    arrived(weights_in)

    def partial(which, at):
        n = which
        where = pl.ds(pl.multiple_of(n * piece, piece), piece)
        total = mm_nt(r.dlog[where, :].astype(bf16), r.wb[...])
        for k in range(3):
            total = total + mm_nt(r.dproj[where, k * half : (k + 1) * half], r.sv[k])
        r.mine[at] = total.astype(bf16)

    sent = []
    later.tick()
    for k in range(pieces // 2):
        partial(2 * k + 1 - pc.t, 2 + k)
        sent.append(rem.start(r.mine.at[2 + k], r.theirs3.at[k], "core"))
    later.tick()
    for k in range(pieces // 2):
        partial(2 * k + pc.t, k)
    right = r.dlog[...].astype(bf16)
    g_beta = jnp.concatenate(
        [
            mm_tn(
                r.theirs[:, :, n * piece : (n + 1) * piece].reshape(rows, piece), right
            ).astype(bf16)
            for n in range(width // piece)
        ],
        axis=0,
    )
    x_in = [
        loc.start(r.x_in.at[2 * k + pc.t], r.theirs.at[2 + k]) for k in range(pieces // 2)
    ]

    later.tick()
    arrived(x_in)
    g0 = r.gains[0:1, :]
    gain0 = jnp.zeros((1, width), f32)
    for k in range(pieces // 2):
        sent[k].wait_recv()
        v = r.theirs[2 + k].astype(f32)
        grad = r.mine[k].astype(f32) + r.theirs3[k].astype(f32)
        inv = lax.rsqrt(jnp.mean(v * v, axis=-1, keepdims=True) + 1e-5)
        scaled = grad * g0
        back = inv * scaled - v * (inv * inv * inv * jnp.mean(scaled * v, axis=-1, keepdims=True))
        gain0 = gain0 + jnp.sum(grad * v * inv, axis=0, keepdims=True)
        r.theirs[k] = (back + r.res[k]).astype(bf16)
    crossing.append(rem.start(r.theirs.at[1 - pc.x], r.dx_out.at[pc.x], "x"))
    loc.start(r.theirs.at[pc.x], r.dx_out.at[pc.x])
    r.cols[0:1, :] = gain0
    r.cols[2 : 2 + 3 * CONV, cut(half, pc.t)] = r.dtaps[0 : 3 * CONV, :]
    place_r = lax.broadcasted_iota(jnp.int32, (HD, width), 0)
    place_c = lax.broadcasted_iota(jnp.int32, (HD, width), 1)
    spread = ((place_c // share * per + place_c % share == place_r) & (place_c % share < per)).astype(bf16)
    at = 2 + 3 * CONV + heads_all
    r.cols[at : at + 1, :] = mm(jnp.broadcast_to(dgain, (8, HD)).astype(bf16), spread)[0:1, :]
    pick_r = lax.broadcasted_iota(jnp.int32, (HD, HD), 0)
    pick_c = lax.broadcasted_iota(jnp.int32, (HD, HD), 1)
    chosen = ((pick_c == 2 + 3 * CONV + heads * pc.t + pick_r) & (pick_r < heads)).astype(bf16)
    beta = mm(g_beta, chosen)
    for n in range(width // SPAN):
        at = n * SPAN
        rows_in = jnp.concatenate(
            [r.cols[:, at : at + SPAN], jnp.zeros((HD - 32, SPAN), f32)], axis=0
        )
        block = jnp.transpose(rows_in) + beta[at : at + SPAN]
        r.g_small[at // share : (at + SPAN) // share] = unflat(block, share)
    later.finish()
    for s in streams:
        s.finish()
    for name in ("gu", "out", "q", "small"):
        src, dst = r.__dict__["f_" + name], r.__dict__["o_" + name]
        loc.start(src.at[pc.t], dst.at[pc.t])
        crossing.append(rem.start(src.at[1 - pc.t], dst.at[pc.t], "core"))
    for copy in crossing:
        copy.wait_recv()
    for s in streams:
        s.drain(ordered)
    rem.drain()
    loc.done()


RETURNS = (
    ("gu", None, 0, None, "zxy"),
    ("gu", None, 1, (0, 14), "zyx"),
    ("gu", None, 1, (14, None), "xyz"),
    ("out", None, None, None, "zyx"),
    ("q", 0, None, None, "zxy"),
    ("q", 1, None, None, "zyx"),
    ("q", 2, None, None, "zxy"),
    ("q", 3, None, None, "zyx"),
    ("small", None, None, None, "zxy"),
)


def backward(f, mine, g_gu, lo, levels, per, heads_all):
    width = f["normed_out"].shape[1]
    rows = f["normed_out"].shape[0]
    half = f["out_out"].shape[1]
    piece = rows // 4
    share = f["wo_out"].shape[1]
    heads = half // HD
    spans = rows // SPAN
    shards = levels * 8
    sds = jax.ShapeDtypeStruct
    ins = dict(
        mine_in=mine,
        res_in=f["res_out"].reshape(4, piece, width),
        dy_in=f["dy"],
        x_in=f["x_out"],
        gains_in=f["gains_out"], hgain_in=f["hgain_out"], taps_in=f["taps_out"],
        segc_in=f["segc_out"], segr_in=f["segr_out"], headed_in=f["headed_out"],
        wo_in=f["wo_out"], out_in=f["out_out"], blog_in=f["blog_out"], proj_in=f["proj_out"],
        normed_in=f["normed_out"].reshape(4, piece, width), wmix_in=f["wmix_out"].reshape(width, 3 * half),
        wb_in=f["wb_out"].reshape(width, HD),
        g_gu_in=g_gu, lo_in=lo,
    )
    ins.update({k + "_in": f[k + "_out"] for k in ("qs", "ks", "vs", "fs", "ws", "ns", "ps", "ss")})
    cols = dict(gu=(g_gu.shape[2],), out=(half,), q=(3 * HD,), small=(HD,))
    tops = dict(gu=(2,), out=(2,), q=(2, heads), small=(2,))
    outs = dict(
        dx_out=sds((2, piece, width), bf16),
        lo_out=sds((2, piece, width), bf16),
        **{"o_" + n: sds(tops[n] + (share,) + cols[n], f32) for n in cols},
    )
    scratch = dict(
        mine=VM((4, piece, width), bf16),
        theirs=VM((4, piece, width), bf16),
        theirs3=VM((2, piece, width), bf16),
        res=VM((4, piece, width), f32),
        gains=VM((8, width), f32),
        hgain=VM((8, HD), f32),
        taps=VM((16, half), f32),
        dtaps=VM((16, half), f32),
        segc=VM((rows, HD), f32),
        segr=VM((8, rows), f32),
        headed=VM((rows, half), bf16),
        wo=VM((shards // 2, share, width), bf16),
        datt=VM((2, rows, half), bf16),
        cols=VM((32, width), f32),
        g_out=VM((shards, share, half), bf16),
        g_q=VM((heads, shards, share, 3 * HD), bf16),
        g_small=VM((shards, share, HD), bf16),
        dheaded=VM((rows, half), bf16),
        sv=VM((5, rows, half), bf16),
        sq=VM((3, heads * spans, SPAN, SPAN), bf16),
        out=VM((rows, half), f32),
        blog=VM((rows, HD), f32),
        dproj=VM((rows, 3 * half), bf16),
        dlog=VM((rows, HD), f32),
        wb=VM((width, HD), bf16),
        keep=VM((CONV - 1, rows, HD), f32),
        g_gu=VM(g_gu.shape, bf16),
        **{"f_" + n: VM(tops[n] + (share,) + cols[n], f32) for n in cols},
        loc_sem=pltpu.SemaphoreType.DMA((64,)),
        send_sem=pltpu.SemaphoreType.DMA((16,)),
        recv_sem=pltpu.SemaphoreType.DMA((16,)),
    )
    for k, (name, h, hf, tiles, order) in enumerate(RETURNS):
        slots, sent = Scatter.slots_of(levels, order)
        first, last = span_of(tiles, sds((1, 1) + cols[name], bf16))
        both = () if hf is not None else (2,)
        scratch["room%d" % k] = VM((slots,) + both + (share, last - first), bf16)
        scratch["ss%d" % k] = pltpu.SemaphoreType.DMA((sent,))
        scratch["sr%d" % k] = pltpu.SemaphoreType.DMA((slots,))
    cfg = dict(
        heads=heads, spans=spans, per=per, share=share, width=width, half=half,
        heads_all=heads_all, piece=piece, rows=rows,
        program=[4.0] + [1.5] * 4 + [3.0, 4.0] + [2.5] * heads + [5.0]
        + [7.0] * heads + [2.5] * 2 + [3.0],
    )
    return call(backward_kernel, ins, outs, scratch, 2, 63, levels, cfg)
SLACK_M = 2.0


MIDDLE = (
    (2, 0, None, "zxy"),
    (2, 1, None, "zyx"),
)


def middle_kernel(r, levels, cfg):
    share, width, fhalf = cfg["share"], cfg["width"], cfg["fhalf"]
    piece, rows = cfg["piece"], cfg["rows"]
    pieces = rows // piece
    pc = Place(levels)
    loc = Local(Sems(r.loc_sem))
    rem = Remote(pc, Sems(r.send_sem), Sems(r.recv_sem))
    loads = [
        [loc.start(a, b) for a, b in group]
        for group in (
            ((r.dy_in, r.dy), (r.act_in, r.act)),
            ((r.w_down_in, r.w_down),),
            ((r.fgate_in, r.fgate), (r.fup_in, r.fup)),
            ((r.normed2_in, r.normed2), (r.w_gu_in, r.w_gu)),
        )
    ]

    def loaded(k):
        for copy in loads[k]:
            loc.wait(copy)

    pc.meet(NEIGHBOURS)
    streams = [
        Scatter(pc, r.g_down, r.__dict__["room%d" % k], r.f_down, hf, span_of(cols, r.g_down),
                order, r.__dict__["ss%d" % k], r.__dict__["sr%d" % k])
        for k, (a, hf, cols, order) in enumerate(MIDDLE)
    ]
    mb = lambda n, m: 2e-6 * n * m
    steps = scatter_steps(
        streams, [0] * len(streams),
        [mb(share, s.cols.stop - s.cols.start) for s in streams], levels,
    )
    later = Planned(plan(steps, cfg["program"], levels, {0: 0.0}, {}, SLACK_M)[0])
    ordered = blocks_of(levels)

    loaded(0)
    dy = r.dy[...].reshape(rows, width)
    strip = width // 4
    for n in range(4):
        at = slice(n * strip // share, (n + 1) * strip // share)
        r.g_down[at] = unflat(
            mm_tn(dy[:, n * strip : (n + 1) * strip], r.act[...]), share
        )
    later.tick()

    loaded(1)
    w_down = flat(r.w_down, slice(None))
    sent = []
    for k in range(pieces // 2):
        which = 2 * k + 1 - pc.t
        at = pl.ds(pl.multiple_of(which * piece, piece), piece)
        r.mine[2 + k] = mm_nt(r.act[at, :], w_down).astype(bf16)
        sent.append(rem.start(r.mine.at[2 + k], r.theirs.at[k], "core"))
    later.tick()
    residuals = []
    for k in range(pieces // 2):
        which = 2 * k + pc.t
        at = pl.ds(pl.multiple_of(which * piece, piece), piece)
        residuals.append(loc.start(r.res_in.at[which], r.res.at[k]))
        r.mine[k] = mm_nt(r.act[at, :], w_down).astype(bf16)
    loaded(2)
    for n in range(pieces):
        later.tick()
        at = slice(n * piece, (n + 1) * piece)
        dact = mm(r.dy[n], w_down)
        r.dgu[at, :fhalf] = (dact * r.fgate[at, :].astype(f32)).astype(bf16)
        r.dgu[at, fhalf:] = (dact * r.fup[at, :].astype(f32)).astype(bf16)
    later.tick()
    for k in range(pieces // 2):
        sent[k].wait_recv()
        loc.wait(residuals[k])
        r.mine[k] = (
            r.res[k] + r.mine[k].astype(f32) + r.theirs[k].astype(f32)
        ).astype(bf16)
        loc.start(r.mine.at[k], r.result.at[k])

    loaded(3)
    w_gu = flat(r.w_gu, slice(None))
    for n in range(pieces):
        later.tick()
        at = slice(n * piece, (n + 1) * piece)
        r.part[n] = mm_nt(r.dgu[at, :], w_gu).astype(bf16)
        loc.start(r.part.at[n], r.part_out.at[n])
    for n in range(4):
        later.tick()
        at = slice(n * strip // share, (n + 1) * strip // share)
        r.ggu[n % 2] = unflat(mm_tn(r.normed2[:, n * strip : (n + 1) * strip], r.dgu[...]), share)
        loc.wait(loc.start(r.ggu.at[n % 2], r.ggu_out.at[pl.ds(at.start, strip // share)]))
    later.finish()
    for s in streams:
        s.finish()
    loc.start(r.f_down.at[pc.t], r.o_down.at[pc.t])
    last = rem.start(r.f_down.at[1 - pc.t], r.o_down.at[pc.t], "core")
    last.wait_recv()
    for s in streams:
        s.drain(ordered)
    rem.drain()
    loc.done()


def middle(f, levels):
    shards, share, two = f["w_gu_out"].shape
    fhalf = two // 2
    rows, width = f["normed2_out"].shape
    piece = rows // 4
    sds = jax.ShapeDtypeStruct
    ins = dict(
        dy_in=f["dy"], act_in=f["act_out"], w_down_in=f["w_down"], fgate_in=f["fgate_out"],
        fup_in=f["fup_out"], normed2_in=f["normed2_out"], w_gu_in=f["w_gu_out"],
        res_in=f["res_out"].reshape(4, piece, width),
    )
    outs = dict(
        ggu_out=sds((shards, share, two), bf16),
        part_out=sds((4, piece, width), bf16),
        result=sds((2, piece, width), bf16),
        o_down=sds((2, share, fhalf), f32),
    )
    scratch = dict(
        dy=VM((4, piece, width), bf16),
        act=VM((rows, fhalf), bf16),
        w_down=VM((shards, share, fhalf), bf16),
        fgate=VM((rows, fhalf), bf16),
        fup=VM((rows, fhalf), bf16),
        normed2=VM((rows, width), bf16),
        w_gu=VM((shards, share, two), bf16),
        res=VM((2, piece, width), f32),
        mine=VM((4, piece, width), bf16),
        theirs=VM((2, piece, width), bf16),
        part=VM((4, piece, width), bf16),
        dgu=VM((rows, two), bf16),
        g_down=VM((shards, share, fhalf), bf16),
        f_down=VM((2, share, fhalf), f32),
        ggu=VM((2, shards // 4, share, two), bf16),
        loc_sem=pltpu.SemaphoreType.DMA((40,)),
        send_sem=pltpu.SemaphoreType.DMA((8,)),
        recv_sem=pltpu.SemaphoreType.DMA((8,)),
    )
    for k, (a, hf, cols, order) in enumerate(MIDDLE):
        slots, sent = Scatter.slots_of(levels, order)
        first, last = span_of(cols, f["w_down"])
        scratch["room%d" % k] = VM((slots, share, last - first), bf16)
        scratch["ss%d" % k] = pltpu.SemaphoreType.DMA((sent,))
        scratch["sr%d" % k] = pltpu.SemaphoreType.DMA((slots,))
    cfg = dict(
        share=share, width=width, fhalf=fhalf, piece=piece, rows=rows,
        program=[2.5, 2.5] + [1.0] * 4 + [2.0] + [1.8] * 4 + [1.8] * 4,
    )
    return call(middle_kernel, ins, outs, scratch, 4, 63, levels, cfg)


def body(tokens, cotangent, starts, norm_gain, qkv_weight, conv_weight, beta_weight,
         head_gain, out_weight, gate_up_weight, down_weight):
    levels = lax.axis_size("dp") // 2
    ctx = lax.axis_size("ctx")
    device = lax.axis_index("dp") * ctx + lax.axis_index("ctx")
    t = lax.axis_index("ctx") % 2
    m = lax.axis_index("ctx") // 2
    batches, _, piece, width = tokens.shape
    rows = ctx * piece
    share = qkv_weight.shape[1]
    hidden = gate_up_weight.shape[2]
    half, fhalf = width // 2, hidden // 2
    heads_all = beta_weight.shape[1]
    heads = heads_all // 2
    per = head_gain.shape[0]
    small = 2 + 3 * CONV + heads_all + 1

    gain_rows = jnp.zeros((share, 1), bf16).at[:per, 0].set(head_gain)
    ext = jnp.concatenate(
        [norm_gain.T, conv_weight.T, beta_weight, gain_rows, jnp.zeros((share, HD - small), bf16)],
        axis=1,
    )
    flags = jnp.broadcast_to(
        starts.reshape(batches, piece, 1).astype(bf16), (batches, piece, HD)
    )
    f = forward(
        qkv_weight, out_weight, gate_up_weight, down_weight, ext,
        tokens[:, 0], cotangent[:, 0], flags, levels, per, heads_all,
    )
    g = middle(f, levels)
    b = backward(f, g["part_out"], g["ggu_out"], g["result"], levels, per, heads_all)
    join = lambda o, n: jnp.moveaxis(o.reshape(2, share, n, -1), (2, 1), (0, 1)).reshape(n, share, -1)
    o_small = jnp.sum(b["o_small"], axis=0)
    o_q = b["o_q"].reshape(2, half // HD, share, 3, HD)
    return (
        b["lo_out"][:, None],
        b["dx_out"][:, None],
        o_small[:, 0:2].T,
        jnp.transpose(o_q, (3, 2, 0, 1, 4)).reshape(3, share, width),
        o_small[:, 2 : 2 + 3 * CONV].T,
        o_small[:, 2 + 3 * CONV : 2 + 3 * CONV + heads_all],
        o_small[:per, small - 1],
        join(b["o_out"], 1)[0],
        join(b["o_gu"], 2),
        join(g["o_down"], 1)[0],
    )


def solution(mesh):
    both = ("dp", "ctx")
    acts = P(None, "dp", "ctx", None)
    return jax.shard_map(
        body,
        mesh=mesh,
        in_specs=(
            acts,
            acts,
            P(None, "dp", "ctx"),
            P(None, both),
            P(None, both, None),
            P(None, both),
            P(both, None),
            P(both),
            P(both, None),
            P(None, both, None),
            P(both, None),
        ),
        out_specs=(
            acts,
            acts,
            P(None, both),
            P(None, both, None),
            P(None, both),
            P(both, None),
            P(both),
            P(both, None),
            P(None, both, None),
            P(both, None),
        ),
        check_vma=False,
    )
```

```python
import functools

import jax
import jax.numpy as jnp
from jax import lax
from jax.experimental import pallas as pl
from jax.experimental.pallas import tpu as pltpu
from jax.sharding import PartitionSpec as P

MESH = pl.DeviceIdType.MESH
ANY = pl.ANY
VM = pltpu.VMEM
MIB = 1 << 20
f32 = jnp.float32
bf16 = jnp.bfloat16


def route(block, order):
    dz, fx, fy = block
    rank = {dim: place for place, dim in enumerate(order)}
    last = max([-1] + [rank[d] for d, on in (("z", dz), ("x", fx), ("y", fy)) if on])
    hops = []
    for dim in order:
        if dim == "z":
            if dz == 0 and rank["z"] > last:
                hops += ["up", "dn"]
            elif dz != 0 and last == rank["z"]:
                hops.append("up" if dz < 0 else "dn")
        elif rank[dim] > last:
            hops.append(dim)
    came = None
    if last >= 0:
        came = order[last]
        if came == "z":
            came = "up" if dz < 0 else "dn"
    return hops, came


def blocks_of(levels):
    named = [
        (dz, fx, fy)
        for dz in range(1 - levels, levels)
        for fx in (0, 1)
        for fy in (0, 1)
    ]
    return sorted(named, key=lambda b: (abs(b[0]) + b[1] + b[2], abs(b[0]), b))


class Place:
    def __init__(self, levels):
        i = lax.axis_index("dp")
        c = lax.axis_index("ctx")
        self.levels = levels
        self.i, self.c = i, c
        self.z, self.y = i // 2, i % 2
        self.x, self.t = c // 2, c % 2

    def device(self, hop):
        i, c = self.i, self.c
        if hop == "x":
            return {"dp": i, "ctx": (1 - self.x) * 2 + self.t}
        if hop == "y":
            return {"dp": self.z * 2 + 1 - self.y, "ctx": c}
        if hop == "up":
            return {"dp": i + 2, "ctx": c}
        if hop == "dn":
            return {"dp": i - 2, "ctx": c}
        return {"dp": i, "ctx": self.x * 2 + 1 - self.t}

    def valid(self, block, hop=None):
        dz = block[0]
        terms = []
        if dz > 0:
            terms.append(self.z + dz < self.levels)
        if dz < 0:
            terms.append(self.z + dz >= 0)
        if hop == "up" and dz <= 0:
            terms.append(self.z + 1 < self.levels)
        if hop == "dn" and dz >= 0:
            terms.append(self.z >= 1)
        if not terms:
            return None
        return functools.reduce(jnp.logical_and, terms)

    def level(self, block):
        return self.z + block[0]

    def shard(self, block, half):
        z = self.z + block[0]
        y = 1 - self.y if block[2] else self.y
        x = 1 - self.x if block[1] else self.x
        chip = (z * 2 + y) * 2 + x
        if half is None:
            return pl.ds(chip * 2, 2)
        return chip * 2 + half

    def meet(self, hops):
        barrier = pltpu.get_barrier_semaphore()
        count = 0
        for hop in hops:
            def greet(hop=hop):
                pl.semaphore_signal(
                    barrier, inc=1, device_id=self.device(hop), device_id_type=MESH
                )
            if hop in ("up", "dn"):
                here = (self.z + 1 < self.levels) if hop == "up" else (self.z >= 1)
                pl.when(here)(greet)
                count = count + here.astype(jnp.int32)
            else:
                greet()
                count = count + 1
        pl.semaphore_wait(barrier, count)


def when(condition, action):
    if condition is None:
        action()
    else:
        pl.when(condition)(action)


def send_slots(order):
    table = {}
    for fx in (0, 1):
        for fy in (0, 1):
            for dz in (-1, 0, 1):
                for hop in route((dz, fx, fy), order)[0]:
                    table.setdefault((hop, fx, fy), len(table))
    return table


class Gather:
    def __init__(self, place, ref, half, cols, order, send_sem, recv_sem):
        self.place, self.ref, self.half = place, ref, half
        self.cols = slice(*cols)
        self.order = order
        self.slots = send_slots(order)
        self.send_sem, self.recv_sem = send_sem, recv_sem

    @staticmethod
    def sems(levels, order):
        return len(send_slots(order)) * levels, 4 * levels

    def copy(self, block, hop):
        place = self.place
        dz, fx, fy = block
        where = place.shard(block, self.half)
        level = place.level(block)
        there = (fx ^ (hop == "x"), fy ^ (hop == "y"))
        return pltpu.make_async_remote_copy(
            src_ref=self.ref.at[where, :, self.cols],
            dst_ref=self.ref.at[where, :, self.cols],
            send_sem=self.send_sem.at[self.slots[hop, fx, fy] * place.levels + level],
            recv_sem=self.recv_sem.at[(there[0] * 2 + there[1]) * place.levels + level],
            device_id=place.device(hop),
            device_id_type=MESH,
        )

    def arrival(self, block):
        place = self.place
        dz, fx, fy = block
        where = place.shard(block, self.half)
        came = route(block, self.order)[1]
        back = {"up": "dn", "dn": "up"}.get(came, came)
        return pltpu.make_async_remote_copy(
            src_ref=self.ref.at[where, :, self.cols],
            dst_ref=self.ref.at[where, :, self.cols],
            send_sem=self.send_sem.at[0],
            recv_sem=self.recv_sem.at[(fx * 2 + fy) * place.levels + place.level(block)],
            device_id=place.device(back),
            device_id_type=MESH,
        )

    def wait(self, block):
        when(self.place.valid(block), lambda: self.arrival(block).wait_recv())

    def pass_on(self, block, only=("x", "y", "up", "dn")):
        for hop in route(block, self.order)[0]:
            if hop not in only:
                continue
            when(self.place.valid(block, hop), lambda hop=hop: self.copy(block, hop).start())

    def drain(self, blocks):
        for block in blocks:
            for hop in route(block, self.order)[0]:
                when(
                    self.place.valid(block, hop),
                    lambda hop=hop: self.copy(block, hop).wait_send(),
                )


def room_table(order, levels):
    table, used = {}, 0
    for fx in (0, 1):
        for fy in (0, 1):
            here = route((0, fx, fy), order)[0]
            away = route((1, fx, fy), order)[0] + route((-1, fx, fy), order)[0]
            for hop in ("x", "y"):
                if hop in here or hop in away:
                    table[hop, fx, fy] = (used, hop in away)
                    used += levels if hop in away else 1
            if "up" in here + away or "dn" in here + away:
                table["z", fx, fy] = (used, True)
                used += levels + 1
    return table, used


class Scatter:
    def __init__(self, place, ref, room, final, half, cols, order, send_sem, recv_sem):
        self.place, self.ref, self.room, self.final = place, ref, room, final
        self.half, self.order = half, order
        self.cols = slice(*cols)
        self.table = room_table(order, place.levels)[0]
        self.send_sem, self.recv_sem = send_sem, recv_sem

    @staticmethod
    def slots_of(levels, order):
        return room_table(order, levels)[1], 4 * levels

    def slot_at(self, hop, dz, fx, fy, level):
        base, many = self.table["z" if hop in ("up", "dn") else hop, fx, fy]
        if hop == "dn" and dz == 0:
            return base + self.place.levels + 0 * self.place.z
        return base + level if many else base + 0 * self.place.z

    def slot(self, block, hop):
        return self.slot_at(hop, *block, self.place.level(block))

    def copy(self, block, src):
        place = self.place
        dz, fx, fy = block
        came = route(block, self.order)[1]
        back = {"up": "dn", "dn": "up"}.get(came, came)
        there = (
            dz + (came == "up") - (came == "dn"),
            fx ^ (came == "x"),
            fy ^ (came == "y"),
        )
        slot = self.slot_at(came, *there, place.level(block))
        return pltpu.make_async_remote_copy(
            src_ref=src,
            dst_ref=self.room.at[slot],
            send_sem=self.send_sem.at[(fx * 2 + fy) * place.levels + place.level(block)],
            recv_sem=self.recv_sem.at[slot],
            device_id=place.device(back),
            device_id_type=MESH,
        )

    def arrive(self, block, hop):
        slot = self.slot(block, hop)
        pltpu.make_async_remote_copy(
            src_ref=self.room.at[slot],
            dst_ref=self.room.at[slot],
            send_sem=self.send_sem.at[0],
            recv_sem=self.recv_sem.at[slot],
            device_id=self.place.device(hop),
            device_id_type=MESH,
        ).wait_recv()

    def in_room(self, slot, at):
        return (slot, at) if self.half is not None else (slot, slice(None), at)

    def in_final(self, at):
        return (slice(None) if self.half is None else self.half, at, self.cols)

    def total(self, block, hops, put):
        where = self.place.shard(block, self.half)
        slots = [self.slot(block, hop) for hop in hops]
        rows = self.ref.shape[1]
        step = min(16, rows)

        def one(k, carry):
            at = pl.ds(pl.multiple_of(k * step, step), step)
            value = self.ref[where, at, self.cols].astype(f32)
            for slot in slots:
                value = value + self.room[self.in_room(slot, at)].astype(f32)
            put(at, value)
            return carry

        lax.fori_loop(0, rows // step, one, 0)

    def branch(self, maybe, using, go):
        if not maybe:
            go(using)
            return
        hop, place = maybe[0], self.place
        here = place.z + 1 < place.levels if hop == "up" else place.z >= 1
        pl.when(here)(lambda: self.branch(maybe[1:], using + [hop], go))
        pl.when(jnp.logical_not(here))(lambda: self.branch(maybe[1:], using, go))

    def forward(self, block):
        place = self.place
        hops = route(block, self.order)[0]
        sure = [h for h in hops if h in ("x", "y")]
        maybe = [h for h in hops if h not in ("x", "y")]

        def go(using):
            for hop in using:
                self.arrive(block, hop)
            if not using:
                self.copy(block, self.ref.at[place.shard(block, self.half), :, self.cols]).start()
                return
            slot = self.slot(block, using[0])

            def put(at, value):
                self.room[self.in_room(slot, at)] = value.astype(bf16)

            self.total(block, using, put)
            self.copy(block, self.room.at[slot]).start()

        def both():
            self.branch(maybe, sure, go)

        when(place.valid(block), both)

    def finish(self):
        own = (0, 0, 0)
        place = self.place
        hops = route(own, self.order)[0]
        sure = [h for h in hops if h in ("x", "y")]
        for hop in sure:
            self.arrive(own, hop)

        def put(at, value):
            self.final[self.in_final(at)] = value

        self.total(own, sure, put)
        for hop in hops:
            if hop in sure:
                continue

            def add(hop=hop):
                self.arrive(own, hop)
                slot = self.slot(own, hop)
                every = self.in_final(slice(None))
                self.final[every] = self.final[every] + self.room[slot].astype(f32)

            when(place.valid(own, hop), add)

    def drain(self, blocks):
        for block in blocks:
            if block == (0, 0, 0):
                continue
            when(
                self.place.valid(block),
                lambda block=block: self.copy(
                    block, self.ref.at[self.place.shard(block, self.half), :, self.cols]
                ).wait_send(),
            )


OWN = (0, 0, 0)

RATE = 0.038
LATE = 2
HOP = 1.6


class Step:
    def __init__(self, run, valid, needs, sends, cost, group, rank):
        self.run, self.valid, self.needs, self.sends = run, valid, needs, sends
        self.cost, self.group, self.rank = cost, group, rank


def exists(block, z, levels):
    return 0 <= z + block[0] < levels


def can_hop(z, hop, levels):
    return {"up": z + 1 < levels, "dn": z >= 1}.get(hop, True)


def moved(block, hop):
    dz, fx, fy = block
    return (dz - (hop == "up") + (hop == "dn"), fx ^ (hop == "x"), fy ^ (hop == "y"))


def level_of(z, hop):
    return z + (hop == "up") - (hop == "dn")


def height(block, order, levels):
    if abs(block[0]) >= levels:
        return -1
    return max([0] + [1 + height(moved(block, h), order, levels) for h in route(block, order)[0]])


def crossing_step(run, size, group, key):
    return Step(
        run, lambda z: True, lambda z: [("own", group)], lambda z: [("x", size, (key, z))],
        0.2, group, 0,
    )


def gather_steps(streams, group_of, size_of, levels, begin=None):
    steps = []
    for k, s in enumerate(streams):
        for block in blocks_of(levels):
            seen = []
            for ways in (("up", "dn"), ("x",), ("y",)):
                hops = [h for h in route(block, s.order)[0] if h in ways]
                if not hops:
                    continue

                def needs(z, k=k, block=block):
                    return [("own", group_of[k])] if block == OWN else [(k, z, block)]

                def sends(z, k=k, block=block, hops=hops):
                    return [
                        (h, size_of[k], (k, level_of(z, h), moved(block, h)))
                        for h in hops
                        if can_hop(z, h, levels)
                    ]

                def run(s=s, k=k, block=block, ways=ways, seen=seen):
                    if not seen:
                        seen.append(True)
                        if block != OWN:
                            s.wait(block)
                        else:
                            begin(group_of[k])
                    s.pass_on(block, ways)

                lane = group_of[k]
                if s.order[0] != "z":
                    lane = LATE if "up" in ways else 0
                steps.append(
                    Step(
                        run,
                        lambda z, block=block: exists(block, z, levels),
                        needs,
                        sends,
                        0.15,
                        lane,
                        -max(1 + height(moved(block, h), s.order, levels) for h in hops),
                    )
                )
    return steps


def scatter_steps(streams, group_of, size_of, levels):
    steps = []
    for k, s in enumerate(streams):
        for block in blocks_of(levels)[::-1]:
            if block == OWN:
                continue
            hops, came = route(block, s.order)
            back = {"up": "dn", "dn": "up"}.get(came, came)

            def needs(z, k=k, block=block, hops=hops):
                got = [(k, z, block, h) for h in hops if can_hop(z, h, levels)]
                return got or [("own", group_of[k])]

            def sends(z, k=k, block=block, came=came, back=back):
                there = moved(block, back)
                return [(back, size_of[k], (k, level_of(z, back), there, came))]

            steps.append(
                Step(
                    lambda s=s, block=block: s.forward(block),
                    lambda z, block=block: exists(block, z, levels),
                    needs,
                    sends,
                    0.15 + (1.5 * size_of[k] if hops else 0.0),
                    group_of[k],
                    -abs(block[0]) - block[1] - block[2],
                )
            )
    return steps


def plan(steps, program, levels, own, gates, slack=0.0, events=None):
    now = [0.0] * levels
    free = [dict(x=0.0, y=0.0, up=0.0, dn=0.0) for _ in range(levels)]
    there = {("own", g): at for g, at in own.items()}
    left = list(steps)
    out = []

    def ready(step):
        times = []
        for z in range(levels):
            if not step.valid(z):
                continue
            for key in step.needs(z):
                if key not in there:
                    return None
                times.append((there[key], now[z]))
        return times

    def do(step):
        for z in range(levels):
            if not step.valid(z):
                continue
            now[z] = max([now[z]] + [there[key] for key in step.needs(z)]) + step.cost
        for z in range(levels):
            if not step.valid(z):
                continue
            for hop, size, key in step.sends(z):
                begin = max(now[z], free[z][hop])
                free[z][hop] = begin + size / RATE
                there[key] = free[z][hop] + HOP
        left.remove(step)

    def quick(step):
        times = ready(step)
        return times is not None and all(at + slack <= when + 0.3 for at, when in times)

    def drain_ready(batch, held):
        while True:
            able = [s for s in left if s.group not in held and quick(s)]
            if not able:
                return
            step = min(able, key=lambda s: (s.group, s.rank))
            do(step)
            batch.append(step)

    def wait_for(step):
        return max([max(at - when, 0.0) for at, when in ready(step)] + [0.0])

    def until(batch, done):
        while left and not done():
            able = [s for s in left if ready(s) is not None]
            if not able:
                return
            first = min(s.group for s in able)

            def idle(s):
                return all(
                    free[z][hop] <= now[z] + 1.0
                    for z in range(levels)
                    if s.valid(z)
                    for hop, _, _ in s.sends(z)
                )

            pool = [s for s in able if s.group == first or idle(s)]
            step = min(pool, key=lambda s: (round(wait_for(s), 1), s.group, s.rank))
            do(step)
            batch.append(step)

    for place, duration in enumerate(program):
        batch = []
        for group in (events or {}).get(place, ()):
            there["own", group] = max(now)
        keys = gates.get(place)
        if keys:
            until(batch, lambda: all(k in there for z in range(levels) for k in keys(z)))
            limit = [max(there[k] for k in keys(z)) for z in range(levels)]
            while True:
                able = [
                    s
                    for s in left
                    if ready(s) is not None
                    and all(
                        max(now[z], *(there[k] for k in s.needs(z))) + s.cost <= limit[z]
                        for z in range(levels)
                        if s.valid(z)
                    )
                ]
                if not able:
                    break
                step = min(able, key=lambda s: (round(wait_for(s), 1), s.group, s.rank))
                do(step)
                batch.append(step)
            for z in range(levels):
                now[z] = max(now[z], limit[z])
        drain_ready(batch, ())
        out.append(batch)
        for z in range(levels):
            now[z] += duration
    batch = []
    for group in (events or {}).get(len(program), ()):
        there["own", group] = max(now)
    until(batch, lambda: False)
    out.append(batch)
    return out, max(now), max([at for at in there.values()] + [0.0])


class Planned:
    def __init__(self, batches):
        self.batches = list(batches)

    def take(self):
        return self.batches.pop(0)

    def tick(self):
        for step in self.take():
            step.run()

    def looped(self, count, each=1):
        now = [self.take() for _ in range(count * each)]

        def at(index, which=0):
            for k, steps in enumerate(now[which::each]):
                if steps:
                    pl.when(index == k)(lambda steps=steps: [s.run() for s in steps] and None)

        return at

    def finish(self):
        while self.batches:
            self.tick()


HD = 128
CONV = 4
SPAN = 128


def mm(a, b):
    return jnp.dot(a, b, preferred_element_type=f32)


def mm_nt(a, b):
    return lax.dot_general(a, b, (((1,), (1,)), ((), ())), preferred_element_type=f32)


def mm_tn(a, b):
    return lax.dot_general(a, b, (((0,), (0,)), ((), ())), preferred_element_type=f32)


def lanes(h):
    return pl.ds(pl.multiple_of(h * HD, HD), HD)


def set_masks(segc, keep):
    rows = lax.broadcasted_iota(jnp.int32, segc.shape, 0)
    seg = segc[...]
    for o in range(1, CONV):
        same = (pltpu.roll(seg, o, 0) == seg) & (rows >= o)
        keep[o - 1] = same.astype(f32)


def shifted(value, keep, o):
    return value if o == 0 else pltpu.roll(value, o, 0) * keep[o - 1]


def conv_of(proj, taps, keep, j, h, heads):
    at = lanes(j * heads + h)
    value = proj[:, at].astype(f32)
    total = taps[pl.ds(j * CONV + CONV - 1, 1), lanes(h)] * value
    for o in range(1, CONV):
        total = total + taps[pl.ds(j * CONV + CONV - 1 - o, 1), lanes(h)] * shifted(value, keep, o)
    return total


def span_masks(segc, segr, n):
    at = slice(n * SPAN, (n + 1) * SPAN)
    col = segc[at, :]
    same = col == jnp.broadcast_to(segr[0:1, at], (SPAN, SPAN))
    if n:
        carried = (col == segc[n * SPAN - 1 : n * SPAN, :]).astype(f32)
    else:
        carried = jnp.zeros((SPAN, HD), f32)
    ending = (col == col[SPAN - 1 : SPAN, :]).astype(f32)
    return carried, same, ending


def iotas():
    i = lax.broadcasted_iota(jnp.int32, (SPAN, SPAN), 0)
    j = lax.broadcasted_iota(jnp.int32, (SPAN, SPAN), 1)
    return i, j


def unit_inverses(lowers):
    i, j = iotas()
    apart = i ^ j
    invs = [jnp.where(apart == 1, -low, 0.0) for low in lowers]
    size, bits = 2, 1
    while size < SPAN:
        pairs = lax.shift_right_logical(apart, bits) == 1
        part = [jnp.where(pairs, low, 0.0) for low in lowers]
        small = [inv.astype(bf16) for inv in invs]
        left = [p + mm(s, p.astype(bf16)) for p, s in zip(part, small)]
        both = [w + mm(w.astype(bf16), s) for w, s in zip(left, small)]
        invs = [inv - b for inv, b in zip(invs, both)]
        size, bits = size * 2, bits + 1
    return invs


SLACK_F = 0.0


class Names:
    def __init__(self, names, refs):
        self.__dict__.update(zip(names, refs, strict=True))


class Sems:
    def __init__(self, ref):
        self.ref, self.used = ref, 0

    def take(self):
        self.used += 1
        return self.ref.at[self.used - 1]


def call(kernel, ins, outs, scratch, number, limit, *static):
    names = list(ins) + list(outs) + list(scratch)

    def run(*refs):
        kernel(Names(names, refs), *static)

    results = pl.pallas_call(
        run,
        out_shape=list(outs.values()),
        in_specs=[pl.BlockSpec(memory_space=ANY)] * len(ins),
        out_specs=[pl.BlockSpec(memory_space=ANY)] * len(outs),
        scratch_shapes=list(scratch.values()),
        compiler_params=pltpu.CompilerParams(
            collective_id=number, has_side_effects=True, vmem_limit_bytes=limit * MIB
        ),
    )(*ins.values())
    return dict(zip(outs, results, strict=True))


class Local:
    def __init__(self, sems):
        self.sems, self.open = sems, []

    def start(self, src, dst):
        copy = pltpu.make_async_copy(src, dst, self.sems.take())
        copy.start()
        self.open.append(copy)
        return copy

    def holds(self, copy):
        return any(copy is other for other in self.open)

    def wait(self, copy):
        copy.wait()
        self.open = [other for other in self.open if other is not copy]

    def done(self):
        for copy in self.open:
            copy.wait()
        self.open = []


class Remote:
    def __init__(self, place, sent, got):
        self.place, self.sent, self.got, self.open = place, sent, got, []

    def start(self, src, dst, hop):
        copy = self.make(src, dst, hop)
        copy.start()
        return copy

    def make(self, src, dst, hop):
        copy = pltpu.make_async_remote_copy(
            src_ref=src,
            dst_ref=dst,
            send_sem=self.sent.take(),
            recv_sem=self.got.take(),
            device_id=self.place.device(hop),
            device_id_type=MESH,
        )
        self.open.append(copy)
        return copy

    def drain(self):
        for copy in self.open:
            copy.wait_send()
        self.open = []


def unflat(value, share):
    return value.reshape(value.shape[0] // share, share, value.shape[1]).astype(bf16)


def flat(ref, cols):
    value = ref[:, :, cols]
    shape = (value.shape[0] * value.shape[1], value.shape[2])
    if value.shape[1] % 16:
        return value.astype(f32).reshape(shape).astype(bf16)
    return value.reshape(shape)


STREAMS = (
    (0, 0, (0, 6), "zxy"),
    (0, 0, (6, None), "zyx"),
    (0, 1, (0, 10), "zxy"),
    (0, 1, (10, None), "zyx"),
    (1, 0, None, "zxy"),
    (1, 1, None, "xyz"),
    (2, 0, None, "zyx"),
    (2, 1, None, "zxy"),
)


def span_of(cols, ref):
    if cols is None:
        return 0, ref.shape[2]
    first, last = cols
    return first * HD, ref.shape[2] if last is None else last * HD


NEIGHBOURS = ("x", "y", "up", "dn", "core")


def forward_kernel(r, levels, cfg):
    heads, spans, per, share = cfg["heads"], cfg["spans"], cfg["per"], cfg["share"]
    width, half, fhalf, heads_all = cfg["width"], cfg["half"], cfg["fhalf"], cfg["heads_all"]
    piece, rows = cfg["piece"], cfg["rows"]
    pc = Place(levels)
    loc = Local(Sems(r.loc_sem))
    rem = Remote(pc, Sems(r.send_sem), Sems(r.recv_sem))
    pc.meet(NEIGHBOURS)
    own = pc.shard(OWN, pc.t)
    targets = (r.w1, r.w_gu, r.w_down)
    streams = [
        Gather(pc, targets[a], hf, span_of(cols, targets[a]), order,
               r.__dict__["gs%d" % k], r.__dict__["gr%d" % k])
        for k, (a, hf, cols, order) in enumerate(STREAMS)
    ]
    def both(src_at, dst):
        return [loc.start(src_at(pc.t), dst), rem.start(src_at(1 - pc.t), dst, "core")]

    def cut(n, t):
        return pl.ds(pl.multiple_of(t * n, n), n)

    opening = []
    for j in range(3):
        opening += both(
            lambda t, j=j: r.qkv.at[j, :, cut(half, t)],
            r.w1.at[own, :, j * half : (j + 1) * half],
        )
    opening += both(lambda t: r.out_w.at[:, cut(half, t)], r.w1.at[own, :, 3 * half : 4 * half])
    opening += both(lambda t: r.ext, r.w1.at[own, :, 4 * half : 4 * half + HD])
    pieces = both(lambda t: r.tok.at[pc.x], r.x.at[pc.c])
    pieces += both(lambda t: r.flags.at[pc.x], r.marks.at[pc.c])

    def arrived(copies):
        for copy in copies:
            if loc.holds(copy):
                loc.wait(copy)
            else:
                copy.wait_recv()

    arrived(opening)
    second = []
    for j in range(2):
        second += both(
            lambda t, j=j: r.gu.at[j, :, cut(fhalf, t)],
            r.w_gu.at[own, :, j * fhalf : (j + 1) * fhalf],
        )
    second += both(lambda t: r.dn.at[:, cut(fhalf, t)], r.w_down.at[own])
    second += both(lambda t: r.cot.at[pc.x], r.dy.at[pc.c])
    hold = {1: second[:4], 2: second[4:6]}
    far = (1 - pc.x) * 2 + pc.t
    crossed = {
        name: rem.make(src.at[1 - pc.x], dst.at[pc.c], "x")
        for name, src, dst in (("x", r.tok, r.x), ("m", r.flags, r.marks), ("dy", r.cot, r.dy))
    }

    groups = [a for a, *_ in STREAMS]
    firsts = [k for k, a in enumerate(groups) if a == 0]
    mb = lambda n, m: 2e-6 * n * m
    steps = gather_steps(
        streams, groups, [mb(share, s.cols.stop - s.cols.start) for s in streams], levels,
        lambda a: arrived(hold.pop(a, [])),
    )
    steps.append(crossing_step(lambda: (crossed["x"].start(), crossed["m"].start()),
                               mb(piece, width + HD), 0, "tok"))
    steps.append(crossing_step(crossed["dy"].start, mb(piece, width), 3, "cot"))
    ordered = blocks_of(levels)

    def gate(z):
        return [("tok", z)] + [
            (k, z, block)
            for k in firsts
            for block in ordered
            if block != OWN and exists(block, z, levels)
        ]

    def gate1(z):
        return [
            (k, z, block)
            for k, a in enumerate(groups)
            for block in ordered
            if a == 1 and block != OWN and exists(block, z, levels)
        ]

    later = Planned(
        plan(
            steps, cfg["program"], levels, {0: 4.0, 1: 6.0, 2: 7.0, 3: 7.0},
            {0: gate, len(cfg["program"]) - rows // piece: gate1}, SLACK_F,
        )[0]
    )
    later.tick()
    crossed["x"].wait_recv()
    crossed["m"].wait_recv()
    arrived(pieces)
    pieces = [
        rem.start(r.x.at[far], r.x.at[far], "core"),
        rem.start(r.marks.at[far], r.marks.at[far], "core"),
    ]
    for block in ordered:
        for k in firsts:
            s = streams[k]
            if block != OWN and not route(block, s.order)[0]:
                s.wait(block)
    arrived(pieces)

    i, j = iotas()
    upto = (i >= j).astype(bf16)
    base = jnp.zeros((1, HD), f32)
    for n in range(spans):
        q, at = divmod(n * SPAN, piece)
        marks = r.marks[q, at : at + SPAN, :]
        seg = mm(upto, marks) + base
        r.segc[n * SPAN : (n + 1) * SPAN, :] = seg
        r.segr[:, n * SPAN : (n + 1) * SPAN] = jnp.transpose(seg)[0:8, :]
        base = seg[SPAN - 1 : SPAN, :]
    set_masks(r.segc, r.keep)
    loc.start(r.segc, r.segc_out)
    loc.start(r.segr, r.segr_out)

    shards = levels * 8 // 2
    mine = cut(half, pc.t)
    rows_of = lambda t: pl.ds(pl.multiple_of(t * shards, shards), shards)
    side = pl.ds(3 * half, half)
    swap_out = [
        loc.start(r.w1.at[rows_of(pc.t), :, side], r.wo.at[:, :, mine]),
        rem.start(r.w1.at[rows_of(1 - pc.t), :, side], r.wo.at[:, :, mine], "core"),
    ]

    extra = flat(r.w1, slice(4 * half, 4 * half + HD))
    for n in range(width // SPAN):
        at = slice(n * SPAN, (n + 1) * SPAN)
        r.small[:, at] = jnp.transpose(extra[at, :].astype(f32))[0:32, :]
    r.gains[...] = r.small[0:8, :]
    r.taps[...] = jnp.zeros(r.taps.shape, f32)
    r.taps[0 : 3 * CONV, :] = r.small[2 : 2 + 3 * CONV, cut(half, pc.t)]
    place_r = lax.broadcasted_iota(jnp.int32, (width, HD), 0)
    place_c = lax.broadcasted_iota(jnp.int32, (width, HD), 1)
    chosen = (place_r == share * (place_c // per) + place_c % per).astype(bf16)
    at = 2 + 3 * CONV + heads_all
    r.hgain[...] = jnp.broadcast_to(
        mm(r.small[at - at % 8 : at - at % 8 + 8, :].astype(bf16), chosen)[at % 8 : at % 8 + 1, :],
        (8, HD),
    )
    pick_r = lax.broadcasted_iota(jnp.int32, (HD, half), 0)
    pick_c = lax.broadcasted_iota(jnp.int32, (HD, half), 1)
    chosen = (pick_r == 2 + 3 * CONV + heads * pc.t + pick_c // HD).astype(bf16)
    w_beta = mm(extra, chosen)
    r.wbeta[...] = unflat(w_beta, share)
    pick_r = lax.broadcasted_iota(jnp.int32, (HD, HD), 0)
    pick_c = lax.broadcasted_iota(jnp.int32, (HD, HD), 1)
    chosen = ((pick_r == 2 + 3 * CONV + heads * pc.t + pick_c) & (pick_c < heads)).astype(bf16)
    r.wb[...] = unflat(mm(extra, chosen), share)
    loc.start(r.wb, r.wb_out)
    loc.start(r.w1.at[:, :, pl.ds(0, 3 * half)], r.wmix_out)
    loc.start(r.taps, r.taps_out)
    loc.start(r.gains, r.gains_out)
    loc.start(r.hgain, r.hgain_out)

    g0 = r.gains[0:1, :]
    for n in range(rows // piece):
        x = r.x[n].astype(f32)
        inv = lax.rsqrt(jnp.mean(x * x, axis=-1, keepdims=True) + 1e-5)
        value = x * inv * g0
        r.normed[n * piece : (n + 1) * piece, :] = value.astype(bf16)
        turned = jnp.transpose(value).astype(bf16)
        for m in range(width // piece):
            r.mine[m, :, n * piece : (n + 1) * piece] = turned[m * piece : (m + 1) * piece]
    normt = loc.start(r.mine, r.normt_out)
    loc.start(r.x, r.x_out)

    steps_at = later.looped(rows // piece)

    def project(k, carry):
        steps_at(k)
        at = pl.ds(pl.multiple_of(k * piece, piece), piece)
        left = r.normed[at, :]
        r.proj[at, :] = mm(left, flat(r.w1, slice(0, 3 * half))).astype(bf16)
        r.logit[at, :] = mm(left, flat(r.wbeta, slice(None)))
        r.blog[at, :] = mm(left, flat(r.wb, slice(None)))
        return carry

    lax.fori_loop(0, rows // piece, project, 0)
    loc.start(r.proj, r.proj_out)
    loc.start(r.blog, r.blog_out)

    prepare_at = later.looped(heads)

    def prepare(h, carry):
        prepare_at(h)
        delta_prepare(r, h, heads, spans)
        return carry

    lax.fori_loop(0, heads, prepare, 0)
    for src, dst in ((r.qs, r.qs_out), (r.ks, r.ks_out), (r.vs, r.vs_out), (r.ws, r.ws_out),
                     (r.ns, r.ns_out), (r.ps, r.ps_out)):
        loc.start(src, dst)
    delta_chain(r, heads, spans, later.tick)
    for h in range(heads):
        head = slice(h * HD, (h + 1) * HD)
        o = r.out[:, head]
        scale = lax.rsqrt(jnp.mean(o * o, axis=-1, keepdims=True) + 1e-5)
        r.headed[:, head] = (o * scale * r.hgain[0:1, :]).astype(bf16)
    for src, dst in ((r.fs, r.fs_out), (r.ss, r.ss_out), (r.out, r.out_out),
                     (r.headed, r.headed_out)):
        loc.start(src, dst)
    later.tick()
    arrived(swap_out)
    loc.start(r.wo, r.wo_out)
    wo = flat(r.wo, slice(None))
    loc.wait(normt)
    sent = []
    for n in range(rows // piece):
        r.mine[n] = mm(r.headed[n * piece : (n + 1) * piece, :], wo).astype(bf16)
        sent.append(rem.start(r.mine.at[n], r.theirs.at[n], "core"))
    later.tick()
    g1 = r.gains[1:2, :]
    for n in range(rows // piece):
        sent[n].wait_recv()
        at = slice(n * piece, (n + 1) * piece)
        res = r.x[n].astype(f32) + r.mine[n].astype(f32) + r.theirs[n].astype(f32)
        r.res[at, :] = res
        inv = lax.rsqrt(jnp.mean(res * res, axis=-1, keepdims=True) + 1e-5)
        r.normed2[at, :] = (res * inv * g1).astype(bf16)
    loc.start(r.res, r.res_out)
    loc.start(r.normed2, r.normed2_out)
    later.tick()
    for block in ordered:
        for n, s in enumerate(streams):
            if groups[n] == 1 and block != OWN and not route(block, s.order)[0]:
                s.wait(block)
    w_gate, w_up = flat(r.w_gu, slice(0, fhalf)), flat(r.w_gu, slice(fhalf, 2 * fhalf))
    loc.start(r.w_gu, r.w_gu_out)
    writes = {}
    few = piece // 2
    for n in range(rows // few):
        if n and n % 2 == 0:
            later.tick()
        at = slice(n * few, (n + 1) * few)
        left = r.normed2[at, :]
        gate, up = mm(left, w_gate), mm(left, w_up)
        sg = jax.nn.sigmoid(gate)
        for copy in writes.get(n % 2, ()):
            loc.wait(copy)
        r.act[n % 2] = (gate * sg * up).astype(bf16)
        r.fgate[n % 2] = (up * sg * (1.0 + gate * (1.0 - sg))).astype(bf16)
        r.fup[n % 2] = (gate * sg).astype(bf16)
        writes[n % 2] = [
            loc.start(src.at[n % 2], dst.at[pl.ds(n * few, few), :])
            for src, dst in ((r.act, r.act_out), (r.fgate, r.fgate_out), (r.fup, r.fup_out))
        ]
    later.finish()
    crossed["dy"].wait_recv()
    arrived(second[6:])
    last = rem.start(r.dy.at[far], r.dy.at[far], "core")
    for block in ordered:
        for k, s in enumerate(streams):
            if groups[k] == 2 and block != OWN and not route(block, s.order)[0]:
                s.wait(block)
    last.wait_recv()
    for s in streams:
        s.drain(ordered)
    rem.drain()
    loc.done()


def delta_prepare(r, h, heads, spans):
    i, j = iotas()
    mixed = []
    for which in range(3):
        value = conv_of(r.proj, r.taps, r.keep, which, h, heads)
        mixed.append(value * jax.nn.sigmoid(value))
    for which, dest in ((0, r.qs), (1, r.ks)):
        w = mixed[which]
        unit = w * lax.rsqrt(jnp.sum(w * w, axis=-1, keepdims=True) + 1e-6)
        dest[:, lanes(h)] = unit.astype(bf16)
    r.vs[:, lanes(h)] = mixed[2].astype(bf16)
    lowers, rights = [], []
    for n in range(spans):
        at = slice(n * SPAN, (n + 1) * SPAN)
        k = r.ks[at, lanes(h)]
        q = r.qs[at, lanes(h)]
        v = r.vs[at, lanes(h)]
        beta = jax.nn.sigmoid(r.logit[at, lanes(h)])
        carried, same, ending = span_masks(r.segc, r.segr, n)
        lowers.append(jnp.where(same & (i > j), beta * mm_nt(k, k), 0.0))
        r.ps[h * spans + n] = jnp.where(same & (i >= j), mm_nt(q, k), 0.0).astype(bf16)
        rights.append(
            jnp.concatenate([beta * v.astype(f32), (beta * carried) * k.astype(f32)], axis=1)
        )
    for n, inv in enumerate(unit_inverses(lowers)):
        at = slice(n * SPAN, (n + 1) * SPAN)
        small = inv.astype(bf16)
        r.ns[h * spans + n] = small
        both = rights[n] + mm(small, rights[n].astype(bf16))
        r.us[at, lanes(h)] = both[:, :HD]
        r.ws[at, lanes(h)] = both[:, HD:].astype(bf16)


def delta_chain(r, heads, spans, between):
    states = [jnp.zeros((HD, HD), f32) for _ in range(heads)]
    for n in range(spans):
        at = slice(n * SPAN, (n + 1) * SPAN)
        between()
        carried, same, ending = span_masks(r.segc, r.segr, n)
        for h in range(heads):
            head = slice(h * HD, (h + 1) * HD)
            state = states[h].astype(bf16)
            r.ss[h * spans + n] = state
            queries = (carried * r.qs[at, head].astype(f32)).astype(bf16)
            seen = mm(jnp.concatenate([r.ws[at, head], queries], axis=0), state)
            fresh = r.us[at, head] - seen[:SPAN]
            small = fresh.astype(bf16)
            r.fs[at, head] = small
            r.out[at, head] = seen[SPAN:] + mm(r.ps[h * spans + n], small)
            states[h] = carried[SPAN - 1 : SPAN, :] * states[h] + mm_tn(
                r.ks[at, head], (ending * fresh).astype(bf16)
            )


def forward(qkv, out_w, gu, dn, ext, tok, cot, flags, levels, per, heads_all):
    share = qkv.shape[1]
    width = qkv.shape[2]
    half, fhalf = width // 2, dn.shape[1] // 2
    piece = tok.shape[1]
    rows = 4 * piece
    heads = half // HD
    spans = rows // SPAN
    shards = levels * 8
    sds = jax.ShapeDtypeStruct
    wide, square = sds((rows, half), bf16), sds((heads * spans, SPAN, SPAN), bf16)
    seg = dict(
        segc=sds((rows, HD), f32),
        segr=sds((8, rows), f32),
        taps=sds((16, half), f32),
        gains=sds((8, width), f32),
        hgain=sds((8, HD), f32),
        x=sds((4, piece, width), bf16),
        proj=sds((rows, 3 * half), bf16),
        blog=sds((rows, HD), f32),
        qs=wide, ks=wide, vs=wide, fs=wide, ws=wide, headed=wide,
        ns=square, ps=square, ss=square,
        out=sds((rows, half), f32),
        wo=sds((shards // 2, share, width), bf16),
        res=sds((rows, width), f32),
        normed2=sds((rows, width), bf16),
    )
    ins = dict(qkv=qkv, out_w=out_w, gu=gu, dn=dn, ext=ext, tok=tok, cot=cot, flags=flags)
    outs = {
        "normt_out": sds((4, piece, width), bf16),
        "wmix_out": sds((shards, share, 3 * half), bf16),
        "wb_out": sds((shards, share, HD), bf16),
        "w_gu_out": sds((shards, share, 2 * fhalf), bf16),
        "act_out": sds((rows, fhalf), bf16),
        "fgate_out": sds((rows, fhalf), bf16),
        "fup_out": sds((rows, fhalf), bf16),
        "w_down": sds((shards, share, fhalf), bf16),
        "dy": sds((4, piece, width), bf16),
    }
    outs.update({k + "_out": v for k, v in seg.items()})
    scratch = {k: VM(v.shape, v.dtype) for k, v in seg.items()}
    scratch.update(
        w1=VM((shards, share, 4 * half + HD), bf16),
        w_gu=VM((shards, share, 2 * fhalf), bf16),
        act=VM((2, piece // 2, fhalf), bf16),
        fgate=VM((2, piece // 2, fhalf), bf16),
        fup=VM((2, piece // 2, fhalf), bf16),
        wbeta=VM((shards, share, half), bf16),
        wb=VM((shards, share, HD), bf16),
        marks=VM((4, piece, HD), bf16),
        keep=VM((CONV - 1, rows, HD), f32),
        small=VM((32, width), f32),
        us=VM((rows, half), f32),
        normed=VM((rows, width), bf16),
        logit=VM((rows, half), f32),
        mine=VM((4, piece, width), bf16),
        theirs=VM((4, piece, width), bf16),
        loc_sem=pltpu.SemaphoreType.DMA((80,)),
        send_sem=pltpu.SemaphoreType.DMA((32,)),
        recv_sem=pltpu.SemaphoreType.DMA((32,)),
    )
    for k, (a, hf, cols, order) in enumerate(STREAMS):
        sent, got = Gather.sems(levels, order)
        scratch["gs%d" % k] = pltpu.SemaphoreType.DMA((sent,))
        scratch["gr%d" % k] = pltpu.SemaphoreType.DMA((got,))
    cfg = dict(
        heads=heads, spans=spans, per=per, share=share, width=width, half=half, fhalf=fhalf,
        heads_all=heads_all, piece=piece, rows=rows,
        program=[6.0] + [2.0] * (rows // piece) + [4.0] * heads + [0.6] * spans + [1.0, 4.0]
        + [3.0] * (rows // piece),
    )
    return call(forward_kernel, ins, outs, scratch, 1, 63, levels, cfg)
SLACK_B = 4.0


def backward_kernel(r, levels, cfg):
    heads, spans, per, share = cfg["heads"], cfg["spans"], cfg["per"], cfg["share"]
    width, half, heads_all = cfg["width"], cfg["half"], cfg["heads_all"]
    piece, rows = cfg["piece"], cfg["rows"]
    pc = Place(levels)
    loc = Local(Sems(r.loc_sem))
    rem = Remote(pc, Sems(r.send_sem), Sems(r.recv_sem))
    pc.meet(NEIGHBOURS)
    pieces = rows // piece
    small_in = [loc.start(a, b) for a, b in (
        (r.gains_in, r.gains), (r.hgain_in, r.hgain), (r.taps_in, r.taps), (r.segc_in, r.segc),
        (r.segr_in, r.segr), (r.dheaded_in, r.dheaded))]
    normed_in = [loc.start(r.normed_in.at[n], r.theirs.at[n]) for n in range(pieces)]
    last_in = [loc.start(r.dres_in.at[k], r.res.at[k]) for k in range(pieces // 2)]
    last_in.append(loc.start(r.gain1_in, r.gain1))
    load = [loc.start(r.g_up_in, r.g_up), loc.start(r.g_out_in, r.g_out)]
    delta_in = [loc.start(a, b) for a, b in (
        (r.out_in, r.out), (r.blog_in, r.blog), (r.proj_in, r.dproj), (r.wb_in, r.wb),
        (r.qs_in, r.sv.at[0]), (r.ks_in, r.sv.at[1]), (r.vs_in, r.sv.at[2]),
        (r.fs_in, r.sv.at[3]), (r.ws_in, r.sv.at[4]),
        (r.ns_in, r.sq.at[0]), (r.ps_in, r.sq.at[1]), (r.ss_in, r.sq.at[2]))]
    streams = []
    for k, (name, h, hf, cols, order) in enumerate(RETURNS):
        grad, final = r.__dict__["g_" + name], r.__dict__["f_" + name]
        if h is not None:
            grad, final = grad.at[h], final.at[:, h]
        streams.append(
            Scatter(pc, grad, r.__dict__["room%d" % k], final, hf, span_of(cols, grad),
                    order, r.__dict__["ss%d" % k], r.__dict__["sr%d" % k])
        )

    def arrived(copies):
        for copy in copies:
            if loc.holds(copy):
                loc.wait(copy)
            else:
                copy.wait_recv()

    ordered = blocks_of(levels)[::-1]
    arrived(load)
    crossing = [
        rem.make(r.lo_in.at[1 - pc.x], r.lo_out.at[pc.x], "x"),
        rem.make(r.theirs.at[1 - pc.x], r.dx_out.at[pc.x], "x"),
    ]
    mb = lambda n, m: 2e-6 * n * m
    groups = [
        {"up": 0, "out": 1, "q": 2 + (h or 0), "small": 2 + heads}[name]
        for name, h, *_ in RETURNS
    ]
    steps = scatter_steps(
        streams, groups,
        [
            mb(share * (1 if s.half is not None else 2), s.cols.stop - s.cols.start)
            for s in streams
        ],
        levels,
    )
    steps.append(crossing_step(crossing[0].start, mb(piece, width), 0, "lo"))
    loc.start(r.lo_in.at[pc.x], r.lo_out.at[pc.x])
    start = heads + 2
    events = {len(cfg["program"]): [2 + heads]}
    for h in range(heads):
        events[start + h + 1] = [2 + h]
    later = Planned(plan(steps, cfg["program"], levels, {0: 0.0, 1: 0.0}, {}, SLACK_B, events)[0])
    later.tick()

    def cut(n, t):
        return pl.ds(pl.multiple_of(t * n, n), n)

    arrived(small_in)
    set_masks(r.segc, r.keep)
    arrived(delta_in)
    qs, ks, vs, fs, ws = (r.sv.at[k] for k in range(5))
    ns, ps, ss = (r.sq.at[k] for k in range(3))
    douts, xs = r.datt.at[0], r.datt.at[1]
    ys, hs, gs = r.headed, r.out, r.dheaded
    i, j = iotas()
    lane = lax.broadcasted_iota(jnp.int32, (SPAN, HD), 1)
    r.dlog[...] = jnp.zeros(r.dlog.shape, f32)

    norm_at = later.looped(heads)

    def norm_back(h, dgain_sum):
        norm_at(h)
        o = r.out[:, lanes(h)]
        dyh = r.dheaded[:, lanes(h)].astype(f32)
        inv = lax.rsqrt(jnp.mean(o * o, axis=-1, keepdims=True) + 1e-5)
        scaled = dyh * r.hgain[0:1, :]
        dout = inv * scaled - o * (inv * inv * inv * jnp.mean(scaled * o, axis=-1, keepdims=True))
        dgain_sum = dgain_sum + jnp.sum(dyh * o * inv, axis=0, keepdims=True)
        for n in range(spans):
            at = slice(n * SPAN, (n + 1) * SPAN)
            carried, same, ending = span_masks(r.segc, r.segr, n)
            small = dout[at].astype(bf16)
            douts[at, lanes(h)] = small
            x = mm_tn(ps[h * spans + n], small).astype(bf16)
            xs[at, lanes(h)] = x
            cdout = (carried * dout[at]).astype(bf16)
            hs[at, lanes(h)] = mm_tn(qs[at, lanes(h)], cdout) - mm_tn(ws[at, lanes(h)], x)
        return dgain_sum

    dgain = lax.fori_loop(0, heads, norm_back, jnp.zeros((1, HD), f32))
    grads_s = [jnp.zeros((HD, HD), f32) for _ in range(heads)]
    later.tick()
    for n in reversed(range(spans)):
        at = slice(n * SPAN, (n + 1) * SPAN)
        carried, same, ending = span_masks(r.segc, r.segr, n)
        for h in range(heads):
            head = slice(h * HD, (h + 1) * HD)
            g = grads_s[h].astype(bf16)
            gs[at, head] = g
            y = (ending * mm(ks[at, head], g)).astype(bf16)
            ys[at, head] = y
            if n:
                grads_s[h] = (
                    carried[SPAN - 1 : SPAN, :] * grads_s[h]
                    - mm_tn(ws[at, head], y)
                    + hs[at, head]
                )

    per_piece = piece // SPAN

    def spot(which, n):
        return (
            pieces // 2 + which // 2,
            slice((n % per_piece) * SPAN, (n % per_piece + 1) * SPAN),
            slice(
                ((which % 2) * pieces + n // per_piece) * HD,
                ((which % 2) * pieces + n // per_piece + 1) * HD,
            ),
        )

    def put(which, n, value):
        r.res[spot(which, n)] = value

    def taken(which):
        return jnp.concatenate([r.res[spot(which, n)] for n in range(spans)], axis=0)

    arrived(normed_in)
    pull_at = later.looped(heads)

    def pull(h, carry):
        head = lanes(h)
        pull_at(h)
        for n in range(spans):
            at = slice(n * SPAN, (n + 1) * SPAN)
            carried, same, ending = span_masks(r.segc, r.segr, n)
            which = h * spans + n
            q, k, v, f = qs[at, head], ks[at, head], vs[at, head], fs[at, head]
            state, g, p, inv = ss[which], gs[at, head], ps[which], ns[which]
            b = jax.nn.sigmoid(
                jnp.sum(jnp.where(lane == h, r.blog[at, :], 0.0), axis=-1, keepdims=True)
            )
            beta = jnp.broadcast_to(b, (SPAN, HD))
            small = douts[at, head]
            df = xs[at, head].astype(f32) + ys[at, head].astype(f32)
            z = df + mm_tn(inv, df.astype(bf16))
            zb = z.astype(bf16)
            dp = jnp.where(same & (i >= j), mm_nt(small, f), 0.0).astype(bf16)
            dl = jnp.where(same & (i > j), -mm_nt(zb, f), 0.0)
            known = v.astype(f32) - carried * mm(k, state)
            dbeta = jnp.sum(z * known + dl * mm_nt(k, k), axis=-1, keepdims=True)
            dlogit = dbeta * b * (1.0 - b)
            r.dlog[at, :] = jnp.where(
                lane == h, jnp.broadcast_to(dlogit, (SPAN, HD)), r.dlog[at, :]
            )
            e = (beta * dl).astype(bf16)
            put(0, n, carried * mm_nt(small, state) + mm(dp, k))
            put(2, n, beta * z)
            put(1, n, (
                mm(e, k)
                + mm_tn(e, k)
                + mm_tn(dp, q)
                - (carried * beta) * mm_nt(zb, state)
                + ending * mm_nt(f, g)
            ))
        for which in range(3):
            c = conv_of(r.dproj, r.taps, r.keep, which, h, heads)
            s = jax.nn.sigmoid(c)
            d = taken(which)
            if which < 2:
                w = c * s
                n = lax.rsqrt(jnp.sum(w * w, axis=-1, keepdims=True) + 1e-6)
                d = n * d - w * (n * n * n * jnp.sum(w * d, axis=-1, keepdims=True))
            dc = d * (s * (1.0 + c * (1.0 - s)))
            at = lanes(which * heads + h)
            value = r.dproj[:, at].astype(f32)
            total = None
            for o in range(CONV):
                row = which * CONV + CONV - 1 - o
                tap = r.taps[pl.ds(row, 1), lanes(h)]
                r.dtaps[pl.ds(row, 1), lanes(h)] = jnp.sum(
                    dc * shifted(value, r.keep, o), axis=0, keepdims=True
                )
                if o == 0:
                    total = tap * dc
                else:
                    total = total + tap * pltpu.roll(dc * r.keep[o - 1], rows - o, 0)
            r.dproj[:, at] = total.astype(bf16)
        grads = jnp.concatenate(
            [r.dproj[:, lanes(which * heads + h)] for which in range(3)], axis=1
        )
        for n in range(width // piece):
            at = slice(n * piece // share, (n + 1) * piece // share)
            r.g_q[h, at] = unflat(mm(r.theirs[n], grads), share)
        return carry

    lax.fori_loop(0, heads, pull, 0)

    weights_in = [
        loc.start(r.wmix_in.at[:, pl.ds(k * half, half)], r.sv.at[k]) for k in range(3)
    ]
    arrived(weights_in)

    def partial(which, at):
        n = which
        where = pl.ds(pl.multiple_of(n * piece, piece), piece)
        total = mm_nt(r.dlog[where, :].astype(bf16), r.wb[...])
        for k in range(3):
            total = total + mm_nt(r.dproj[where, k * half : (k + 1) * half], r.sv[k])
        r.mine[at] = total.astype(bf16)

    turn = [1 - pc.x, pc.x]
    sent = [rem.make(r.mine.at[2 + k], r.theirs3.at[k], "core") for k in turn]
    later.tick()
    for n, k in enumerate(turn):
        partial(2 * k + 1 - pc.t, 2 + k)
        sent[n].start()
    later.tick()
    for k in turn:
        partial(2 * k + pc.t, k)
    right = r.dlog[...].astype(bf16)
    g_beta = jnp.concatenate(
        [
            mm(r.theirs[n], right).astype(bf16)
            for n in range(width // piece)
        ],
        axis=0,
    )
    x_in = [
        loc.start(r.x_in.at[2 * k + pc.t], r.theirs.at[2 + k]) for k in range(pieces // 2)
    ]

    later.tick()
    arrived(x_in)
    arrived(last_in)
    g0 = r.gains[0:1, :]
    gain0 = jnp.zeros((1, width), f32)
    for n, k in enumerate(turn):
        sent[n].wait_recv()
        v = r.theirs[2 + k].astype(f32)
        grad = r.mine[k].astype(f32) + r.theirs3[k].astype(f32)
        inv = lax.rsqrt(jnp.mean(v * v, axis=-1, keepdims=True) + 1e-5)
        scaled = grad * g0
        back = inv * scaled - v * (inv * inv * inv * jnp.mean(scaled * v, axis=-1, keepdims=True))
        gain0 = gain0 + jnp.sum(grad * v * inv, axis=0, keepdims=True)
        r.theirs[k] = (back + r.res[k]).astype(bf16)
        if n == 0:
            crossing[1].start()
    loc.start(r.theirs.at[pc.x], r.dx_out.at[pc.x])
    r.cols[...] = jnp.zeros(r.cols.shape, f32)
    r.cols[0:1, :] = gain0
    r.cols[1:2, :] = r.gain1[0:1, :]
    r.cols[2 : 2 + 3 * CONV, cut(half, pc.t)] = r.dtaps[0 : 3 * CONV, :]
    place_r = lax.broadcasted_iota(jnp.int32, (HD, width), 0)
    place_c = lax.broadcasted_iota(jnp.int32, (HD, width), 1)
    spread = ((place_c // share * per + place_c % share == place_r) & (place_c % share < per)).astype(bf16)
    at = 2 + 3 * CONV + heads_all
    r.cols[at : at + 1, :] = mm(jnp.broadcast_to(dgain, (8, HD)).astype(bf16), spread)[0:1, :]
    pick_r = lax.broadcasted_iota(jnp.int32, (HD, HD), 0)
    pick_c = lax.broadcasted_iota(jnp.int32, (HD, HD), 1)
    chosen = ((pick_c == 2 + 3 * CONV + heads * pc.t + pick_r) & (pick_r < heads)).astype(bf16)
    beta = mm(g_beta, chosen)
    for n in range(width // SPAN):
        at = n * SPAN
        rows_in = jnp.concatenate(
            [r.cols[:, at : at + SPAN], jnp.zeros((HD - 32, SPAN), f32)], axis=0
        )
        block = jnp.transpose(rows_in) + beta[at : at + SPAN]
        r.g_small[at // share : (at + SPAN) // share] = unflat(block, share)
    later.finish()
    for s in streams:
        s.finish()
    for name in ("up", "out", "q", "small"):
        src, dst = r.__dict__["f_" + name], r.__dict__["o_" + name]
        loc.start(src.at[pc.t], dst.at[pc.t])
        crossing.append(rem.start(src.at[1 - pc.t], dst.at[pc.t], "core"))
    for copy in crossing:
        copy.wait_recv()
    for s in streams:
        s.drain(ordered)
    rem.drain()
    loc.done()


RETURNS = (
    ("up", None, 0, None, "zyx"),
    ("up", None, 1, None, "zxy"),
    ("out", None, None, None, "xyz"),
    ("q", 0, None, None, "zxy"),
    ("q", 1, None, None, "zyx"),
    ("q", 2, None, None, "zyx"),
    ("q", 3, None, None, "zyx"),
    ("small", None, None, None, "xyz"),
)


def backward(f, g, levels, per, heads_all):
    rows, width = f["normed2_out"].shape
    half = f["out_out"].shape[1]
    piece = rows // 4
    share = f["wo_out"].shape[1]
    heads = half // HD
    spans = rows // SPAN
    shards = levels * 8
    sds = jax.ShapeDtypeStruct
    ins = dict(
        dheaded_in=g["dheaded_out"], dres_in=g["dres_out"], gain1_in=g["gain1_out"],
        g_up_in=g["gup_out"], g_out_in=g["gout_out"], lo_in=g["result"],
        x_in=f["x_out"],
        gains_in=f["gains_out"], hgain_in=f["hgain_out"], taps_in=f["taps_out"],
        segc_in=f["segc_out"], segr_in=f["segr_out"], out_in=f["out_out"], blog_in=f["blog_out"], proj_in=f["proj_out"],
        normed_in=f["normt_out"], wmix_in=f["wmix_out"].reshape(width, 3 * half),
        wb_in=f["wb_out"].reshape(width, HD),
    )
    ins.update({k + "_in": f[k + "_out"] for k in ("qs", "ks", "vs", "fs", "ws", "ns", "ps", "ss")})
    cols = dict(up=(g["gup_out"].shape[2],), out=(half,), q=(3 * HD,), small=(HD,))
    tops = dict(up=(2,), out=(2,), q=(2, heads), small=(2,))
    outs = dict(
        dx_out=sds((2, piece, width), bf16),
        lo_out=sds((2, piece, width), bf16),
        **{"o_" + n: sds(tops[n] + (share,) + cols[n], f32) for n in cols},
    )
    scratch = dict(
        mine=VM((4, piece, width), bf16),
        theirs=VM((4, piece, width), bf16),
        theirs3=VM((2, piece, width), bf16),
        res=VM((4, piece, width), f32),
        gains=VM((8, width), f32),
        hgain=VM((8, HD), f32),
        taps=VM((16, half), f32),
        dtaps=VM((16, half), f32),
        segc=VM((rows, HD), f32),
        segr=VM((8, rows), f32),
        headed=VM((rows, half), bf16),
        gain1=VM((8, width), f32),
        datt=VM((2, rows, half), bf16),
        cols=VM((32, width), f32),
        g_out=VM((shards, share, half), bf16),
        g_q=VM((heads, shards, share, 3 * HD), bf16),
        g_small=VM((shards, share, HD), bf16),
        dheaded=VM((rows, half), bf16),
        sv=VM((5, rows, half), bf16),
        sq=VM((3, heads * spans, SPAN, SPAN), bf16),
        out=VM((rows, half), f32),
        blog=VM((rows, HD), f32),
        dproj=VM((rows, 3 * half), bf16),
        dlog=VM((rows, HD), f32),
        wb=VM((width, HD), bf16),
        keep=VM((CONV - 1, rows, HD), f32),
        g_up=VM(g["gup_out"].shape, bf16),
        **{"f_" + n: VM(tops[n] + (share,) + cols[n], f32) for n in cols},
        loc_sem=pltpu.SemaphoreType.DMA((64,)),
        send_sem=pltpu.SemaphoreType.DMA((16,)),
        recv_sem=pltpu.SemaphoreType.DMA((16,)),
    )
    for k, (name, h, hf, tiles, order) in enumerate(RETURNS):
        slots, sent = Scatter.slots_of(levels, order)
        first, last = span_of(tiles, sds((1, 1) + cols[name], bf16))
        both = () if hf is not None else (2,)
        scratch["room%d" % k] = VM((slots,) + both + (share, last - first), bf16)
        scratch["ss%d" % k] = pltpu.SemaphoreType.DMA((sent,))
        scratch["sr%d" % k] = pltpu.SemaphoreType.DMA((slots,))
    cfg = dict(
        heads=heads, spans=spans, per=per, share=share, width=width, half=half,
        heads_all=heads_all, piece=piece, rows=rows,
        program=[4.0] + [2.5] * heads + [5.0] + [7.0] * heads + [2.5] * 2 + [3.0],
    )
    return call(backward_kernel, ins, outs, scratch, 2, 63, levels, cfg)
SLACK_M = 2.0


MIDDLE = (
    ("down", 0, None, "zxy"),
    ("down", 1, None, "zyx"),
    ("gate", 0, None, "zxy"),
    ("gate", 1, None, "zyx"),
)


def middle_kernel(r, levels, cfg):
    share, width, fhalf = cfg["share"], cfg["width"], cfg["fhalf"]
    piece, rows = cfg["piece"], cfg["rows"]
    pieces = rows // piece
    pc = Place(levels)
    loc = Local(Sems(r.loc_sem))
    rem = Remote(pc, Sems(r.send_sem), Sems(r.recv_sem))
    loads = [
        [loc.start(a, b) for a, b in group]
        for group in (
            ((r.dy_in, r.dy), (r.act_in, r.act)),
            ((r.w_down_in, r.w_down),),
            ((r.fgate_in, r.fgate), (r.fup_in, r.fup)),
            ((r.normed2_in, r.normed2), (r.w_gu_in, r.w_gu)),
            ((r.gains_in, r.gains), (r.wo_in, r.wo)),
        )
    ]

    def loaded(k):
        for copy in loads[k]:
            loc.wait(copy)

    residuals = [loc.start(r.res_in.at[n], r.res.at[n]) for n in range(pieces)]
    pc.meet(NEIGHBOURS)
    grads = dict(down=r.g_down, gate=r.w_down)
    streams = [
        Scatter(pc, grads[name], r.__dict__["room%d" % k], r.__dict__["f_" + name], hf,
                span_of(cols, grads[name]), order, r.__dict__["ss%d" % k], r.__dict__["sr%d" % k])
        for k, (name, hf, cols, order) in enumerate(MIDDLE)
    ]
    mb = lambda n, m: 2e-6 * n * m
    steps = scatter_steps(
        streams, [int(name == "gate") for name, *_ in MIDDLE],
        [mb(share, s.cols.stop - s.cols.start) for s in streams], levels,
    )
    later = Planned(
        plan(steps, cfg["program"], levels, {0: 0.0}, {}, SLACK_M, {3 * pieces: [1]})[0]
    )
    ordered = blocks_of(levels)

    loaded(0)
    dy = r.dy[...].reshape(rows, width)
    strip = width // 4
    for n in range(4):
        at = slice(n * strip // share, (n + 1) * strip // share)
        r.g_down[at] = unflat(
            mm_tn(dy[:, n * strip : (n + 1) * strip], r.act[...]), share
        )
    later.tick()

    loaded(1)
    w_down = flat(r.w_down, slice(None))
    sent = []
    for k in range(pieces // 2):
        which = 2 * k + 1 - pc.t
        at = pl.ds(pl.multiple_of(which * piece, piece), piece)
        r.mine[2 + k] = mm_nt(r.act[at, :], w_down).astype(bf16)
        sent.append(rem.start(r.mine.at[2 + k], r.theirs.at[k], "core"))
    later.tick()
    for k in range(pieces // 2):
        which = 2 * k + pc.t
        at = pl.ds(pl.multiple_of(which * piece, piece), piece)
        r.mine[k] = mm_nt(r.act[at, :], w_down).astype(bf16)
    loaded(2)
    for n in range(pieces):
        later.tick()
        at = slice(n * piece, (n + 1) * piece)
        dact = mm(r.dy[n], w_down)
        r.dgu[at, :fhalf] = (dact * r.fgate[at, :].astype(f32)).astype(bf16)
        r.dgu[at, fhalf:] = (dact * r.fup[at, :].astype(f32)).astype(bf16)
    later.tick()
    for copy in residuals:
        loc.wait(copy)
    for k in range(pieces // 2):
        sent[k].wait_recv()
        r.mine[k] = (
            r.res[2 * k + pc.t] + r.mine[k].astype(f32) + r.theirs[k].astype(f32)
        ).astype(bf16)
        loc.start(r.mine.at[k], r.result.at[k])

    loaded(3)
    w_gu = flat(r.w_gu, slice(None))
    parts, writes = [], []
    for n in range(pieces):
        later.tick()
        at = slice(n * piece, (n + 1) * piece)
        r.part[n] = mm_nt(r.dgu[at, :], w_gu).astype(bf16)
        parts.append(rem.start(r.part.at[n], r.theirs2.at[n], "core"))
    later.tick()
    for n in range(4):
        at = slice(n * strip // share, (n + 1) * strip // share)
        r.w_down[at] = unflat(
            mm_tn(r.normed2[:, n * strip : (n + 1) * strip], r.dgu[:, :fhalf]), share
        )

    half = width // 2
    halves = [slice(c * half, (c + 1) * half) for c in range(2)]
    headed_in = loc.start(r.headed_in, r.fup.at[:, pl.ds(half, half)])
    loaded(4)
    g1 = r.gains[1:2, :]
    gain1 = jnp.zeros((1, width), f32)
    for n in range(pieces):
        later.tick()
        parts[n].wait_recv()
        at = slice(n * piece, (n + 1) * piece)
        v = r.res[n]
        grad = r.part[n].astype(f32) + r.theirs2[n].astype(f32)
        inv = lax.rsqrt(jnp.mean(v * v, axis=-1, keepdims=True) + 1e-5)
        scaled = grad * g1
        back = inv * scaled - v * (inv * inv * inv * jnp.mean(scaled * v, axis=-1, keepdims=True))
        ours = (pc.t == n % 2).astype(f32)
        gain1 = gain1 + ours * jnp.sum(grad * v * inv, axis=0, keepdims=True)
        dres = back + r.dy[n].astype(f32)
        r.res[n] = dres
        low = dres.astype(bf16)
        r.fgate[at, 0:width] = low
    r.gains[...] = jnp.broadcast_to(gain1, r.gains.shape)
    loc.start(r.gains, r.gain1_out)
    for k in range(pieces // 2):
        loc.start(r.res.at[2 * k + pc.t], r.dres_out.at[k])

    later.tick()
    wo = flat(r.wo, slice(None))
    for n in range(pieces):
        at = slice(n * piece, (n + 1) * piece)
        r.fup[at, 0:half] = mm_nt(r.fgate[at, 0:width], wo).astype(bf16)
    loc.start(r.fup.at[:, pl.ds(0, half)], r.dheaded_out)
    later.tick()
    loc.wait(headed_in)
    for c in range(2):
        for n in range(half // piece):
            left = r.fup[:, half + n * piece : half + (n + 1) * piece]
            at = slice(n * piece // share, (n + 1) * piece // share)
            r.wo[at, :, halves[c]] = unflat(mm_tn(left, r.fgate[:, halves[c]]), share)
    shards = levels * 8 // 2
    ours = pl.ds(pl.multiple_of(pc.t * shards, shards), shards)
    side = lambda t: pl.ds(pl.multiple_of(t * half, half), half)
    loc.start(r.wo.at[:, :, side(pc.t)], r.gout_out.at[ours])
    gout = rem.start(r.wo.at[:, :, side(1 - pc.t)], r.gout_out.at[ours], "core")
    later.tick()
    for n in range(4):
        at = slice(n * strip // share, (n + 1) * strip // share)
        if n > 1:
            loc.wait(writes[n - 2])
        r.gup[n % 2] = unflat(
            mm_tn(r.normed2[:, n * strip : (n + 1) * strip], r.dgu[:, fhalf:]), share
        )
        writes.append(loc.start(r.gup.at[n % 2], r.gup_out.at[pl.ds(at.start, strip // share)]))
    gout.wait_recv()
    later.finish()
    for s in streams:
        s.finish()
    last = []
    for src, dst in ((r.f_down, r.o_down), (r.f_gate, r.o_gate)):
        loc.start(src.at[pc.t], dst.at[pc.t])
        last.append(rem.start(src.at[1 - pc.t], dst.at[pc.t], "core"))
    for copy in last:
        copy.wait_recv()
    for s in streams:
        s.drain(ordered)
    rem.drain()
    loc.done()


def middle(f, levels):
    shards, share, two = f["w_gu_out"].shape
    fhalf = two // 2
    rows, width = f["normed2_out"].shape
    piece = rows // 4
    sds = jax.ShapeDtypeStruct
    ins = dict(
        dy_in=f["dy"], act_in=f["act_out"], w_down_in=f["w_down"], fgate_in=f["fgate_out"],
        fup_in=f["fup_out"], normed2_in=f["normed2_out"], w_gu_in=f["w_gu_out"],
        res_in=f["res_out"].reshape(4, piece, width), gains_in=f["gains_out"],
        wo_in=f["wo_out"], headed_in=f["headed_out"],
    )
    outs = dict(
        gup_out=sds((shards, share, fhalf), bf16),
        gout_out=sds((shards, share, width // 2), bf16),
        dheaded_out=sds((rows, width // 2), bf16),
        dres_out=sds((2, piece, width), f32),
        gain1_out=sds((8, width), f32),
        o_gate=sds((2, share, fhalf), f32),
        result=sds((2, piece, width), bf16),
        o_down=sds((2, share, fhalf), f32),
    )
    scratch = dict(
        dy=VM((4, piece, width), bf16),
        act=VM((rows, fhalf), bf16),
        w_down=VM((shards, share, fhalf), bf16),
        fgate=VM((rows, fhalf), bf16),
        fup=VM((rows, fhalf), bf16),
        normed2=VM((rows, width), bf16),
        w_gu=VM((shards, share, two), bf16),
        res=VM((4, piece, width), f32),
        gains=VM((8, width), f32),
        wo=VM((shards // 2, share, width), bf16),
        theirs2=VM((4, piece, width), bf16),
        f_gate=VM((2, share, fhalf), f32),
        mine=VM((4, piece, width), bf16),
        theirs=VM((2, piece, width), bf16),
        part=VM((4, piece, width), bf16),
        dgu=VM((rows, two), bf16),
        g_down=VM((shards, share, fhalf), bf16),
        f_down=VM((2, share, fhalf), f32),
        gup=VM((2, shards // 4, share, fhalf), bf16),
        loc_sem=pltpu.SemaphoreType.DMA((40,)),
        send_sem=pltpu.SemaphoreType.DMA((16,)),
        recv_sem=pltpu.SemaphoreType.DMA((16,)),
    )
    for k, (name, hf, cols, order) in enumerate(MIDDLE):
        slots, sent = Scatter.slots_of(levels, order)
        first, last = span_of(cols, f["w_down"])
        scratch["room%d" % k] = VM((slots, share, last - first), bf16)
        scratch["ss%d" % k] = pltpu.SemaphoreType.DMA((sent,))
        scratch["sr%d" % k] = pltpu.SemaphoreType.DMA((slots,))
    cfg = dict(
        share=share, width=width, fhalf=fhalf, piece=piece, rows=rows,
        program=[2.5, 2.5] + [1.0] * 4 + [2.0] + [1.8] * 4 + [4.0] + [1.5] * 4 + [4.0, 3.0, 4.0],
    )
    return call(middle_kernel, ins, outs, scratch, 4, 63, levels, cfg)


def body(tokens, cotangent, starts, norm_gain, qkv_weight, conv_weight, beta_weight,
         head_gain, out_weight, gate_up_weight, down_weight):
    levels = lax.axis_size("dp") // 2
    ctx = lax.axis_size("ctx")
    device = lax.axis_index("dp") * ctx + lax.axis_index("ctx")
    t = lax.axis_index("ctx") % 2
    m = lax.axis_index("ctx") // 2
    batches, _, piece, width = tokens.shape
    rows = ctx * piece
    share = qkv_weight.shape[1]
    hidden = gate_up_weight.shape[2]
    half, fhalf = width // 2, hidden // 2
    heads_all = beta_weight.shape[1]
    heads = heads_all // 2
    per = head_gain.shape[0]
    small = 2 + 3 * CONV + heads_all + 1

    gain_rows = jnp.zeros((share, 1), bf16).at[:per, 0].set(head_gain)
    ext = jnp.concatenate(
        [norm_gain.T, conv_weight.T, beta_weight, gain_rows, jnp.zeros((share, HD - small), bf16)],
        axis=1,
    )
    flags = jnp.broadcast_to(
        starts.reshape(batches, piece, 1).astype(bf16), (batches, piece, HD)
    )
    f = forward(
        qkv_weight, out_weight, gate_up_weight, down_weight, ext,
        tokens[:, 0], cotangent[:, 0], flags, levels, per, heads_all,
    )
    g = middle(f, levels)
    b = backward(f, g, levels, per, heads_all)
    join = lambda o, n: jnp.moveaxis(o.reshape(2, share, n, -1), (2, 1), (0, 1)).reshape(n, share, -1)
    o_small = jnp.sum(b["o_small"], axis=0)
    o_q = b["o_q"].reshape(2, half // HD, share, 3, HD)
    return (
        b["lo_out"][:, None],
        b["dx_out"][:, None],
        o_small[:, 0:2].T,
        jnp.transpose(o_q, (3, 2, 0, 1, 4)).reshape(3, share, width),
        o_small[:, 2 : 2 + 3 * CONV].T,
        o_small[:, 2 + 3 * CONV : 2 + 3 * CONV + heads_all],
        o_small[:per, small - 1],
        join(b["o_out"], 1)[0],
        jnp.stack([join(g["o_gate"], 1)[0], join(b["o_up"], 1)[0]]),
        join(g["o_down"], 1)[0],
    )


def solution(mesh):
    both = ("dp", "ctx")
    acts = P(None, "dp", "ctx", None)
    return jax.shard_map(
        body,
        mesh=mesh,
        in_specs=(
            acts,
            acts,
            P(None, "dp", "ctx"),
            P(None, both),
            P(None, both, None),
            P(None, both),
            P(both, None),
            P(both),
            P(both, None),
            P(None, both, None),
            P(both, None),
        ),
        out_specs=(
            acts,
            acts,
            P(None, both),
            P(None, both, None),
            P(None, both),
            P(both, None),
            P(both),
            P(both, None),
            P(None, both, None),
            P(both, None),
        ),
        check_vma=False,
    )
```

```python
import functools

import jax
import jax.numpy as jnp
from jax import lax
from jax.experimental import pallas as pl
from jax.experimental.pallas import tpu as pltpu
from jax.sharding import PartitionSpec as P

MESH = pl.DeviceIdType.MESH
ANY = pl.ANY
VM = pltpu.VMEM
MIB = 1 << 20
f32 = jnp.float32
bf16 = jnp.bfloat16


def route(block, order):
    dz, fx, fy = block
    rank = {dim: place for place, dim in enumerate(order)}
    last = max([-1] + [rank[d] for d, on in (("z", dz), ("x", fx), ("y", fy)) if on])
    hops = []
    for dim in order:
        if dim == "z":
            if dz == 0 and rank["z"] > last:
                hops += ["up", "dn"]
            elif dz != 0 and last == rank["z"]:
                hops.append("up" if dz < 0 else "dn")
        elif rank[dim] > last:
            hops.append(dim)
    came = None
    if last >= 0:
        came = order[last]
        if came == "z":
            came = "up" if dz < 0 else "dn"
    return hops, came


def blocks_of(levels):
    named = [
        (dz, fx, fy)
        for dz in range(1 - levels, levels)
        for fx in (0, 1)
        for fy in (0, 1)
    ]
    return sorted(named, key=lambda b: (abs(b[0]) + b[1] + b[2], abs(b[0]), b))


class Place:
    def __init__(self, levels):
        i = lax.axis_index("dp")
        c = lax.axis_index("ctx")
        self.levels = levels
        self.i, self.c = i, c
        self.z, self.y = i // 2, i % 2
        self.x, self.t = c // 2, c % 2

    def device(self, hop):
        i, c = self.i, self.c
        if hop == "x":
            return {"dp": i, "ctx": (1 - self.x) * 2 + self.t}
        if hop == "y":
            return {"dp": self.z * 2 + 1 - self.y, "ctx": c}
        if hop == "up":
            return {"dp": i + 2, "ctx": c}
        if hop == "dn":
            return {"dp": i - 2, "ctx": c}
        return {"dp": i, "ctx": self.x * 2 + 1 - self.t}

    def valid(self, block, hop=None):
        dz = block[0]
        terms = []
        if dz > 0:
            terms.append(self.z + dz < self.levels)
        if dz < 0:
            terms.append(self.z + dz >= 0)
        if hop == "up" and dz <= 0:
            terms.append(self.z + 1 < self.levels)
        if hop == "dn" and dz >= 0:
            terms.append(self.z >= 1)
        if not terms:
            return None
        return functools.reduce(jnp.logical_and, terms)

    def level(self, block):
        return self.z + block[0]

    def shard(self, block, half):
        z = self.z + block[0]
        y = 1 - self.y if block[2] else self.y
        x = 1 - self.x if block[1] else self.x
        chip = (z * 2 + y) * 2 + x
        if half is None:
            return pl.ds(chip * 2, 2)
        return chip * 2 + half

    def meet(self, hops):
        barrier = pltpu.get_barrier_semaphore()
        count = 0
        for hop in hops:
            def greet(hop=hop):
                pl.semaphore_signal(
                    barrier, inc=1, device_id=self.device(hop), device_id_type=MESH
                )
            if hop in ("up", "dn"):
                here = (self.z + 1 < self.levels) if hop == "up" else (self.z >= 1)
                pl.when(here)(greet)
                count = count + here.astype(jnp.int32)
            else:
                greet()
                count = count + 1
        pl.semaphore_wait(barrier, count)


def when(condition, action):
    if condition is None:
        action()
    else:
        pl.when(condition)(action)


def send_slots(order):
    table = {}
    for fx in (0, 1):
        for fy in (0, 1):
            for dz in (-1, 0, 1):
                for hop in route((dz, fx, fy), order)[0]:
                    table.setdefault((hop, fx, fy), len(table))
    return table


class Gather:
    def __init__(self, place, ref, half, cols, order, send_sem, recv_sem):
        self.place, self.ref, self.half = place, ref, half
        self.cols = slice(*cols)
        self.order = order
        self.slots = send_slots(order)
        self.send_sem, self.recv_sem = send_sem, recv_sem

    @staticmethod
    def sems(levels, order):
        return len(send_slots(order)) * levels, 4 * levels

    def copy(self, block, hop):
        place = self.place
        dz, fx, fy = block
        where = place.shard(block, self.half)
        level = place.level(block)
        there = (fx ^ (hop == "x"), fy ^ (hop == "y"))
        return pltpu.make_async_remote_copy(
            src_ref=self.ref.at[where, :, self.cols],
            dst_ref=self.ref.at[where, :, self.cols],
            send_sem=self.send_sem.at[self.slots[hop, fx, fy] * place.levels + level],
            recv_sem=self.recv_sem.at[(there[0] * 2 + there[1]) * place.levels + level],
            device_id=place.device(hop),
            device_id_type=MESH,
        )

    def arrival(self, block):
        place = self.place
        dz, fx, fy = block
        where = place.shard(block, self.half)
        came = route(block, self.order)[1]
        back = {"up": "dn", "dn": "up"}.get(came, came)
        return pltpu.make_async_remote_copy(
            src_ref=self.ref.at[where, :, self.cols],
            dst_ref=self.ref.at[where, :, self.cols],
            send_sem=self.send_sem.at[0],
            recv_sem=self.recv_sem.at[(fx * 2 + fy) * place.levels + place.level(block)],
            device_id=place.device(back),
            device_id_type=MESH,
        )

    def wait(self, block):
        when(self.place.valid(block), lambda: self.arrival(block).wait_recv())

    def pass_on(self, block, only=("x", "y", "up", "dn")):
        for hop in route(block, self.order)[0]:
            if hop not in only:
                continue
            when(self.place.valid(block, hop), lambda hop=hop: self.copy(block, hop).start())

    def drain(self, blocks):
        for block in blocks:
            for hop in route(block, self.order)[0]:
                when(
                    self.place.valid(block, hop),
                    lambda hop=hop: self.copy(block, hop).wait_send(),
                )


def room_table(order, levels):
    table, used = {}, 0
    for fx in (0, 1):
        for fy in (0, 1):
            here = route((0, fx, fy), order)[0]
            away = route((1, fx, fy), order)[0] + route((-1, fx, fy), order)[0]
            for hop in ("x", "y"):
                if hop in here or hop in away:
                    table[hop, fx, fy] = (used, hop in away)
                    used += levels if hop in away else 1
            if "up" in here + away or "dn" in here + away:
                table["z", fx, fy] = (used, True)
                used += levels + 1
    return table, used


class Scatter:
    def __init__(self, place, ref, room, final, half, cols, order, send_sem, recv_sem):
        self.place, self.ref, self.room, self.final = place, ref, room, final
        self.half, self.order = half, order
        self.cols = slice(*cols)
        self.table = room_table(order, place.levels)[0]
        self.send_sem, self.recv_sem = send_sem, recv_sem

    @staticmethod
    def slots_of(levels, order):
        return room_table(order, levels)[1], 4 * levels

    def slot_at(self, hop, dz, fx, fy, level):
        base, many = self.table["z" if hop in ("up", "dn") else hop, fx, fy]
        if hop == "dn" and dz == 0:
            return base + self.place.levels + 0 * self.place.z
        return base + level if many else base + 0 * self.place.z

    def slot(self, block, hop):
        return self.slot_at(hop, *block, self.place.level(block))

    def copy(self, block, src):
        place = self.place
        dz, fx, fy = block
        came = route(block, self.order)[1]
        back = {"up": "dn", "dn": "up"}.get(came, came)
        there = (
            dz + (came == "up") - (came == "dn"),
            fx ^ (came == "x"),
            fy ^ (came == "y"),
        )
        slot = self.slot_at(came, *there, place.level(block))
        return pltpu.make_async_remote_copy(
            src_ref=src,
            dst_ref=self.room.at[slot],
            send_sem=self.send_sem.at[(fx * 2 + fy) * place.levels + place.level(block)],
            recv_sem=self.recv_sem.at[slot],
            device_id=place.device(back),
            device_id_type=MESH,
        )

    def arrive(self, block, hop):
        slot = self.slot(block, hop)
        pltpu.make_async_remote_copy(
            src_ref=self.room.at[slot],
            dst_ref=self.room.at[slot],
            send_sem=self.send_sem.at[0],
            recv_sem=self.recv_sem.at[slot],
            device_id=self.place.device(hop),
            device_id_type=MESH,
        ).wait_recv()

    def in_room(self, slot, at):
        return (slot, at) if self.half is not None else (slot, slice(None), at)

    def in_final(self, at):
        return (slice(None) if self.half is None else self.half, at, self.cols)

    def total(self, block, hops, put):
        where = self.place.shard(block, self.half)
        slots = [self.slot(block, hop) for hop in hops]
        rows = self.ref.shape[1]
        step = min(16, rows)

        def one(k, carry):
            at = pl.ds(pl.multiple_of(k * step, step), step)
            value = self.ref[where, at, self.cols].astype(f32)
            for slot in slots:
                value = value + self.room[self.in_room(slot, at)].astype(f32)
            put(at, value)
            return carry

        lax.fori_loop(0, rows // step, one, 0)

    def branch(self, maybe, using, go):
        if not maybe:
            go(using)
            return
        hop, place = maybe[0], self.place
        here = place.z + 1 < place.levels if hop == "up" else place.z >= 1
        pl.when(here)(lambda: self.branch(maybe[1:], using + [hop], go))
        pl.when(jnp.logical_not(here))(lambda: self.branch(maybe[1:], using, go))

    def forward(self, block):
        place = self.place
        hops = route(block, self.order)[0]
        sure = [h for h in hops if h in ("x", "y")]
        maybe = [h for h in hops if h not in ("x", "y")]

        def go(using):
            for hop in using:
                self.arrive(block, hop)
            if not using:
                self.copy(block, self.ref.at[place.shard(block, self.half), :, self.cols]).start()
                return
            slot = self.slot(block, using[0])

            def put(at, value):
                self.room[self.in_room(slot, at)] = value.astype(bf16)

            self.total(block, using, put)
            self.copy(block, self.room.at[slot]).start()

        def both():
            self.branch(maybe, sure, go)

        when(place.valid(block), both)

    def finish(self):
        own = (0, 0, 0)
        place = self.place
        hops = route(own, self.order)[0]
        sure = [h for h in hops if h in ("x", "y")]
        for hop in sure:
            self.arrive(own, hop)

        def put(at, value):
            self.final[self.in_final(at)] = value

        self.total(own, sure, put)
        for hop in hops:
            if hop in sure:
                continue

            def add(hop=hop):
                self.arrive(own, hop)
                slot = self.slot(own, hop)
                every = self.in_final(slice(None))
                self.final[every] = self.final[every] + self.room[slot].astype(f32)

            when(place.valid(own, hop), add)

    def drain(self, blocks):
        for block in blocks:
            if block == (0, 0, 0):
                continue
            when(
                self.place.valid(block),
                lambda block=block: self.copy(
                    block, self.ref.at[self.place.shard(block, self.half), :, self.cols]
                ).wait_send(),
            )


OWN = (0, 0, 0)

RATE = 0.038
LATE = 2
HOP = 1.6


class Step:
    def __init__(self, run, valid, needs, sends, cost, group, rank):
        self.run, self.valid, self.needs, self.sends = run, valid, needs, sends
        self.cost, self.group, self.rank = cost, group, rank


def exists(block, z, levels):
    return 0 <= z + block[0] < levels


def can_hop(z, hop, levels):
    return {"up": z + 1 < levels, "dn": z >= 1}.get(hop, True)


def moved(block, hop):
    dz, fx, fy = block
    return (dz - (hop == "up") + (hop == "dn"), fx ^ (hop == "x"), fy ^ (hop == "y"))


def level_of(z, hop):
    return z + (hop == "up") - (hop == "dn")


def height(block, order, levels):
    if abs(block[0]) >= levels:
        return -1
    return max([0] + [1 + height(moved(block, h), order, levels) for h in route(block, order)[0]])


def crossing_step(run, size, group, key):
    return Step(
        run, lambda z: True, lambda z: [("own", group)], lambda z: [("x", size, (key, z))],
        0.2, group, 0,
    )


def gather_steps(streams, group_of, size_of, levels, begin=None):
    steps = []
    for k, s in enumerate(streams):
        for block in blocks_of(levels):
            seen = []
            for ways in (("up", "dn"), ("x",), ("y",)):
                hops = [h for h in route(block, s.order)[0] if h in ways]
                if not hops:
                    continue

                def needs(z, k=k, block=block):
                    return [("own", group_of[k])] if block == OWN else [(k, z, block)]

                def sends(z, k=k, block=block, hops=hops):
                    return [
                        (h, size_of[k], (k, level_of(z, h), moved(block, h)))
                        for h in hops
                        if can_hop(z, h, levels)
                    ]

                def run(s=s, k=k, block=block, ways=ways, seen=seen):
                    if not seen:
                        seen.append(True)
                        if block != OWN:
                            s.wait(block)
                        else:
                            begin(group_of[k])
                    s.pass_on(block, ways)

                lane = group_of[k]
                if s.order[0] != "z":
                    lane = LATE if "up" in ways else 0
                steps.append(
                    Step(
                        run,
                        lambda z, block=block: exists(block, z, levels),
                        needs,
                        sends,
                        0.15,
                        lane,
                        -max(1 + height(moved(block, h), s.order, levels) for h in hops),
                    )
                )
    return steps


def scatter_steps(streams, group_of, size_of, levels):
    steps = []
    for k, s in enumerate(streams):
        for block in blocks_of(levels)[::-1]:
            if block == OWN:
                continue
            hops, came = route(block, s.order)
            back = {"up": "dn", "dn": "up"}.get(came, came)

            def needs(z, k=k, block=block, hops=hops):
                got = [(k, z, block, h) for h in hops if can_hop(z, h, levels)]
                return got or [("own", group_of[k])]

            def sends(z, k=k, block=block, came=came, back=back):
                there = moved(block, back)
                return [(back, size_of[k], (k, level_of(z, back), there, came))]

            steps.append(
                Step(
                    lambda s=s, block=block: s.forward(block),
                    lambda z, block=block: exists(block, z, levels),
                    needs,
                    sends,
                    0.15 + (1.5 * size_of[k] if hops else 0.0),
                    group_of[k],
                    -abs(block[0]) - block[1] - block[2],
                )
            )
    return steps


def plan(steps, program, levels, own, gates, slack=0.0, events=None):
    now = [0.0] * levels
    free = [dict(x=0.0, y=0.0, up=0.0, dn=0.0) for _ in range(levels)]
    there = {("own", g): at for g, at in own.items()}
    left = list(steps)
    out = []

    def ready(step):
        times = []
        for z in range(levels):
            if not step.valid(z):
                continue
            for key in step.needs(z):
                if key not in there:
                    return None
                times.append((there[key], now[z]))
        return times

    def do(step):
        for z in range(levels):
            if not step.valid(z):
                continue
            now[z] = max([now[z]] + [there[key] for key in step.needs(z)]) + step.cost
        for z in range(levels):
            if not step.valid(z):
                continue
            for hop, size, key in step.sends(z):
                begin = max(now[z], free[z][hop])
                free[z][hop] = begin + size / RATE
                there[key] = free[z][hop] + HOP
        left.remove(step)

    def quick(step):
        times = ready(step)
        return times is not None and all(at + slack <= when + 0.3 for at, when in times)

    def drain_ready(batch, held):
        while True:
            able = [s for s in left if s.group not in held and quick(s)]
            if not able:
                return
            step = min(able, key=lambda s: (s.group, s.rank))
            do(step)
            batch.append(step)

    def wait_for(step):
        return max([max(at - when, 0.0) for at, when in ready(step)] + [0.0])

    def until(batch, done):
        while left and not done():
            able = [s for s in left if ready(s) is not None]
            if not able:
                return
            first = min(s.group for s in able)

            def idle(s):
                return all(
                    free[z][hop] <= now[z] + 1.0
                    for z in range(levels)
                    if s.valid(z)
                    for hop, _, _ in s.sends(z)
                )

            pool = [s for s in able if s.group == first or idle(s)]
            step = min(pool, key=lambda s: (round(wait_for(s), 1), s.group, s.rank))
            do(step)
            batch.append(step)

    for place, duration in enumerate(program):
        batch = []
        for group in (events or {}).get(place, ()):
            there["own", group] = max(now)
        keys = gates.get(place)
        if keys:
            until(batch, lambda: all(k in there for z in range(levels) for k in keys(z)))
            limit = [max(there[k] for k in keys(z)) for z in range(levels)]
            while True:
                able = [
                    s
                    for s in left
                    if ready(s) is not None
                    and all(
                        max(now[z], *(there[k] for k in s.needs(z))) + s.cost <= limit[z]
                        for z in range(levels)
                        if s.valid(z)
                    )
                ]
                if not able:
                    break
                step = min(able, key=lambda s: (round(wait_for(s), 1), s.group, s.rank))
                do(step)
                batch.append(step)
            for z in range(levels):
                now[z] = max(now[z], limit[z])
        drain_ready(batch, ())
        out.append(batch)
        for z in range(levels):
            now[z] += duration
    batch = []
    for group in (events or {}).get(len(program), ()):
        there["own", group] = max(now)
    until(batch, lambda: False)
    out.append(batch)
    return out, max(now), max([at for at in there.values()] + [0.0])


class Planned:
    def __init__(self, batches):
        self.batches = list(batches)

    def take(self):
        return self.batches.pop(0)

    def tick(self):
        for step in self.take():
            step.run()

    def looped(self, count, each=1):
        now = [self.take() for _ in range(count * each)]

        def at(index, which=0):
            for k, steps in enumerate(now[which::each]):
                if steps:
                    pl.when(index == k)(lambda steps=steps: [s.run() for s in steps] and None)

        return at

    def finish(self):
        while self.batches:
            self.tick()


HD = 128
CONV = 4
SPAN = 128


def mm(a, b):
    return jnp.dot(a, b, preferred_element_type=f32)


def mm_nt(a, b):
    return lax.dot_general(a, b, (((1,), (1,)), ((), ())), preferred_element_type=f32)


def mm_tn(a, b):
    return lax.dot_general(a, b, (((0,), (0,)), ((), ())), preferred_element_type=f32)


def lanes(h):
    return pl.ds(pl.multiple_of(h * HD, HD), HD)


def set_masks(segc, keep):
    rows = lax.broadcasted_iota(jnp.int32, segc.shape, 0)
    seg = segc[...]
    for o in range(1, CONV):
        same = (pltpu.roll(seg, o, 0) == seg) & (rows >= o)
        keep[o - 1] = same.astype(f32)


def shifted(value, keep, o):
    return value if o == 0 else pltpu.roll(value, o, 0) * keep[o - 1]


def conv_of(proj, taps, keep, j, h, heads):
    at = lanes(j * heads + h)
    value = proj[:, at].astype(f32)
    total = taps[pl.ds(j * CONV + CONV - 1, 1), lanes(h)] * value
    for o in range(1, CONV):
        total = total + taps[pl.ds(j * CONV + CONV - 1 - o, 1), lanes(h)] * shifted(value, keep, o)
    return total


def span_masks(segc, segr, n):
    at = slice(n * SPAN, (n + 1) * SPAN)
    col = segc[at, :]
    same = col == jnp.broadcast_to(segr[0:1, at], (SPAN, SPAN))
    if n:
        carried = (col == segc[n * SPAN - 1 : n * SPAN, :]).astype(f32)
    else:
        carried = jnp.zeros((SPAN, HD), f32)
    ending = (col == col[SPAN - 1 : SPAN, :]).astype(f32)
    return carried, same, ending


def iotas():
    i = lax.broadcasted_iota(jnp.int32, (SPAN, SPAN), 0)
    j = lax.broadcasted_iota(jnp.int32, (SPAN, SPAN), 1)
    return i, j


def unit_inverses(lowers):
    i, j = iotas()
    apart = i ^ j
    invs = [jnp.where(apart == 1, -low, 0.0) for low in lowers]
    size, bits = 2, 1
    while size < SPAN:
        pairs = lax.shift_right_logical(apart, bits) == 1
        part = [jnp.where(pairs, low, 0.0) for low in lowers]
        small = [inv.astype(bf16) for inv in invs]
        left = [p + mm(s, p.astype(bf16)) for p, s in zip(part, small)]
        both = [w + mm(w.astype(bf16), s) for w, s in zip(left, small)]
        invs = [inv - b for inv, b in zip(invs, both)]
        size, bits = size * 2, bits + 1
    return invs


SLACK_F = 0.0


class Names:
    def __init__(self, names, refs):
        self.__dict__.update(zip(names, refs, strict=True))


class Sems:
    def __init__(self, ref):
        self.ref, self.used = ref, 0

    def take(self):
        self.used += 1
        return self.ref.at[self.used - 1]


def call(kernel, ins, outs, scratch, number, limit, *static):
    names = list(ins) + list(outs) + list(scratch)

    def run(*refs):
        kernel(Names(names, refs), *static)

    results = pl.pallas_call(
        run,
        out_shape=list(outs.values()),
        in_specs=[pl.BlockSpec(memory_space=ANY)] * len(ins),
        out_specs=[pl.BlockSpec(memory_space=ANY)] * len(outs),
        scratch_shapes=list(scratch.values()),
        compiler_params=pltpu.CompilerParams(
            collective_id=number, has_side_effects=True, vmem_limit_bytes=limit * MIB
        ),
    )(*ins.values())
    return dict(zip(outs, results, strict=True))


class Local:
    def __init__(self, sems):
        self.sems, self.open = sems, []

    def start(self, src, dst):
        copy = pltpu.make_async_copy(src, dst, self.sems.take())
        copy.start()
        self.open.append(copy)
        return copy

    def holds(self, copy):
        return any(copy is other for other in self.open)

    def wait(self, copy):
        copy.wait()
        self.open = [other for other in self.open if other is not copy]

    def done(self):
        for copy in self.open:
            copy.wait()
        self.open = []


class Remote:
    def __init__(self, place, sent, got):
        self.place, self.sent, self.got, self.open = place, sent, got, []

    def start(self, src, dst, hop):
        copy = self.make(src, dst, hop)
        copy.start()
        return copy

    def make(self, src, dst, hop):
        copy = pltpu.make_async_remote_copy(
            src_ref=src,
            dst_ref=dst,
            send_sem=self.sent.take(),
            recv_sem=self.got.take(),
            device_id=self.place.device(hop),
            device_id_type=MESH,
        )
        self.open.append(copy)
        return copy

    def drain(self):
        for copy in self.open:
            copy.wait_send()
        self.open = []


def unflat(value, share):
    return value.reshape(value.shape[0] // share, share, value.shape[1]).astype(bf16)


def flat(ref, cols):
    value = ref[:, :, cols]
    shape = (value.shape[0] * value.shape[1], value.shape[2])
    if value.shape[1] % 16:
        return value.astype(f32).reshape(shape).astype(bf16)
    return value.reshape(shape)


STREAMS = (
    (0, 0, (0, 6), "zxy"),
    (0, 0, (6, None), "zyx"),
    (0, 1, (0, 10), "zxy"),
    (0, 1, (10, None), "zyx"),
    (1, 0, None, "zxy"),
    (1, 1, None, "xyz"),
    (2, 0, None, "zyx"),
    (2, 1, None, "zxy"),
)


def span_of(cols, ref):
    if cols is None:
        return 0, ref.shape[2]
    first, last = cols
    return first * HD, ref.shape[2] if last is None else last * HD


NEIGHBOURS = ("x", "y", "up", "dn", "core")


def forward_kernel(r, levels, cfg):
    heads, spans, per, share = cfg["heads"], cfg["spans"], cfg["per"], cfg["share"]
    width, half, fhalf, heads_all = cfg["width"], cfg["half"], cfg["fhalf"], cfg["heads_all"]
    piece, rows = cfg["piece"], cfg["rows"]
    pc = Place(levels)
    loc = Local(Sems(r.loc_sem))
    rem = Remote(pc, Sems(r.send_sem), Sems(r.recv_sem))
    pc.meet(NEIGHBOURS)
    own = pc.shard(OWN, pc.t)
    targets = (r.w1, r.w_gu, r.w_down)
    streams = [
        Gather(pc, targets[a], hf, span_of(cols, targets[a]), order,
               r.__dict__["gs%d" % k], r.__dict__["gr%d" % k])
        for k, (a, hf, cols, order) in enumerate(STREAMS)
    ]
    def both(src_at, dst):
        return [loc.start(src_at(pc.t), dst), rem.start(src_at(1 - pc.t), dst, "core")]

    def cut(n, t):
        return pl.ds(pl.multiple_of(t * n, n), n)

    opening = []
    for j in range(3):
        opening += both(
            lambda t, j=j: r.qkv.at[j, :, cut(half, t)],
            r.w1.at[own, :, j * half : (j + 1) * half],
        )
    opening += both(lambda t: r.out_w.at[:, cut(half, t)], r.w1.at[own, :, 3 * half : 4 * half])
    opening += both(lambda t: r.ext, r.w1.at[own, :, 4 * half : 4 * half + HD])
    pieces = both(lambda t: r.tok.at[pc.x], r.x.at[pc.c])
    pieces += both(lambda t: r.flags.at[pc.x], r.marks.at[pc.c])

    def arrived(copies):
        for copy in copies:
            if loc.holds(copy):
                loc.wait(copy)
            else:
                copy.wait_recv()

    arrived(opening)
    second = []
    for j in range(2):
        second += both(
            lambda t, j=j: r.gu.at[j, :, cut(fhalf, t)],
            r.w_gu.at[own, :, j * fhalf : (j + 1) * fhalf],
        )
    second += both(lambda t: r.dn.at[:, cut(fhalf, t)], r.w_down.at[own])
    second += both(lambda t: r.cot.at[pc.x], r.dy.at[pc.c])
    hold = {1: second[:4], 2: second[4:6]}
    far = (1 - pc.x) * 2 + pc.t
    crossed = {
        name: rem.make(src.at[1 - pc.x], dst.at[pc.c], "x")
        for name, src, dst in (("x", r.tok, r.x), ("m", r.flags, r.marks), ("dy", r.cot, r.dy))
    }

    groups = [a for a, *_ in STREAMS]
    firsts = [k for k, a in enumerate(groups) if a == 0]
    mb = lambda n, m: 2e-6 * n * m
    steps = gather_steps(
        streams, groups, [mb(share, s.cols.stop - s.cols.start) for s in streams], levels,
        lambda a: arrived(hold.pop(a, [])),
    )
    steps.append(crossing_step(lambda: (crossed["x"].start(), crossed["m"].start()),
                               mb(piece, width + HD), 0, "tok"))
    steps.append(crossing_step(crossed["dy"].start, mb(piece, width), 3, "cot"))
    ordered = blocks_of(levels)

    def gate(z):
        return [("tok", z)] + [
            (k, z, block)
            for k in firsts
            for block in ordered
            if block != OWN and exists(block, z, levels)
        ]

    def gate1(z):
        return [
            (k, z, block)
            for k, a in enumerate(groups)
            for block in ordered
            if a == 1 and block != OWN and exists(block, z, levels)
        ]

    later = Planned(
        plan(
            steps, cfg["program"], levels, {0: 4.0, 1: 6.0, 2: 7.0, 3: 7.0},
            {0: gate, len(cfg["program"]) - rows // piece: gate1}, SLACK_F,
        )[0]
    )
    later.tick()
    crossed["x"].wait_recv()
    crossed["m"].wait_recv()
    arrived(pieces)
    pieces = [
        rem.start(r.x.at[far], r.x.at[far], "core"),
        rem.start(r.marks.at[far], r.marks.at[far], "core"),
    ]
    for block in ordered:
        for k in firsts:
            s = streams[k]
            if block != OWN and not route(block, s.order)[0]:
                s.wait(block)
    arrived(pieces)

    i, j = iotas()
    upto = (i >= j).astype(bf16)
    base = jnp.zeros((1, HD), f32)
    for n in range(spans):
        q, at = divmod(n * SPAN, piece)
        marks = r.marks[q, at : at + SPAN, :]
        seg = mm(upto, marks) + base
        r.segc[n * SPAN : (n + 1) * SPAN, :] = seg
        r.segr[:, n * SPAN : (n + 1) * SPAN] = jnp.transpose(seg)[0:8, :]
        base = seg[SPAN - 1 : SPAN, :]
    set_masks(r.segc, r.keep)
    loc.start(r.segc, r.segc_out)
    loc.start(r.segr, r.segr_out)

    shards = levels * 8 // 2
    mine = cut(half, pc.t)
    rows_of = lambda t: pl.ds(pl.multiple_of(t * shards, shards), shards)
    side = pl.ds(3 * half, half)
    swap_out = [
        loc.start(r.w1.at[rows_of(pc.t), :, side], r.wo.at[:, :, mine]),
        rem.start(r.w1.at[rows_of(1 - pc.t), :, side], r.wo.at[:, :, mine], "core"),
    ]

    extra = flat(r.w1, slice(4 * half, 4 * half + HD))
    for n in range(width // SPAN):
        at = slice(n * SPAN, (n + 1) * SPAN)
        r.small[:, at] = jnp.transpose(extra[at, :].astype(f32))[0:32, :]
    r.gains[...] = r.small[0:8, :]
    r.taps[...] = jnp.zeros(r.taps.shape, f32)
    r.taps[0 : 3 * CONV, :] = r.small[2 : 2 + 3 * CONV, cut(half, pc.t)]
    place_r = lax.broadcasted_iota(jnp.int32, (width, HD), 0)
    place_c = lax.broadcasted_iota(jnp.int32, (width, HD), 1)
    chosen = (place_r == share * (place_c // per) + place_c % per).astype(bf16)
    at = 2 + 3 * CONV + heads_all
    r.hgain[...] = jnp.broadcast_to(
        mm(r.small[at - at % 8 : at - at % 8 + 8, :].astype(bf16), chosen)[at % 8 : at % 8 + 1, :],
        (8, HD),
    )
    pick_r = lax.broadcasted_iota(jnp.int32, (HD, half), 0)
    pick_c = lax.broadcasted_iota(jnp.int32, (HD, half), 1)
    chosen = (pick_r == 2 + 3 * CONV + heads * pc.t + pick_c // HD).astype(bf16)
    w_beta = mm(extra, chosen)
    r.wbeta[...] = unflat(w_beta, share)
    pick_r = lax.broadcasted_iota(jnp.int32, (HD, HD), 0)
    pick_c = lax.broadcasted_iota(jnp.int32, (HD, HD), 1)
    chosen = ((pick_r == 2 + 3 * CONV + heads * pc.t + pick_c) & (pick_c < heads)).astype(bf16)
    r.wb[...] = unflat(mm(extra, chosen), share)
    loc.start(r.wb, r.wb_out)
    loc.start(r.w1.at[:, :, pl.ds(0, 3 * half)], r.wmix_out)
    loc.start(r.taps, r.taps_out)
    loc.start(r.gains, r.gains_out)
    loc.start(r.hgain, r.hgain_out)

    g0 = r.gains[0:1, :]
    for n in range(rows // piece):
        x = r.x[n].astype(f32)
        inv = lax.rsqrt(jnp.mean(x * x, axis=-1, keepdims=True) + 1e-5)
        value = x * inv * g0
        r.normed[n * piece : (n + 1) * piece, :] = value.astype(bf16)
        turned = jnp.transpose(value).astype(bf16)
        for m in range(width // piece):
            r.mine[m, :, n * piece : (n + 1) * piece] = turned[m * piece : (m + 1) * piece]
    normt = loc.start(r.mine, r.normt_out)
    loc.start(r.x, r.x_out)

    steps_at = later.looped(rows // piece)

    def project(k, carry):
        steps_at(k)
        at = pl.ds(pl.multiple_of(k * piece, piece), piece)
        left = r.normed[at, :]
        r.proj[at, :] = mm(left, flat(r.w1, slice(0, 3 * half))).astype(bf16)
        r.logit[at, :] = mm(left, flat(r.wbeta, slice(None)))
        r.blog[at, :] = mm(left, flat(r.wb, slice(None)))
        return carry

    lax.fori_loop(0, rows // piece, project, 0)
    loc.start(r.proj, r.proj_out)
    loc.start(r.blog, r.blog_out)

    prepare_at = later.looped(heads)

    def prepare(h, carry):
        prepare_at(h)
        delta_prepare(r, h, heads, spans)
        return carry

    lax.fori_loop(0, heads, prepare, 0)
    for src, dst in ((r.qs, r.qs_out), (r.ks, r.ks_out), (r.vs, r.vs_out), (r.ws, r.ws_out),
                     (r.ns, r.ns_out), (r.ps, r.ps_out)):
        loc.start(src, dst)
    delta_chain(r, heads, spans, later.tick)
    for h in range(heads):
        head = slice(h * HD, (h + 1) * HD)
        o = r.out[:, head]
        scale = lax.rsqrt(jnp.mean(o * o, axis=-1, keepdims=True) + 1e-5)
        r.headed[:, head] = (o * scale * r.hgain[0:1, :]).astype(bf16)
    for src, dst in ((r.fs, r.fs_out), (r.ss, r.ss_out), (r.out, r.out_out),
                     (r.headed, r.headed_out)):
        loc.start(src, dst)
    later.tick()
    arrived(swap_out)
    loc.start(r.wo, r.wo_out)
    wo = flat(r.wo, slice(None))
    loc.wait(normt)
    sent = []
    for n in range(rows // piece):
        r.mine[n] = mm(r.headed[n * piece : (n + 1) * piece, :], wo).astype(bf16)
        sent.append(rem.start(r.mine.at[n], r.theirs.at[n], "core"))
    later.tick()
    g1 = r.gains[1:2, :]
    for n in range(rows // piece):
        sent[n].wait_recv()
        at = slice(n * piece, (n + 1) * piece)
        res = r.x[n].astype(f32) + r.mine[n].astype(f32) + r.theirs[n].astype(f32)
        r.res[at, :] = res
        inv = lax.rsqrt(jnp.mean(res * res, axis=-1, keepdims=True) + 1e-5)
        r.normed2[at, :] = (res * inv * g1).astype(bf16)
    loc.start(r.res, r.res_out)
    loc.start(r.normed2, r.normed2_out)
    later.tick()
    for block in ordered:
        for n, s in enumerate(streams):
            if groups[n] == 1 and block != OWN and not route(block, s.order)[0]:
                s.wait(block)
    w_gate, w_up = flat(r.w_gu, slice(0, fhalf)), flat(r.w_gu, slice(fhalf, 2 * fhalf))
    loc.start(r.w_gu, r.w_gu_out)
    writes = {}
    few = piece // 2
    for n in range(rows // few):
        if n and n % 2 == 0:
            later.tick()
        at = slice(n * few, (n + 1) * few)
        left = r.normed2[at, :]
        gate, up = mm(left, w_gate), mm(left, w_up)
        sg = jax.nn.sigmoid(gate)
        for copy in writes.get(n % 2, ()):
            loc.wait(copy)
        r.act[n % 2] = (gate * sg * up).astype(bf16)
        r.fgate[n % 2] = (up * sg * (1.0 + gate * (1.0 - sg))).astype(bf16)
        r.fup[n % 2] = (gate * sg).astype(bf16)
        writes[n % 2] = [
            loc.start(src.at[n % 2], dst.at[pl.ds(n * few, few), :])
            for src, dst in ((r.act, r.act_out), (r.fgate, r.fgate_out), (r.fup, r.fup_out))
        ]
    later.finish()
    crossed["dy"].wait_recv()
    arrived(second[6:])
    last = rem.start(r.dy.at[far], r.dy.at[far], "core")
    for block in ordered:
        for k, s in enumerate(streams):
            if groups[k] == 2 and block != OWN and not route(block, s.order)[0]:
                s.wait(block)
    last.wait_recv()
    for s in streams:
        s.drain(ordered)
    rem.drain()
    loc.done()


def delta_prepare(r, h, heads, spans):
    i, j = iotas()
    mixed = []
    for which in range(3):
        value = conv_of(r.proj, r.taps, r.keep, which, h, heads)
        mixed.append(value * jax.nn.sigmoid(value))
    for which, dest in ((0, r.qs), (1, r.ks)):
        w = mixed[which]
        unit = w * lax.rsqrt(jnp.sum(w * w, axis=-1, keepdims=True) + 1e-6)
        dest[:, lanes(h)] = unit.astype(bf16)
    r.vs[:, lanes(h)] = mixed[2].astype(bf16)
    lowers, rights = [], []
    for n in range(spans):
        at = slice(n * SPAN, (n + 1) * SPAN)
        k = r.ks[at, lanes(h)]
        q = r.qs[at, lanes(h)]
        v = r.vs[at, lanes(h)]
        beta = jax.nn.sigmoid(r.logit[at, lanes(h)])
        carried, same, ending = span_masks(r.segc, r.segr, n)
        lowers.append(jnp.where(same & (i > j), beta * mm_nt(k, k), 0.0))
        r.ps[h * spans + n] = jnp.where(same & (i >= j), mm_nt(q, k), 0.0).astype(bf16)
        rights.append(
            jnp.concatenate([beta * v.astype(f32), (beta * carried) * k.astype(f32)], axis=1)
        )
    for n, inv in enumerate(unit_inverses(lowers)):
        at = slice(n * SPAN, (n + 1) * SPAN)
        small = inv.astype(bf16)
        r.ns[h * spans + n] = small
        both = rights[n] + mm(small, rights[n].astype(bf16))
        r.us[at, lanes(h)] = both[:, :HD]
        r.ws[at, lanes(h)] = both[:, HD:].astype(bf16)


def delta_chain(r, heads, spans, between):
    states = [jnp.zeros((HD, HD), f32) for _ in range(heads)]
    for n in range(spans):
        at = slice(n * SPAN, (n + 1) * SPAN)
        between()
        carried, same, ending = span_masks(r.segc, r.segr, n)
        for h in range(heads):
            head = slice(h * HD, (h + 1) * HD)
            state = states[h].astype(bf16)
            r.ss[h * spans + n] = state
            queries = (carried * r.qs[at, head].astype(f32)).astype(bf16)
            seen = mm(jnp.concatenate([r.ws[at, head], queries], axis=0), state)
            fresh = r.us[at, head] - seen[:SPAN]
            small = fresh.astype(bf16)
            r.fs[at, head] = small
            r.out[at, head] = seen[SPAN:] + mm(r.ps[h * spans + n], small)
            states[h] = carried[SPAN - 1 : SPAN, :] * states[h] + mm_tn(
                r.ks[at, head], (ending * fresh).astype(bf16)
            )


def forward(qkv, out_w, gu, dn, ext, tok, cot, flags, levels, per, heads_all):
    share = qkv.shape[1]
    width = qkv.shape[2]
    half, fhalf = width // 2, dn.shape[1] // 2
    piece = tok.shape[1]
    rows = 4 * piece
    heads = half // HD
    spans = rows // SPAN
    shards = levels * 8
    sds = jax.ShapeDtypeStruct
    wide, square = sds((rows, half), bf16), sds((heads * spans, SPAN, SPAN), bf16)
    seg = dict(
        segc=sds((rows, HD), f32),
        segr=sds((8, rows), f32),
        taps=sds((16, half), f32),
        gains=sds((8, width), f32),
        hgain=sds((8, HD), f32),
        x=sds((4, piece, width), bf16),
        proj=sds((rows, 3 * half), bf16),
        blog=sds((rows, HD), f32),
        qs=wide, ks=wide, vs=wide, fs=wide, ws=wide, headed=wide,
        ns=square, ps=square, ss=square,
        out=sds((rows, half), f32),
        wo=sds((shards // 2, share, width), bf16),
        res=sds((rows, width), f32),
        normed2=sds((rows, width), bf16),
    )
    ins = dict(qkv=qkv, out_w=out_w, gu=gu, dn=dn, ext=ext, tok=tok, cot=cot, flags=flags)
    outs = {
        "normt_out": sds((4, piece, width), bf16),
        "wmix_out": sds((shards, share, 3 * half), bf16),
        "wb_out": sds((shards, share, HD), bf16),
        "w_gu_out": sds((shards, share, 2 * fhalf), bf16),
        "act_out": sds((rows, fhalf), bf16),
        "fgate_out": sds((rows, fhalf), bf16),
        "fup_out": sds((rows, fhalf), bf16),
        "w_down": sds((shards, share, fhalf), bf16),
        "dy": sds((4, piece, width), bf16),
    }
    outs.update({k + "_out": v for k, v in seg.items()})
    scratch = {k: VM(v.shape, v.dtype) for k, v in seg.items()}
    scratch.update(
        w1=VM((shards, share, 4 * half + HD), bf16),
        w_gu=VM((shards, share, 2 * fhalf), bf16),
        act=VM((2, piece // 2, fhalf), bf16),
        fgate=VM((2, piece // 2, fhalf), bf16),
        fup=VM((2, piece // 2, fhalf), bf16),
        wbeta=VM((shards, share, half), bf16),
        wb=VM((shards, share, HD), bf16),
        marks=VM((4, piece, HD), bf16),
        keep=VM((CONV - 1, rows, HD), f32),
        small=VM((32, width), f32),
        us=VM((rows, half), f32),
        normed=VM((rows, width), bf16),
        logit=VM((rows, half), f32),
        mine=VM((4, piece, width), bf16),
        theirs=VM((4, piece, width), bf16),
        loc_sem=pltpu.SemaphoreType.DMA((80,)),
        send_sem=pltpu.SemaphoreType.DMA((32,)),
        recv_sem=pltpu.SemaphoreType.DMA((32,)),
    )
    for k, (a, hf, cols, order) in enumerate(STREAMS):
        sent, got = Gather.sems(levels, order)
        scratch["gs%d" % k] = pltpu.SemaphoreType.DMA((sent,))
        scratch["gr%d" % k] = pltpu.SemaphoreType.DMA((got,))
    cfg = dict(
        heads=heads, spans=spans, per=per, share=share, width=width, half=half, fhalf=fhalf,
        heads_all=heads_all, piece=piece, rows=rows,
        program=[6.0] + [2.0] * (rows // piece) + [4.0] * heads + [0.6] * spans + [1.0, 4.0]
        + [3.0] * (rows // piece),
    )
    return call(forward_kernel, ins, outs, scratch, 1, 63, levels, cfg)
SLACK_B = 4.0


def backward_kernel(r, levels, cfg):
    heads, spans, per, share = cfg["heads"], cfg["spans"], cfg["per"], cfg["share"]
    width, half, heads_all = cfg["width"], cfg["half"], cfg["heads_all"]
    piece, rows = cfg["piece"], cfg["rows"]
    pc = Place(levels)
    loc = Local(Sems(r.loc_sem))
    rem = Remote(pc, Sems(r.send_sem), Sems(r.recv_sem))
    pc.meet(NEIGHBOURS)
    pieces = rows // piece
    small_in = [loc.start(a, b) for a, b in (
        (r.gains_in, r.gains), (r.hgain_in, r.hgain), (r.taps_in, r.taps), (r.segc_in, r.segc),
        (r.segr_in, r.segr), (r.dheaded_in, r.dheaded))]
    normed_in = [loc.start(r.normed_in.at[n], r.theirs.at[n]) for n in range(pieces)]
    last_in = [loc.start(r.dres_in.at[k], r.res.at[k]) for k in range(pieces // 2)]
    last_in.append(loc.start(r.gain1_in, r.gain1))
    load = [loc.start(r.g_up_in, r.g_up), loc.start(r.g_out_in, r.g_out)]
    delta_in = [loc.start(a, b) for a, b in (
        (r.out_in, r.out), (r.blog_in, r.blog), (r.proj_in, r.dproj), (r.wb_in, r.wb),
        (r.qs_in, r.sv.at[0]), (r.ks_in, r.sv.at[1]), (r.vs_in, r.sv.at[2]),
        (r.fs_in, r.sv.at[3]), (r.ws_in, r.sv.at[4]),
        (r.ns_in, r.sq.at[0]), (r.ps_in, r.sq.at[1]), (r.ss_in, r.sq.at[2]))]
    streams = []
    for k, (name, h, hf, cols, order) in enumerate(RETURNS):
        grad, final = r.__dict__["g_" + name], r.__dict__["f_" + name]
        if h is not None:
            grad, final = grad.at[h], final.at[:, h]
        streams.append(
            Scatter(pc, grad, r.__dict__["room%d" % k], final, hf, span_of(cols, grad),
                    order, r.__dict__["ss%d" % k], r.__dict__["sr%d" % k])
        )

    def arrived(copies):
        for copy in copies:
            if loc.holds(copy):
                loc.wait(copy)
            else:
                copy.wait_recv()

    ordered = blocks_of(levels)[::-1]
    arrived(load)
    crossing = [
        rem.make(r.lo_in.at[1 - pc.x], r.lo_out.at[pc.x], "x"),
        rem.make(r.theirs.at[1 - pc.x], r.dx_out.at[pc.x], "x"),
    ]
    mb = lambda n, m: 2e-6 * n * m
    groups = [
        {"up": 0, "out": 1, "q": 2 + (h or 0), "small": 2 + heads}[name]
        for name, h, *_ in RETURNS
    ]
    steps = scatter_steps(
        streams, groups,
        [
            mb(share * (1 if s.half is not None else 2), s.cols.stop - s.cols.start)
            for s in streams
        ],
        levels,
    )
    steps.append(crossing_step(crossing[0].start, mb(piece, width), 0, "lo"))
    loc.start(r.lo_in.at[pc.x], r.lo_out.at[pc.x])
    start = heads + 2
    events = {len(cfg["program"]): [2 + heads]}
    for h in range(heads):
        events[start + h + 1] = [2 + h]
    later = Planned(plan(steps, cfg["program"], levels, {0: 0.0, 1: 0.0}, {}, SLACK_B, events)[0])
    later.tick()

    def cut(n, t):
        return pl.ds(pl.multiple_of(t * n, n), n)

    arrived(small_in)
    set_masks(r.segc, r.keep)
    arrived(delta_in)
    qs, ks, vs, fs, ws = (r.sv.at[k] for k in range(5))
    ns, ps, ss = (r.sq.at[k] for k in range(3))
    douts, xs = r.datt.at[0], r.datt.at[1]
    ys, hs, gs = r.headed, r.out, r.dheaded
    i, j = iotas()
    lane = lax.broadcasted_iota(jnp.int32, (SPAN, HD), 1)
    r.dlog[...] = jnp.zeros(r.dlog.shape, f32)

    norm_at = later.looped(heads)

    def norm_back(h, dgain_sum):
        norm_at(h)
        o = r.out[:, lanes(h)]
        dyh = r.dheaded[:, lanes(h)].astype(f32)
        inv = lax.rsqrt(jnp.mean(o * o, axis=-1, keepdims=True) + 1e-5)
        scaled = dyh * r.hgain[0:1, :]
        dout = inv * scaled - o * (inv * inv * inv * jnp.mean(scaled * o, axis=-1, keepdims=True))
        dgain_sum = dgain_sum + jnp.sum(dyh * o * inv, axis=0, keepdims=True)
        for n in range(spans):
            at = slice(n * SPAN, (n + 1) * SPAN)
            carried, same, ending = span_masks(r.segc, r.segr, n)
            small = dout[at].astype(bf16)
            douts[at, lanes(h)] = small
            x = mm_tn(ps[h * spans + n], small).astype(bf16)
            xs[at, lanes(h)] = x
            cdout = (carried * dout[at]).astype(bf16)
            hs[at, lanes(h)] = mm_tn(qs[at, lanes(h)], cdout) - mm_tn(ws[at, lanes(h)], x)
        return dgain_sum

    dgain = lax.fori_loop(0, heads, norm_back, jnp.zeros((1, HD), f32))
    grads_s = [jnp.zeros((HD, HD), f32) for _ in range(heads)]
    later.tick()
    for n in reversed(range(spans)):
        at = slice(n * SPAN, (n + 1) * SPAN)
        carried, same, ending = span_masks(r.segc, r.segr, n)
        for h in range(heads):
            head = slice(h * HD, (h + 1) * HD)
            g = grads_s[h].astype(bf16)
            gs[at, head] = g
            y = (ending * mm(ks[at, head], g)).astype(bf16)
            ys[at, head] = y
            if n:
                grads_s[h] = (
                    carried[SPAN - 1 : SPAN, :] * grads_s[h]
                    - mm_tn(ws[at, head], y)
                    + hs[at, head]
                )

    per_piece = piece // SPAN

    def spot(which, n):
        return (
            pieces // 2 + which // 2,
            slice((n % per_piece) * SPAN, (n % per_piece + 1) * SPAN),
            slice(
                ((which % 2) * pieces + n // per_piece) * HD,
                ((which % 2) * pieces + n // per_piece + 1) * HD,
            ),
        )

    def put(which, n, value):
        r.res[spot(which, n)] = value

    def taken(which):
        return jnp.concatenate([r.res[spot(which, n)] for n in range(spans)], axis=0)

    arrived(normed_in)
    pull_at = later.looped(heads)

    def pull(h, carry):
        head = lanes(h)
        pull_at(h)
        for n in range(spans):
            at = slice(n * SPAN, (n + 1) * SPAN)
            carried, same, ending = span_masks(r.segc, r.segr, n)
            which = h * spans + n
            q, k, v, f = qs[at, head], ks[at, head], vs[at, head], fs[at, head]
            state, g, p, inv = ss[which], gs[at, head], ps[which], ns[which]
            b = jax.nn.sigmoid(
                jnp.sum(jnp.where(lane == h, r.blog[at, :], 0.0), axis=-1, keepdims=True)
            )
            beta = jnp.broadcast_to(b, (SPAN, HD))
            small = douts[at, head]
            df = xs[at, head].astype(f32) + ys[at, head].astype(f32)
            z = df + mm_tn(inv, df.astype(bf16))
            zb = z.astype(bf16)
            dp = jnp.where(same & (i >= j), mm_nt(small, f), 0.0).astype(bf16)
            dl = jnp.where(same & (i > j), -mm_nt(zb, f), 0.0)
            known = v.astype(f32) - carried * mm(k, state)
            dbeta = jnp.sum(z * known + dl * mm_nt(k, k), axis=-1, keepdims=True)
            dlogit = dbeta * b * (1.0 - b)
            r.dlog[at, :] = jnp.where(
                lane == h, jnp.broadcast_to(dlogit, (SPAN, HD)), r.dlog[at, :]
            )
            e = (beta * dl).astype(bf16)
            put(0, n, carried * mm_nt(small, state) + mm(dp, k))
            put(2, n, beta * z)
            put(1, n, (
                mm(e, k)
                + mm_tn(e, k)
                + mm_tn(dp, q)
                - (carried * beta) * mm_nt(zb, state)
                + ending * mm_nt(f, g)
            ))
        for which in range(3):
            c = conv_of(r.dproj, r.taps, r.keep, which, h, heads)
            s = jax.nn.sigmoid(c)
            d = taken(which)
            if which < 2:
                w = c * s
                n = lax.rsqrt(jnp.sum(w * w, axis=-1, keepdims=True) + 1e-6)
                d = n * d - w * (n * n * n * jnp.sum(w * d, axis=-1, keepdims=True))
            dc = d * (s * (1.0 + c * (1.0 - s)))
            at = lanes(which * heads + h)
            value = r.dproj[:, at].astype(f32)
            total = None
            for o in range(CONV):
                row = which * CONV + CONV - 1 - o
                tap = r.taps[pl.ds(row, 1), lanes(h)]
                r.dtaps[pl.ds(row, 1), lanes(h)] = jnp.sum(
                    dc * shifted(value, r.keep, o), axis=0, keepdims=True
                )
                if o == 0:
                    total = tap * dc
                else:
                    total = total + tap * pltpu.roll(dc * r.keep[o - 1], rows - o, 0)
            r.dproj[:, at] = total.astype(bf16)
        grads = jnp.concatenate(
            [r.dproj[:, lanes(which * heads + h)] for which in range(3)], axis=1
        )
        for n in range(width // piece):
            at = slice(n * piece // share, (n + 1) * piece // share)
            r.g_q[h, at] = unflat(mm(r.theirs[n], grads), share)
        return carry

    lax.fori_loop(0, heads, pull, 0)

    weights_in = [
        loc.start(r.wmix_in.at[:, pl.ds(k * half, half)], r.sv.at[k]) for k in range(3)
    ]
    arrived(weights_in)

    def partial(which, at):
        n = which
        where = pl.ds(pl.multiple_of(n * piece, piece), piece)
        total = mm_nt(r.dlog[where, :].astype(bf16), r.wb[...])
        for k in range(3):
            total = total + mm_nt(r.dproj[where, k * half : (k + 1) * half], r.sv[k])
        r.mine[at] = total.astype(bf16)

    turn = [1 - pc.x, pc.x]
    sent = [rem.make(r.mine.at[2 + k], r.theirs3.at[k], "core") for k in turn]
    later.tick()
    for n, k in enumerate(turn):
        partial(2 * k + 1 - pc.t, 2 + k)
        sent[n].start()
    later.tick()
    for k in turn:
        partial(2 * k + pc.t, k)
    right = r.dlog[...].astype(bf16)
    g_beta = jnp.concatenate(
        [
            mm(r.theirs[n], right).astype(bf16)
            for n in range(width // piece)
        ],
        axis=0,
    )
    x_in = [
        loc.start(r.x_in.at[2 * k + pc.t], r.theirs.at[2 + k]) for k in range(pieces // 2)
    ]

    later.tick()
    arrived(x_in)
    arrived(last_in)
    g0 = r.gains[0:1, :]
    gain0 = jnp.zeros((1, width), f32)
    for n, k in enumerate(turn):
        sent[n].wait_recv()
        v = r.theirs[2 + k].astype(f32)
        grad = r.mine[k].astype(f32) + r.theirs3[k].astype(f32)
        inv = lax.rsqrt(jnp.mean(v * v, axis=-1, keepdims=True) + 1e-5)
        scaled = grad * g0
        back = inv * scaled - v * (inv * inv * inv * jnp.mean(scaled * v, axis=-1, keepdims=True))
        gain0 = gain0 + jnp.sum(grad * v * inv, axis=0, keepdims=True)
        r.theirs[k] = (back + r.res[k]).astype(bf16)
        if n == 0:
            crossing[1].start()
    loc.start(r.theirs.at[pc.x], r.dx_out.at[pc.x])
    r.cols[...] = jnp.zeros(r.cols.shape, f32)
    r.cols[0:1, :] = gain0
    r.cols[1:2, :] = r.gain1[0:1, :]
    r.cols[2 : 2 + 3 * CONV, cut(half, pc.t)] = r.dtaps[0 : 3 * CONV, :]
    place_r = lax.broadcasted_iota(jnp.int32, (HD, width), 0)
    place_c = lax.broadcasted_iota(jnp.int32, (HD, width), 1)
    spread = ((place_c // share * per + place_c % share == place_r) & (place_c % share < per)).astype(bf16)
    at = 2 + 3 * CONV + heads_all
    r.cols[at : at + 1, :] = mm(jnp.broadcast_to(dgain, (8, HD)).astype(bf16), spread)[0:1, :]
    pick_r = lax.broadcasted_iota(jnp.int32, (HD, HD), 0)
    pick_c = lax.broadcasted_iota(jnp.int32, (HD, HD), 1)
    chosen = ((pick_c == 2 + 3 * CONV + heads * pc.t + pick_r) & (pick_r < heads)).astype(bf16)
    beta = mm(g_beta, chosen)
    for n in range(width // SPAN):
        at = n * SPAN
        rows_in = jnp.concatenate(
            [r.cols[:, at : at + SPAN], jnp.zeros((HD - 32, SPAN), f32)], axis=0
        )
        block = jnp.transpose(rows_in) + beta[at : at + SPAN]
        r.g_small[at // share : (at + SPAN) // share] = unflat(block, share)
    later.finish()
    for s in streams:
        s.finish()
    for name in ("up", "out", "q", "small"):
        src, dst = r.__dict__["f_" + name], r.__dict__["o_" + name]
        loc.start(src.at[pc.t], dst.at[pc.t])
        crossing.append(rem.start(src.at[1 - pc.t], dst.at[pc.t], "core"))
    for copy in crossing:
        copy.wait_recv()
    for s in streams:
        s.drain(ordered)
    rem.drain()
    loc.done()


RETURNS = (
    ("up", None, 0, None, "zyx"),
    ("up", None, 1, None, "zxy"),
    ("out", None, None, None, "xyz"),
    ("q", 0, None, None, "zxy"),
    ("q", 1, None, None, "zyx"),
    ("q", 2, None, None, "zyx"),
    ("q", 3, None, None, "zyx"),
    ("small", None, None, None, "xyz"),
)


def backward(f, g, levels, per, heads_all):
    rows, width = f["normed2_out"].shape
    half = f["out_out"].shape[1]
    piece = rows // 4
    share = f["wo_out"].shape[1]
    heads = half // HD
    spans = rows // SPAN
    shards = levels * 8
    sds = jax.ShapeDtypeStruct
    ins = dict(
        dheaded_in=g["dheaded_out"], dres_in=g["dres_out"], gain1_in=g["gain1_out"],
        g_up_in=g["gup_out"], g_out_in=g["gout_out"], lo_in=g["result"],
        x_in=f["x_out"],
        gains_in=f["gains_out"], hgain_in=f["hgain_out"], taps_in=f["taps_out"],
        segc_in=f["segc_out"], segr_in=f["segr_out"], out_in=f["out_out"], blog_in=f["blog_out"], proj_in=f["proj_out"],
        normed_in=f["normt_out"], wmix_in=f["wmix_out"].reshape(width, 3 * half),
        wb_in=f["wb_out"].reshape(width, HD),
    )
    ins.update({k + "_in": f[k + "_out"] for k in ("qs", "ks", "vs", "fs", "ws", "ns", "ps", "ss")})
    cols = dict(up=(g["gup_out"].shape[2],), out=(half,), q=(3 * HD,), small=(HD,))
    tops = dict(up=(2,), out=(2,), q=(2, heads), small=(2,))
    outs = dict(
        dx_out=sds((2, piece, width), bf16),
        lo_out=sds((2, piece, width), bf16),
        **{"o_" + n: sds(tops[n] + (share,) + cols[n], f32) for n in cols},
    )
    scratch = dict(
        mine=VM((4, piece, width), bf16),
        theirs=VM((4, piece, width), bf16),
        theirs3=VM((2, piece, width), bf16),
        res=VM((4, piece, width), f32),
        gains=VM((8, width), f32),
        hgain=VM((8, HD), f32),
        taps=VM((16, half), f32),
        dtaps=VM((16, half), f32),
        segc=VM((rows, HD), f32),
        segr=VM((8, rows), f32),
        headed=VM((rows, half), bf16),
        gain1=VM((8, width), f32),
        datt=VM((2, rows, half), bf16),
        cols=VM((32, width), f32),
        g_out=VM((shards, share, half), bf16),
        g_q=VM((heads, shards, share, 3 * HD), bf16),
        g_small=VM((shards, share, HD), bf16),
        dheaded=VM((rows, half), bf16),
        sv=VM((5, rows, half), bf16),
        sq=VM((3, heads * spans, SPAN, SPAN), bf16),
        out=VM((rows, half), f32),
        blog=VM((rows, HD), f32),
        dproj=VM((rows, 3 * half), bf16),
        dlog=VM((rows, HD), f32),
        wb=VM((width, HD), bf16),
        keep=VM((CONV - 1, rows, HD), f32),
        g_up=VM(g["gup_out"].shape, bf16),
        **{"f_" + n: VM(tops[n] + (share,) + cols[n], f32) for n in cols},
        loc_sem=pltpu.SemaphoreType.DMA((64,)),
        send_sem=pltpu.SemaphoreType.DMA((16,)),
        recv_sem=pltpu.SemaphoreType.DMA((16,)),
    )
    for k, (name, h, hf, tiles, order) in enumerate(RETURNS):
        slots, sent = Scatter.slots_of(levels, order)
        first, last = span_of(tiles, sds((1, 1) + cols[name], bf16))
        both = () if hf is not None else (2,)
        scratch["room%d" % k] = VM((slots,) + both + (share, last - first), bf16)
        scratch["ss%d" % k] = pltpu.SemaphoreType.DMA((sent,))
        scratch["sr%d" % k] = pltpu.SemaphoreType.DMA((slots,))
    cfg = dict(
        heads=heads, spans=spans, per=per, share=share, width=width, half=half,
        heads_all=heads_all, piece=piece, rows=rows,
        program=[4.0] + [2.5] * heads + [5.0] + [7.0] * heads + [2.5] * 2 + [3.0],
    )
    return call(backward_kernel, ins, outs, scratch, 2, 63, levels, cfg)
SLACK_M = 2.0


MIDDLE = (
    ("down", 0, None, "zyx"),
    ("down", 1, None, "zxy"),
    ("gate", 0, None, "zyx"),
    ("gate", 1, (0, 4), "xyz"),
    ("gate", 1, (4, None), "zyx"),
)


def middle_kernel(r, levels, cfg):
    share, width, fhalf = cfg["share"], cfg["width"], cfg["fhalf"]
    piece, rows = cfg["piece"], cfg["rows"]
    pieces = rows // piece
    pc = Place(levels)
    loc = Local(Sems(r.loc_sem))
    rem = Remote(pc, Sems(r.send_sem), Sems(r.recv_sem))
    loads = [
        [loc.start(a, b) for a, b in group]
        for group in (
            ((r.dy_in, r.dy), (r.act_in, r.act)),
            ((r.w_down_in, r.w_down),),
            ((r.fgate_in, r.fgate), (r.fup_in, r.fup)),
            ((r.normed2_in, r.normed2), (r.w_gu_in, r.w_gu)),
            ((r.gains_in, r.gains), (r.wo_in, r.wo)),
        )
    ]

    def loaded(k):
        for copy in loads[k]:
            loc.wait(copy)

    residuals = [loc.start(r.res_in.at[n], r.res.at[n]) for n in range(pieces)]
    pc.meet(NEIGHBOURS)
    grads = dict(down=r.g_down, gate=r.w_down)
    streams = [
        Scatter(pc, grads[name], r.__dict__["room%d" % k], r.__dict__["f_" + name], hf,
                span_of(cols, grads[name]), order, r.__dict__["ss%d" % k], r.__dict__["sr%d" % k])
        for k, (name, hf, cols, order) in enumerate(MIDDLE)
    ]
    mb = lambda n, m: 2e-6 * n * m
    steps = scatter_steps(
        streams, [int(name == "gate") for name, *_ in MIDDLE],
        [mb(share, s.cols.stop - s.cols.start) for s in streams], levels,
    )
    later = Planned(
        plan(steps, cfg["program"], levels, {0: 0.0}, {}, SLACK_M, {3 * pieces: [1]})[0]
    )
    ordered = blocks_of(levels)

    loaded(0)
    dy = r.dy[...].reshape(rows, width)
    strip = width // 4
    for n in range(4):
        at = slice(n * strip // share, (n + 1) * strip // share)
        r.g_down[at] = unflat(
            mm_tn(dy[:, n * strip : (n + 1) * strip], r.act[...]), share
        )
    later.tick()

    loaded(1)
    w_down = flat(r.w_down, slice(None))
    sent = []
    for k in range(pieces // 2):
        which = 2 * k + 1 - pc.t
        at = pl.ds(pl.multiple_of(which * piece, piece), piece)
        r.mine[2 + k] = mm_nt(r.act[at, :], w_down).astype(bf16)
        sent.append(rem.start(r.mine.at[2 + k], r.theirs.at[k], "core"))
    later.tick()
    for k in range(pieces // 2):
        which = 2 * k + pc.t
        at = pl.ds(pl.multiple_of(which * piece, piece), piece)
        r.mine[k] = mm_nt(r.act[at, :], w_down).astype(bf16)
    loaded(2)
    for n in range(pieces):
        later.tick()
        at = slice(n * piece, (n + 1) * piece)
        dact = mm(r.dy[n], w_down)
        r.dgu[at, :fhalf] = (dact * r.fgate[at, :].astype(f32)).astype(bf16)
        r.dgu[at, fhalf:] = (dact * r.fup[at, :].astype(f32)).astype(bf16)
    later.tick()
    for copy in residuals:
        loc.wait(copy)
    for k in range(pieces // 2):
        sent[k].wait_recv()
        r.mine[k] = (
            r.res[2 * k + pc.t] + r.mine[k].astype(f32) + r.theirs[k].astype(f32)
        ).astype(bf16)
        loc.start(r.mine.at[k], r.result.at[k])

    loaded(3)
    w_gu = flat(r.w_gu, slice(None))
    parts, writes = [], []
    for n in range(pieces):
        later.tick()
        at = slice(n * piece, (n + 1) * piece)
        r.part[n] = mm_nt(r.dgu[at, :], w_gu).astype(bf16)
        parts.append(rem.start(r.part.at[n], r.theirs2.at[n], "core"))
    later.tick()
    for n in range(4):
        at = slice(n * strip // share, (n + 1) * strip // share)
        r.w_down[at] = unflat(
            mm_tn(r.normed2[:, n * strip : (n + 1) * strip], r.dgu[:, :fhalf]), share
        )

    half = width // 2
    halves = [slice(c * half, (c + 1) * half) for c in range(2)]
    headed_in = loc.start(r.headed_in, r.fup.at[:, pl.ds(half, half)])
    loaded(4)
    g1 = r.gains[1:2, :]
    gain1 = jnp.zeros((1, width), f32)
    for n in range(pieces):
        later.tick()
        parts[n].wait_recv()
        at = slice(n * piece, (n + 1) * piece)
        v = r.res[n]
        grad = r.part[n].astype(f32) + r.theirs2[n].astype(f32)
        inv = lax.rsqrt(jnp.mean(v * v, axis=-1, keepdims=True) + 1e-5)
        scaled = grad * g1
        back = inv * scaled - v * (inv * inv * inv * jnp.mean(scaled * v, axis=-1, keepdims=True))
        ours = (pc.t == n % 2).astype(f32)
        gain1 = gain1 + ours * jnp.sum(grad * v * inv, axis=0, keepdims=True)
        dres = back + r.dy[n].astype(f32)
        r.res[n] = dres
        low = dres.astype(bf16)
        r.fgate[at, 0:width] = low
    r.gains[...] = jnp.broadcast_to(gain1, r.gains.shape)
    loc.start(r.gains, r.gain1_out)
    for k in range(pieces // 2):
        loc.start(r.res.at[2 * k + pc.t], r.dres_out.at[k])

    later.tick()
    wo = flat(r.wo, slice(None))
    for n in range(pieces):
        at = slice(n * piece, (n + 1) * piece)
        r.fup[at, 0:half] = mm_nt(r.fgate[at, 0:width], wo).astype(bf16)
    loc.start(r.fup.at[:, pl.ds(0, half)], r.dheaded_out)
    later.tick()
    loc.wait(headed_in)
    for c in range(2):
        for n in range(half // piece):
            left = r.fup[:, half + n * piece : half + (n + 1) * piece]
            at = slice(n * piece // share, (n + 1) * piece // share)
            r.wo[at, :, halves[c]] = unflat(mm_tn(left, r.fgate[:, halves[c]]), share)
    shards = levels * 8 // 2
    ours = pl.ds(pl.multiple_of(pc.t * shards, shards), shards)
    side = lambda t: pl.ds(pl.multiple_of(t * half, half), half)
    loc.start(r.wo.at[:, :, side(pc.t)], r.gout_out.at[ours])
    gout = rem.start(r.wo.at[:, :, side(1 - pc.t)], r.gout_out.at[ours], "core")
    later.tick()
    for n in range(4):
        at = slice(n * strip // share, (n + 1) * strip // share)
        if n > 1:
            loc.wait(writes[n - 2])
        r.gup[n % 2] = unflat(
            mm_tn(r.normed2[:, n * strip : (n + 1) * strip], r.dgu[:, fhalf:]), share
        )
        writes.append(loc.start(r.gup.at[n % 2], r.gup_out.at[pl.ds(at.start, strip // share)]))
    gout.wait_recv()
    later.finish()
    for s in streams:
        s.finish()
    last = []
    for src, dst in ((r.f_down, r.o_down), (r.f_gate, r.o_gate)):
        loc.start(src.at[pc.t], dst.at[pc.t])
        last.append(rem.start(src.at[1 - pc.t], dst.at[pc.t], "core"))
    for copy in last:
        copy.wait_recv()
    for s in streams:
        s.drain(ordered)
    rem.drain()
    loc.done()


def middle(f, levels):
    shards, share, two = f["w_gu_out"].shape
    fhalf = two // 2
    rows, width = f["normed2_out"].shape
    piece = rows // 4
    sds = jax.ShapeDtypeStruct
    ins = dict(
        dy_in=f["dy"], act_in=f["act_out"], w_down_in=f["w_down"], fgate_in=f["fgate_out"],
        fup_in=f["fup_out"], normed2_in=f["normed2_out"], w_gu_in=f["w_gu_out"],
        res_in=f["res_out"].reshape(4, piece, width), gains_in=f["gains_out"],
        wo_in=f["wo_out"], headed_in=f["headed_out"],
    )
    outs = dict(
        gup_out=sds((shards, share, fhalf), bf16),
        gout_out=sds((shards, share, width // 2), bf16),
        dheaded_out=sds((rows, width // 2), bf16),
        dres_out=sds((2, piece, width), f32),
        gain1_out=sds((8, width), f32),
        o_gate=sds((2, share, fhalf), f32),
        result=sds((2, piece, width), bf16),
        o_down=sds((2, share, fhalf), f32),
    )
    scratch = dict(
        dy=VM((4, piece, width), bf16),
        act=VM((rows, fhalf), bf16),
        w_down=VM((shards, share, fhalf), bf16),
        fgate=VM((rows, fhalf), bf16),
        fup=VM((rows, fhalf), bf16),
        normed2=VM((rows, width), bf16),
        w_gu=VM((shards, share, two), bf16),
        res=VM((4, piece, width), f32),
        gains=VM((8, width), f32),
        wo=VM((shards // 2, share, width), bf16),
        theirs2=VM((4, piece, width), bf16),
        f_gate=VM((2, share, fhalf), f32),
        mine=VM((4, piece, width), bf16),
        theirs=VM((2, piece, width), bf16),
        part=VM((4, piece, width), bf16),
        dgu=VM((rows, two), bf16),
        g_down=VM((shards, share, fhalf), bf16),
        f_down=VM((2, share, fhalf), f32),
        gup=VM((2, shards // 4, share, fhalf), bf16),
        loc_sem=pltpu.SemaphoreType.DMA((40,)),
        send_sem=pltpu.SemaphoreType.DMA((16,)),
        recv_sem=pltpu.SemaphoreType.DMA((16,)),
    )
    for k, (name, hf, cols, order) in enumerate(MIDDLE):
        slots, sent = Scatter.slots_of(levels, order)
        first, last = span_of(cols, f["w_down"])
        scratch["room%d" % k] = VM((slots, share, last - first), bf16)
        scratch["ss%d" % k] = pltpu.SemaphoreType.DMA((sent,))
        scratch["sr%d" % k] = pltpu.SemaphoreType.DMA((slots,))
    cfg = dict(
        share=share, width=width, fhalf=fhalf, piece=piece, rows=rows,
        program=[2.5, 2.5] + [1.0] * 4 + [2.0] + [1.8] * 4 + [4.0] + [1.5] * 4 + [4.0, 3.0, 4.0],
    )
    return call(middle_kernel, ins, outs, scratch, 4, 63, levels, cfg)


def body(tokens, cotangent, starts, norm_gain, qkv_weight, conv_weight, beta_weight,
         head_gain, out_weight, gate_up_weight, down_weight):
    levels = lax.axis_size("dp") // 2
    ctx = lax.axis_size("ctx")
    device = lax.axis_index("dp") * ctx + lax.axis_index("ctx")
    t = lax.axis_index("ctx") % 2
    m = lax.axis_index("ctx") // 2
    batches, _, piece, width = tokens.shape
    rows = ctx * piece
    share = qkv_weight.shape[1]
    hidden = gate_up_weight.shape[2]
    half, fhalf = width // 2, hidden // 2
    heads_all = beta_weight.shape[1]
    heads = heads_all // 2
    per = head_gain.shape[0]
    small = 2 + 3 * CONV + heads_all + 1

    gain_rows = jnp.zeros((share, 1), bf16).at[:per, 0].set(head_gain)
    ext = jnp.concatenate(
        [norm_gain.T, conv_weight.T, beta_weight, gain_rows, jnp.zeros((share, HD - small), bf16)],
        axis=1,
    )
    flags = jnp.broadcast_to(
        starts.reshape(batches, piece, 1).astype(bf16), (batches, piece, HD)
    )
    f = forward(
        qkv_weight, out_weight, gate_up_weight, down_weight, ext,
        tokens[:, 0], cotangent[:, 0], flags, levels, per, heads_all,
    )
    g = middle(f, levels)
    b = backward(f, g, levels, per, heads_all)
    join = lambda o, n: jnp.moveaxis(o.reshape(2, share, n, -1), (2, 1), (0, 1)).reshape(n, share, -1)
    o_small = jnp.sum(b["o_small"], axis=0)
    o_q = b["o_q"].reshape(2, half // HD, share, 3, HD)
    return (
        b["lo_out"][:, None],
        b["dx_out"][:, None],
        o_small[:, 0:2].T,
        jnp.transpose(o_q, (3, 2, 0, 1, 4)).reshape(3, share, width),
        o_small[:, 2 : 2 + 3 * CONV].T,
        o_small[:, 2 + 3 * CONV : 2 + 3 * CONV + heads_all],
        o_small[:per, small - 1],
        join(b["o_out"], 1)[0],
        jnp.stack([join(g["o_gate"], 1)[0], join(b["o_up"], 1)[0]]),
        join(g["o_down"], 1)[0],
    )


def solution(mesh):
    both = ("dp", "ctx")
    acts = P(None, "dp", "ctx", None)
    return jax.shard_map(
        body,
        mesh=mesh,
        in_specs=(
            acts,
            acts,
            P(None, "dp", "ctx"),
            P(None, both),
            P(None, both, None),
            P(None, both),
            P(both, None),
            P(both),
            P(both, None),
            P(None, both, None),
            P(both, None),
        ),
        out_specs=(
            acts,
            acts,
            P(None, both),
            P(None, both, None),
            P(None, both),
            P(both, None),
            P(both),
            P(both, None),
            P(None, both, None),
            P(both, None),
        ),
        check_vma=False,
    )
```
